32 devices in a mesh: strip: 8 (over y, x, core), frame: 4 (over z).
Axes of the slice: x: 2, y: 2, z: 4, core: 2. Of those that a mesh axis runs over, the one named last changes fastest.
Arguments:
- estimate: float32 [1024, 2048], P('strip'), may hold values from -6 to 6
- observed: float32 [8, 1024, 2048], P('frame', 'strip'), may hold values from -6 to 6
- weights: float32 [8, 1024, 2048], P('frame', 'strip'), may hold values from 0.3 to 9, as said below
- column_kernels: float32 [8, 65], P('frame'), may hold values from 0.05 to 1
- row_kernels: float32 [8, 65], P('frame'), may hold values from 0.05 to 1
Outputs:
- solution: float32 [1024, 2048], P('strip')
- residual: float32 [1024, 2048], P('strip')
The draws below stay inside these ranges and needn't reach their ends.
Inputs may be any that keep to these rules, and one draw needn't show every extreme that they name: Positive weights of each pixel.
All inputs are finite; a program needn't handle non-finite values.
Results may differ from the reference program's by a relative error of at most 0.00013.
Values sent between devices are 32-bit elements; how exact they have to be, the bound alone decides.
No kernel may reach another device: no remote copies, remote signals or barrier semaphores. Data moves between devices by JAX's collectives and lax.ppermute only.
A program may use at most 128 MiB of HBM per device.

```python
import math
import jax
import jax.numpy as jnp
from jax import lax

NC = 2048
TAPS = 65
ITERS = 2
NR = 1024
FRAMES = 8


def draw_weights(key, part):
    base = jnp.exp(jax.random.uniform(key, (FRAMES, NR, NC), jnp.float32, math.log(0.3), math.log(3.0)))
    rising = 3.0 ** (jnp.arange(NR).astype(jnp.float32) / NR)
    return base * rising[None, :, None]


def levels(key, extent, split, least, top_value):
    loudness = 1.0
    for dim, shards_of in split:
        steps = jax.random.uniform(jax.random.fold_in(jax.random.fold_in(key, 6), dim), (shards_of,), jnp.float32, least / len(split), top_value / len(split))
        loudness = loudness * jnp.repeat(jnp.exp(steps), extent[dim] // shards_of).reshape((-1,) + (1,) * (len(extent) - 1 - dim))
    return loudness


def normal_values(own_key, dims, scale, limit, split=(), kind=jnp.bfloat16):
    values = jax.random.normal(own_key, dims, jnp.float32) * scale
    if len(split) > 0:
        values = levels(own_key, dims, split, -0.22, 0.18) * values
    return jnp.clip(values, min=-limit, max=limit).astype(kind)


def setup_inputs(seed: int = 0) -> dict:
    key_of = jax.random.split(jax.random.key(seed), 6)
    estimate = normal_values(key_of[0], (NR, NC), 1.0, 6.0, ((0, 8),), jnp.float32)
    observed = normal_values(key_of[1], (FRAMES, NR, NC), 1.0, 6.0, ((0, 4), (1, 8)), jnp.float32)
    weights = draw_weights(jax.random.fold_in(key_of[5], 71), 0)
    column_kernels = jnp.clip(jnp.exp(math.log(1.0) - 2.9957323 * jax.random.uniform(key_of[3], (FRAMES, TAPS), jnp.float32) ** levels(key_of[3], (FRAMES, TAPS), ((0, 4),), -0.2, 0.2)), 0.05, 1.0)
    row_kernels = jnp.clip(jnp.exp(math.log(1.0) - 2.9957323 * jax.random.uniform(key_of[4], (FRAMES, TAPS), jnp.float32) ** levels(key_of[4], (FRAMES, TAPS), ((0, 4),), -0.2, 0.2)), 0.05, 1.0)
    return {"estimate": estimate, "observed": observed, "weights": weights, "column_kernels": column_kernels, "row_kernels": row_kernels}


damping = 0.05
highest = lax.Precision.HIGHEST


def unit_kernels(kernels):
    return kernels / jnp.sum(kernels, axis=1, keepdims=True)


def single_band(kernel):
    width = kernel.shape[0]
    offset = jnp.arange(256)[:, None] - jnp.arange(128)[None, :] - (width // 2)
    onehot = (offset[:, :, None] == jnp.arange(width)[None, None, :]).astype(jnp.float32)
    return jnp.einsum("amt,t->am", onehot, kernel, precision=highest)


def conv_last(values_in, kernel):
    length = values_in.shape[-1]
    blocks = length // 128
    padded = jnp.pad(values_in, ((0, 0), (64, 64)))
    left_part = padded[:, :length].reshape(values_in.shape[0], blocks, 128)
    right_part = padded[:, 128:length + 128].reshape(values_in.shape[0], blocks, 128)
    window = jnp.concatenate([left_part, right_part], axis=-1)
    result = jnp.einsum("rna,am->rnm", window, single_band(kernel), precision=highest)
    return result.reshape(values_in.shape)


def forward(image, col_kernel, row_kernel):
    spread = conv_last(image, col_kernel)
    return conv_last(spread.T, row_kernel).T


def backward(values_in, col_kernel, row_kernel):
    rows_back = conv_last(values_in.T, row_kernel[::-1]).T
    return conv_last(rows_back, col_kernel[::-1])


def reference(estimate, observed, weights, column_kernels, row_kernels):
    col_unit = unit_kernels(column_kernels)
    row_unit = unit_kernels(row_kernels)

    def normal(image, factor):
        def one_frame(total, items):
            col_kernel, row_kernel, weight_now, observed_now = items
            misfit = forward(image, col_kernel, row_kernel) - factor * observed_now
            return total + backward(weight_now * misfit, col_kernel, row_kernel), None

        total, unused = lax.scan(one_frame, jnp.zeros_like(image), (col_unit, row_unit, weights, observed))
        return total

    solution = estimate
    residual = -(normal(estimate, 1.0) + damping * estimate)
    direction = residual
    norm_now = jnp.sum(residual * residual)
    for iteration in range(ITERS):
        image = normal(direction, 0.0) + damping * direction
        alpha = norm_now / jnp.sum(direction * image)
        solution = solution + alpha * direction
        residual = residual - alpha * image
        norm_next = jnp.sum(residual * residual)
        direction = residual + (norm_next / norm_now) * direction
        norm_now = norm_next
    return solution, residual
```

```python
import functools

import jax
import jax.numpy as jnp
from jax import lax
from jax.experimental import pallas as pl
from jax.experimental.pallas import tpu as pltpu
from jax.sharding import PartitionSpec as P

damping = 0.05
f32 = jnp.float32
bf16 = jnp.bfloat16
LANE = 128
VMEM = pl.BlockSpec(memory_space=pltpu.VMEM)
ANY = pl.BlockSpec(memory_space=pl.ANY)


def split(x):
    hi = x.astype(bf16)
    lo = (x - hi.astype(f32)).astype(bf16)
    return hi, lo


def dot(a, b):
    return jnp.dot(a, b, preferred_element_type=f32)


def tiles(width, step=256):
    return [(s, min(step, width - s)) for s in range(0, width, step)]


def kernel_bases(col_unit, row_unit):
    count, taps = col_unit.shape
    wide = 2 * LANE

    def at(values, start):
        return jnp.pad(values, ((0, 0), (start, wide - taps - start)))

    def turned(values):
        gap = jnp.zeros((count, wide - taps), f32)
        return jnp.concatenate([values[:, :1], gap, values[:, :0:-1]], axis=1)

    return jnp.stack(
        [at(row_unit, 0), turned(col_unit), at(col_unit, LANE), turned(row_unit)], axis=1
    )


def setup_kernel(per_group, rows, halo, base_ref, t_ref, b_ref, bp_ref, ta_ref):
    frames = base_ref.shape[0]

    def toeplitz(f, which, count):
        base = jnp.broadcast_to(base_ref[f, which : which + 1, :], (count, 2 * LANE))
        return pltpu.roll(base, 0, 1, stride=1, stride_axis=0)

    ext = rows + 2 * halo
    for f in range(frames):
        hi, lo = split(toeplitz(f, 0, rows))
        t_ref[f, :rows, :] = hi
        t_ref[f, rows:, :] = lo
        hi, lo = split(toeplitz(f, 1, 2 * LANE)[:, :LANE])
        b_ref[f, :, :LANE] = hi
        b_ref[f, :, LANE:] = lo
        hi, lo = split(toeplitz(f, 2, 2 * LANE)[:, :LANE])
        bp_ref[f, :, :LANE] = hi
        bp_ref[f, :, LANE:] = lo
        hi, lo = split(toeplitz(f, 3, ext)[:, :rows])
        g, s = divmod(f, per_group)
        ta_ref[g, :ext, s * rows : (s + 1) * rows] = hi
        ta_ref[g, ext:, s * rows : (s + 1) * rows] = lo


def setup_matrices(bases, per_group, rows, halo):
    frames = bases.shape[0]
    ext = rows + 2 * halo
    shapes = (
        (frames, 2 * rows, 2 * LANE),
        (frames, 2 * LANE, 2 * LANE),
        (frames, 2 * LANE, 2 * LANE),
        (frames // per_group, 2 * ext, per_group * rows),
    )
    return pl.pallas_call(
        functools.partial(setup_kernel, per_group, rows, halo),
        out_shape=[jax.ShapeDtypeStruct(s, bf16) for s in shapes],
        in_specs=[VMEM],
        out_specs=[VMEM] * 4,
        name="setup_matrices",
    )(bases)


def load_image(y_hi, y_lo, image, halo):
    ext, full = image.shape
    shift = LANE - halo
    y = pltpu.roll(image, full - shift, 1)[:, : full - LANE]
    hi, lo = split(y)
    y_hi[:ext, :] = hi
    y_lo[:ext, :] = lo


def group_terms(frames, rows, w, y_hi, y_lo, t, b, bp, ta, weight, data, us, qs, vs_hi, vs_lo, acc, stat):
    total = None
    for f in range(frames):
        for c, size in tiles(w + LANE):
            r1 = dot(t(f)[...], y_hi[:, c : c + size])
            r2 = dot(t(f)[:rows, :], y_lo[:, c : c + size])
            hi, lo = split(r1[:rows] + r1[rows:] + r2)
            us[:rows, c : c + size] = hi
            us[rows:, c : c + size] = lo
        for k in range(w // LANE):
            c = k * LANE
            r = dot(us[:, c : c + 2 * LANE], b(f)[...])
            a = r[:rows, :LANE] + r[:rows, LANE:] + r[rows:, :LANE]
            if data is not None:
                a = a - data(f)[:, c : c + LANE]
            q = weight(f)[:, c : c + LANE] * a
            if stat is not None:
                part = jnp.sum((a * q).reshape(rows // 8, 8, LANE), axis=0)
                total = part if total is None else total + part
            hi, lo = split(q)
            qs[:rows, c + LANE : c + 2 * LANE] = hi
            qs[rows:, c + LANE : c + 2 * LANE] = lo
        for k in range(w // LANE + 1):
            c = k * LANE
            r = dot(qs[:, c : c + 2 * LANE], bp(f)[...])
            hi, lo = split(r[:rows, :LANE] + r[:rows, LANE:] + r[rows:, :LANE])
            vs_hi[f * rows : (f + 1) * rows, c : c + LANE] = hi
            vs_lo[f * rows : (f + 1) * rows, c : c + LANE] = lo
    ext = acc.shape[0]
    for c, size in tiles(w + LANE):
        r1 = dot(ta[...], vs_hi[:, c : c + size])
        r2 = dot(ta[:ext, :], vs_lo[:, c : c + size])
        acc[:, c : c + size] += r1[:ext] + r1[ext:] + r2
    if stat is not None:
        stat[...] += total


def work_scratch(frames, rows, halo, w):
    ext = rows + 2 * halo
    return [
        pltpu.VMEM((2 * LANE, w + LANE), bf16),
        pltpu.VMEM((2 * LANE, w + LANE), bf16),
        pltpu.VMEM((2 * rows, w + LANE), bf16),
        pltpu.VMEM((2 * rows, w + 2 * LANE), bf16),
        pltpu.VMEM((frames * rows, w + LANE), bf16),
        pltpu.VMEM((frames * rows, w + LANE), bf16),
        pltpu.VMEM((ext, w + LANE), f32),
    ]


def clear_edges(y_hi, y_lo, qs, ext, rows, w):
    zero = jnp.zeros((y_hi.shape[0] - ext, y_hi.shape[1]), bf16)
    y_hi[ext:, :] = zero
    y_lo[ext:, :] = zero
    qs[:, :LANE] = jnp.zeros((2 * rows, LANE), bf16)
    qs[:, w + LANE :] = jnp.zeros((2 * rows, LANE), bf16)


def unshift(acc, halo):
    return pltpu.roll(acc, acc.shape[1] - halo, 1)


def first_kernel(
    frames, rows, halo, w,
    est, lo, hi, t_ref, b_ref, bp_ref, ta_ref, w_hbm, d_hbm,
    top, mid, bot,
    y_hi, y_lo, us, qs, vs_hi, vs_lo, acc, estp, outp, wbuf, dbuf, sem,
):
    ext = rows + 2 * halo
    cols = est.shape[1]
    blocks = cols // w

    def copies(j, slot):
        window = pl.ds(pl.multiple_of(j * w, LANE), w)
        return (
            pltpu.make_async_copy(w_hbm.at[:, :, window], wbuf.at[slot], sem.at[0, slot]),
            pltpu.make_async_copy(d_hbm.at[:, :, window], dbuf.at[slot], sem.at[1, slot]),
        )

    for c in copies(0, 0):
        c.start()
    clear_edges(y_hi, y_lo, qs, ext, rows, w)
    for edge in (0, LANE + cols):
        estp[:, edge : edge + LANE] = jnp.zeros((ext, LANE), f32)
    inner = slice(LANE, LANE + cols)
    estp[:halo, inner] = lo[...]
    estp[halo : halo + rows, inner] = est[...]
    estp[halo + rows :, inner] = hi[...]
    outp[...] = jnp.zeros_like(outp)
    lane = lax.broadcasted_iota(jnp.int32, (ext, LANE), 1)

    @pl.loop(0, blocks)
    def _(j):
        slot = lax.rem(j, 2)

        @pl.when(j + 1 < blocks)
        def _():
            for c in copies(j + 1, 1 - slot):
                c.start()

        start = pl.multiple_of(j * w, LANE)
        load_image(y_hi, y_lo, estp[:, pl.ds(start, w + 2 * LANE)], halo)
        acc[...] = jnp.zeros_like(acc)
        for c in copies(j, slot):
            c.wait()
        group_terms(
            frames, rows, w, y_hi, y_lo,
            lambda f: t_ref.at[f], lambda f: b_ref.at[f], lambda f: bp_ref.at[f], ta_ref.at[0],
            lambda f: wbuf.at[slot, f], lambda f: dbuf.at[slot, f],
            us, qs, vs_hi, vs_lo, acc, None,
        )
        z = unshift(acc[...], halo)
        edge = z[:, w:]
        outp[:, pl.ds(start, LANE)] += jnp.where(lane >= LANE - halo, edge, 0.0)
        outp[:, pl.ds(pl.multiple_of(start + LANE, LANE), w)] += z[:, :w]
        outp[:, pl.ds(pl.multiple_of(start + LANE + w, LANE), LANE)] += jnp.where(lane < halo, edge, 0.0)

    top[...] = outp[:halo, inner]
    mid[...] = outp[halo : halo + rows, inner]
    bot[...] = outp[halo + rows :, inner]


def first_terms(est, lo, hi, mats, weights, observed, w):
    frames, rows, cols = weights.shape
    halo = lo.shape[0]
    ext = rows + 2 * halo
    return pl.pallas_call(
        functools.partial(first_kernel, frames, rows, halo, w),
        out_shape=[
            jax.ShapeDtypeStruct((halo, cols), f32),
            jax.ShapeDtypeStruct((rows, cols), f32),
            jax.ShapeDtypeStruct((halo, cols), f32),
        ],
        in_specs=[VMEM] * 7 + [ANY, ANY],
        out_specs=[VMEM] * 3,
        scratch_shapes=work_scratch(frames, rows, halo, w)
        + [
            pltpu.VMEM((ext, cols + 2 * LANE), f32),
            pltpu.VMEM((ext, cols + 2 * LANE), f32),
            pltpu.VMEM((2, frames, rows, w), f32),
            pltpu.VMEM((2, frames, rows, w), f32),
            pltpu.SemaphoreType.DMA((2, 2)),
        ],
        cost_estimate=pl.CostEstimate(flops=8 * 10**9, bytes_accessed=8 * 2**20, transcendentals=0),
        name="first_terms",
    )(est, lo, hi, *mats, weights, observed)


def apply_kernel(frames, rows, halo, w, groups, base, has_acc, final, *refs):
    image, t_hbm, b_hbm, bp_hbm, ta_hbm = refs[:5]
    weights = refs[5 : 5 + groups]
    refs = refs[5 + groups :]
    if has_acc:
        acc_in, stat_in = refs[:2]
        refs = refs[2:]
    out, stat, y_hi, y_lo, us, qs, vs_hi, vs_lo, acc, tb, bb, bpb, tab, wbuf, sem = refs
    ext = rows + 2 * halo

    def copies(g):
        span = pl.ds((base + g) * frames, frames)
        return [
            pltpu.make_async_copy(t_hbm.at[span], tb.at[g], sem.at[0, g]),
            pltpu.make_async_copy(b_hbm.at[span], bb.at[g], sem.at[1, g]),
            pltpu.make_async_copy(bp_hbm.at[span], bpb.at[g], sem.at[2, g]),
            pltpu.make_async_copy(ta_hbm.at[base + g], tab.at[g], sem.at[3, g]),
        ]

    for g in range(groups):
        for c in copies(g):
            c.start()
        pltpu.make_async_copy(weights[g], wbuf.at[g], sem.at[4, g]).start()
    clear_edges(y_hi, y_lo, qs, ext, rows, w)
    load_image(y_hi, y_lo, image[...], halo)
    if has_acc:
        acc[...] = acc_in[...]
        stat[...] = stat_in[...]
    else:
        acc[...] = jnp.zeros_like(acc)
        stat[...] = jnp.zeros_like(stat)

    @pl.loop(0, groups)
    def _(g):
        for c in copies(g):
            c.wait()
        pltpu.make_async_copy(weights[0], wbuf.at[g], sem.at[4, g]).wait()
        group_terms(
            frames, rows, w, y_hi, y_lo,
            lambda f: tb.at[g, f], lambda f: bb.at[g, f], lambda f: bpb.at[g, f], tab.at[g],
            lambda f: wbuf.at[g, f], None,
            us, qs, vs_hi, vs_lo, acc, stat,
        )

    out[...] = unshift(acc[...], halo) if final else acc[...]


def apply_terms(image, mats, weights, base, halo, carry=None, final=True):
    frames, rows, w = weights[0].shape
    ext = rows + 2 * halo
    groups = len(weights)
    t, b, bp, ta = mats
    args = [image, t, b, bp, ta, *weights]
    specs = [VMEM] + [ANY] * (4 + groups)
    if carry is not None:
        args += list(carry)
        specs += [VMEM, VMEM]
    return pl.pallas_call(
        functools.partial(apply_kernel, frames, rows, halo, w, groups, base, carry is not None, final),
        out_shape=[
            jax.ShapeDtypeStruct((ext, w + LANE), f32),
            jax.ShapeDtypeStruct((8, LANE), f32),
        ],
        in_specs=specs,
        out_specs=[VMEM, VMEM],
        scratch_shapes=work_scratch(frames, rows, halo, w)
        + [
            pltpu.VMEM((groups, frames) + t.shape[1:], bf16),
            pltpu.VMEM((groups, frames) + b.shape[1:], bf16),
            pltpu.VMEM((groups, frames) + bp.shape[1:], bf16),
            pltpu.VMEM((groups,) + ta.shape[1:], bf16),
            pltpu.VMEM((groups, frames, rows, w), f32),
            pltpu.SemaphoreType.DMA((5, groups)),
        ],
        cost_estimate=pl.CostEstimate(
            flops=groups * 3 * 10**9, bytes_accessed=groups * 2**20, transcendentals=0
        ),
        name="apply_terms",
    )(*args)


def shift_up(x, axis):
    n = lax.axis_size(axis)
    return lax.ppermute(x, axis, [(i, i + 1) for i in range(n - 1)])


def shift_down(x, axis):
    n = lax.axis_size(axis)
    return lax.ppermute(x, axis, [(i + 1, i) for i in range(n - 1)])


def swap(x, axis, distance):
    n = lax.axis_size(axis)
    return lax.ppermute(x, axis, [(i, i ^ distance) for i in range(n)])


def body(estimate, observed, weights, column_kernels, row_kernels):
    n = lax.axis_size("frame")
    me = lax.axis_index("frame")
    strips = lax.axis_size("strip")
    strip = lax.axis_index("strip")
    rows, cols = estimate.shape
    frames = weights.shape[0]
    halo = column_kernels.shape[1] // 2
    w = cols // n
    ext = rows + 2 * halo
    distances = [1 << k for k in range(n.bit_length() - 1)]

    unit = lambda k: k / jnp.sum(k, axis=1, keepdims=True)
    bases = kernel_bases(unit(column_kernels), unit(row_kernels))
    est_lo = shift_up(estimate[rows - halo :], "strip")
    est_hi = shift_down(estimate[:halo], "strip")

    def block_of(x, j):
        return lax.dynamic_slice_in_dim(x, j * w, w, axis=x.ndim - 1)

    my_weights = [block_of(weights, me)]
    for d in range(1, n):
        my_weights.append(swap(block_of(weights, me ^ d), "frame", d))

    own_mats = setup_matrices(bases, frames, rows, halo)
    top, mid, bot = first_terms(estimate, est_lo, est_hi, own_mats, weights, observed, w)

    all_bases = bases
    for d in distances:
        all_bases = jnp.concatenate([all_bases, swap(all_bases, "frame", d)], axis=0)
    mats = setup_matrices(all_bases, frames, rows, halo)

    from_up = shift_up(bot, "strip")
    from_dn = shift_down(top, "strip")
    terms = jnp.concatenate(
        [mid[:halo] + from_up, mid[halo : rows - halo], mid[rows - halo :] + from_dn], axis=0
    )

    left = terms
    for k, d in enumerate(distances):
        bit = (me // d) % 2
        half = left.shape[1] // w // 2

        def pick(which, left=left, half=half):
            return jnp.concatenate(
                [block_of(left, 2 * i + which) for i in range(half)], axis=1
            )

        left = pick(bit) + swap(pick(1 - bit), "frame", d)
    k0 = -(left + damping * block_of(estimate, me))

    lane = lax.broadcasted_iota(jnp.int32, (ext, LANE), 1)
    row = lax.broadcasted_iota(jnp.int32, (ext, 1), 0)
    inside = ((row >= halo) | (strip > 0)) & ((row < halo + rows) | (strip < strips - 1))
    first = me == 0
    last = me == n - 1

    k0_rows = jnp.concatenate(
        [shift_up(k0[rows - halo :], "strip"), k0, shift_down(k0[:halo], "strip")], axis=0
    )
    k0x = jnp.concatenate(
        [
            shift_up(k0_rows[:, w - LANE :], "frame"),
            k0_rows,
            shift_down(k0_rows[:, :LANE], "frame"),
        ],
        axis=1,
    )

    def complete(part, before):
        up = shift_up(part[rows:], "strip")
        dn = shift_down(part[: 2 * halo], "strip")
        q = jnp.concatenate(
            [part[: 2 * halo] + up, part[2 * halo : rows], part[rows:] + dn], axis=0
        )
        q = jnp.where(inside, q, 0.0)
        edge = q[:, w:]
        to_right = jnp.where(lane >= LANE - halo, q[:, w - LANE : w], edge)
        to_left = jnp.where(lane < halo, q[:, :LANE], edge)
        from_left = shift_up(to_right, "frame")
        from_right = shift_down(to_left, "frame")
        left_tile = jnp.where(first, 0.0, edge + from_left)
        right_tile = jnp.where(last, 0.0, edge + from_right)
        own_left = jnp.where(lane < halo, from_left, 0.0)
        own_right = jnp.where(lane >= LANE - halo, from_right, 0.0)
        pad = jnp.zeros((ext, w - LANE), f32)
        own = (
            q[:, :w]
            + jnp.concatenate([own_left, pad], axis=1)
            + jnp.concatenate([pad, own_right], axis=1)
        )
        return jnp.concatenate([left_tile, own, right_tile], axis=1) + damping * before

    def own_block(x):
        return x[halo : halo + rows, LANE : LANE + w]

    carry = apply_terms(k0x, mats, my_weights[: n - 1], 0, halo, final=False)
    part1, stat1 = apply_terms(k0x, mats, my_weights[n - 1 :], n - 1, halo, carry)
    k1x = complete(part1, k0x)
    part2, stat2 = apply_terms(k1x, mats, my_weights, 0, halo)
    k1 = own_block(k1x)
    k2 = own_block(complete(part2, k1x))

    def fold(x):
        return jnp.sum(x.reshape(rows * w // (8 * LANE), 8, LANE), axis=0)

    sums = jnp.stack([fold(k0 * k0), stat1, fold(k1 * k1), stat2])
    for axis, size in (("strip", strips), ("frame", n)):
        d = 1
        while d < size:
            sums = sums + swap(sums, axis, d)
            d *= 2
    sums = jnp.sum(sums, axis=(1, 2))
    k00, k11 = sums[0], sums[2]
    k01 = sums[1] + damping * k00
    k12 = sums[3] + damping * k11
    alpha0 = k00 / k01
    norm1 = k00 - 2.0 * alpha0 * k01 + alpha0 * alpha0 * k11
    beta = norm1 / k00
    curve1 = (1.0 + beta) ** 2 * k01 - 2.0 * (1.0 + beta) * alpha0 * k11 + alpha0 * alpha0 * k12
    alpha1 = norm1 / curve1
    c1 = alpha0 + alpha1 * (1.0 + beta)
    c2 = alpha0 * alpha1

    def gathered(x):
        parts = [x] + [None] * (n - 1)
        for d in reversed(distances):
            known = [i for i in range(n) if parts[i] is not None]
            sent = swap(jnp.stack([parts[i] for i in known]), "frame", d)
            for s, i in enumerate(known):
                parts[i ^ d] = sent[s]
        both = jnp.stack(parts)
        return jnp.concatenate(
            [lax.dynamic_index_in_dim(both, me ^ j, 0, keepdims=False) for j in range(n)], axis=1
        )

    g0, g1, g2 = gathered(k0), gathered(k1), gathered(k2)
    return estimate + c1 * g0 - c2 * g1, g0 - c1 * g1 + c2 * g2


def solution(mesh):
    return jax.shard_map(
        body,
        mesh=mesh,
        in_specs=(
            P("strip", None),
            P("frame", "strip", None),
            P("frame", "strip", None),
            P("frame", None),
            P("frame", None),
        ),
        out_specs=(P("strip", None), P("strip", None)),
        check_vma=False,
    )
```

```python
import functools

import jax
import jax.numpy as jnp
from jax import lax
from jax.experimental import pallas as pl
from jax.experimental.pallas import tpu as pltpu
from jax.sharding import PartitionSpec as P


damping = 0.05
f32 = jnp.float32
bf16 = jnp.bfloat16
LANE = 128
VMEM = pl.BlockSpec(memory_space=pltpu.VMEM)
ANY = pl.BlockSpec(memory_space=pl.ANY)


def split(x):
    hi = x.astype(bf16)
    lo = (x - hi.astype(f32)).astype(bf16)
    return hi, lo


def dot(a, b):
    return jnp.dot(a, b, preferred_element_type=f32)


def tiles(width, step=256):
    return [(s, min(step, width - s)) for s in range(0, width, step)]


def kernel_bases(col_unit, row_unit):
    count, taps = col_unit.shape
    wide = 2 * LANE

    def at(values, start):
        return jnp.pad(values, ((0, 0), (start, wide - taps - start)))

    def turned(values):
        gap = jnp.zeros((count, wide - taps), f32)
        return jnp.concatenate([values[:, :1], gap, values[:, :0:-1]], axis=1)

    return jnp.stack(
        [at(row_unit, 0), turned(col_unit), at(col_unit, LANE), turned(row_unit)], axis=1
    )


def setup_kernel(per_group, rows, halo, base_ref, t_ref, b_ref, bp_ref, ta_ref):
    frames = base_ref.shape[0]

    def toeplitz(f, which, count):
        base = jnp.broadcast_to(base_ref[f, which : which + 1, :], (count, 2 * LANE))
        return pltpu.roll(base, 0, 1, stride=1, stride_axis=0)

    ext = rows + 2 * halo
    for f in range(frames):
        hi, lo = split(toeplitz(f, 0, rows))
        t_ref[f, :rows, :] = hi
        t_ref[f, rows:, :] = lo
        hi, lo = split(toeplitz(f, 1, 2 * LANE)[:, :LANE])
        b_ref[f, :, :LANE] = hi
        b_ref[f, :, LANE:] = lo
        hi, lo = split(toeplitz(f, 2, 2 * LANE)[:, :LANE])
        bp_ref[f, :, :LANE] = hi
        bp_ref[f, :, LANE:] = lo
        hi, lo = split(toeplitz(f, 3, ext)[:, :rows])
        g, s = divmod(f, per_group)
        ta_ref[g, :ext, s * rows : (s + 1) * rows] = hi
        ta_ref[g, ext:, s * rows : (s + 1) * rows] = lo


def setup_matrices(bases, per_group, rows, halo):
    frames = bases.shape[0]
    ext = rows + 2 * halo
    shapes = (
        (frames, 2 * rows, 2 * LANE),
        (frames, 2 * LANE, 2 * LANE),
        (frames, 2 * LANE, 2 * LANE),
        (frames // per_group, 2 * ext, per_group * rows),
    )
    return pl.pallas_call(
        functools.partial(setup_kernel, per_group, rows, halo),
        out_shape=[jax.ShapeDtypeStruct(s, bf16) for s in shapes],
        in_specs=[VMEM],
        out_specs=[VMEM] * 4,
        name="setup_matrices",
    )(bases)


def load_image(y_hi, y_lo, image, halo):
    ext, full = image.shape
    shift = LANE - halo
    y = pltpu.roll(image, full - shift, 1)[:, : full - LANE]
    hi, lo = split(y)
    y_hi[:ext, :] = hi
    y_lo[:ext, :] = lo


def group_terms(frames, rows, w, y_hi, y_lo, t, b, bp, ta, weight, data, us, qs, vs_hi, vs_lo, acc, stat):
    total = None
    for f in range(frames):
        for c, size in tiles(w + LANE):
            r1 = dot(t(f)[...], y_hi[:, c : c + size])
            r2 = dot(t(f)[:rows, :], y_lo[:, c : c + size])
            hi, lo = split(r1[:rows] + r1[rows:] + r2)
            us[:rows, c : c + size] = hi
            us[rows:, c : c + size] = lo
        for k in range(w // LANE):
            c = k * LANE
            r = dot(us[:, c : c + 2 * LANE], b(f)[...])
            a = r[:rows, :LANE] + r[:rows, LANE:] + r[rows:, :LANE]
            if data is not None:
                a = a - data(f)[:, c : c + LANE]
            q = weight(f)[:, c : c + LANE] * a
            if stat is not None:
                part = jnp.sum((a * q).reshape(rows // 8, 8, LANE), axis=0)
                total = part if total is None else total + part
            hi, lo = split(q)
            qs[:rows, c + LANE : c + 2 * LANE] = hi
            qs[rows:, c + LANE : c + 2 * LANE] = lo
        for k in range(w // LANE + 1):
            c = k * LANE
            r = dot(qs[:, c : c + 2 * LANE], bp(f)[...])
            hi, lo = split(r[:rows, :LANE] + r[:rows, LANE:] + r[rows:, :LANE])
            vs_hi[f * rows : (f + 1) * rows, c : c + LANE] = hi
            vs_lo[f * rows : (f + 1) * rows, c : c + LANE] = lo
    ext = acc.shape[0]
    for c, size in tiles(w + LANE):
        r1 = dot(ta[...], vs_hi[:, c : c + size])
        r2 = dot(ta[:ext, :], vs_lo[:, c : c + size])
        acc[:, c : c + size] += r1[:ext] + r1[ext:] + r2
    if stat is not None:
        stat[...] += total


def work_scratch(frames, rows, halo, w):
    ext = rows + 2 * halo
    return [
        pltpu.VMEM((2 * LANE, w + LANE), bf16),
        pltpu.VMEM((2 * LANE, w + LANE), bf16),
        pltpu.VMEM((2 * rows, w + LANE), bf16),
        pltpu.VMEM((2 * rows, w + 2 * LANE), bf16),
        pltpu.VMEM((frames * rows, w + LANE), bf16),
        pltpu.VMEM((frames * rows, w + LANE), bf16),
        pltpu.VMEM((ext, w + LANE), f32),
    ]


def clear_edges(y_hi, y_lo, qs, ext, rows, w):
    zero = jnp.zeros((y_hi.shape[0] - ext, y_hi.shape[1]), bf16)
    y_hi[ext:, :] = zero
    y_lo[ext:, :] = zero
    qs[:, :LANE] = jnp.zeros((2 * rows, LANE), bf16)
    qs[:, w + LANE :] = jnp.zeros((2 * rows, LANE), bf16)


def unshift(acc, halo):
    return pltpu.roll(acc, acc.shape[1] - halo, 1)


def first_kernel(
    frames, rows, halo, w,
    est, lo, hi, t_ref, b_ref, bp_ref, ta_ref, w_hbm, d_hbm,
    top, mid, bot,
    y_hi, y_lo, us, qs, vs_hi, vs_lo, acc, estp, outp, wbuf, dbuf, sem,
):
    ext = rows + 2 * halo
    cols = est.shape[1]
    blocks = cols // w

    def copies(j, slot):
        window = pl.ds(pl.multiple_of(j * w, LANE), w)
        return (
            pltpu.make_async_copy(w_hbm.at[:, :, window], wbuf.at[slot], sem.at[0, slot]),
            pltpu.make_async_copy(d_hbm.at[:, :, window], dbuf.at[slot], sem.at[1, slot]),
        )

    for c in copies(0, 0):
        c.start()
    clear_edges(y_hi, y_lo, qs, ext, rows, w)
    for edge in (0, LANE + cols):
        estp[:, edge : edge + LANE] = jnp.zeros((ext, LANE), f32)
    inner = slice(LANE, LANE + cols)
    estp[:halo, inner] = lo[...]
    estp[halo : halo + rows, inner] = est[...]
    estp[halo + rows :, inner] = hi[...]
    outp[...] = jnp.zeros_like(outp)
    lane = lax.broadcasted_iota(jnp.int32, (ext, LANE), 1)

    @pl.loop(0, blocks)
    def _(j):
        slot = lax.rem(j, 2)

        @pl.when(j + 1 < blocks)
        def _():
            for c in copies(j + 1, 1 - slot):
                c.start()

        start = pl.multiple_of(j * w, LANE)
        load_image(y_hi, y_lo, estp[:, pl.ds(start, w + 2 * LANE)], halo)
        acc[...] = jnp.zeros_like(acc)
        for c in copies(j, slot):
            c.wait()
        group_terms(
            frames, rows, w, y_hi, y_lo,
            lambda f: t_ref.at[f], lambda f: b_ref.at[f], lambda f: bp_ref.at[f], ta_ref.at[0],
            lambda f: wbuf.at[slot, f], lambda f: dbuf.at[slot, f],
            us, qs, vs_hi, vs_lo, acc, None,
        )
        z = unshift(acc[...], halo)
        edge = z[:, w:]
        outp[:, pl.ds(start, LANE)] += jnp.where(lane >= LANE - halo, edge, 0.0)
        outp[:, pl.ds(pl.multiple_of(start + LANE, LANE), w)] += z[:, :w]
        outp[:, pl.ds(pl.multiple_of(start + LANE + w, LANE), LANE)] += jnp.where(lane < halo, edge, 0.0)

    top[...] = outp[:halo, inner]
    mid[...] = outp[halo : halo + rows, inner]
    bot[...] = outp[halo + rows :, inner]


def first_terms(est, lo, hi, mats, weights, observed, w):
    frames, rows, cols = weights.shape
    halo = lo.shape[0]
    ext = rows + 2 * halo
    return pl.pallas_call(
        functools.partial(first_kernel, frames, rows, halo, w),
        out_shape=[
            jax.ShapeDtypeStruct((halo, cols), f32),
            jax.ShapeDtypeStruct((rows, cols), f32),
            jax.ShapeDtypeStruct((halo, cols), f32),
        ],
        in_specs=[VMEM] * 7 + [ANY, ANY],
        out_specs=[VMEM] * 3,
        scratch_shapes=work_scratch(frames, rows, halo, w)
        + [
            pltpu.VMEM((ext, cols + 2 * LANE), f32),
            pltpu.VMEM((ext, cols + 2 * LANE), f32),
            pltpu.VMEM((2, frames, rows, w), f32),
            pltpu.VMEM((2, frames, rows, w), f32),
            pltpu.SemaphoreType.DMA((2, 2)),
        ],
        cost_estimate=pl.CostEstimate(flops=8 * 10**9, bytes_accessed=8 * 2**20, transcendentals=0),
        name="first_terms",
    )(est, lo, hi, *mats, weights, observed)


def apply_kernel(frames, rows, halo, w, groups, base, has_acc, final, *refs):
    image, t_hbm, b_hbm, bp_hbm, ta_hbm = refs[:5]
    weights = refs[5 : 5 + groups]
    refs = refs[5 + groups :]
    if has_acc:
        acc_in, stat_in = refs[:2]
        refs = refs[2:]
    out, stat, y_hi, y_lo, us, qs, vs_hi, vs_lo, acc, tb, bb, bpb, tab, wbuf, sem = refs
    ext = rows + 2 * halo

    def copies(g):
        span = pl.ds((base + g) * frames, frames)
        return [
            pltpu.make_async_copy(t_hbm.at[span], tb.at[g], sem.at[0, g]),
            pltpu.make_async_copy(b_hbm.at[span], bb.at[g], sem.at[1, g]),
            pltpu.make_async_copy(bp_hbm.at[span], bpb.at[g], sem.at[2, g]),
            pltpu.make_async_copy(ta_hbm.at[base + g], tab.at[g], sem.at[3, g]),
        ]

    for g in range(groups):
        for c in copies(g):
            c.start()
        pltpu.make_async_copy(weights[g], wbuf.at[g], sem.at[4, g]).start()
    clear_edges(y_hi, y_lo, qs, ext, rows, w)
    load_image(y_hi, y_lo, image[...], halo)
    if has_acc:
        acc[...] = acc_in[...]
        stat[...] = stat_in[...]
    else:
        acc[...] = jnp.zeros_like(acc)
        stat[...] = jnp.zeros_like(stat)

    @pl.loop(0, groups)
    def _(g):
        for c in copies(g):
            c.wait()
        pltpu.make_async_copy(weights[0], wbuf.at[g], sem.at[4, g]).wait()
        group_terms(
            frames, rows, w, y_hi, y_lo,
            lambda f: tb.at[g, f], lambda f: bb.at[g, f], lambda f: bpb.at[g, f], tab.at[g],
            lambda f: wbuf.at[g, f], None,
            us, qs, vs_hi, vs_lo, acc, stat,
        )

    out[...] = unshift(acc[...], halo) if final else acc[...]


def apply_terms(image, mats, weights, base, halo, carry=None, final=True):
    frames, rows, w = weights[0].shape
    ext = rows + 2 * halo
    groups = len(weights)
    t, b, bp, ta = mats
    args = [image, t, b, bp, ta, *weights]
    specs = [VMEM] + [ANY] * (4 + groups)
    if carry is not None:
        args += list(carry)
        specs += [VMEM, VMEM]
    return pl.pallas_call(
        functools.partial(apply_kernel, frames, rows, halo, w, groups, base, carry is not None, final),
        out_shape=[
            jax.ShapeDtypeStruct((ext, w + LANE), f32),
            jax.ShapeDtypeStruct((8, LANE), f32),
        ],
        in_specs=specs,
        out_specs=[VMEM, VMEM],
        scratch_shapes=work_scratch(frames, rows, halo, w)
        + [
            pltpu.VMEM((groups, frames) + t.shape[1:], bf16),
            pltpu.VMEM((groups, frames) + b.shape[1:], bf16),
            pltpu.VMEM((groups, frames) + bp.shape[1:], bf16),
            pltpu.VMEM((groups,) + ta.shape[1:], bf16),
            pltpu.VMEM((groups, frames, rows, w), f32),
            pltpu.SemaphoreType.DMA((5, groups)),
        ],
        cost_estimate=pl.CostEstimate(
            flops=groups * 3 * 10**9, bytes_accessed=groups * 2**20, transcendentals=0
        ),
    )(*args)


def shift_up(x, axis):
    n = lax.axis_size(axis)
    return lax.ppermute(x, axis, [(i, i + 1) for i in range(n - 1)])


def shift_down(x, axis):
    n = lax.axis_size(axis)
    return lax.ppermute(x, axis, [(i + 1, i) for i in range(n - 1)])


def swap(x, axis, distance):
    n = lax.axis_size(axis)
    return lax.ppermute(x, axis, [(i, i ^ distance) for i in range(n)])


def steps(estimate, observed, weights, column_kernels, row_kernels):
    n = lax.axis_size("frame")
    me = lax.axis_index("frame")
    strips = lax.axis_size("strip")
    strip = lax.axis_index("strip")
    rows, cols = estimate.shape
    frames = weights.shape[0]
    halo = column_kernels.shape[1] // 2
    w = cols // n
    ext = rows + 2 * halo
    distances = [1 << k for k in range(n.bit_length() - 1)]

    unit = lambda k: k / jnp.sum(k, axis=1, keepdims=True)
    est_lo = shift_up(estimate[rows - halo :], "strip")
    est_hi = shift_down(estimate[:halo], "strip")
    taps = jnp.stack([column_kernels, row_kernels])
    all_taps = [taps]
    for d in range(1, n):
        all_taps.append(swap(taps, "frame", d))
    bases = kernel_bases(unit(column_kernels), unit(row_kernels))
    all_taps = jnp.concatenate(all_taps, axis=1)

    def block_of(x, j):
        return lax.dynamic_slice_in_dim(x, j * w, w, axis=x.ndim - 1)

    my_weights = [block_of(weights, me)]
    for d in range(1, n):
        my_weights.append(swap(block_of(weights, me ^ d), "frame", d))

    own_mats = setup_matrices(bases, frames, rows, halo)
    top, mid, bot = first_terms(estimate, est_lo, est_hi, own_mats, weights, observed, w)

    all_bases = kernel_bases(unit(all_taps[0]), unit(all_taps[1]))
    mats = setup_matrices(all_bases, frames, rows, halo)

    from_up = shift_up(bot, "strip")
    from_dn = shift_down(top, "strip")
    terms = jnp.concatenate(
        [mid[:halo] + from_up, mid[halo : rows - halo], mid[rows - halo :] + from_dn], axis=0
    )

    left = terms
    for d in distances:
        bit = (me // d) % 2
        half = left.shape[1] // w // 2

        def pick(which, left=left, half=half):
            return jnp.concatenate(
                [block_of(left, 2 * i + which) for i in range(half)], axis=1
            )

        left = pick(bit) + swap(pick(1 - bit), "frame", d)
    k0 = -(left + damping * block_of(estimate, me))

    lane = lax.broadcasted_iota(jnp.int32, (ext, LANE), 1)
    row = lax.broadcasted_iota(jnp.int32, (ext, 1), 0)
    inside = ((row >= halo) | (strip > 0)) & ((row < halo + rows) | (strip < strips - 1))
    first = me == 0
    last = me == n - 1

    k0_rows = jnp.concatenate(
        [shift_up(k0[rows - halo :], "strip"), k0, shift_down(k0[:halo], "strip")], axis=0
    )
    k0x = jnp.concatenate(
        [
            shift_up(k0_rows[:, w - LANE :], "frame"),
            k0_rows,
            shift_down(k0_rows[:, :LANE], "frame"),
        ],
        axis=1,
    )

    def complete(part, before):
        up = shift_up(part[rows:], "strip")
        dn = shift_down(part[: 2 * halo], "strip")
        q = jnp.concatenate(
            [part[: 2 * halo] + up, part[2 * halo : rows], part[rows:] + dn], axis=0
        )
        q = jnp.where(inside, q, 0.0)
        edge = q[:, w:]
        to_right = jnp.where(lane >= LANE - halo, q[:, w - LANE : w], edge)
        to_left = jnp.where(lane < halo, q[:, :LANE], edge)
        from_left = shift_up(to_right, "frame")
        from_right = shift_down(to_left, "frame")
        left_tile = jnp.where(first, 0.0, edge + from_left)
        right_tile = jnp.where(last, 0.0, edge + from_right)
        own_left = jnp.where(lane < halo, from_left, 0.0)
        own_right = jnp.where(lane >= LANE - halo, from_right, 0.0)
        pad = jnp.zeros((ext, w - LANE), f32)
        own = (
            q[:, :w]
            + jnp.concatenate([own_left, pad], axis=1)
            + jnp.concatenate([pad, own_right], axis=1)
        )
        return jnp.concatenate([left_tile, own, right_tile], axis=1) + damping * before

    def own_block(x):
        return x[halo : halo + rows, LANE : LANE + w]

    def fold(x):
        return jnp.sum(x.reshape(rows * w // (8 * LANE), 8, LANE), axis=0)

    k00_part = fold(k0 * k0)
    carry = apply_terms(k0x, mats, my_weights[: n - 1], 0, halo, final=False)
    part1, stat1 = apply_terms(k0x, mats, my_weights[n - 1 :], n - 1, halo, carry)
    k1x = complete(part1, k0x)
    k1, k1x = lax.optimization_barrier((own_block(k1x), k1x))
    k11_part = fold(k1 * k1)
    part2, stat2 = apply_terms(k1x, mats, my_weights, 0, halo)
    k2 = own_block(complete(part2, k1x))

    sums = jnp.stack([k00_part, stat1, k11_part, stat2])
    for axis, size in (("frame", n), ("strip", strips)):
        d = 1
        while d < size:
            sums = sums + swap(sums, axis, d)
            d *= 2
    sums = jnp.sum(sums, axis=(1, 2))
    k00, k11 = sums[0], sums[2]
    k01 = sums[1] + damping * k00
    k12 = sums[3] + damping * k11
    alpha0 = k00 / k01
    norm1 = k00 - 2.0 * alpha0 * k01 + alpha0 * alpha0 * k11
    beta = norm1 / k00
    curve1 = (1.0 + beta) ** 2 * k01 - 2.0 * (1.0 + beta) * alpha0 * k11 + alpha0 * alpha0 * k12
    alpha1 = norm1 / curve1
    c1 = alpha0 + alpha1 * (1.0 + beta)
    c2 = alpha0 * alpha1

    def ordered(parts):
        both = jnp.stack(parts)
        return jnp.concatenate(
            [lax.dynamic_index_in_dim(both, me ^ j, 0, keepdims=False) for j in range(n)], axis=1
        )

    def gathered(x):
        parts = [x] + [None] * (n - 1)
        for d in reversed(distances):
            known = [i for i in range(n) if parts[i] is not None]
            sent = swap(jnp.stack([parts[i] for i in known]), "frame", d)
            for s, i in enumerate(known):
                parts[i ^ d] = sent[s]
        return ordered(parts)

    def gathered_soon(x):
        parts = [x] + [None] * (n - 1)
        for i in range(0, n):
            for d in reversed(distances):
                if i % (2 * d) == 0:
                    parts[i + d] = swap(parts[i], "frame", d)
        return ordered(parts)

    g0, g1, g2 = gathered(k0), gathered(k1), gathered_soon(k2)
    return estimate + c1 * g0 - c2 * g1, g0 - c1 * g1 + c2 * g2


def solution(mesh):
    return jax.shard_map(
        steps,
        mesh=mesh,
        in_specs=(
            P("strip", None),
            P("frame", "strip", None),
            P("frame", "strip", None),
            P("frame", None),
            P("frame", None),
        ),
        out_specs=(P("strip", None), P("strip", None)),
        check_vma=False,
    )
```

```python
import functools

import jax
import jax.numpy as jnp
from jax import lax
from jax.experimental import pallas as pl
from jax.experimental.pallas import tpu as pltpu
from jax.sharding import PartitionSpec as P


damping = 0.05
f32 = jnp.float32
bf16 = jnp.bfloat16
LANE = 128
VMEM = pl.BlockSpec(memory_space=pltpu.VMEM)
ANY = pl.BlockSpec(memory_space=pl.ANY)


def split(x):
    hi = x.astype(bf16)
    lo = (x - hi.astype(f32)).astype(bf16)
    return hi, lo


def dot(a, b):
    return jnp.dot(a, b, preferred_element_type=f32)


def tiles(width, step=256):
    return [(s, min(step, width - s)) for s in range(0, width, step)]


def taps_tile(column_kernels, row_kernels, w):
    both = jnp.concatenate([column_kernels, row_kernels], axis=0)
    count, taps = both.shape
    return jnp.pad(both, ((0, -count % 8), (0, w - taps)))


def setup_kernel(frames, rows, halo, sources, *refs):
    tiles_in = refs[: len(sources)]
    t_ref, b_ref, bp_ref, ta_ref, taps, sem = refs[len(sources) :]
    wide = 2 * LANE
    ext = rows + 2 * halo

    def copy(g):
        start, count = sources[g]
        return pltpu.make_async_copy(
            tiles_in[g].at[pl.ds(start, count), pl.ds(0, wide)], taps.at[g], sem.at[g]
        )

    def toeplitz(base, count):
        return pltpu.roll(jnp.broadcast_to(base, (count, wide)), 0, 1, stride=1, stride_axis=0)

    for g in range(len(sources)):
        copy(g).start()
    for g in range(len(sources)):
        copy(g).wait()
        unit = taps[g] / jnp.sum(taps[g], axis=1, keepdims=True)
        for s in range(frames):
            f = g * frames + s
            col = unit[s : s + 1]
            row = unit[frames + s : frames + s + 1]
            by_rows = toeplitz(row, rows)
            hi, lo = split(by_rows)
            t_ref[f, :rows, :] = hi
            t_ref[f, rows:, :] = lo
            hi, lo = split(by_rows.T[:ext])
            ta_ref[g, :ext, s * rows : (s + 1) * rows] = hi
            ta_ref[g, ext:, s * rows : (s + 1) * rows] = lo
            hi, lo = split(toeplitz(col, LANE).T)
            b_ref[f, :, :LANE] = hi
            b_ref[f, :, LANE:] = lo
            hi, lo = split(toeplitz(pltpu.roll(col, LANE, 1), wide)[:, :LANE])
            bp_ref[f, :, :LANE] = hi
            bp_ref[f, :, LANE:] = lo


def setup_matrices(tiles_in, starts, frames, rows, halo):
    groups = len(tiles_in)
    ext = rows + 2 * halo
    height = -(-2 * frames // 8) * 8
    shapes = (
        (groups * frames, 2 * rows, 2 * LANE),
        (groups * frames, 2 * LANE, 2 * LANE),
        (groups * frames, 2 * LANE, 2 * LANE),
        (groups, 2 * ext, frames * rows),
    )
    return pl.pallas_call(
        functools.partial(setup_kernel, frames, rows, halo, [(start, height) for start in starts]),
        out_shape=[jax.ShapeDtypeStruct(s, bf16) for s in shapes],
        in_specs=[ANY] * groups,
        out_specs=[VMEM] * 4,
        scratch_shapes=[
            pltpu.VMEM((groups, height, 2 * LANE), f32),
            pltpu.SemaphoreType.DMA((groups,)),
        ],
        name="setup_matrices",
    )(*tiles_in)


def load_image(y_hi, y_lo, image, halo):
    ext, full = image.shape
    shift = LANE - halo
    y = pltpu.roll(image, full - shift, 1)[:, : full - LANE]
    hi, lo = split(y)
    y_hi[:ext, :] = hi
    y_lo[:ext, :] = lo


def group_terms(frames, rows, w, y_hi, y_lo, t, b, bp, ta, weight, data, us, qs, vs_hi, vs_lo, acc, stat):
    total = None
    for f in range(frames):
        for c, size in tiles(w + LANE):
            r1 = dot(t(f)[...], y_hi[:, c : c + size])
            r2 = dot(t(f)[:rows, :], y_lo[:, c : c + size])
            hi, lo = split(r1[:rows] + r1[rows:] + r2)
            us[:rows, c : c + size] = hi
            us[rows:, c : c + size] = lo
        for k in range(w // LANE):
            c = k * LANE
            r = dot(us[:, c : c + 2 * LANE], b(f)[...])
            a = r[:rows, :LANE] + r[:rows, LANE:] + r[rows:, :LANE]
            if data is not None:
                a = a - data(f)[:, c : c + LANE]
            q = weight(f)[:, c : c + LANE] * a
            if stat is not None:
                part = jnp.sum((a * q).reshape(rows // 8, 8, LANE), axis=0)
                total = part if total is None else total + part
            hi, lo = split(q)
            qs[:rows, c + LANE : c + 2 * LANE] = hi
            qs[rows:, c + LANE : c + 2 * LANE] = lo
        for k in range(w // LANE + 1):
            c = k * LANE
            r = dot(qs[:, c : c + 2 * LANE], bp(f)[...])
            hi, lo = split(r[:rows, :LANE] + r[:rows, LANE:] + r[rows:, :LANE])
            vs_hi[f * rows : (f + 1) * rows, c : c + LANE] = hi
            vs_lo[f * rows : (f + 1) * rows, c : c + LANE] = lo
    ext = acc.shape[0]
    for c, size in tiles(w + LANE):
        r1 = dot(ta[...], vs_hi[:, c : c + size])
        r2 = dot(ta[:ext, :], vs_lo[:, c : c + size])
        acc[:, c : c + size] += r1[:ext] + r1[ext:] + r2
    if stat is not None:
        stat[...] += total


def work_scratch(frames, rows, halo, w):
    ext = rows + 2 * halo
    return [
        pltpu.VMEM((2 * LANE, w + LANE), bf16),
        pltpu.VMEM((2 * LANE, w + LANE), bf16),
        pltpu.VMEM((2 * rows, w + LANE), bf16),
        pltpu.VMEM((2 * rows, w + 2 * LANE), bf16),
        pltpu.VMEM((frames * rows, w + LANE), bf16),
        pltpu.VMEM((frames * rows, w + LANE), bf16),
        pltpu.VMEM((ext, w + LANE), f32),
    ]


def clear_edges(y_hi, y_lo, qs, ext, rows, w):
    zero = jnp.zeros((y_hi.shape[0] - ext, y_hi.shape[1]), bf16)
    y_hi[ext:, :] = zero
    y_lo[ext:, :] = zero
    qs[:, :LANE] = jnp.zeros((2 * rows, LANE), bf16)
    qs[:, w + LANE :] = jnp.zeros((2 * rows, LANE), bf16)


def unshift(acc, halo):
    return pltpu.roll(acc, acc.shape[1] - halo, 1)


def first_kernel(
    frames, rows, halo, w,
    est, lo, hi, t_ref, b_ref, bp_ref, ta_ref, w_hbm, d_hbm,
    top, mid, bot,
    y_hi, y_lo, us, qs, vs_hi, vs_lo, acc, estp, outp, wbuf, dbuf, sem,
):
    ext = rows + 2 * halo
    cols = est.shape[1]
    blocks = cols // w

    def copies(j, slot):
        window = pl.ds(pl.multiple_of(j * w, LANE), w)
        return (
            pltpu.make_async_copy(w_hbm.at[:, :, window], wbuf.at[slot], sem.at[0, slot]),
            pltpu.make_async_copy(d_hbm.at[:, :, window], dbuf.at[slot], sem.at[1, slot]),
        )

    for c in copies(0, 0):
        c.start()
    clear_edges(y_hi, y_lo, qs, ext, rows, w)
    for edge in (0, LANE + cols):
        estp[:, edge : edge + LANE] = jnp.zeros((ext, LANE), f32)
    inner = slice(LANE, LANE + cols)
    estp[:halo, inner] = lo[...]
    estp[halo : halo + rows, inner] = est[...]
    estp[halo + rows :, inner] = hi[...]
    outp[...] = jnp.zeros_like(outp)
    lane = lax.broadcasted_iota(jnp.int32, (ext, LANE), 1)

    @pl.loop(0, blocks)
    def _(j):
        slot = lax.rem(j, 2)

        @pl.when(j + 1 < blocks)
        def _():
            for c in copies(j + 1, 1 - slot):
                c.start()

        start = pl.multiple_of(j * w, LANE)
        load_image(y_hi, y_lo, estp[:, pl.ds(start, w + 2 * LANE)], halo)
        acc[...] = jnp.zeros_like(acc)
        for c in copies(j, slot):
            c.wait()
        group_terms(
            frames, rows, w, y_hi, y_lo,
            lambda f: t_ref.at[f], lambda f: b_ref.at[f], lambda f: bp_ref.at[f], ta_ref.at[0],
            lambda f: wbuf.at[slot, f], lambda f: dbuf.at[slot, f],
            us, qs, vs_hi, vs_lo, acc, None,
        )
        z = unshift(acc[...], halo)
        edge = z[:, w:]
        outp[:, pl.ds(start, LANE)] += jnp.where(lane >= LANE - halo, edge, 0.0)
        outp[:, pl.ds(pl.multiple_of(start + LANE, LANE), w)] += z[:, :w]
        outp[:, pl.ds(pl.multiple_of(start + LANE + w, LANE), LANE)] += jnp.where(lane < halo, edge, 0.0)

    top[...] = outp[:halo, inner]
    mid[...] = outp[halo : halo + rows, inner]
    bot[...] = outp[halo + rows :, inner]


def first_terms(est, lo, hi, mats, weights, observed, w):
    frames, rows, cols = weights.shape
    halo = lo.shape[0]
    ext = rows + 2 * halo
    return pl.pallas_call(
        functools.partial(first_kernel, frames, rows, halo, w),
        out_shape=[
            jax.ShapeDtypeStruct((halo, cols), f32),
            jax.ShapeDtypeStruct((rows, cols), f32),
            jax.ShapeDtypeStruct((halo, cols), f32),
        ],
        in_specs=[VMEM] * 7 + [ANY, ANY],
        out_specs=[VMEM] * 3,
        scratch_shapes=work_scratch(frames, rows, halo, w)
        + [
            pltpu.VMEM((ext, cols + 2 * LANE), f32),
            pltpu.VMEM((ext, cols + 2 * LANE), f32),
            pltpu.VMEM((2, frames, rows, w), f32),
            pltpu.VMEM((2, frames, rows, w), f32),
            pltpu.SemaphoreType.DMA((2, 2)),
        ],
        cost_estimate=pl.CostEstimate(flops=8 * 10**9, bytes_accessed=8 * 2**20, transcendentals=0),
        name="first_terms",
    )(est, lo, hi, *mats, weights, observed)


def pack_kernel(plan, rows, w, place, weights, tile, *refs):
    outs, sem = refs[:-1], refs[-1]
    pending = []
    for i, (distance, lead, count, with_taps) in enumerate(plan):
        start = pl.multiple_of(jnp.bitwise_xor(place[0], distance) * w, LANE)
        for k in range(count):
            copy = pltpu.make_async_copy(
                weights.at[lead + k, :, pl.ds(start, w)],
                outs[i].at[pl.ds(k * rows, rows), :],
                sem.at[i, k],
            )
            copy.start()
            pending.append(copy)
        if with_taps:
            outs[i][count * rows :, :] = tile[...]
    for copy in pending:
        copy.wait()


def pack_weights(plan, place, weights, tile):
    frames, rows, _ = weights.shape
    w = tile.shape[1]
    return pl.pallas_call(
        functools.partial(pack_kernel, plan, rows, w),
        out_shape=[
            jax.ShapeDtypeStruct((count * rows + (tile.shape[0] if taps else 0), w), f32)
            for _, _, count, taps in plan
        ],
        in_specs=[pl.BlockSpec(memory_space=pltpu.SMEM), ANY, VMEM],
        out_specs=[VMEM] * len(plan),
        scratch_shapes=[pltpu.SemaphoreType.DMA((len(plan), frames))],
        name="pack_weights",
    )(place, weights, tile)


def apply_kernel(frames, rows, halo, w, groups, origin, cut, count, place, image, *refs):
    t_hbm, b_hbm, bp_hbm, ta_hbm, own = refs[:5]
    moved = refs[5 : 5 + count]
    top, mid, bot, stat = refs[5 + count : 9 + count]
    y_hi, y_lo, us, qs, vs_hi, vs_lo, acc, tb, bb, bpb, tab, wbuf, sem, wsem = refs[9 + count :]
    ext = rows + 2 * halo

    def copies(g):
        span = pl.ds(g * frames, frames)
        return [
            pltpu.make_async_copy(t_hbm.at[span], tb.at[g], sem.at[0, g]),
            pltpu.make_async_copy(b_hbm.at[span], bb.at[g], sem.at[1, g]),
            pltpu.make_async_copy(bp_hbm.at[span], bpb.at[g], sem.at[2, g]),
            pltpu.make_async_copy(ta_hbm.at[g], tab.at[g], sem.at[3, g]),
        ]

    mine = pl.ds(pl.multiple_of(place[0] * w, LANE), w)
    for g in range(groups):
        for c in copies(g):
            c.start()
        for f in range(frames):
            if g == 0:
                source = own.at[f, :, mine]
            else:
                ref, start = origin[g, f]
                source = moved[ref].at[pl.ds(start, rows), :]
            pltpu.make_async_copy(source, wbuf.at[g, f], wsem.at[g, f]).start()
    clear_edges(y_hi, y_lo, qs, ext, rows, w)
    load_image(y_hi, y_lo, image[...], halo)
    acc[...] = jnp.zeros_like(acc)
    stat[...] = jnp.zeros_like(stat)

    @pl.loop(0, groups)
    def _(g):
        for c in copies(g):
            c.wait()
        for f in range(frames):
            pltpu.make_async_copy(own.at[f, :, mine], wbuf.at[g, f], wsem.at[g, f]).wait()
        group_terms(
            frames, rows, w, y_hi, y_lo,
            lambda f: tb.at[g, f], lambda f: bb.at[g, f], lambda f: bpb.at[g, f], tab.at[g],
            lambda f: wbuf.at[g, f], None,
            us, qs, vs_hi, vs_lo, acc, stat,
        )

    z = unshift(acc[...], halo)
    top[...] = z[:cut]
    mid[...] = z[cut : ext - cut]
    bot[...] = z[ext - cut :]


def apply_terms(place, image, mats, weights, moved, origin, cut, halo):
    frames, rows, _ = weights.shape
    w = image.shape[1] - 2 * LANE
    ext = rows + 2 * halo
    t, b, bp, ta = mats
    groups = ta.shape[0]
    wide = w + LANE
    return pl.pallas_call(
        functools.partial(apply_kernel, frames, rows, halo, w, groups, origin, cut, len(moved)),
        out_shape=[
            jax.ShapeDtypeStruct((cut, wide), f32),
            jax.ShapeDtypeStruct((ext - 2 * cut, wide), f32),
            jax.ShapeDtypeStruct((cut, wide), f32),
            jax.ShapeDtypeStruct((8, LANE), f32),
        ],
        in_specs=[pl.BlockSpec(memory_space=pltpu.SMEM), VMEM] + [ANY] * (5 + len(moved)),
        out_specs=[VMEM] * 4,
        scratch_shapes=work_scratch(frames, rows, halo, w)
        + [
            pltpu.VMEM((groups, frames) + t.shape[1:], bf16),
            pltpu.VMEM((groups, frames) + b.shape[1:], bf16),
            pltpu.VMEM((groups, frames) + bp.shape[1:], bf16),
            pltpu.VMEM((groups,) + ta.shape[1:], bf16),
            pltpu.VMEM((groups, frames, rows, w), f32),
            pltpu.SemaphoreType.DMA((4, groups)),
            pltpu.SemaphoreType.DMA((groups, frames)),
        ],
        cost_estimate=pl.CostEstimate(
            flops=groups * 3 * 10**9, bytes_accessed=groups * 2**20, transcendentals=0
        ),
    )(place, image, t, b, bp, ta, weights, *moved)


def wrap_kernel(rows, halo, w, top, mid, bot, up, dn, before, sums, out):
    keep = rows - 2 * halo
    pieces = (
        (0, halo, mid[:halo, :] + up[...]),
        (halo, keep, mid[halo : rows - halo, :]),
        (rows - halo, halo, mid[rows - halo :, :] + dn[...]),
    )
    edges = []
    for start, size, value in pieces:
        span = slice(start, start + size)
        out[span, :] = value[:, :w] + damping * before[span, :]
        edges.append(pltpu.roll(value[:, w:], halo, 1))
    edge = jnp.concatenate(edges, axis=0)
    short = rows * 2 * halo // w
    lane = lax.broadcasted_iota(jnp.int32, (short, LANE), 1)
    per = LANE // (2 * halo)
    for t in range(w // LANE):
        tile = None
        for p in range(per):
            k = t * per + p
            part = edge[k * short : (k + 1) * short]
            part = pltpu.roll(part, p * 2 * halo, 1) if p else part
            tile = part if tile is None else jnp.where(lane >= p * 2 * halo, part, tile)
        out[rows : rows + short, t * LANE : (t + 1) * LANE] = tile
    out[rows + short :, :] = jnp.zeros((8, w), f32)
    for i in range(4):
        out[rows + short + i : rows + short + i + 1, :LANE] = jnp.sum(sums[i], axis=0, keepdims=True)


def wrap(top, mid, bot, up, dn, before, sums, halo):
    rows, w = before.shape
    height = rows + rows * 2 * halo // w + 8
    return pl.pallas_call(
        functools.partial(wrap_kernel, rows, halo, w),
        out_shape=jax.ShapeDtypeStruct((height, w), f32),
        in_specs=[VMEM] * 7,
        out_specs=VMEM,
        name="wrap",
    )(top, mid, bot, up, dn, before, sums)


def final_kernel(n, rows, halo, w, place, est, *refs):
    k0, k1, k2 = refs[:n], refs[n : 2 * n], refs[2 * n : 3 * n]
    sol, res, full = refs[3 * n :]
    short = rows * 2 * halo // w
    per = LANE // (2 * halo)
    total = k2[0][rows + short :, :LANE]
    for i in range(1, n):
        total = total + k2[i][rows + short :, :LANE]
    total = jnp.sum(total, axis=1, keepdims=True)
    k00, k11 = total[0:1], total[2:3]
    k01 = total[1:2] + damping * k00
    k12 = total[3:4] + damping * k11
    alpha0 = k00 / k01
    norm1 = k00 - 2.0 * alpha0 * k01 + alpha0 * alpha0 * k11
    beta = norm1 / k00
    curve1 = (1.0 + beta) * (1.0 + beta) * k01 - 2.0 * (1.0 + beta) * alpha0 * k11
    curve1 = curve1 + alpha0 * alpha0 * k12
    alpha1 = norm1 / curve1
    c1 = alpha0 + alpha1 * (1.0 + beta)
    c2 = alpha0 * alpha1

    lane = lax.broadcasted_iota(jnp.int32, (rows, LANE), 1)
    spot = [jnp.bitwise_xor(place[0], i) for i in range(n)]
    for end in (0, LANE + n * w):
        full[:, end : end + LANE] = jnp.zeros((rows, LANE), f32)
    for i in range(n):
        full[:, pl.ds(pl.multiple_of(spot[i] * w + LANE, LANE), w)] = k2[i][:rows, :]
    for i in range(n):
        parts = []
        for k in range(w // (2 * halo)):
            t, p = divmod(k, per)
            part = k2[i][rows : rows + short, t * LANE : (t + 1) * LANE]
            back = (LANE - halo - p * 2 * halo) % LANE
            parts.append(pltpu.roll(part, back, 1) if back else part)
        edge = jnp.concatenate(parts, axis=0)
        left = pl.ds(pl.multiple_of(spot[i] * w, LANE), LANE)
        right = pl.ds(pl.multiple_of(spot[i] * w + w + LANE, LANE), LANE)
        full[:, left] += jnp.where(lane >= LANE - halo, edge, 0.0)
        full[:, right] += jnp.where(lane < halo, edge, 0.0)
    for i in range(n):
        cols = pl.ds(pl.multiple_of(spot[i] * w, LANE), w)
        a0, a1 = k0[i][...], k1[i][...]
        sol[:, cols] = est[:, cols] + c1 * a0 - c2 * a1
        res[:, cols] = a0 - c1 * a1 + c2 * full[:, pl.ds(pl.multiple_of(spot[i] * w + LANE, LANE), w)]


def final_images(place, est, k0, k1, k2, halo):
    n = len(k0)
    rows, w = k0[0].shape
    return pl.pallas_call(
        functools.partial(final_kernel, n, rows, halo, w),
        out_shape=[jax.ShapeDtypeStruct(est.shape, f32)] * 2,
        in_specs=[pl.BlockSpec(memory_space=pltpu.SMEM)] + [VMEM] * (1 + 3 * n),
        out_specs=[VMEM] * 2,
        scratch_shapes=[pltpu.VMEM((rows, n * w + 2 * LANE), f32)],
        name="final_images",
    )(place, est, *k0, *k1, *k2)


def shift_up(x, axis):
    n = lax.axis_size(axis)
    return lax.ppermute(x, axis, [(i, i + 1) for i in range(n - 1)])


def shift_down(x, axis):
    n = lax.axis_size(axis)
    return lax.ppermute(x, axis, [(i + 1, i) for i in range(n - 1)])


def swap(x, axis, distance):
    n = lax.axis_size(axis)
    return lax.ppermute(x, axis, [(i, i ^ distance) for i in range(n)])


def steps(estimate, observed, weights, column_kernels, row_kernels):
    n = lax.axis_size("frame")
    me = lax.axis_index("frame")
    place = me.reshape(1).astype(jnp.int32)
    strips = lax.axis_size("strip")
    strip = lax.axis_index("strip")
    rows, cols = estimate.shape
    frames = weights.shape[0]
    halo = column_kernels.shape[1] // 2
    w = cols // n
    ext = rows + 2 * halo
    distances = [1 << k for k in range(n.bit_length() - 1)]

    def block_of(x, j):
        return lax.dynamic_slice_in_dim(x, j * w, w, axis=x.ndim - 1)

    def fold(x):
        return jnp.sum(x.reshape(rows * w // (8 * LANE), 8, LANE), axis=0)

    est_lo = shift_up(estimate[rows - halo :], "strip")
    est_hi = shift_down(estimate[:halo], "strip")

    early = frames // 2
    plan = [(d, 0, frames, True) for d in range(1, n - 1)]
    plan += [(n - 1, 0, early, True), (n - 1, early, frames - early, False)]
    tile = taps_tile(column_kernels, row_kernels, w)
    packed = pack_weights(plan, place, weights, tile)
    moved = []
    for i, (d, _, _, taps) in enumerate(plan):
        moved.append(swap(packed[i], "frame", d))
    origin = {}
    starts = [0]
    for i, (d, lead, count, taps) in enumerate(plan):
        for k in range(count):
            origin[d, lead + k] = (i, k * rows)
        if taps:
            starts.append(count * rows)

    own_mats = setup_matrices([tile], [0], frames, rows, halo)
    top, mid, bot = first_terms(estimate, est_lo, est_hi, own_mats, weights, observed, w)
    mats = setup_matrices([tile] + moved[: n - 1], starts, frames, rows, halo)

    from_up = shift_up(bot, "strip")
    from_dn = shift_down(top, "strip")
    left = jnp.concatenate(
        [mid[:halo] + from_up, mid[halo : rows - halo], mid[rows - halo :] + from_dn], axis=0
    )

    for d in distances:
        bit = (me // d) % 2
        half = left.shape[1] // w // 2

        def pick(which, left=left, half=half):
            return jnp.concatenate(
                [block_of(left, 2 * i + which) for i in range(half)], axis=1
            )

        sent = swap(pick(1 - bit), "frame", d)
        left = pick(bit) + sent
    k0 = -(left + damping * block_of(estimate, me))
    k00_part = fold(k0 * k0)

    lane = lax.broadcasted_iota(jnp.int32, (ext, LANE), 1)
    row = lax.broadcasted_iota(jnp.int32, (ext, 1), 0)
    inside = ((row >= halo) | (strip > 0)) & ((row < halo + rows) | (strip < strips - 1))
    first = me == 0
    last = me == n - 1

    k0_rows = jnp.concatenate(
        [shift_up(k0[rows - halo :], "strip"), k0, shift_down(k0[:halo], "strip")], axis=0
    )
    k0x = jnp.concatenate(
        [
            shift_up(k0_rows[:, w - LANE :], "frame"),
            k0_rows,
            shift_down(k0_rows[:, :LANE], "frame"),
        ],
        axis=1,
    )

    def complete(top, mid, bot, before):
        up = shift_up(bot, "strip")
        dn = shift_down(top, "strip")
        q = jnp.where(inside, jnp.concatenate([top + up, mid, bot + dn], axis=0), 0.0)
        edge = q[:, w:]
        to_right = jnp.where(lane >= LANE - halo, q[:, w - LANE : w], edge)
        to_left = jnp.where(lane < halo, q[:, :LANE], edge)
        from_left = shift_up(to_right, "frame")
        from_right = shift_down(to_left, "frame")
        left_tile = jnp.where(first, 0.0, edge + from_left)
        right_tile = jnp.where(last, 0.0, edge + from_right)
        own_left = jnp.where(lane < halo, from_left, 0.0)
        own_right = jnp.where(lane >= LANE - halo, from_right, 0.0)
        pad = jnp.zeros((ext, w - LANE), f32)
        own = (
            q[:, :w]
            + jnp.concatenate([own_left, pad], axis=1)
            + jnp.concatenate([pad, own_right], axis=1)
        )
        return jnp.concatenate([left_tile, own, right_tile], axis=1) + damping * before

    top, mid, bot, stat1 = apply_terms(place, k0x, mats, weights, moved, origin, 2 * halo, halo)
    k1x = complete(top, mid, bot, k0x)
    k1, k1x = lax.optimization_barrier((k1x[halo : halo + rows, LANE : LANE + w], k1x))
    k11_part = fold(k1 * k1)
    top, mid, bot, stat2 = apply_terms(place, k1x, mats, weights, moved, origin, halo, halo)
    up = shift_up(bot, "strip")
    dn = shift_down(top, "strip")
    sums = jnp.stack([k00_part, stat1, k11_part, stat2])
    d = 1
    while d < strips:
        sums = sums + swap(sums, "strip", d)
        d *= 2
    k2 = wrap(top, mid, bot, up, dn, k1, sums, halo)

    def gathered(x):
        parts = [x] + [None] * (n - 1)
        for d in reversed(distances):
            known = [i for i in range(n) if parts[i] is not None]
            for i in known:
                parts[i ^ d] = swap(parts[i], "frame", d)
        return parts

    def gathered_soon(x):
        parts = [x] + [None] * (n - 1)
        for i in range(n):
            for d in reversed(distances):
                if i % (2 * d) == 0:
                    parts[i + d] = swap(parts[i], "frame", d)
        return parts

    g0, g1, g2 = gathered(k0), gathered(k1), gathered_soon(k2)
    return tuple(final_images(place, estimate, g0, g1, g2, halo))


def solution(mesh):
    return jax.shard_map(
        steps,
        mesh=mesh,
        in_specs=(
            P("strip", None),
            P("frame", "strip", None),
            P("frame", "strip", None),
            P("frame", None),
            P("frame", None),
        ),
        out_specs=(P("strip", None), P("strip", None)),
        check_vma=False,
    )
```

```python
import functools

import jax
import jax.numpy as jnp
from jax import lax
from jax.experimental import pallas as pl
from jax.experimental.pallas import tpu as pltpu
from jax.sharding import PartitionSpec as P


damping = 0.05
f32 = jnp.float32
bf16 = jnp.bfloat16
LANE = 128
VMEM = pl.BlockSpec(memory_space=pltpu.VMEM)
ANY = pl.BlockSpec(memory_space=pl.ANY)


def split(x):
    hi = x.astype(bf16)
    lo = (x - hi.astype(f32)).astype(bf16)
    return hi, lo


def dot(a, b):
    return jnp.dot(a, b, preferred_element_type=f32)


def tiles(width, step=256):
    return [(s, min(step, width - s)) for s in range(0, width, step)]


def taps_tile(column_kernels, row_kernels, w):
    both = jnp.concatenate([column_kernels, row_kernels], axis=0)
    count, taps = both.shape
    return jnp.pad(both, ((0, -count % 8), (0, w - taps)))


def setup_kernel(frames, rows, halo, sources, *refs):
    tiles_in = refs[: len(sources)]
    t_ref, b_ref, bp_ref, ta_ref, taps, sem = refs[len(sources) :]
    wide = 2 * LANE
    ext = rows + 2 * halo

    def copy(g):
        start, count = sources[g]
        return pltpu.make_async_copy(
            tiles_in[g].at[pl.ds(start, count), pl.ds(0, wide)], taps.at[g], sem.at[g]
        )

    def toeplitz(base, count):
        return pltpu.roll(jnp.broadcast_to(base, (count, wide)), 0, 1, stride=1, stride_axis=0)

    for g in range(len(sources)):
        copy(g).start()
    for g in range(len(sources)):
        copy(g).wait()
        unit = taps[g] / jnp.sum(taps[g], axis=1, keepdims=True)
        for s in range(frames):
            f = g * frames + s
            col = unit[s : s + 1]
            row = unit[frames + s : frames + s + 1]
            by_rows = toeplitz(row, rows)
            hi, lo = split(by_rows)
            t_ref[f, :rows, :] = hi
            t_ref[f, rows:, :] = lo
            hi, lo = split(by_rows.T[:ext])
            ta_ref[g, :ext, s * rows : (s + 1) * rows] = hi
            ta_ref[g, ext:, s * rows : (s + 1) * rows] = lo
            hi, lo = split(toeplitz(col, LANE).T)
            b_ref[f, :, :LANE] = hi
            b_ref[f, :, LANE:] = lo
            hi, lo = split(toeplitz(pltpu.roll(col, LANE, 1), wide)[:, :LANE])
            bp_ref[f, :, :LANE] = hi
            bp_ref[f, :, LANE:] = lo


def setup_matrices(tiles_in, starts, frames, rows, halo):
    groups = len(tiles_in)
    ext = rows + 2 * halo
    height = -(-2 * frames // 8) * 8
    shapes = (
        (groups * frames, 2 * rows, 2 * LANE),
        (groups * frames, 2 * LANE, 2 * LANE),
        (groups * frames, 2 * LANE, 2 * LANE),
        (groups, 2 * ext, frames * rows),
    )
    return pl.pallas_call(
        functools.partial(setup_kernel, frames, rows, halo, [(start, height) for start in starts]),
        out_shape=[jax.ShapeDtypeStruct(s, bf16) for s in shapes],
        in_specs=[ANY] * groups,
        out_specs=[VMEM] * 4,
        scratch_shapes=[
            pltpu.VMEM((groups, height, 2 * LANE), f32),
            pltpu.SemaphoreType.DMA((groups,)),
        ],
    )(*tiles_in)


def load_image(y_hi, y_lo, image, halo):
    ext, full = image.shape
    shift = LANE - halo
    y = pltpu.roll(image, full - shift, 1)[:, : full - LANE]
    hi, lo = split(y)
    y_hi[:ext, :] = hi
    y_lo[:ext, :] = lo


def group_terms(frames, rows, w, y_hi, y_lo, t, b, bp, ta, weight, data, us, qs, vs_hi, vs_lo, acc, stat):
    total = None
    for f in range(frames):
        for c, size in tiles(w + LANE):
            r1 = dot(t(f)[...], y_hi[:, c : c + size])
            r2 = dot(t(f)[:rows, :], y_lo[:, c : c + size])
            hi, lo = split(r1[:rows] + r1[rows:] + r2)
            us[:rows, c : c + size] = hi
            us[rows:, c : c + size] = lo
        for k in range(w // LANE):
            c = k * LANE
            r = dot(us[:, c : c + 2 * LANE], b(f)[...])
            a = r[:rows, :LANE] + r[:rows, LANE:] + r[rows:, :LANE]
            if data is not None:
                a = a - data(f)[:, c : c + LANE]
            q = weight(f)[:, c : c + LANE] * a
            if stat is not None:
                part = jnp.sum((a * q).reshape(rows // 8, 8, LANE), axis=0)
                total = part if total is None else total + part
            hi, lo = split(q)
            qs[:rows, c + LANE : c + 2 * LANE] = hi
            qs[rows:, c + LANE : c + 2 * LANE] = lo
        for k in range(w // LANE + 1):
            c = k * LANE
            r = dot(qs[:, c : c + 2 * LANE], bp(f)[...])
            hi, lo = split(r[:rows, :LANE] + r[:rows, LANE:] + r[rows:, :LANE])
            vs_hi[f * rows : (f + 1) * rows, c : c + LANE] = hi
            vs_lo[f * rows : (f + 1) * rows, c : c + LANE] = lo
    ext = acc.shape[0]
    for c, size in tiles(w + LANE):
        r1 = dot(ta[...], vs_hi[:, c : c + size])
        r2 = dot(ta[:ext, :], vs_lo[:, c : c + size])
        acc[:, c : c + size] += r1[:ext] + r1[ext:] + r2
    if stat is not None:
        stat[...] += total


def work_scratch(frames, rows, halo, w):
    ext = rows + 2 * halo
    return [
        pltpu.VMEM((2 * LANE, w + LANE), bf16),
        pltpu.VMEM((2 * LANE, w + LANE), bf16),
        pltpu.VMEM((2 * rows, w + LANE), bf16),
        pltpu.VMEM((2 * rows, w + 2 * LANE), bf16),
        pltpu.VMEM((frames * rows, w + LANE), bf16),
        pltpu.VMEM((frames * rows, w + LANE), bf16),
        pltpu.VMEM((ext, w + LANE), f32),
    ]


def clear_edges(y_hi, y_lo, qs, ext, rows, w):
    zero = jnp.zeros((y_hi.shape[0] - ext, y_hi.shape[1]), bf16)
    y_hi[ext:, :] = zero
    y_lo[ext:, :] = zero
    qs[:, :LANE] = jnp.zeros((2 * rows, LANE), bf16)
    qs[:, w + LANE :] = jnp.zeros((2 * rows, LANE), bf16)


def unshift(acc, halo):
    return pltpu.roll(acc, acc.shape[1] - halo, 1)


def first_kernel(
    frames, rows, halo, w,
    est, lo, hi, t_ref, b_ref, bp_ref, ta_ref, w_hbm, d_hbm,
    top, mid, bot,
    y_hi, y_lo, us, qs, vs_hi, vs_lo, acc, estp, outp, wbuf, dbuf, sem,
):
    ext = rows + 2 * halo
    cols = est.shape[1]
    blocks = cols // w

    def copies(j, slot):
        window = pl.ds(pl.multiple_of(j * w, LANE), w)
        return (
            pltpu.make_async_copy(w_hbm.at[:, :, window], wbuf.at[slot], sem.at[0, slot]),
            pltpu.make_async_copy(d_hbm.at[:, :, window], dbuf.at[slot], sem.at[1, slot]),
        )

    for c in copies(0, 0):
        c.start()
    clear_edges(y_hi, y_lo, qs, ext, rows, w)
    for edge in (0, LANE + cols):
        estp[:, edge : edge + LANE] = jnp.zeros((ext, LANE), f32)
    inner = slice(LANE, LANE + cols)
    estp[:halo, inner] = lo[...]
    estp[halo : halo + rows, inner] = est[...]
    estp[halo + rows :, inner] = hi[...]
    outp[...] = jnp.zeros_like(outp)
    lane = lax.broadcasted_iota(jnp.int32, (ext, LANE), 1)

    @pl.loop(0, blocks)
    def _(j):
        slot = lax.rem(j, 2)

        @pl.when(j + 1 < blocks)
        def _():
            for c in copies(j + 1, 1 - slot):
                c.start()

        start = pl.multiple_of(j * w, LANE)
        load_image(y_hi, y_lo, estp[:, pl.ds(start, w + 2 * LANE)], halo)
        acc[...] = jnp.zeros_like(acc)
        for c in copies(j, slot):
            c.wait()
        group_terms(
            frames, rows, w, y_hi, y_lo,
            lambda f: t_ref.at[f], lambda f: b_ref.at[f], lambda f: bp_ref.at[f], ta_ref.at[0],
            lambda f: wbuf.at[slot, f], lambda f: dbuf.at[slot, f],
            us, qs, vs_hi, vs_lo, acc, None,
        )
        z = unshift(acc[...], halo)
        edge = z[:, w:]
        outp[:, pl.ds(start, LANE)] += jnp.where(lane >= LANE - halo, edge, 0.0)
        outp[:, pl.ds(pl.multiple_of(start + LANE, LANE), w)] += z[:, :w]
        outp[:, pl.ds(pl.multiple_of(start + LANE + w, LANE), LANE)] += jnp.where(lane < halo, edge, 0.0)

    top[...] = outp[:halo, inner]
    mid[...] = outp[halo : halo + rows, inner]
    bot[...] = outp[halo + rows :, inner]


def first_terms(est, lo, hi, mats, weights, observed, w):
    frames, rows, cols = weights.shape
    halo = lo.shape[0]
    ext = rows + 2 * halo
    return pl.pallas_call(
        functools.partial(first_kernel, frames, rows, halo, w),
        out_shape=[
            jax.ShapeDtypeStruct((halo, cols), f32),
            jax.ShapeDtypeStruct((rows, cols), f32),
            jax.ShapeDtypeStruct((halo, cols), f32),
        ],
        in_specs=[VMEM] * 7 + [ANY, ANY],
        out_specs=[VMEM] * 3,
        scratch_shapes=work_scratch(frames, rows, halo, w)
        + [
            pltpu.VMEM((ext, cols + 2 * LANE), f32),
            pltpu.VMEM((ext, cols + 2 * LANE), f32),
            pltpu.VMEM((2, frames, rows, w), f32),
            pltpu.VMEM((2, frames, rows, w), f32),
            pltpu.SemaphoreType.DMA((2, 2)),
        ],
        cost_estimate=pl.CostEstimate(flops=8 * 10**9, bytes_accessed=8 * 2**20, transcendentals=0),
        name="first_terms",
    )(est, lo, hi, *mats, weights, observed)


def pack_kernel(plan, rows, w, place, weights, tile, *refs):
    outs, sem = refs[:-1], refs[-1]
    pending = []
    for i, (distance, lead, count, with_taps) in enumerate(plan):
        start = pl.multiple_of(jnp.bitwise_xor(place[0], distance) * w, LANE)
        for k in range(count):
            copy = pltpu.make_async_copy(
                weights.at[lead + k, :, pl.ds(start, w)],
                outs[i].at[pl.ds(k * rows, rows), :],
                sem.at[i, k],
            )
            copy.start()
            pending.append(copy)
        if with_taps:
            outs[i][count * rows :, :] = tile[...]
    for copy in pending:
        copy.wait()


def pack_weights(plan, place, weights, tile):
    frames, rows, _ = weights.shape
    w = tile.shape[1]
    return pl.pallas_call(
        functools.partial(pack_kernel, plan, rows, w),
        out_shape=[
            jax.ShapeDtypeStruct((count * rows + (tile.shape[0] if taps else 0), w), f32)
            for _, _, count, taps in plan
        ],
        in_specs=[pl.BlockSpec(memory_space=pltpu.SMEM), ANY, VMEM],
        out_specs=[VMEM] * len(plan),
        scratch_shapes=[pltpu.SemaphoreType.DMA((len(plan), frames))],
        name="pack_weights",
    )(place, weights, tile)


def apply_kernel(frames, rows, halo, w, groups, origin, cut, count, place, image, *refs):
    t_hbm, b_hbm, bp_hbm, ta_hbm, own = refs[:5]
    moved = refs[5 : 5 + count]
    top, mid, bot, stat = refs[5 + count : 9 + count]
    y_hi, y_lo, us, qs, vs_hi, vs_lo, acc, tb, bb, bpb, tab, wbuf, sem, wsem = refs[9 + count :]
    ext = rows + 2 * halo

    def copies(g):
        span = pl.ds(g * frames, frames)
        return [
            pltpu.make_async_copy(t_hbm.at[span], tb.at[g], sem.at[0, g]),
            pltpu.make_async_copy(b_hbm.at[span], bb.at[g], sem.at[1, g]),
            pltpu.make_async_copy(bp_hbm.at[span], bpb.at[g], sem.at[2, g]),
            pltpu.make_async_copy(ta_hbm.at[g], tab.at[g], sem.at[3, g]),
        ]

    mine = pl.ds(pl.multiple_of(place[0] * w, LANE), w)
    for g in range(groups):
        for c in copies(g):
            c.start()
        for f in range(frames):
            if g == 0:
                source = own.at[f, :, mine]
            else:
                ref, start = origin[g, f]
                source = moved[ref].at[pl.ds(start, rows), :]
            pltpu.make_async_copy(source, wbuf.at[g, f], wsem.at[g, f]).start()
    clear_edges(y_hi, y_lo, qs, ext, rows, w)
    load_image(y_hi, y_lo, image[...], halo)
    acc[...] = jnp.zeros_like(acc)
    stat[...] = jnp.zeros_like(stat)

    @pl.loop(0, groups)
    def _(g):
        for c in copies(g):
            c.wait()
        for f in range(frames):
            pltpu.make_async_copy(own.at[f, :, mine], wbuf.at[g, f], wsem.at[g, f]).wait()
        group_terms(
            frames, rows, w, y_hi, y_lo,
            lambda f: tb.at[g, f], lambda f: bb.at[g, f], lambda f: bpb.at[g, f], tab.at[g],
            lambda f: wbuf.at[g, f], None,
            us, qs, vs_hi, vs_lo, acc, stat,
        )

    z = unshift(acc[...], halo)
    top[...] = z[:cut]
    mid[...] = z[cut : ext - cut]
    bot[...] = z[ext - cut :]


def apply_terms(place, image, mats, weights, moved, origin, cut, halo):
    frames, rows, _ = weights.shape
    w = image.shape[1] - 2 * LANE
    ext = rows + 2 * halo
    t, b, bp, ta = mats
    groups = ta.shape[0]
    wide = w + LANE
    return pl.pallas_call(
        functools.partial(apply_kernel, frames, rows, halo, w, groups, origin, cut, len(moved)),
        out_shape=[
            jax.ShapeDtypeStruct((cut, wide), f32),
            jax.ShapeDtypeStruct((ext - 2 * cut, wide), f32),
            jax.ShapeDtypeStruct((cut, wide), f32),
            jax.ShapeDtypeStruct((8, LANE), f32),
        ],
        in_specs=[pl.BlockSpec(memory_space=pltpu.SMEM), VMEM] + [ANY] * (5 + len(moved)),
        out_specs=[VMEM] * 4,
        scratch_shapes=work_scratch(frames, rows, halo, w)
        + [
            pltpu.VMEM((groups, frames) + t.shape[1:], bf16),
            pltpu.VMEM((groups, frames) + b.shape[1:], bf16),
            pltpu.VMEM((groups, frames) + bp.shape[1:], bf16),
            pltpu.VMEM((groups,) + ta.shape[1:], bf16),
            pltpu.VMEM((groups, frames, rows, w), f32),
            pltpu.SemaphoreType.DMA((4, groups)),
            pltpu.SemaphoreType.DMA((groups, frames)),
        ],
        cost_estimate=pl.CostEstimate(
            flops=groups * 3 * 10**9, bytes_accessed=groups * 2**20, transcendentals=0
        ),
    )(place, image, t, b, bp, ta, weights, *moved)


def wrap_kernel(rows, halo, w, top, mid, bot, up, dn, before, out):
    keep = rows - 2 * halo
    pieces = (
        (0, halo, mid[:halo, :] + up[...]),
        (halo, keep, mid[halo : rows - halo, :]),
        (rows - halo, halo, mid[rows - halo :, :] + dn[...]),
    )
    edges = []
    for start, size, value in pieces:
        span = slice(start, start + size)
        out[span, :] = value[:, :w] + damping * before[span, :]
        edges.append(pltpu.roll(value[:, w:], halo, 1))
    edge = jnp.concatenate(edges, axis=0)
    short = rows * 2 * halo // w
    lane = lax.broadcasted_iota(jnp.int32, (short, LANE), 1)
    per = LANE // (2 * halo)
    for t in range(w // LANE):
        tile = None
        for p in range(per):
            k = t * per + p
            part = edge[k * short : (k + 1) * short]
            part = pltpu.roll(part, p * 2 * halo, 1) if p else part
            tile = part if tile is None else jnp.where(lane >= p * 2 * halo, part, tile)
        out[rows : rows + short, t * LANE : (t + 1) * LANE] = tile


def wrap(top, mid, bot, up, dn, before, halo):
    rows, w = before.shape
    height = rows + rows * 2 * halo // w
    return pl.pallas_call(
        functools.partial(wrap_kernel, rows, halo, w),
        out_shape=jax.ShapeDtypeStruct((height, w), f32),
        in_specs=[VMEM] * 6,
        out_specs=VMEM,
        name="wrap",
    )(top, mid, bot, up, dn, before)


def final_kernel(n, rows, halo, w, place, est, sums, *refs):
    k0, k1, k2 = refs[:n], refs[n : 2 * n], refs[2 * n : 3 * n]
    sol, res, full = refs[3 * n :]
    short = rows * 2 * halo // w
    per = LANE // (2 * halo)
    total = [jnp.sum(jnp.sum(sums[i], axis=0, keepdims=True), axis=1, keepdims=True) for i in range(4)]
    k00, k11 = total[0], total[2]
    k01 = total[1] + damping * k00
    k12 = total[3] + damping * k11
    alpha0 = k00 / k01
    norm1 = k00 - 2.0 * alpha0 * k01 + alpha0 * alpha0 * k11
    beta = norm1 / k00
    curve1 = (1.0 + beta) * (1.0 + beta) * k01 - 2.0 * (1.0 + beta) * alpha0 * k11
    curve1 = curve1 + alpha0 * alpha0 * k12
    alpha1 = norm1 / curve1
    c1 = alpha0 + alpha1 * (1.0 + beta)
    c2 = alpha0 * alpha1

    lane = lax.broadcasted_iota(jnp.int32, (rows, LANE), 1)
    spot = [jnp.bitwise_xor(place[0], i) for i in range(n)]
    for end in (0, LANE + n * w):
        full[:, end : end + LANE] = jnp.zeros((rows, LANE), f32)
    for i in range(n):
        full[:, pl.ds(pl.multiple_of(spot[i] * w + LANE, LANE), w)] = k2[i][:rows, :]
    for i in range(n):
        parts = []
        for k in range(w // (2 * halo)):
            t, p = divmod(k, per)
            part = k2[i][rows : rows + short, t * LANE : (t + 1) * LANE]
            back = (LANE - halo - p * 2 * halo) % LANE
            parts.append(pltpu.roll(part, back, 1) if back else part)
        edge = jnp.concatenate(parts, axis=0)
        left = pl.ds(pl.multiple_of(spot[i] * w, LANE), LANE)
        right = pl.ds(pl.multiple_of(spot[i] * w + w + LANE, LANE), LANE)
        full[:, left] += jnp.where(lane >= LANE - halo, edge, 0.0)
        full[:, right] += jnp.where(lane < halo, edge, 0.0)
    for i in range(n):
        cols = pl.ds(pl.multiple_of(spot[i] * w, LANE), w)
        a0, a1 = k0[i][...], k1[i][...]
        sol[:, cols] = est[:, cols] + c1 * a0 - c2 * a1
        res[:, cols] = a0 - c1 * a1 + c2 * full[:, pl.ds(pl.multiple_of(spot[i] * w + LANE, LANE), w)]


def final_images(place, est, sums, k0, k1, k2, halo):
    n = len(k0)
    rows, w = k0[0].shape
    return pl.pallas_call(
        functools.partial(final_kernel, n, rows, halo, w),
        out_shape=[jax.ShapeDtypeStruct(est.shape, f32)] * 2,
        in_specs=[pl.BlockSpec(memory_space=pltpu.SMEM)] + [VMEM] * (2 + 3 * n),
        out_specs=[VMEM] * 2,
        scratch_shapes=[pltpu.VMEM((rows, n * w + 2 * LANE), f32)],
        name="final_images",
    )(place, est, sums, *k0, *k1, *k2)


def shift_up(x, axis):
    n = lax.axis_size(axis)
    return lax.ppermute(x, axis, [(i, i + 1) for i in range(n - 1)])


def shift_down(x, axis):
    n = lax.axis_size(axis)
    return lax.ppermute(x, axis, [(i + 1, i) for i in range(n - 1)])


def swap(x, axis, distance):
    n = lax.axis_size(axis)
    return lax.ppermute(x, axis, [(i, i ^ distance) for i in range(n)])


def steps(estimate, observed, weights, column_kernels, row_kernels):
    n = lax.axis_size("frame")
    me = lax.axis_index("frame")
    place = me.reshape(1).astype(jnp.int32)
    strips = lax.axis_size("strip")
    strip = lax.axis_index("strip")
    rows, cols = estimate.shape
    frames = weights.shape[0]
    halo = column_kernels.shape[1] // 2
    w = cols // n
    ext = rows + 2 * halo
    distances = [1 << k for k in range(n.bit_length() - 1)]

    def block_of(x, j):
        return lax.dynamic_slice_in_dim(x, j * w, w, axis=x.ndim - 1)

    def fold(x):
        return jnp.sum(x.reshape(rows * w // (8 * LANE), 8, LANE), axis=0)

    est_lo = shift_up(estimate[rows - halo :], "strip")
    est_hi = shift_down(estimate[:halo], "strip")

    early = frames // 2
    plan = [(d, 0, frames, True) for d in range(1, n - 1)]
    plan += [(n - 1, 0, early, True), (n - 1, early, frames - early, False)]
    tile = taps_tile(column_kernels, row_kernels, w)
    packed = pack_weights(plan, place, weights, tile)
    moved = []
    for i, (d, _, _, taps) in enumerate(plan):
        moved.append(swap(packed[i], "frame", d))
    origin = {}
    starts = [0]
    for i, (d, lead, count, taps) in enumerate(plan):
        for k in range(count):
            origin[d, lead + k] = (i, k * rows)
        if taps:
            starts.append(count * rows)

    own_mats = setup_matrices([tile], [0], frames, rows, halo)
    top, mid, bot = first_terms(estimate, est_lo, est_hi, own_mats, weights, observed, w)
    mats = setup_matrices([tile] + moved[: n - 1], starts, frames, rows, halo)

    from_up = shift_up(bot, "strip")
    from_dn = shift_down(top, "strip")
    left = jnp.concatenate(
        [mid[:halo] + from_up, mid[halo : rows - halo], mid[rows - halo :] + from_dn], axis=0
    )

    part = [block_of(left, me ^ i) for i in range(n)]
    for i in range(n - 1, 0, -1):
        d = i & -i
        part[i ^ d] = part[i ^ d] + swap(part[i], "frame", d)
    k0 = -(part[0] + damping * block_of(estimate, me))
    k00_part = fold(k0 * k0)

    lane = lax.broadcasted_iota(jnp.int32, (ext, LANE), 1)
    row = lax.broadcasted_iota(jnp.int32, (ext, 1), 0)
    inside = ((row >= halo) | (strip > 0)) & ((row < halo + rows) | (strip < strips - 1))
    first = me == 0
    last = me == n - 1

    k0_rows = jnp.concatenate(
        [shift_up(k0[rows - halo :], "strip"), k0, shift_down(k0[:halo], "strip")], axis=0
    )
    k0x = jnp.concatenate(
        [
            shift_up(k0_rows[:, w - LANE :], "frame"),
            k0_rows,
            shift_down(k0_rows[:, :LANE], "frame"),
        ],
        axis=1,
    )

    def complete(top, mid, bot, before):
        up = shift_up(bot, "strip")
        dn = shift_down(top, "strip")
        q = jnp.where(inside, jnp.concatenate([top + up, mid, bot + dn], axis=0), 0.0)
        edge = q[:, w:]
        to_right = jnp.where(lane >= LANE - halo, q[:, w - LANE : w], edge)
        to_left = jnp.where(lane < halo, q[:, :LANE], edge)
        from_left = shift_up(to_right, "frame")
        from_right = shift_down(to_left, "frame")
        left_tile = jnp.where(first, 0.0, edge + from_left)
        right_tile = jnp.where(last, 0.0, edge + from_right)
        own_left = jnp.where(lane < halo, from_left, 0.0)
        own_right = jnp.where(lane >= LANE - halo, from_right, 0.0)
        pad = jnp.zeros((ext, w - LANE), f32)
        own = (
            q[:, :w]
            + jnp.concatenate([own_left, pad], axis=1)
            + jnp.concatenate([pad, own_right], axis=1)
        )
        return jnp.concatenate([left_tile, own, right_tile], axis=1) + damping * before

    top, mid, bot, stat1 = apply_terms(place, k0x, mats, weights, moved, origin, 2 * halo, halo)
    k1x = complete(top, mid, bot, k0x)
    k1, k1x = lax.optimization_barrier((k1x[halo : halo + rows, LANE : LANE + w], k1x))
    k11_part = fold(k1 * k1)
    top, mid, bot, stat2 = apply_terms(place, k1x, mats, weights, moved, origin, halo, halo)
    up = shift_up(bot, "strip")
    dn = shift_down(top, "strip")
    sums = jnp.stack([k00_part, stat1, k11_part, stat2])
    for axis, size in (("frame", n), ("strip", strips)):
        d = 1
        while d < size:
            sums = sums + swap(sums, axis, d)
            d *= 2
    k2 = wrap(top, mid, bot, up, dn, k1, halo)

    def gathered(x):
        parts = [x] + [None] * (n - 1)
        for i in range(n):
            for d in reversed(distances):
                if i % (2 * d) == 0:
                    parts[i + d] = swap(parts[i], "frame", d)
        return parts

    g0, g1, g2 = gathered(k0), gathered(k1), gathered(k2)
    return tuple(final_images(place, estimate, sums, g0, g1, g2, halo))


def solution(mesh):
    return jax.shard_map(
        steps,
        mesh=mesh,
        in_specs=(
            P("strip", None),
            P("frame", "strip", None),
            P("frame", "strip", None),
            P("frame", None),
            P("frame", None),
        ),
        out_specs=(P("strip", None), P("strip", None)),
        check_vma=False,
    )
```

```python
import functools

import jax
import jax.numpy as jnp
from jax import lax
from jax.experimental import pallas as pl
from jax.experimental.pallas import tpu as pltpu
from jax.sharding import PartitionSpec as P


damping = 0.05
f32 = jnp.float32
bf16 = jnp.bfloat16
LANE = 128
VMEM = pl.BlockSpec(memory_space=pltpu.VMEM)
ANY = pl.BlockSpec(memory_space=pl.ANY)
SMEM = pl.BlockSpec(memory_space=pltpu.SMEM)


def split(x):
    hi = x.astype(bf16)
    lo = (x - hi.astype(f32)).astype(bf16)
    return hi, lo


def dot(a, b):
    return jnp.dot(a, b, preferred_element_type=f32)


def choose(flag, a, b):
    return jnp.where(jnp.full(a.shape, flag, jnp.int32) == 1, a, b)


def pack_edge(edge, halo, w):
    rows = edge.shape[0]
    per = LANE // (2 * halo)
    short = rows * 2 * halo // w
    edge = pltpu.roll(edge, halo, 1)
    lane = lax.broadcasted_iota(jnp.int32, (short, LANE), 1)
    out = []
    for t in range(w // LANE):
        tile = None
        for p in range(per):
            k = t * per + p
            part = edge[k * short : (k + 1) * short]
            part = pltpu.roll(part, p * 2 * halo, 1) if p else part
            tile = part if tile is None else jnp.where(lane >= p * 2 * halo, part, tile)
        out.append(tile)
    return jnp.concatenate(out, axis=1)


def unpack_edge(packed, halo):
    _, w = packed.shape
    per = LANE // (2 * halo)
    parts = []
    for k in range(w // (2 * halo)):
        t, p = divmod(k, per)
        part = packed[:, t * LANE : (t + 1) * LANE]
        back = (LANE - halo - p * 2 * halo) % LANE
        parts.append(pltpu.roll(part, back, 1) if back else part)
    return jnp.concatenate(parts, axis=0)


def tiles(width, step=256):
    return [(s, min(step, width - s)) for s in range(0, width, step)]


def toeplitz(base, count):
    wide = base.shape[1]
    return pltpu.roll(jnp.broadcast_to(base, (count, wide)), 0, 1, stride=1, stride_axis=0)


def build_group(taps, g, frames, rows, halo, t_ref, b_ref, bp_ref, ta_ref):
    ext = rows + 2 * halo
    unit = taps / jnp.sum(taps, axis=1, keepdims=True)
    for s in range(frames):
        f = g * frames + s
        col = unit[s : s + 1]
        row = unit[frames + s : frames + s + 1]
        by_rows = toeplitz(row, rows)
        hi, lo = split(by_rows)
        t_ref[f, :rows, :] = hi
        t_ref[f, rows:, :] = lo
        hi, lo = split(by_rows.T[:ext])
        ta_ref[g, :ext, s * rows : (s + 1) * rows] = hi
        ta_ref[g, ext:, s * rows : (s + 1) * rows] = lo
        hi, lo = split(toeplitz(col, LANE).T)
        b_ref[f, :, :LANE] = hi
        b_ref[f, :, LANE:] = lo
        hi, lo = split(toeplitz(pltpu.roll(col, LANE, 1), 2 * LANE)[:, :LANE])
        bp_ref[f, :, :LANE] = hi
        bp_ref[f, :, LANE:] = lo


def matrix_shapes(groups, frames, rows, halo):
    ext = rows + 2 * halo
    return [
        jax.ShapeDtypeStruct(s, bf16)
        for s in (
            (groups * frames, 2 * rows, 2 * LANE),
            (groups * frames, 2 * LANE, 2 * LANE),
            (groups * frames, 2 * LANE, 2 * LANE),
            (groups, 2 * ext, frames * rows),
        )
    ]


def tile_height(frames):
    return -(-2 * frames // 8) * 8


def setup_kernel(frames, rows, halo, starts, *refs):
    tiles_in = refs[: len(starts)]
    mats, taps, sem = refs[len(starts) : -2], refs[-2], refs[-1]
    height = tile_height(frames)

    def copy(g):
        source = tiles_in[g].at[pl.ds(starts[g], height), pl.ds(0, 2 * LANE)]
        return pltpu.make_async_copy(source, taps.at[g], sem.at[g])

    for g in range(len(starts)):
        copy(g).start()
    for g in range(len(starts)):
        copy(g).wait()
        build_group(taps[g], g, frames, rows, halo, *mats)


def setup_matrices(tiles_in, starts, frames, rows, halo):
    groups = len(tiles_in)
    return pl.pallas_call(
        functools.partial(setup_kernel, frames, rows, halo, starts),
        out_shape=matrix_shapes(groups, frames, rows, halo),
        in_specs=[ANY] * groups,
        out_specs=[VMEM] * 4,
        scratch_shapes=[
            pltpu.VMEM((groups, tile_height(frames), 2 * LANE), f32),
            pltpu.SemaphoreType.DMA((groups,)),
        ],
        name="setup_all",
    )(*tiles_in)


def load_image(y_hi, y_lo, image, halo):
    ext, full = image.shape
    shift = LANE - halo
    y = pltpu.roll(image, full - shift, 1)[:, : full - LANE]
    hi, lo = split(y)
    y_hi[:ext, :] = hi
    y_lo[:ext, :] = lo


def group_terms(frames, rows, w, y_hi, y_lo, t, b, bp, ta, weight, data, us, qs, vs_hi, vs_lo, acc, stat):
    total = None
    for f in range(frames):
        for c, size in tiles(w + LANE):
            r1 = dot(t(f)[...], y_hi[:, c : c + size])
            r2 = dot(t(f)[:rows, :], y_lo[:, c : c + size])
            hi, lo = split(r1[:rows] + r1[rows:] + r2)
            us[:rows, c : c + size] = hi
            us[rows:, c : c + size] = lo
        for k in range(w // LANE):
            c = k * LANE
            r = dot(us[:, c : c + 2 * LANE], b(f)[...])
            a = r[:rows, :LANE] + r[:rows, LANE:] + r[rows:, :LANE]
            if data is not None:
                a = a - data(f)[:, c : c + LANE]
            q = weight(f)[:, c : c + LANE] * a
            if stat is not None:
                part = jnp.sum((a * q).reshape(rows // 8, 8, LANE), axis=0)
                total = part if total is None else total + part
            hi, lo = split(q)
            qs[:rows, c + LANE : c + 2 * LANE] = hi
            qs[rows:, c + LANE : c + 2 * LANE] = lo
        for k in range(w // LANE + 1):
            c = k * LANE
            r = dot(qs[:, c : c + 2 * LANE], bp(f)[...])
            hi, lo = split(r[:rows, :LANE] + r[:rows, LANE:] + r[rows:, :LANE])
            vs_hi[f * rows : (f + 1) * rows, c : c + LANE] = hi
            vs_lo[f * rows : (f + 1) * rows, c : c + LANE] = lo
    ext = acc.shape[0]
    for c, size in tiles(w + LANE):
        r1 = dot(ta[...], vs_hi[:, c : c + size])
        r2 = dot(ta[:ext, :], vs_lo[:, c : c + size])
        acc[:, c : c + size] += r1[:ext] + r1[ext:] + r2
    if stat is not None:
        stat[...] += total


def work_scratch(frames, rows, halo, w):
    ext = rows + 2 * halo
    return [
        pltpu.VMEM((2 * LANE, w + LANE), bf16),
        pltpu.VMEM((2 * LANE, w + LANE), bf16),
        pltpu.VMEM((2 * rows, w + LANE), bf16),
        pltpu.VMEM((2 * rows, w + 2 * LANE), bf16),
        pltpu.VMEM((frames * rows, w + LANE), bf16),
        pltpu.VMEM((frames * rows, w + LANE), bf16),
        pltpu.VMEM((ext, w + LANE), f32),
    ]


def clear_edges(y_hi, y_lo, qs, ext, rows, w):
    zero = jnp.zeros((y_hi.shape[0] - ext, y_hi.shape[1]), bf16)
    y_hi[ext:, :] = zero
    y_lo[ext:, :] = zero
    qs[:, :LANE] = jnp.zeros((2 * rows, LANE), bf16)
    qs[:, w + LANE :] = jnp.zeros((2 * rows, LANE), bf16)


def unshift(acc, halo):
    return pltpu.roll(acc, acc.shape[1] - halo, 1)


def first_kernel(
    frames, rows, halo, w,
    place, est, recv_a, recv_b, t_ref, b_ref, bp_ref, ta_ref, w_hbm, d_hbm,
    send_a, mid, send_b,
    y_hi, y_lo, us, qs, vs_hi, vs_lo, acc, estp, outp, wbuf, dbuf, sem,
):
    ext = rows + 2 * halo
    cols = est.shape[1]
    blocks = cols // w

    def copies(j, slot):
        window = pl.ds(pl.multiple_of(j * w, LANE), w)
        return (
            pltpu.make_async_copy(w_hbm.at[:, :, window], wbuf.at[slot], sem.at[0, slot]),
            pltpu.make_async_copy(d_hbm.at[:, :, window], dbuf.at[slot], sem.at[1, slot]),
        )

    for c in copies(0, 0):
        c.start()
    clear_edges(y_hi, y_lo, qs, ext, rows, w)
    for edge in (0, LANE + cols):
        estp[:, edge : edge + LANE] = jnp.zeros((ext, LANE), f32)
    inner = slice(LANE, LANE + cols)
    odd = lax.rem(place[1], 2)
    estp[:halo, inner] = choose(odd, recv_a[...], recv_b[...])
    estp[halo : halo + rows, inner] = est[...]
    estp[halo + rows :, inner] = choose(odd, recv_b[...], recv_a[...])
    outp[...] = jnp.zeros_like(outp)
    lane = lax.broadcasted_iota(jnp.int32, (ext, LANE), 1)

    @pl.loop(0, blocks)
    def _(j):
        slot = lax.rem(j, 2)

        @pl.when(j + 1 < blocks)
        def _():
            for c in copies(j + 1, 1 - slot):
                c.start()

        start = pl.multiple_of(j * w, LANE)
        load_image(y_hi, y_lo, estp[:, pl.ds(start, w + 2 * LANE)], halo)
        acc[...] = jnp.zeros_like(acc)
        for c in copies(j, slot):
            c.wait()
        group_terms(
            frames, rows, w, y_hi, y_lo,
            lambda f: t_ref.at[f], lambda f: b_ref.at[f], lambda f: bp_ref.at[f], ta_ref.at[0],
            lambda f: wbuf.at[slot, f], lambda f: dbuf.at[slot, f],
            us, qs, vs_hi, vs_lo, acc, None,
        )
        z = unshift(acc[...], halo)
        edge = z[:, w:]
        outp[:, pl.ds(start, LANE)] += jnp.where(lane >= LANE - halo, edge, 0.0)
        outp[:, pl.ds(pl.multiple_of(start + LANE, LANE), w)] += z[:, :w]
        outp[:, pl.ds(pl.multiple_of(start + LANE + w, LANE), LANE)] += jnp.where(lane < halo, edge, 0.0)

    send_a[...] = choose(odd, outp[:halo, inner], outp[halo + rows :, inner])
    send_b[...] = choose(odd, outp[halo + rows :, inner], outp[:halo, inner])
    mid[...] = outp[halo : halo + rows, inner]


def first_terms(place, est, recv_a, recv_b, mats, weights, observed, w):
    frames, rows, cols = weights.shape
    halo = recv_a.shape[0]
    ext = rows + 2 * halo
    return pl.pallas_call(
        functools.partial(first_kernel, frames, rows, halo, w),
        out_shape=[
            jax.ShapeDtypeStruct((halo, cols), f32),
            jax.ShapeDtypeStruct((rows, cols), f32),
            jax.ShapeDtypeStruct((halo, cols), f32),
        ],
        in_specs=[SMEM] + [VMEM] * 7 + [ANY, ANY],
        out_specs=[VMEM] * 3,
        scratch_shapes=work_scratch(frames, rows, halo, w)
        + [
            pltpu.VMEM((ext, cols + 2 * LANE), f32),
            pltpu.VMEM((ext, cols + 2 * LANE), f32),
            pltpu.VMEM((2, frames, rows, w), f32),
            pltpu.VMEM((2, frames, rows, w), f32),
            pltpu.SemaphoreType.DMA((2, 2)),
        ],
        cost_estimate=pl.CostEstimate(flops=8 * 10**9, bytes_accessed=8 * 2**20, transcendentals=0),
        name="first_terms",
    )(place, est, recv_a, recv_b, *mats, weights, observed)


def prepare_kernel(plan, frames, rows, halo, w, place, cols_in, rows_in, weights, *refs):
    outs, tile, mats, sem = refs[: len(plan)], refs[len(plan)], refs[len(plan) + 1 : -1], refs[-1]
    taps = cols_in.shape[1]
    pending = []
    for i, (distance, lead, count, _) in enumerate(plan):
        start = pl.multiple_of(jnp.bitwise_xor(place[0], distance) * w, LANE)
        for k in range(count):
            copy = pltpu.make_async_copy(
                weights.at[lead + k, :, pl.ds(start, w)],
                outs[i].at[pl.ds(k * rows, rows), :],
                sem.at[i, k],
            )
            copy.start()
            pending.append(copy)
    tile[...] = jnp.zeros_like(tile)
    tile[:frames, :taps] = cols_in[...]
    tile[frames : 2 * frames, :taps] = rows_in[...]
    for i, (_, _, count, with_taps) in enumerate(plan):
        if with_taps:
            outs[i][count * rows :, :] = tile[...]
    build_group(tile[:, : 2 * LANE], 0, frames, rows, halo, *mats)
    for copy in pending:
        copy.wait()


def prepare(plan, place, column_kernels, row_kernels, weights, w, halo):
    frames, rows, _ = weights.shape
    height = tile_height(frames)
    out = pl.pallas_call(
        functools.partial(prepare_kernel, plan, frames, rows, halo, w),
        out_shape=[
            jax.ShapeDtypeStruct((count * rows + (height if taps else 0), w), f32)
            for _, _, count, taps in plan
        ]
        + [jax.ShapeDtypeStruct((height, w), f32)]
        + matrix_shapes(1, frames, rows, halo),
        in_specs=[SMEM, VMEM, VMEM, ANY],
        out_specs=[VMEM] * (len(plan) + 5),
        scratch_shapes=[pltpu.SemaphoreType.DMA((len(plan), frames))],
        name="prepare",
    )(place, column_kernels, row_kernels, weights)
    return out[: len(plan)], out[len(plan)], out[len(plan) + 1 :]


def blocks_kernel(n, halo, w, place, send_a, mid, send_b, recv_a, recv_b, *refs):
    outs, full = refs[:-1], refs[-1]
    rows, cols = mid.shape
    odd = lax.rem(place[1], 2)
    inner = slice(LANE, LANE + cols)
    for end in (0, LANE + cols):
        full[:, end : end + LANE] = jnp.zeros((rows, LANE), f32)
    full[:halo, inner] = mid[:halo, :] + choose(odd, recv_a[...], recv_b[...])
    full[halo : rows - halo, inner] = mid[halo : rows - halo, :]
    full[rows - halo :, inner] = mid[rows - halo :, :] + choose(odd, recv_b[...], recv_a[...])
    lane = lax.broadcasted_iota(jnp.int32, (rows, LANE), 1)
    for i in range(n):
        start = jnp.bitwise_xor(place[0], i) * w
        outs[i][:rows, :] = full[:, pl.ds(pl.multiple_of(start + LANE, LANE), w)]
        before = full[:, pl.ds(pl.multiple_of(start, LANE), LANE)]
        after = full[:, pl.ds(pl.multiple_of(start + LANE + w, LANE), LANE)]
        outs[i][rows:, :] = pack_edge(jnp.where(lane >= LANE - halo, before, after), halo, w)


def column_blocks(n, place, send_a, mid, send_b, recv_a, recv_b, w):
    rows, cols = mid.shape
    halo = send_a.shape[0]
    height = rows + rows * 2 * halo // w
    return pl.pallas_call(
        functools.partial(blocks_kernel, n, halo, w),
        out_shape=[jax.ShapeDtypeStruct((height, w), f32)] * n,
        in_specs=[SMEM] + [VMEM] * 5,
        out_specs=[VMEM] * n,
        scratch_shapes=[pltpu.VMEM((rows, cols + 2 * LANE), f32)],
        name="column_blocks",
    )(place, send_a, mid, send_b, recv_a, recv_b)


def start_kernel(n, rows, halo, w, place, est, *refs):
    parts = refs[:-5]
    k0, wide, send_a, send_b, stat = refs[-5:]
    total = parts[0][...]
    for p in parts[1:]:
        total = total + p[...]
    me = place[0]
    odd = lax.rem(place[1], 2)
    at = lambda start, size: est[:, pl.ds(pl.multiple_of(start, LANE), size)]
    own = -(total[:rows] + damping * at(me * w, w))
    edge = unpack_edge(total[rows:], halo)
    before = at(jnp.maximum(me * w - LANE, 0), LANE)
    after = at(jnp.minimum(me * w + w, (n * w) - LANE), LANE)
    none = jnp.zeros((rows, LANE), f32)
    left = choose((me > 0).astype(jnp.int32), -(edge + damping * before), none)
    right = choose((me < n - 1).astype(jnp.int32), -(edge + damping * after), none)
    k0[...] = own
    wide[:, :LANE] = left
    wide[:, LANE : LANE + w] = own
    wide[:, LANE + w :] = right
    low, high = wide[:halo, :], wide[rows - halo :, :]
    send_a[...] = choose(odd, low, high)
    send_b[...] = choose(odd, high, low)
    square = own * own
    acc = square[:, :LANE]
    for c in range(LANE, w, LANE):
        acc = acc + square[:, c : c + LANE]
    stat[...] = jnp.sum(acc.reshape(rows // 8, 8, LANE), axis=0)


def start_image(n, place, est, parts, halo):
    rows, cols = est.shape
    w = cols // n
    return pl.pallas_call(
        functools.partial(start_kernel, n, rows, halo, w),
        out_shape=[
            jax.ShapeDtypeStruct((rows, w), f32),
            jax.ShapeDtypeStruct((rows, w + 2 * LANE), f32),
            jax.ShapeDtypeStruct((halo, w + 2 * LANE), f32),
            jax.ShapeDtypeStruct((halo, w + 2 * LANE), f32),
            jax.ShapeDtypeStruct((8, LANE), f32),
        ],
        in_specs=[SMEM] + [VMEM] * (1 + len(parts)),
        out_specs=[VMEM] * 5,
        name="start_image",
    )(place, est, *parts)


def apply_kernel(frames, rows, halo, w, groups, origin, cut, count, pieces, place, *refs):
    image, refs = refs[:pieces], refs[pieces:]
    t_hbm, b_hbm, bp_hbm, ta_hbm, own = refs[:5]
    moved = refs[5 : 5 + count]
    send_a, mid, send_b, stat = refs[5 + count : 9 + count]
    refs = refs[9 + count :]
    if pieces > 1:
        whole, refs = refs[0], refs[1:]
    y_hi, y_lo, us, qs, vs_hi, vs_lo, acc, tb, bb, bpb, tab, wbuf, sem, wsem = refs
    odd = lax.rem(place[1], 2)
    ext = rows + 2 * halo

    def copies(g):
        span = pl.ds(g * frames, frames)
        return [
            pltpu.make_async_copy(t_hbm.at[span], tb.at[g], sem.at[0, g]),
            pltpu.make_async_copy(b_hbm.at[span], bb.at[g], sem.at[1, g]),
            pltpu.make_async_copy(bp_hbm.at[span], bpb.at[g], sem.at[2, g]),
            pltpu.make_async_copy(ta_hbm.at[g], tab.at[g], sem.at[3, g]),
        ]

    mine = pl.ds(pl.multiple_of(place[0] * w, LANE), w)
    for g in range(groups):
        for c in copies(g):
            c.start()
        for f in range(frames):
            if g == 0:
                source = own.at[f, :, mine]
            else:
                ref, start = origin[g, f]
                source = moved[ref].at[pl.ds(start, rows), :]
            pltpu.make_async_copy(source, wbuf.at[g, f], wsem.at[g, f]).start()
    clear_edges(y_hi, y_lo, qs, ext, rows, w)
    if pieces > 1:
        wide, recv_a, recv_b = image
        whole[:halo, :] = choose(odd, recv_a[...], recv_b[...])
        whole[halo : halo + rows, :] = wide[...]
        whole[halo + rows :, :] = choose(odd, recv_b[...], recv_a[...])
        load_image(y_hi, y_lo, whole[...], halo)
    else:
        load_image(y_hi, y_lo, image[0][...], halo)
    acc[...] = jnp.zeros_like(acc)
    stat[...] = jnp.zeros_like(stat)

    @pl.loop(0, groups)
    def _(g):
        for c in copies(g):
            c.wait()
        for f in range(frames):
            pltpu.make_async_copy(own.at[f, :, mine], wbuf.at[g, f], wsem.at[g, f]).wait()
        group_terms(
            frames, rows, w, y_hi, y_lo,
            lambda f: tb.at[g, f], lambda f: bb.at[g, f], lambda f: bpb.at[g, f], tab.at[g],
            lambda f: wbuf.at[g, f], None,
            us, qs, vs_hi, vs_lo, acc, stat,
        )

    z = unshift(acc[...], halo)
    send_a[...] = choose(odd, z[:cut], z[ext - cut :])
    send_b[...] = choose(odd, z[ext - cut :], z[:cut])
    mid[...] = z[cut : ext - cut]


def apply_terms(place, image, mats, weights, moved, origin, cut, halo):
    frames, rows, _ = weights.shape
    w = image[0].shape[1] - 2 * LANE
    ext = rows + 2 * halo
    t, b, bp, ta = mats
    groups = ta.shape[0]
    wide = w + LANE
    return pl.pallas_call(
        functools.partial(apply_kernel, frames, rows, halo, w, groups, origin, cut, len(moved), len(image)),
        out_shape=[
            jax.ShapeDtypeStruct((cut, wide), f32),
            jax.ShapeDtypeStruct((ext - 2 * cut, wide), f32),
            jax.ShapeDtypeStruct((cut, wide), f32),
            jax.ShapeDtypeStruct((8, LANE), f32),
        ]
        + [jax.ShapeDtypeStruct((ext, w + 2 * LANE), f32)] * (len(image) > 1),
        in_specs=[SMEM] + [VMEM] * len(image) + [ANY] * (5 + len(moved)),
        out_specs=[VMEM] * (4 + (len(image) > 1)),
        scratch_shapes=work_scratch(frames, rows, halo, w)
        + [
            pltpu.VMEM((groups, frames) + t.shape[1:], bf16),
            pltpu.VMEM((groups, frames) + b.shape[1:], bf16),
            pltpu.VMEM((groups, frames) + bp.shape[1:], bf16),
            pltpu.VMEM((groups,) + ta.shape[1:], bf16),
            pltpu.VMEM((groups, frames, rows, w), f32),
            pltpu.SemaphoreType.DMA((4, groups)),
            pltpu.SemaphoreType.DMA((groups, frames)),
        ],
        cost_estimate=pl.CostEstimate(
            flops=groups * 3 * 10**9, bytes_accessed=groups * 2**20, transcendentals=0
        ),
    )(place, *image, t, b, bp, ta, weights, *moved)


def rows_kernel(strips, halo, w, place, send_a, mid, send_b, recv_a, recv_b, q, col_a, col_b):
    odd = lax.rem(place[1], 2)
    odd_col = lax.rem(place[0], 2)
    edge_rows, wide = send_a.shape
    ext = q.shape[0]
    row = lax.broadcasted_iota(jnp.int32, (edge_rows, wide), 0)
    strip = jnp.full((edge_rows, wide), place[1], jnp.int32)
    low = choose(odd, send_a[...], send_b[...]) + choose(odd, recv_a[...], recv_b[...])
    high = choose(odd, send_b[...], send_a[...]) + choose(odd, recv_b[...], recv_a[...])
    q[:edge_rows, :] = jnp.where((row >= halo) | (strip > 0), low, 0.0)
    q[edge_rows : ext - edge_rows, :] = mid[...]
    q[ext - edge_rows :, :] = jnp.where((row < edge_rows - halo) | (strip < strips - 1), high, 0.0)
    lane = lax.broadcasted_iota(jnp.int32, (ext, LANE), 1)
    edge = q[:, w:]
    to_left = jnp.where(lane < halo, q[:, :LANE], edge)
    to_right = jnp.where(lane >= LANE - halo, q[:, w - LANE : w], edge)
    col_a[...] = choose(odd_col, to_left, to_right)
    col_b[...] = choose(odd_col, to_right, to_left)


def merge_rows(strips, place, send_a, mid, send_b, recv_a, recv_b, halo):
    ext = mid.shape[0] + 2 * send_a.shape[0]
    wide = mid.shape[1]
    return pl.pallas_call(
        functools.partial(rows_kernel, strips, halo, wide - LANE),
        out_shape=[
            jax.ShapeDtypeStruct((ext, wide), f32),
            jax.ShapeDtypeStruct((ext, LANE), f32),
            jax.ShapeDtypeStruct((ext, LANE), f32),
        ],
        in_specs=[SMEM] + [VMEM] * 5,
        out_specs=[VMEM] * 3,
        name="merge_rows",
    )(place, send_a, mid, send_b, recv_a, recv_b)


def wrap_kernel(rows, halo, w, place, send_a, mid, send_b, recv_a, recv_b, before, out):
    odd = lax.rem(place[1], 2)
    keep = rows - 2 * halo
    pieces = (
        (0, halo, mid[:halo, :] + choose(odd, recv_a[...], recv_b[...])),
        (halo, keep, mid[halo : rows - halo, :]),
        (rows - halo, halo, mid[rows - halo :, :] + choose(odd, recv_b[...], recv_a[...])),
    )
    edges = []
    for start, size, value in pieces:
        span = slice(start, start + size)
        out[span, :] = value[:, :w] + damping * before[span, :]
        edges.append(value[:, w:])
    out[rows:, :] = pack_edge(jnp.concatenate(edges, axis=0), halo, w)


def wrap(place, send_a, mid, send_b, recv_a, recv_b, before, halo):
    rows, w = before.shape
    height = rows + rows * 2 * halo // w
    return pl.pallas_call(
        functools.partial(wrap_kernel, rows, halo, w),
        out_shape=jax.ShapeDtypeStruct((height, w), f32),
        in_specs=[SMEM] + [VMEM] * 6,
        out_specs=VMEM,
        name="wrap",
    )(place, send_a, mid, send_b, recv_a, recv_b, before)


def final_kernel(n, rows, halo, w, place, est, sums, *refs):
    k0, k1, k2 = refs[:n], refs[n : 2 * n], refs[2 * n : 3 * n]
    sol, res, full = refs[3 * n :]
    total = [jnp.sum(jnp.sum(sums[i], axis=0, keepdims=True), axis=1, keepdims=True) for i in range(4)]
    k00, k11 = total[0], total[2]
    k01 = total[1] + damping * k00
    k12 = total[3] + damping * k11
    alpha0 = k00 / k01
    norm1 = k00 - 2.0 * alpha0 * k01 + alpha0 * alpha0 * k11
    beta = norm1 / k00
    curve1 = (1.0 + beta) * (1.0 + beta) * k01 - 2.0 * (1.0 + beta) * alpha0 * k11
    curve1 = curve1 + alpha0 * alpha0 * k12
    alpha1 = norm1 / curve1
    c1 = alpha0 + alpha1 * (1.0 + beta)
    c2 = alpha0 * alpha1

    lane = lax.broadcasted_iota(jnp.int32, (rows, LANE), 1)
    spot = [jnp.bitwise_xor(place[0], i) for i in range(n)]
    for end in (0, LANE + n * w):
        full[:, end : end + LANE] = jnp.zeros((rows, LANE), f32)
    for i in range(n):
        full[:, pl.ds(pl.multiple_of(spot[i] * w + LANE, LANE), w)] = k2[i][:rows, :]
    for i in range(n):
        edge = unpack_edge(k2[i][rows:, :], halo)
        left = pl.ds(pl.multiple_of(spot[i] * w, LANE), LANE)
        right = pl.ds(pl.multiple_of(spot[i] * w + w + LANE, LANE), LANE)
        full[:, left] += jnp.where(lane >= LANE - halo, edge, 0.0)
        full[:, right] += jnp.where(lane < halo, edge, 0.0)
    for i in range(n):
        cols = pl.ds(pl.multiple_of(spot[i] * w, LANE), w)
        a0, a1 = k0[i][...], k1[i][...]
        sol[:, cols] = est[:, cols] + c1 * a0 - c2 * a1
        res[:, cols] = a0 - c1 * a1 + c2 * full[:, pl.ds(pl.multiple_of(spot[i] * w + LANE, LANE), w)]


def final_images(place, est, sums, k0, k1, k2, halo):
    n = len(k0)
    rows, w = k0[0].shape
    return pl.pallas_call(
        functools.partial(final_kernel, n, rows, halo, w),
        out_shape=[jax.ShapeDtypeStruct(est.shape, f32)] * 2,
        in_specs=[SMEM] + [VMEM] * (2 + 3 * n),
        out_specs=[VMEM] * 2,
        scratch_shapes=[pltpu.VMEM((rows, n * w + 2 * LANE), f32)],
        name="final_images",
    )(place, est, sums, *k0, *k1, *k2)


def neighbours(send_a, send_b, axis):
    n = lax.axis_size(axis)
    out = []
    for lead, x in ((0, send_a), (1, send_b)):
        pairs = [(i, i + 1) for i in range(lead, n - 1, 2)]
        out.append(lax.ppermute(x, axis, pairs + [(b, a) for a, b in pairs]))
    return out


def swap(x, axis, distance):
    n = lax.axis_size(axis)
    return lax.ppermute(x, axis, [(i, i ^ distance) for i in range(n)])


def steps(estimate, observed, weights, column_kernels, row_kernels):
    n = lax.axis_size("frame")
    me = lax.axis_index("frame")
    strips = lax.axis_size("strip")
    strip = lax.axis_index("strip")
    place = jnp.stack([me, strip]).astype(jnp.int32)
    rows, cols = estimate.shape
    frames = weights.shape[0]
    halo = column_kernels.shape[1] // 2
    w = cols // n
    ext = rows + 2 * halo
    distances = [1 << k for k in range(n.bit_length() - 1)]

    def fold(x):
        return jnp.sum(x.reshape(rows * w // (8 * LANE), 8, LANE), axis=0)

    low, high = estimate[:halo], estimate[rows - halo :]
    odd = strip % 2 == 1
    est_a, est_b = neighbours(
        jnp.where(odd, low, high), jnp.where(odd, high, low), "strip"
    )

    early = frames // 2
    plan = [(d, 0, frames, True) for d in range(1, n - 1)]
    plan += [(n - 1, 0, early, True), (n - 1, early, frames - early, False)]
    packed, tile, own_mats = prepare(plan, place, column_kernels, row_kernels, weights, w, halo)
    moved = []
    for i, (d, _, _, taps) in enumerate(plan):
        moved.append(swap(packed[i], "frame", d))
    origin = {}
    starts = [0]
    for i, (d, lead, count, taps) in enumerate(plan):
        for k in range(count):
            origin[d, lead + k] = (i, k * rows)
        if taps:
            starts.append(count * rows)

    send_a, mid, send_b = first_terms(
        place, estimate, est_a, est_b, own_mats, weights, observed, w
    )
    mats = setup_matrices([tile] + moved[: n - 1], starts, frames, rows, halo)
    recv_a, recv_b = neighbours(send_a, send_b, "strip")

    part = list(column_blocks(n, place, send_a, mid, send_b, recv_a, recv_b, w))
    mine = [part[0]]
    for i in range(n - 1, 0, -1):
        d = i & -i
        got = swap(part[i], "frame", d)
        if i == d:
            mine.append(got)
        else:
            part[i ^ d] = part[i ^ d] + got
    k0, wide, send_a, send_b, k00_part = start_image(n, place, estimate, mine, halo)
    recv_a, recv_b = neighbours(send_a, send_b, "strip")

    send_a, mid, send_b, stat1, k0x = apply_terms(
        place, (wide, recv_a, recv_b), mats, weights, moved, origin, 2 * halo, halo
    )
    recv_a, recv_b = neighbours(send_a, send_b, "strip")
    q, col_a, col_b = merge_rows(strips, place, send_a, mid, send_b, recv_a, recv_b, halo)
    recv_a, recv_b = neighbours(col_a, col_b, "frame")
    odd = me % 2 == 1
    from_left = jnp.where(odd, recv_a, recv_b)
    from_right = jnp.where(odd, recv_b, recv_a)
    lane = lax.broadcasted_iota(jnp.int32, (ext, LANE), 1)
    left_tile = jnp.where(me == 0, 0.0, q[:, w:] + from_left)
    right_tile = jnp.where(me == n - 1, 0.0, q[:, w:] + from_right)
    own_left = jnp.where(lane < halo, from_left, 0.0)
    own_right = jnp.where(lane >= LANE - halo, from_right, 0.0)
    pad = jnp.zeros((ext, w - LANE), f32)
    own = (
        q[:, :w]
        + jnp.concatenate([own_left, pad], axis=1)
        + jnp.concatenate([pad, own_right], axis=1)
    )
    k1x = jnp.concatenate([left_tile, own, right_tile], axis=1) + damping * k0x
    k1, k1x = lax.optimization_barrier((k1x[halo : halo + rows, LANE : LANE + w], k1x))
    k11_part = fold(k1 * k1)

    send_a, mid, send_b, stat2 = apply_terms(
        place, (k1x,), mats, weights, moved, origin, halo, halo
    )
    recv_a, recv_b = neighbours(send_a, send_b, "strip")
    sums = jnp.stack([k00_part, stat1, k11_part, stat2])
    for axis, size in (("frame", n), ("strip", strips)):
        d = 1
        while d < size:
            sums = sums + swap(sums, axis, d)
            d *= 2
    k2 = wrap(place, send_a, mid, send_b, recv_a, recv_b, k1, halo)

    def gathered(x):
        parts = [x] + [None] * (n - 1)
        for i in range(n):
            for d in reversed(distances):
                if i % (2 * d) == 0:
                    parts[i + d] = swap(parts[i], "frame", d)
        return parts

    g0, g1, g2 = gathered(k0), gathered(k1), gathered(k2)
    return tuple(final_images(place, estimate, sums, g0, g1, g2, halo))


def solution(mesh):
    return jax.shard_map(
        steps,
        mesh=mesh,
        in_specs=(
            P("strip", None),
            P("frame", "strip", None),
            P("frame", "strip", None),
            P("frame", None),
            P("frame", None),
        ),
        out_specs=(P("strip", None), P("strip", None)),
        check_vma=False,
    )
```

```python
import functools

import jax
import jax.numpy as jnp
from jax import lax
from jax.experimental import pallas as pl
from jax.experimental.pallas import tpu as pltpu
from jax.sharding import PartitionSpec as P


damping = 0.05
f32 = jnp.float32
bf16 = jnp.bfloat16
LANE = 128
VMEM = pl.BlockSpec(memory_space=pltpu.VMEM)
ANY = pl.BlockSpec(memory_space=pl.ANY)
SMEM = pl.BlockSpec(memory_space=pltpu.SMEM)


def split(x):
    hi = x.astype(bf16)
    lo = (x - hi.astype(f32)).astype(bf16)
    return hi, lo


def dot(a, b):
    return jnp.dot(a, b, preferred_element_type=f32)


def choose(flag, a, b):
    return jnp.where(jnp.full(a.shape, flag, jnp.int32) == 1, a, b)


def pack_edge(edge, halo, w):
    rows = edge.shape[0]
    per = LANE // (2 * halo)
    short = rows * 2 * halo // w
    edge = pltpu.roll(edge, halo, 1)
    lane = lax.broadcasted_iota(jnp.int32, (short, LANE), 1)
    out = []
    for t in range(w // LANE):
        tile = None
        for p in range(per):
            k = t * per + p
            part = edge[k * short : (k + 1) * short]
            part = pltpu.roll(part, p * 2 * halo, 1) if p else part
            tile = part if tile is None else jnp.where(lane >= p * 2 * halo, part, tile)
        out.append(tile)
    return jnp.concatenate(out, axis=1)


def unpack_edge(packed, halo):
    _, w = packed.shape
    per = LANE // (2 * halo)
    parts = []
    for k in range(w // (2 * halo)):
        t, p = divmod(k, per)
        part = packed[:, t * LANE : (t + 1) * LANE]
        back = (LANE - halo - p * 2 * halo) % LANE
        parts.append(pltpu.roll(part, back, 1) if back else part)
    return jnp.concatenate(parts, axis=0)


def tiles(width, step=256):
    return [(s, min(step, width - s)) for s in range(0, width, step)]


def toeplitz(base, count):
    wide = base.shape[1]
    return pltpu.roll(jnp.broadcast_to(base, (count, wide)), 0, 1, stride=1, stride_axis=0)


def build_group(taps, g, frames, rows, halo, t_ref, b_ref, bp_ref, ta_ref):
    ext = rows + 2 * halo
    unit = taps / jnp.sum(taps, axis=1, keepdims=True)
    for s in range(frames):
        f = g * frames + s
        col = unit[s : s + 1]
        row = unit[frames + s : frames + s + 1]
        by_rows = toeplitz(row, rows)
        hi, lo = split(by_rows)
        t_ref[f, :rows, :] = hi
        t_ref[f, rows:, :] = lo
        hi, lo = split(by_rows.T[:ext])
        ta_ref[g, :ext, s * rows : (s + 1) * rows] = hi
        ta_ref[g, ext:, s * rows : (s + 1) * rows] = lo
        hi, lo = split(toeplitz(col, LANE).T)
        b_ref[f, :, :LANE] = hi
        b_ref[f, :, LANE:] = lo
        hi, lo = split(toeplitz(pltpu.roll(col, LANE, 1), 2 * LANE)[:, :LANE])
        bp_ref[f, :, :LANE] = hi
        bp_ref[f, :, LANE:] = lo


def matrix_shapes(groups, frames, rows, halo):
    ext = rows + 2 * halo
    return [
        jax.ShapeDtypeStruct(s, bf16)
        for s in (
            (groups * frames, 2 * rows, 2 * LANE),
            (groups * frames, 2 * LANE, 2 * LANE),
            (groups * frames, 2 * LANE, 2 * LANE),
            (groups, 2 * ext, frames * rows),
        )
    ]


def tile_height(frames):
    return -(-2 * frames // 8) * 8


def setup_kernel(frames, rows, halo, starts, *refs):
    tiles_in = refs[: len(starts)]
    mats, taps, sem = refs[len(starts) : -2], refs[-2], refs[-1]
    height = tile_height(frames)

    def copy(g):
        source = tiles_in[g].at[pl.ds(starts[g], height), pl.ds(0, 2 * LANE)]
        return pltpu.make_async_copy(source, taps.at[g], sem.at[g])

    for g in range(len(starts)):
        copy(g).start()
    for g in range(len(starts)):
        copy(g).wait()
        build_group(taps[g], g, frames, rows, halo, *mats)


def setup_matrices(tiles_in, starts, frames, rows, halo):
    groups = len(tiles_in)
    return pl.pallas_call(
        functools.partial(setup_kernel, frames, rows, halo, starts),
        out_shape=matrix_shapes(groups, frames, rows, halo),
        in_specs=[ANY] * groups,
        out_specs=[VMEM] * 4,
        scratch_shapes=[
            pltpu.VMEM((groups, tile_height(frames), 2 * LANE), f32),
            pltpu.SemaphoreType.DMA((groups,)),
        ],
        name="setup_all",
    )(*tiles_in)


def load_image(y_hi, y_lo, image, halo):
    ext, full = image.shape
    shift = LANE - halo
    y = pltpu.roll(image, full - shift, 1)[:, : full - LANE]
    hi, lo = split(y)
    y_hi[:ext, :] = hi
    y_lo[:ext, :] = lo


def group_terms(frames, rows, w, y_hi, y_lo, t, b, bp, ta, weight, data, us, qs, vs_hi, vs_lo, acc, stat, ready=None):
    total = None
    for f in range(frames):
        for c, size in tiles(w + LANE):
            r1 = dot(t(f)[...], y_hi[:, c : c + size])
            r2 = dot(t(f)[:rows, :], y_lo[:, c : c + size])
            hi, lo = split(r1[:rows] + r1[rows:] + r2)
            us[:rows, c : c + size] = hi
            us[rows:, c : c + size] = lo
        if ready is not None:
            ready(f)
        for k in range(w // LANE):
            c = k * LANE
            r = dot(us[:, c : c + 2 * LANE], b(f)[...])
            a = r[:rows, :LANE] + r[:rows, LANE:] + r[rows:, :LANE]
            if data is not None:
                a = a - data(f)[:, c : c + LANE]
            q = weight(f)[:, c : c + LANE] * a
            if stat is not None:
                part = jnp.sum((a * q).reshape(rows // 8, 8, LANE), axis=0)
                total = part if total is None else total + part
            hi, lo = split(q)
            qs[:rows, c + LANE : c + 2 * LANE] = hi
            qs[rows:, c + LANE : c + 2 * LANE] = lo
        for k in range(w // LANE + 1):
            c = k * LANE
            r = dot(qs[:, c : c + 2 * LANE], bp(f)[...])
            hi, lo = split(r[:rows, :LANE] + r[:rows, LANE:] + r[rows:, :LANE])
            vs_hi[f * rows : (f + 1) * rows, c : c + LANE] = hi
            vs_lo[f * rows : (f + 1) * rows, c : c + LANE] = lo
    ext = acc.shape[0]
    for c, size in tiles(w + LANE):
        r1 = dot(ta[...], vs_hi[:, c : c + size])
        r2 = dot(ta[:ext, :], vs_lo[:, c : c + size])
        acc[:, c : c + size] += r1[:ext] + r1[ext:] + r2
    if stat is not None:
        stat[...] += total


def work_scratch(frames, rows, halo, w):
    ext = rows + 2 * halo
    return [
        pltpu.VMEM((2 * LANE, w + LANE), bf16),
        pltpu.VMEM((2 * LANE, w + LANE), bf16),
        pltpu.VMEM((2 * rows, w + LANE), bf16),
        pltpu.VMEM((2 * rows, w + 2 * LANE), bf16),
        pltpu.VMEM((frames * rows, w + LANE), bf16),
        pltpu.VMEM((frames * rows, w + LANE), bf16),
        pltpu.VMEM((ext, w + LANE), f32),
    ]


def clear_edges(y_hi, y_lo, qs, ext, rows, w):
    zero = jnp.zeros((y_hi.shape[0] - ext, y_hi.shape[1]), bf16)
    y_hi[ext:, :] = zero
    y_lo[ext:, :] = zero
    qs[:, :LANE] = jnp.zeros((2 * rows, LANE), bf16)
    qs[:, w + LANE :] = jnp.zeros((2 * rows, LANE), bf16)


def unshift(acc, halo):
    return pltpu.roll(acc, acc.shape[1] - halo, 1)


def first_kernel(
    frames, rows, halo,
    place, est, recv_a, recv_b, t_ref, b_ref, bp_ref, ta_ref, w_hbm, d_hbm,
    send_a, mid, send_b,
    y_hi, y_lo, us, qs, vs_hi, vs_lo, acc, wbuf, dbuf, sem,
):
    ext = rows + 2 * halo
    cols = est.shape[1]
    copies = [
        (
            pltpu.make_async_copy(w_hbm.at[f], wbuf.at[f], sem.at[0, f]),
            pltpu.make_async_copy(d_hbm.at[f], dbuf.at[f], sem.at[1, f]),
        )
        for f in range(frames)
    ]
    for pair in copies:
        for c in pair:
            c.start()
    clear_edges(y_hi, y_lo, qs, ext, rows, cols)
    odd = lax.rem(place[1], 2)
    none = jnp.zeros((ext, LANE), f32)
    for start in range(0, cols, 4 * LANE):
        size = 4 * LANE + LANE
        left = max(start - LANE, 0)
        span = slice(left, min(start + 4 * LANE, cols))
        x = jnp.concatenate(
            [
                choose(odd, recv_a[:, span], recv_b[:, span]),
                est[:, span],
                choose(odd, recv_b[:, span], recv_a[:, span]),
            ],
            axis=0,
        )
        if start == 0:
            x = jnp.concatenate([none, x], axis=1)
        if x.shape[1] < size:
            x = jnp.concatenate([x, jnp.zeros((ext, size - x.shape[1]), f32)], axis=1)
        hi, lo = split(pltpu.roll(x, halo, 1)[:, LANE:])
        y_hi[:ext, start : start + 4 * LANE] = hi
        y_lo[:ext, start : start + 4 * LANE] = lo
        if start + 4 * LANE >= cols:
            tail = jnp.concatenate([x[:, 4 * LANE :], none], axis=1)
            hi, lo = split(pltpu.roll(tail, halo, 1)[:, LANE:])
            y_hi[:ext, cols:] = hi
            y_lo[:ext, cols:] = lo
    acc[...] = jnp.zeros_like(acc)

    def ready(f):
        for c in copies[f]:
            c.wait()

    group_terms(
        frames, rows, cols, y_hi, y_lo,
        lambda f: t_ref.at[f], lambda f: b_ref.at[f], lambda f: bp_ref.at[f], ta_ref.at[0],
        lambda f: wbuf.at[f], lambda f: dbuf.at[f],
        us, qs, vs_hi, vs_lo, acc, None, ready,
    )
    for start in range(0, cols, 4 * LANE):
        size = min(4 * LANE, cols - start)
        z = pltpu.roll(acc[:, start : start + size + LANE], size + LANE - halo, 1)[:, :size]
        span = slice(start, start + size)
        low, high = z[:halo], z[halo + rows :]
        send_a[:, span] = choose(odd, low, high)
        send_b[:, span] = choose(odd, high, low)
        mid[:, span] = z[halo : halo + rows]


def first_terms(place, est, recv_a, recv_b, mats, weights, observed):
    frames, rows, cols = weights.shape
    halo = recv_a.shape[0]
    return pl.pallas_call(
        functools.partial(first_kernel, frames, rows, halo),
        out_shape=[
            jax.ShapeDtypeStruct((halo, cols), f32),
            jax.ShapeDtypeStruct((rows, cols), f32),
            jax.ShapeDtypeStruct((halo, cols), f32),
        ],
        in_specs=[SMEM] + [VMEM] * 7 + [ANY, ANY],
        out_specs=[VMEM] * 3,
        scratch_shapes=work_scratch(frames, rows, halo, cols)
        + [
            pltpu.VMEM((frames, rows, cols), f32),
            pltpu.VMEM((frames, rows, cols), f32),
            pltpu.SemaphoreType.DMA((2, frames)),
        ],
        cost_estimate=pl.CostEstimate(flops=8 * 10**9, bytes_accessed=8 * 2**20, transcendentals=0),
        name="first_terms",
    )(place, est, recv_a, recv_b, *mats, weights, observed)


def prepare_kernel(plan, frames, rows, halo, w, place, cols_in, rows_in, weights, *refs):
    outs, tile, mats, sem = refs[: len(plan)], refs[len(plan)], refs[len(plan) + 1 : -1], refs[-1]
    taps = cols_in.shape[1]
    pending = []
    for i, (distance, lead, count, _) in enumerate(plan):
        start = pl.multiple_of(jnp.bitwise_xor(place[0], distance) * w, LANE)
        for k in range(count):
            copy = pltpu.make_async_copy(
                weights.at[lead + k, :, pl.ds(start, w)],
                outs[i].at[pl.ds(k * rows, rows), :],
                sem.at[i, k],
            )
            copy.start()
            pending.append(copy)
    tile[...] = jnp.zeros_like(tile)
    tile[:frames, :taps] = cols_in[...]
    tile[frames : 2 * frames, :taps] = rows_in[...]
    for i, (_, _, count, with_taps) in enumerate(plan):
        if with_taps:
            outs[i][count * rows :, :] = tile[...]
    build_group(tile[:, : 2 * LANE], 0, frames, rows, halo, *mats)
    for copy in pending:
        copy.wait()


def prepare(plan, place, column_kernels, row_kernels, weights, w, halo):
    frames, rows, _ = weights.shape
    height = tile_height(frames)
    out = pl.pallas_call(
        functools.partial(prepare_kernel, plan, frames, rows, halo, w),
        out_shape=[
            jax.ShapeDtypeStruct((count * rows + (height if taps else 0), w), f32)
            for _, _, count, taps in plan
        ]
        + [jax.ShapeDtypeStruct((height, w), f32)]
        + matrix_shapes(1, frames, rows, halo),
        in_specs=[SMEM, VMEM, VMEM, ANY],
        out_specs=[VMEM] * (len(plan) + 5),
        scratch_shapes=[pltpu.SemaphoreType.DMA((len(plan), frames))],
        name="prepare",
    )(place, column_kernels, row_kernels, weights)
    return out[: len(plan)], out[len(plan)], out[len(plan) + 1 :]


def blocks_kernel(n, halo, w, place, send_a, mid, send_b, recv_a, recv_b, *refs):
    outs, full = refs[:-1], refs[-1]
    rows, cols = mid.shape
    odd = lax.rem(place[1], 2)
    inner = slice(LANE, LANE + cols)
    for end in (0, LANE + cols):
        full[:, end : end + LANE] = jnp.zeros((rows, LANE), f32)
    full[:halo, inner] = mid[:halo, :] + choose(odd, recv_a[...], recv_b[...])
    full[halo : rows - halo, inner] = mid[halo : rows - halo, :]
    full[rows - halo :, inner] = mid[rows - halo :, :] + choose(odd, recv_b[...], recv_a[...])
    lane = lax.broadcasted_iota(jnp.int32, (rows, LANE), 1)
    for i in range(n):
        start = jnp.bitwise_xor(place[0], i) * w
        outs[i][:rows, :] = full[:, pl.ds(pl.multiple_of(start + LANE, LANE), w)]
        before = full[:, pl.ds(pl.multiple_of(start, LANE), LANE)]
        after = full[:, pl.ds(pl.multiple_of(start + LANE + w, LANE), LANE)]
        outs[i][rows:, :] = pack_edge(jnp.where(lane >= LANE - halo, before, after), halo, w)


def column_blocks(n, place, send_a, mid, send_b, recv_a, recv_b, w):
    rows, cols = mid.shape
    halo = send_a.shape[0]
    height = rows + rows * 2 * halo // w
    return pl.pallas_call(
        functools.partial(blocks_kernel, n, halo, w),
        out_shape=[jax.ShapeDtypeStruct((height, w), f32)] * n,
        in_specs=[SMEM] + [VMEM] * 5,
        out_specs=[VMEM] * n,
        scratch_shapes=[pltpu.VMEM((rows, cols + 2 * LANE), f32)],
        name="column_blocks",
    )(place, send_a, mid, send_b, recv_a, recv_b)


def start_kernel(n, rows, halo, w, place, est, *refs):
    parts = refs[:-5]
    k0, wide, send_a, send_b, stat = refs[-5:]
    total = parts[0][...]
    for p in parts[1:]:
        total = total + p[...]
    me = place[0]
    odd = lax.rem(place[1], 2)
    at = lambda start, size: est[:, pl.ds(pl.multiple_of(start, LANE), size)]
    own = -(total[:rows] + damping * at(me * w, w))
    edge = unpack_edge(total[rows:], halo)
    before = at(jnp.maximum(me * w - LANE, 0), LANE)
    after = at(jnp.minimum(me * w + w, (n * w) - LANE), LANE)
    none = jnp.zeros((rows, LANE), f32)
    left = choose((me > 0).astype(jnp.int32), -(edge + damping * before), none)
    right = choose((me < n - 1).astype(jnp.int32), -(edge + damping * after), none)
    k0[...] = own
    wide[:, :LANE] = left
    wide[:, LANE : LANE + w] = own
    wide[:, LANE + w :] = right
    low, high = wide[:halo, :], wide[rows - halo :, :]
    send_a[...] = choose(odd, low, high)
    send_b[...] = choose(odd, high, low)
    square = own * own
    acc = square[:, :LANE]
    for c in range(LANE, w, LANE):
        acc = acc + square[:, c : c + LANE]
    stat[...] = jnp.sum(acc.reshape(rows // 8, 8, LANE), axis=0)


def start_image(n, place, est, parts, halo):
    rows, cols = est.shape
    w = cols // n
    return pl.pallas_call(
        functools.partial(start_kernel, n, rows, halo, w),
        out_shape=[
            jax.ShapeDtypeStruct((rows, w), f32),
            jax.ShapeDtypeStruct((rows, w + 2 * LANE), f32),
            jax.ShapeDtypeStruct((halo, w + 2 * LANE), f32),
            jax.ShapeDtypeStruct((halo, w + 2 * LANE), f32),
            jax.ShapeDtypeStruct((8, LANE), f32),
        ],
        in_specs=[SMEM] + [VMEM] * (1 + len(parts)),
        out_specs=[VMEM] * 5,
        name="start_image",
    )(place, est, *parts)


def apply_kernel(frames, rows, halo, w, groups, origin, cut, count, pieces, place, *refs):
    image, refs = refs[:pieces], refs[pieces:]
    t_hbm, b_hbm, bp_hbm, ta_hbm, own = refs[:5]
    moved = refs[5 : 5 + count]
    send_a, mid, send_b, stat = refs[5 + count : 9 + count]
    refs = refs[9 + count :]
    if pieces > 1:
        whole, refs = refs[0], refs[1:]
    y_hi, y_lo, us, qs, vs_hi, vs_lo, acc, tb, bb, bpb, tab, wbuf, sem, wsem = refs
    odd = lax.rem(place[1], 2)
    ext = rows + 2 * halo

    def copies(g):
        span = pl.ds(g * frames, frames)
        return [
            pltpu.make_async_copy(t_hbm.at[span], tb.at[g], sem.at[0, g]),
            pltpu.make_async_copy(b_hbm.at[span], bb.at[g], sem.at[1, g]),
            pltpu.make_async_copy(bp_hbm.at[span], bpb.at[g], sem.at[2, g]),
            pltpu.make_async_copy(ta_hbm.at[g], tab.at[g], sem.at[3, g]),
        ]

    mine = pl.ds(pl.multiple_of(place[0] * w, LANE), w)
    for g in range(groups):
        for c in copies(g):
            c.start()
        for f in range(frames):
            if g == 0:
                source = own.at[f, :, mine]
            else:
                ref, start = origin[g, f]
                source = moved[ref].at[pl.ds(start, rows), :]
            pltpu.make_async_copy(source, wbuf.at[g, f], wsem.at[g, f]).start()
    clear_edges(y_hi, y_lo, qs, ext, rows, w)
    if pieces > 1:
        wide, recv_a, recv_b = image
        whole[:halo, :] = choose(odd, recv_a[...], recv_b[...])
        whole[halo : halo + rows, :] = wide[...]
        whole[halo + rows :, :] = choose(odd, recv_b[...], recv_a[...])
        load_image(y_hi, y_lo, whole[...], halo)
    else:
        load_image(y_hi, y_lo, image[0][...], halo)
    acc[...] = jnp.zeros_like(acc)
    stat[...] = jnp.zeros_like(stat)

    @pl.loop(0, groups)
    def _(g):
        for c in copies(g):
            c.wait()
        for f in range(frames):
            pltpu.make_async_copy(own.at[f, :, mine], wbuf.at[g, f], wsem.at[g, f]).wait()
        group_terms(
            frames, rows, w, y_hi, y_lo,
            lambda f: tb.at[g, f], lambda f: bb.at[g, f], lambda f: bpb.at[g, f], tab.at[g],
            lambda f: wbuf.at[g, f], None,
            us, qs, vs_hi, vs_lo, acc, stat,
        )

    z = unshift(acc[...], halo)
    send_a[...] = choose(odd, z[:cut], z[ext - cut :])
    send_b[...] = choose(odd, z[ext - cut :], z[:cut])
    mid[...] = z[cut : ext - cut]


def apply_terms(place, image, mats, weights, moved, origin, cut, halo):
    frames, rows, _ = weights.shape
    w = image[0].shape[1] - 2 * LANE
    ext = rows + 2 * halo
    t, b, bp, ta = mats
    groups = ta.shape[0]
    wide = w + LANE
    return pl.pallas_call(
        functools.partial(apply_kernel, frames, rows, halo, w, groups, origin, cut, len(moved), len(image)),
        out_shape=[
            jax.ShapeDtypeStruct((cut, wide), f32),
            jax.ShapeDtypeStruct((ext - 2 * cut, wide), f32),
            jax.ShapeDtypeStruct((cut, wide), f32),
            jax.ShapeDtypeStruct((8, LANE), f32),
        ]
        + [jax.ShapeDtypeStruct((ext, w + 2 * LANE), f32)] * (len(image) > 1),
        in_specs=[SMEM] + [VMEM] * len(image) + [ANY] * (5 + len(moved)),
        out_specs=[VMEM] * (4 + (len(image) > 1)),
        scratch_shapes=work_scratch(frames, rows, halo, w)
        + [
            pltpu.VMEM((groups, frames) + t.shape[1:], bf16),
            pltpu.VMEM((groups, frames) + b.shape[1:], bf16),
            pltpu.VMEM((groups, frames) + bp.shape[1:], bf16),
            pltpu.VMEM((groups,) + ta.shape[1:], bf16),
            pltpu.VMEM((groups, frames, rows, w), f32),
            pltpu.SemaphoreType.DMA((4, groups)),
            pltpu.SemaphoreType.DMA((groups, frames)),
        ],
        cost_estimate=pl.CostEstimate(
            flops=groups * 3 * 10**9, bytes_accessed=groups * 2**20, transcendentals=0
        ),
    )(place, *image, t, b, bp, ta, weights, *moved)


def rows_kernel(strips, halo, w, place, send_a, mid, send_b, recv_a, recv_b, q, col_a, col_b):
    odd = lax.rem(place[1], 2)
    odd_col = lax.rem(place[0], 2)
    edge_rows, wide = send_a.shape
    ext = q.shape[0]
    row = lax.broadcasted_iota(jnp.int32, (edge_rows, wide), 0)
    strip = jnp.full((edge_rows, wide), place[1], jnp.int32)
    low = choose(odd, send_a[...], send_b[...]) + choose(odd, recv_a[...], recv_b[...])
    high = choose(odd, send_b[...], send_a[...]) + choose(odd, recv_b[...], recv_a[...])
    q[:edge_rows, :] = jnp.where((row >= halo) | (strip > 0), low, 0.0)
    q[edge_rows : ext - edge_rows, :] = mid[...]
    q[ext - edge_rows :, :] = jnp.where((row < edge_rows - halo) | (strip < strips - 1), high, 0.0)
    lane = lax.broadcasted_iota(jnp.int32, (ext, LANE), 1)
    edge = q[:, w:]
    to_left = jnp.where(lane < halo, q[:, :LANE], edge)
    to_right = jnp.where(lane >= LANE - halo, q[:, w - LANE : w], edge)
    col_a[...] = choose(odd_col, to_left, to_right)
    col_b[...] = choose(odd_col, to_right, to_left)


def merge_rows(strips, place, send_a, mid, send_b, recv_a, recv_b, halo):
    ext = mid.shape[0] + 2 * send_a.shape[0]
    wide = mid.shape[1]
    return pl.pallas_call(
        functools.partial(rows_kernel, strips, halo, wide - LANE),
        out_shape=[
            jax.ShapeDtypeStruct((ext, wide), f32),
            jax.ShapeDtypeStruct((ext, LANE), f32),
            jax.ShapeDtypeStruct((ext, LANE), f32),
        ],
        in_specs=[SMEM] + [VMEM] * 5,
        out_specs=[VMEM] * 3,
        name="merge_rows",
    )(place, send_a, mid, send_b, recv_a, recv_b)


def cols_kernel(n, rows, halo, place, q, recv_a, recv_b, before, out, block, stat):
    odd = lax.rem(place[0], 2)
    ext, wide = q.shape
    w = wide - LANE
    lane = lax.broadcasted_iota(jnp.int32, (ext, LANE), 1)
    at = jnp.full((ext, LANE), place[0], jnp.int32)
    left = choose(odd, recv_a[...], recv_b[...])
    right = choose(odd, recv_b[...], recv_a[...])
    edge = q[:, w:]
    total = None
    out[:, :LANE] = jnp.where(at > 0, edge + left, 0.0) + damping * before[:, :LANE]
    out[:, LANE + w :] = jnp.where(at < n - 1, edge + right, 0.0) + damping * before[:, LANE + w :]
    for c in range(0, w, LANE):
        x = q[:, c : c + LANE] + damping * before[:, c + LANE : c + 2 * LANE]
        if c == 0:
            x = x + jnp.where(lane < halo, left, 0.0)
        if c == w - LANE:
            x = x + jnp.where(lane >= LANE - halo, right, 0.0)
        out[:, c + LANE : c + 2 * LANE] = x
        own = x[halo : halo + rows]
        block[:, c : c + LANE] = own
        part = jnp.sum((own * own).reshape(rows // 8, 8, LANE), axis=0)
        total = part if total is None else total + part
    stat[...] = total


def merge_cols(n, rows, place, q, recv_a, recv_b, before, halo):
    ext, wide = q.shape
    w = wide - LANE
    return pl.pallas_call(
        functools.partial(cols_kernel, n, rows, halo),
        out_shape=[
            jax.ShapeDtypeStruct((ext, w + 2 * LANE), f32),
            jax.ShapeDtypeStruct((rows, w), f32),
            jax.ShapeDtypeStruct((8, LANE), f32),
        ],
        in_specs=[SMEM] + [VMEM] * 4,
        out_specs=[VMEM] * 3,
        name="merge_cols",
    )(place, q, recv_a, recv_b, before)


def wrap_kernel(rows, halo, w, place, send_a, mid, send_b, recv_a, recv_b, before, out):
    odd = lax.rem(place[1], 2)
    keep = rows - 2 * halo
    pieces = (
        (0, halo, mid[:halo, :] + choose(odd, recv_a[...], recv_b[...])),
        (halo, keep, mid[halo : rows - halo, :]),
        (rows - halo, halo, mid[rows - halo :, :] + choose(odd, recv_b[...], recv_a[...])),
    )
    edges = []
    for start, size, value in pieces:
        span = slice(start, start + size)
        out[span, :] = value[:, :w] + damping * before[span, :]
        edges.append(value[:, w:])
    out[rows:, :] = pack_edge(jnp.concatenate(edges, axis=0), halo, w)


def wrap(place, send_a, mid, send_b, recv_a, recv_b, before, halo):
    rows, w = before.shape
    height = rows + rows * 2 * halo // w
    return pl.pallas_call(
        functools.partial(wrap_kernel, rows, halo, w),
        out_shape=jax.ShapeDtypeStruct((height, w), f32),
        in_specs=[SMEM] + [VMEM] * 6,
        out_specs=VMEM,
        name="wrap",
    )(place, send_a, mid, send_b, recv_a, recv_b, before)


def solution_kernel(n, w, place, est, sums, *refs):
    k0, k1 = refs[:n], refs[n : 2 * n]
    sol, res, coef = refs[2 * n :]
    total = [
        jnp.sum(jnp.sum(sums[i], axis=0, keepdims=True), axis=1, keepdims=True) for i in range(4)
    ]
    k00, k11 = total[0], total[2]
    k01 = total[1] + damping * k00
    k12 = total[3] + damping * k11
    alpha0 = k00 / k01
    norm1 = k00 - 2.0 * alpha0 * k01 + alpha0 * alpha0 * k11
    beta = norm1 / k00
    curve1 = (1.0 + beta) * (1.0 + beta) * k01 - 2.0 * (1.0 + beta) * alpha0 * k11
    curve1 = curve1 + alpha0 * alpha0 * k12
    alpha1 = norm1 / curve1
    c1 = alpha0 + alpha1 * (1.0 + beta)
    c2 = alpha0 * alpha1
    coef[...] = jnp.broadcast_to(c2, coef.shape)
    for i in range(n):
        cols = pl.ds(pl.multiple_of(jnp.bitwise_xor(place[0], i) * w, LANE), w)
        a0, a1 = k0[i][...], k1[i][...]
        sol[:, cols] = est[:, cols] + c1 * a0 - c2 * a1
        res[:, cols] = a0 - c1 * a1


def solution_image(place, est, sums, k0, k1):
    n = len(k0)
    w = k0[0].shape[1]
    return pl.pallas_call(
        functools.partial(solution_kernel, n, w),
        out_shape=[jax.ShapeDtypeStruct(est.shape, f32)] * 2
        + [jax.ShapeDtypeStruct((8, LANE), f32)],
        in_specs=[SMEM] + [VMEM] * (2 + 2 * n),
        out_specs=[VMEM] * 3,
        name="solution_image",
    )(place, est, sums, *k0, *k1)


def residual_kernel(n, rows, halo, w, place, base, coef, *refs):
    k2, (res, full) = refs[:n], refs[n:]
    c2 = coef[0:1, 0:1]
    lane = lax.broadcasted_iota(jnp.int32, (rows, LANE), 1)
    spot = [jnp.bitwise_xor(place[0], i) for i in range(n)]
    full[:, :LANE] = jnp.zeros((rows, LANE), f32)
    full[:, LANE + n * w :] = jnp.zeros((rows, LANE), f32)
    for i in range(n):
        full[:, pl.ds(pl.multiple_of(spot[i] * w + LANE, LANE), w)] = k2[i][:rows, :]
    for i in range(n):
        edge = unpack_edge(k2[i][rows:, :], halo)
        left = pl.ds(pl.multiple_of(spot[i] * w, LANE), LANE)
        right = pl.ds(pl.multiple_of(spot[i] * w + w + LANE, LANE), LANE)
        full[:, left] += jnp.where(lane >= LANE - halo, edge, 0.0)
        full[:, right] += jnp.where(lane < halo, edge, 0.0)
    for c in range(0, n * w, LANE):
        res[:, c : c + LANE] = base[:, c : c + LANE] + c2 * full[:, c + LANE : c + 2 * LANE]


def residual_image(place, base, coef, k2, halo):
    n = len(k2)
    rows, cols = base.shape
    w = cols // n
    return pl.pallas_call(
        functools.partial(residual_kernel, n, rows, halo, w),
        out_shape=jax.ShapeDtypeStruct(base.shape, f32),
        in_specs=[SMEM] + [VMEM] * (2 + n),
        out_specs=VMEM,
        scratch_shapes=[pltpu.VMEM((rows, cols + 2 * LANE), f32)],
        name="residual_image",
    )(place, base, coef, *k2)


def neighbours(send_a, send_b, axis):
    n = lax.axis_size(axis)
    out = []
    for lead, x in ((0, send_a), (1, send_b)):
        pairs = [(i, i + 1) for i in range(lead, n - 1, 2)]
        out.append(lax.ppermute(x, axis, pairs + [(b, a) for a, b in pairs]))
    return out


def swap(x, axis, distance):
    n = lax.axis_size(axis)
    return lax.ppermute(x, axis, [(i, i ^ distance) for i in range(n)])


def steps(estimate, observed, weights, column_kernels, row_kernels):
    n = lax.axis_size("frame")
    me = lax.axis_index("frame")
    strips = lax.axis_size("strip")
    strip = lax.axis_index("strip")
    place = jnp.stack([me, strip]).astype(jnp.int32)
    rows, cols = estimate.shape
    frames = weights.shape[0]
    halo = column_kernels.shape[1] // 2
    w = cols // n
    distances = [1 << k for k in range(n.bit_length() - 1)]

    low, high = estimate[:halo], estimate[rows - halo :]
    odd = strip % 2 == 1
    est_a, est_b = neighbours(
        jnp.where(odd, low, high), jnp.where(odd, high, low), "strip"
    )

    early = frames // 2
    plan = [(d, 0, frames, True) for d in range(1, n - 1)]
    plan += [(n - 1, 0, early, True), (n - 1, early, frames - early, False)]
    packed, tile, own_mats = prepare(plan, place, column_kernels, row_kernels, weights, w, halo)
    moved = []
    for i, (d, _, _, taps) in enumerate(plan):
        moved.append(swap(packed[i], "frame", d))
    origin = {}
    starts = [0]
    for i, (d, lead, count, taps) in enumerate(plan):
        for k in range(count):
            origin[d, lead + k] = (i, k * rows)
        if taps:
            starts.append(count * rows)

    send_a, mid, send_b = first_terms(
        place, estimate, est_a, est_b, own_mats, weights, observed
    )
    mats = setup_matrices([tile] + moved[: n - 1], starts, frames, rows, halo)
    recv_a, recv_b = neighbours(send_a, send_b, "strip")

    part = list(column_blocks(n, place, send_a, mid, send_b, recv_a, recv_b, w))
    mine = [part[0]]
    for i in range(n - 1, 0, -1):
        d = i & -i
        got = swap(part[i], "frame", d)
        if i == d:
            mine.append(got)
        else:
            part[i ^ d] = part[i ^ d] + got
    k0, wide, send_a, send_b, k00_part = start_image(n, place, estimate, mine, halo)
    recv_a, recv_b = neighbours(send_a, send_b, "strip")

    send_a, mid, send_b, stat1, k0x = apply_terms(
        place, (wide, recv_a, recv_b), mats, weights, moved, origin, 2 * halo, halo
    )
    recv_a, recv_b = neighbours(send_a, send_b, "strip")
    q, col_a, col_b = merge_rows(strips, place, send_a, mid, send_b, recv_a, recv_b, halo)
    recv_a, recv_b = neighbours(col_a, col_b, "frame")
    k1x, k1, k11_part = merge_cols(n, rows, place, q, recv_a, recv_b, k0x, halo)

    send_a, mid, send_b, stat2 = apply_terms(
        place, (k1x,), mats, weights, moved, origin, halo, halo
    )
    recv_a, recv_b = neighbours(send_a, send_b, "strip")
    sums = jnp.stack([k00_part, stat1, k11_part, stat2])
    for axis, size in (("strip", strips), ("frame", n)):
        d = 1
        while d < size:
            sums = sums + swap(sums, axis, d)
            d *= 2
    k2 = wrap(place, send_a, mid, send_b, recv_a, recv_b, k1, halo)

    def gathered(x):
        parts = [x] + [None] * (n - 1)
        for i in range(n):
            for d in reversed(distances):
                if i % (2 * d) == 0:
                    parts[i + d] = swap(parts[i], "frame", d)
        return parts

    g0, g1, g2 = gathered(k0), gathered(k1), gathered(k2)
    result, base, coef = solution_image(place, estimate, sums, g0, g1)
    return result, residual_image(place, base, coef, g2, halo)


def solution(mesh):
    return jax.shard_map(
        steps,
        mesh=mesh,
        in_specs=(
            P("strip", None),
            P("frame", "strip", None),
            P("frame", "strip", None),
            P("frame", None),
            P("frame", None),
        ),
        out_specs=(P("strip", None), P("strip", None)),
        check_vma=False,
    )
```

```python
import functools

import jax
import jax.numpy as jnp
from jax import lax
from jax.experimental import pallas as pl
from jax.experimental.pallas import tpu as pltpu
from jax.sharding import PartitionSpec as P


damping = 0.05
f32 = jnp.float32
bf16 = jnp.bfloat16
LANE = 128
VMEM = pl.BlockSpec(memory_space=pltpu.VMEM)
ANY = pl.BlockSpec(memory_space=pl.ANY)
SMEM = pl.BlockSpec(memory_space=pltpu.SMEM)


def split(x):
    hi = x.astype(bf16)
    lo = (x - hi.astype(f32)).astype(bf16)
    return hi, lo


def dot(a, b):
    return jnp.dot(a, b, preferred_element_type=f32)


def choose(flag, a, b):
    return jnp.where(jnp.full(a.shape, flag, jnp.int32) == 1, a, b)


def pack_edge(edge, halo, w):
    rows = edge.shape[0]
    per = LANE // (2 * halo)
    short = rows * 2 * halo // w
    edge = pltpu.roll(edge, halo, 1)
    lane = lax.broadcasted_iota(jnp.int32, (short, LANE), 1)
    out = []
    for t in range(w // LANE):
        tile = None
        for p in range(per):
            k = t * per + p
            part = edge[k * short : (k + 1) * short]
            part = pltpu.roll(part, p * 2 * halo, 1) if p else part
            tile = part if tile is None else jnp.where(lane >= p * 2 * halo, part, tile)
        out.append(tile)
    return jnp.concatenate(out, axis=1)


def unpack_edge(packed, halo):
    _, w = packed.shape
    per = LANE // (2 * halo)
    parts = []
    for k in range(w // (2 * halo)):
        t, p = divmod(k, per)
        part = packed[:, t * LANE : (t + 1) * LANE]
        back = (LANE - halo - p * 2 * halo) % LANE
        parts.append(pltpu.roll(part, back, 1) if back else part)
    return jnp.concatenate(parts, axis=0)


def tiles(width, step=256):
    return [(s, min(step, width - s)) for s in range(0, width, step)]


def toeplitz(base, count):
    wide = base.shape[1]
    return pltpu.roll(jnp.broadcast_to(base, (count, wide)), 0, 1, stride=1, stride_axis=0)


def build_group(taps, g, frames, rows, halo, t_ref, b_ref, bp_ref, ta_ref):
    ext = rows + 2 * halo
    unit = taps / jnp.sum(taps, axis=1, keepdims=True)
    for s in range(frames):
        f = g * frames + s
        col = unit[s : s + 1]
        row = unit[frames + s : frames + s + 1]
        by_rows = toeplitz(row, rows)
        hi, lo = split(by_rows)
        t_ref[f, :rows, :] = hi
        t_ref[f, rows:, :] = lo
        hi, lo = split(by_rows.T[:ext])
        ta_ref[g, :ext, s * rows : (s + 1) * rows] = hi
        ta_ref[g, ext:, s * rows : (s + 1) * rows] = lo
        hi, lo = split(toeplitz(col, LANE).T)
        b_ref[f, :, :LANE] = hi
        b_ref[f, :, LANE:] = lo
        hi, lo = split(toeplitz(pltpu.roll(col, LANE, 1), 2 * LANE)[:, :LANE])
        bp_ref[f, :, :LANE] = hi
        bp_ref[f, :, LANE:] = lo


def matrix_shapes(groups, frames, rows, halo):
    ext = rows + 2 * halo
    return [
        jax.ShapeDtypeStruct(s, bf16)
        for s in (
            (groups * frames, 2 * rows, 2 * LANE),
            (groups * frames, 2 * LANE, 2 * LANE),
            (groups * frames, 2 * LANE, 2 * LANE),
            (groups, 2 * ext, frames * rows),
        )
    ]


def tile_height(frames):
    return -(-2 * frames // 8) * 8


def setup_kernel(frames, rows, halo, starts, *refs):
    tiles_in = refs[: len(starts)]
    mats, taps, sem = refs[len(starts) : -2], refs[-2], refs[-1]
    height = tile_height(frames)

    def copy(g):
        source = tiles_in[g].at[pl.ds(starts[g], height), pl.ds(0, 2 * LANE)]
        return pltpu.make_async_copy(source, taps.at[g], sem.at[g])

    for g in range(len(starts)):
        copy(g).start()
    for g in range(len(starts)):
        copy(g).wait()
        build_group(taps[g], g, frames, rows, halo, *mats)


def setup_matrices(tiles_in, starts, frames, rows, halo):
    groups = len(tiles_in)
    return pl.pallas_call(
        functools.partial(setup_kernel, frames, rows, halo, starts),
        out_shape=matrix_shapes(groups, frames, rows, halo),
        in_specs=[ANY] * groups,
        out_specs=[VMEM] * 4,
        scratch_shapes=[
            pltpu.VMEM((groups, tile_height(frames), 2 * LANE), f32),
            pltpu.SemaphoreType.DMA((groups,)),
        ],
        name="setup_all",
    )(*tiles_in)


def load_image(y_hi, y_lo, image, halo):
    ext, full = image.shape
    shift = LANE - halo
    y = pltpu.roll(image, full - shift, 1)[:, : full - LANE]
    hi, lo = split(y)
    y_hi[:ext, :] = hi
    y_lo[:ext, :] = lo


def group_terms(frames, rows, w, y_hi, y_lo, t, b, bp, ta, weight, data, us, qs, vs_hi, vs_lo, acc, stat, ready=None):
    total = None
    for f in range(frames):
        for c, size in tiles(w + LANE):
            r1 = dot(t(f)[...], y_hi[:, c : c + size])
            r2 = dot(t(f)[:rows, :], y_lo[:, c : c + size])
            hi, lo = split(r1[:rows] + r1[rows:] + r2)
            us[:rows, c : c + size] = hi
            us[rows:, c : c + size] = lo
        if ready is not None:
            ready(f)
        for k in range(w // LANE):
            c = k * LANE
            r = dot(us[:, c : c + 2 * LANE], b(f)[...])
            a = r[:rows, :LANE] + r[:rows, LANE:] + r[rows:, :LANE]
            if data is not None:
                a = a - data(f)[:, c : c + LANE]
            q = weight(f)[:, c : c + LANE] * a
            if stat is not None:
                part = jnp.sum((a * q).reshape(rows // 8, 8, LANE), axis=0)
                total = part if total is None else total + part
            hi, lo = split(q)
            qs[:rows, c + LANE : c + 2 * LANE] = hi
            qs[rows:, c + LANE : c + 2 * LANE] = lo
        for k in range(w // LANE + 1):
            c = k * LANE
            r = dot(qs[:, c : c + 2 * LANE], bp(f)[...])
            hi, lo = split(r[:rows, :LANE] + r[:rows, LANE:] + r[rows:, :LANE])
            vs_hi[f * rows : (f + 1) * rows, c : c + LANE] = hi
            vs_lo[f * rows : (f + 1) * rows, c : c + LANE] = lo
    ext = acc.shape[0]
    for c, size in tiles(w + LANE):
        r1 = dot(ta[...], vs_hi[:, c : c + size])
        r2 = dot(ta[:ext, :], vs_lo[:, c : c + size])
        acc[:, c : c + size] += r1[:ext] + r1[ext:] + r2
    if stat is not None:
        stat[...] += total


def work_scratch(frames, rows, halo, w):
    ext = rows + 2 * halo
    return [
        pltpu.VMEM((2 * LANE, w + LANE), bf16),
        pltpu.VMEM((2 * LANE, w + LANE), bf16),
        pltpu.VMEM((2 * rows, w + LANE), bf16),
        pltpu.VMEM((2 * rows, w + 2 * LANE), bf16),
        pltpu.VMEM((frames * rows, w + LANE), bf16),
        pltpu.VMEM((frames * rows, w + LANE), bf16),
        pltpu.VMEM((ext, w + LANE), f32),
    ]


def clear_edges(y_hi, y_lo, qs, ext, rows, w):
    zero = jnp.zeros((y_hi.shape[0] - ext, y_hi.shape[1]), bf16)
    y_hi[ext:, :] = zero
    y_lo[ext:, :] = zero
    qs[:, :LANE] = jnp.zeros((2 * rows, LANE), bf16)
    qs[:, w + LANE :] = jnp.zeros((2 * rows, LANE), bf16)


def unshift(acc, halo):
    return pltpu.roll(acc, acc.shape[1] - halo, 1)


def first_kernel(
    frames, rows, halo,
    place, est, recv_a, recv_b, t_ref, b_ref, bp_ref, ta_ref, w_hbm, d_hbm,
    send_a, mid, send_b,
    y_hi, y_lo, us, qs, vs_hi, vs_lo, acc, wbuf, dbuf, sem,
):
    ext = rows + 2 * halo
    cols = est.shape[1]
    copies = [
        (
            pltpu.make_async_copy(w_hbm.at[f], wbuf.at[f], sem.at[0, f]),
            pltpu.make_async_copy(d_hbm.at[f], dbuf.at[f], sem.at[1, f]),
        )
        for f in range(frames)
    ]
    for pair in copies:
        for c in pair:
            c.start()
    clear_edges(y_hi, y_lo, qs, ext, rows, cols)
    odd = lax.rem(place[1], 2)
    none = jnp.zeros((ext, LANE), f32)
    for start in range(0, cols, 4 * LANE):
        size = 4 * LANE + LANE
        left = max(start - LANE, 0)
        span = slice(left, min(start + 4 * LANE, cols))
        x = jnp.concatenate(
            [
                choose(odd, recv_a[:, span], recv_b[:, span]),
                est[:, span],
                choose(odd, recv_b[:, span], recv_a[:, span]),
            ],
            axis=0,
        )
        if start == 0:
            x = jnp.concatenate([none, x], axis=1)
        if x.shape[1] < size:
            x = jnp.concatenate([x, jnp.zeros((ext, size - x.shape[1]), f32)], axis=1)
        hi, lo = split(pltpu.roll(x, halo, 1)[:, LANE:])
        y_hi[:ext, start : start + 4 * LANE] = hi
        y_lo[:ext, start : start + 4 * LANE] = lo
        if start + 4 * LANE >= cols:
            tail = jnp.concatenate([x[:, 4 * LANE :], none], axis=1)
            hi, lo = split(pltpu.roll(tail, halo, 1)[:, LANE:])
            y_hi[:ext, cols:] = hi
            y_lo[:ext, cols:] = lo
    acc[...] = jnp.zeros_like(acc)

    def ready(f):
        for c in copies[f]:
            c.wait()

    group_terms(
        frames, rows, cols, y_hi, y_lo,
        lambda f: t_ref.at[f], lambda f: b_ref.at[f], lambda f: bp_ref.at[f], ta_ref.at[0],
        lambda f: wbuf.at[f], lambda f: dbuf.at[f],
        us, qs, vs_hi, vs_lo, acc, None, ready,
    )
    for start in range(0, cols, 4 * LANE):
        size = min(4 * LANE, cols - start)
        z = pltpu.roll(acc[:, start : start + size + LANE], size + LANE - halo, 1)[:, :size]
        span = slice(start, start + size)
        low, high = z[:halo], z[halo + rows :]
        send_a[:, span] = choose(odd, low, high)
        send_b[:, span] = choose(odd, high, low)
        mid[:, span] = z[halo : halo + rows]


def first_terms(place, est, recv_a, recv_b, mats, weights, observed):
    frames, rows, cols = weights.shape
    halo = recv_a.shape[0]
    return pl.pallas_call(
        functools.partial(first_kernel, frames, rows, halo),
        out_shape=[
            jax.ShapeDtypeStruct((halo, cols), f32),
            jax.ShapeDtypeStruct((rows, cols), f32),
            jax.ShapeDtypeStruct((halo, cols), f32),
        ],
        in_specs=[SMEM] + [VMEM] * 7 + [ANY, ANY],
        out_specs=[VMEM] * 3,
        scratch_shapes=work_scratch(frames, rows, halo, cols)
        + [
            pltpu.VMEM((frames, rows, cols), f32),
            pltpu.VMEM((frames, rows, cols), f32),
            pltpu.SemaphoreType.DMA((2, frames)),
        ],
        cost_estimate=pl.CostEstimate(flops=8 * 10**9, bytes_accessed=8 * 2**20, transcendentals=0),
        name="first_terms",
    )(place, est, recv_a, recv_b, *mats, weights, observed)


def prepare_kernel(plan, frames, rows, halo, w, place, cols_in, rows_in, weights, *refs):
    outs, tile, mats, sem = refs[: len(plan)], refs[len(plan)], refs[len(plan) + 1 : -1], refs[-1]
    taps = cols_in.shape[1]
    pending = []
    for i, (distance, _) in enumerate(plan):
        start = pl.multiple_of(jnp.bitwise_xor(place[0], distance) * w, LANE)
        for k in range(frames):
            copy = pltpu.make_async_copy(
                weights.at[k, :, pl.ds(start, w)],
                outs[i].at[pl.ds(k * rows, rows), :],
                sem.at[i, k],
            )
            copy.start()
            pending.append(copy)
    tile[...] = jnp.zeros_like(tile)
    tile[:frames, :taps] = cols_in[...]
    tile[frames : 2 * frames, :taps] = rows_in[...]
    for i, (_, with_taps) in enumerate(plan):
        if with_taps:
            outs[i][frames * rows :, :] = tile[...]
    build_group(tile[:, : 2 * LANE], 0, frames, rows, halo, *mats)
    for copy in pending:
        copy.wait()


def prepare(plan, place, column_kernels, row_kernels, weights, w, halo):
    frames, rows, _ = weights.shape
    height = tile_height(frames)
    out = pl.pallas_call(
        functools.partial(prepare_kernel, plan, frames, rows, halo, w),
        out_shape=[
            jax.ShapeDtypeStruct((frames * rows + (height if taps else 0), w), f32)
            for _, taps in plan
        ]
        + [jax.ShapeDtypeStruct((height, w), f32)]
        + matrix_shapes(1, frames, rows, halo),
        in_specs=[SMEM, VMEM, VMEM, ANY],
        out_specs=[VMEM] * (len(plan) + 5),
        scratch_shapes=[pltpu.SemaphoreType.DMA((len(plan), frames))],
        name="prepare",
    )(place, column_kernels, row_kernels, weights)
    return out[: len(plan)], out[len(plan)], out[len(plan) + 1 :]


def blocks_kernel(n, halo, w, place, send_a, mid, send_b, recv_a, recv_b, *refs):
    outs, full = refs[:-1], refs[-1]
    rows, cols = mid.shape
    odd = lax.rem(place[1], 2)
    inner = slice(LANE, LANE + cols)
    for end in (0, LANE + cols):
        full[:, end : end + LANE] = jnp.zeros((rows, LANE), f32)
    full[:halo, inner] = mid[:halo, :] + choose(odd, recv_a[...], recv_b[...])
    full[halo : rows - halo, inner] = mid[halo : rows - halo, :]
    full[rows - halo :, inner] = mid[rows - halo :, :] + choose(odd, recv_b[...], recv_a[...])
    lane = lax.broadcasted_iota(jnp.int32, (rows, LANE), 1)
    for i in range(n):
        start = jnp.bitwise_xor(place[0], i) * w
        outs[i][:rows, :] = full[:, pl.ds(pl.multiple_of(start + LANE, LANE), w)]
        before = full[:, pl.ds(pl.multiple_of(start, LANE), LANE)]
        after = full[:, pl.ds(pl.multiple_of(start + LANE + w, LANE), LANE)]
        outs[i][rows:, :] = pack_edge(jnp.where(lane >= LANE - halo, before, after), halo, w)


def column_blocks(n, place, send_a, mid, send_b, recv_a, recv_b, w):
    rows, cols = mid.shape
    halo = send_a.shape[0]
    height = rows + rows * 2 * halo // w
    return pl.pallas_call(
        functools.partial(blocks_kernel, n, halo, w),
        out_shape=[jax.ShapeDtypeStruct((height, w), f32)] * n,
        in_specs=[SMEM] + [VMEM] * 5,
        out_specs=[VMEM] * n,
        scratch_shapes=[pltpu.VMEM((rows, cols + 2 * LANE), f32)],
        name="column_blocks",
    )(place, send_a, mid, send_b, recv_a, recv_b)


def start_kernel(n, rows, halo, w, place, est, *refs):
    parts = refs[:-5]
    k0, wide, send_a, send_b, stat = refs[-5:]
    total = parts[0][...]
    for p in parts[1:]:
        total = total + p[...]
    me = place[0]
    odd = lax.rem(place[1], 2)
    at = lambda start, size: est[:, pl.ds(pl.multiple_of(start, LANE), size)]
    own = -(total[:rows] + damping * at(me * w, w))
    edge = unpack_edge(total[rows:], halo)
    before = at(jnp.maximum(me * w - LANE, 0), LANE)
    after = at(jnp.minimum(me * w + w, (n * w) - LANE), LANE)
    none = jnp.zeros((rows, LANE), f32)
    left = choose((me > 0).astype(jnp.int32), -(edge + damping * before), none)
    right = choose((me < n - 1).astype(jnp.int32), -(edge + damping * after), none)
    k0[...] = own
    wide[:, :LANE] = left
    wide[:, LANE : LANE + w] = own
    wide[:, LANE + w :] = right
    low, high = wide[:halo, :], wide[rows - halo :, :]
    send_a[...] = choose(odd, low, high)
    send_b[...] = choose(odd, high, low)
    square = own * own
    acc = square[:, :LANE]
    for c in range(LANE, w, LANE):
        acc = acc + square[:, c : c + LANE]
    stat[...] = jnp.sum(acc.reshape(rows // 8, 8, LANE), axis=0)


def start_image(n, place, est, parts, halo):
    rows, cols = est.shape
    w = cols // n
    return pl.pallas_call(
        functools.partial(start_kernel, n, rows, halo, w),
        out_shape=[
            jax.ShapeDtypeStruct((rows, w), f32),
            jax.ShapeDtypeStruct((rows, w + 2 * LANE), f32),
            jax.ShapeDtypeStruct((halo, w + 2 * LANE), f32),
            jax.ShapeDtypeStruct((halo, w + 2 * LANE), f32),
            jax.ShapeDtypeStruct((8, LANE), f32),
        ],
        in_specs=[SMEM] + [VMEM] * (1 + len(parts)),
        out_specs=[VMEM] * 5,
        name="start_image",
    )(place, est, *parts)


def apply_kernel(frames, rows, halo, w, groups, cut, count, pieces, place, *refs):
    image, refs = refs[:pieces], refs[pieces:]
    t_hbm, b_hbm, bp_hbm, ta_hbm, own = refs[:5]
    moved = refs[5 : 5 + count]
    send_a, mid, send_b, stat = refs[5 + count : 9 + count]
    refs = refs[9 + count :]
    if pieces > 1:
        whole, refs = refs[0], refs[1:]
    y_hi, y_lo, us, qs, vs_hi, vs_lo, acc, tb, bb, bpb, tab, wbuf, sem, wsem = refs
    odd = lax.rem(place[1], 2)
    ext = rows + 2 * halo

    def copies(g):
        span = pl.ds(g * frames, frames)
        return [
            pltpu.make_async_copy(t_hbm.at[span], tb.at[g], sem.at[0, g]),
            pltpu.make_async_copy(b_hbm.at[span], bb.at[g], sem.at[1, g]),
            pltpu.make_async_copy(bp_hbm.at[span], bpb.at[g], sem.at[2, g]),
            pltpu.make_async_copy(ta_hbm.at[g], tab.at[g], sem.at[3, g]),
        ]

    mine = pl.ds(pl.multiple_of(place[0] * w, LANE), w)
    for g in range(groups):
        for c in copies(g):
            c.start()
        for f in range(frames):
            span = pl.ds(f * rows, rows)
            if g == 0:
                pltpu.make_async_copy(own.at[f, :, mine], wbuf.at[g, f], wsem.at[g, f]).start()
            elif g < groups - 1:
                pltpu.make_async_copy(moved[g - 1].at[span, :], wbuf.at[g, f], wsem.at[g, f]).start()
            else:
                inside = (place[0] >= groups // 4) & (place[0] < groups - groups // 4)
                for flag, ref in ((inside, moved[-2]), (jnp.logical_not(inside), moved[-1])):

                    @pl.when(flag)
                    def _(ref=ref, span=span, g=g, f=f):
                        pltpu.make_async_copy(ref.at[span, :], wbuf.at[g, f], wsem.at[g, f]).start()
    clear_edges(y_hi, y_lo, qs, ext, rows, w)
    if pieces > 1:
        wide, recv_a, recv_b = image
        whole[:halo, :] = choose(odd, recv_a[...], recv_b[...])
        whole[halo : halo + rows, :] = wide[...]
        whole[halo + rows :, :] = choose(odd, recv_b[...], recv_a[...])
        load_image(y_hi, y_lo, whole[...], halo)
    else:
        load_image(y_hi, y_lo, image[0][...], halo)
    acc[...] = jnp.zeros_like(acc)
    stat[...] = jnp.zeros_like(stat)

    @pl.loop(0, groups)
    def _(g):
        for c in copies(g):
            c.wait()
        for f in range(frames):
            pltpu.make_async_copy(own.at[f, :, mine], wbuf.at[g, f], wsem.at[g, f]).wait()
        group_terms(
            frames, rows, w, y_hi, y_lo,
            lambda f: tb.at[g, f], lambda f: bb.at[g, f], lambda f: bpb.at[g, f], tab.at[g],
            lambda f: wbuf.at[g, f], None,
            us, qs, vs_hi, vs_lo, acc, stat,
        )

    z = unshift(acc[...], halo)
    send_a[...] = choose(odd, z[:cut], z[ext - cut :])
    send_b[...] = choose(odd, z[ext - cut :], z[:cut])
    mid[...] = z[cut : ext - cut]


def apply_terms(place, image, mats, weights, moved, cut, halo):
    frames, rows, _ = weights.shape
    w = image[0].shape[1] - 2 * LANE
    ext = rows + 2 * halo
    t, b, bp, ta = mats
    groups = ta.shape[0]
    wide = w + LANE
    return pl.pallas_call(
        functools.partial(apply_kernel, frames, rows, halo, w, groups, cut, len(moved), len(image)),
        out_shape=[
            jax.ShapeDtypeStruct((cut, wide), f32),
            jax.ShapeDtypeStruct((ext - 2 * cut, wide), f32),
            jax.ShapeDtypeStruct((cut, wide), f32),
            jax.ShapeDtypeStruct((8, LANE), f32),
        ]
        + [jax.ShapeDtypeStruct((ext, w + 2 * LANE), f32)] * (len(image) > 1),
        in_specs=[SMEM] + [VMEM] * len(image) + [ANY] * (5 + len(moved)),
        out_specs=[VMEM] * (4 + (len(image) > 1)),
        scratch_shapes=work_scratch(frames, rows, halo, w)
        + [
            pltpu.VMEM((groups, frames) + t.shape[1:], bf16),
            pltpu.VMEM((groups, frames) + b.shape[1:], bf16),
            pltpu.VMEM((groups, frames) + bp.shape[1:], bf16),
            pltpu.VMEM((groups,) + ta.shape[1:], bf16),
            pltpu.VMEM((groups, frames, rows, w), f32),
            pltpu.SemaphoreType.DMA((4, groups)),
            pltpu.SemaphoreType.DMA((groups, frames)),
        ],
        cost_estimate=pl.CostEstimate(
            flops=groups * 3 * 10**9, bytes_accessed=groups * 2**20, transcendentals=0
        ),
    )(place, *image, t, b, bp, ta, weights, *moved)


def rows_kernel(strips, halo, w, place, send_a, mid, send_b, recv_a, recv_b, q, col_a, col_b):
    odd = lax.rem(place[1], 2)
    odd_col = lax.rem(place[0], 2)
    edge_rows, wide = send_a.shape
    ext = q.shape[0]
    row = lax.broadcasted_iota(jnp.int32, (edge_rows, wide), 0)
    strip = jnp.full((edge_rows, wide), place[1], jnp.int32)
    low = choose(odd, send_a[...], send_b[...]) + choose(odd, recv_a[...], recv_b[...])
    high = choose(odd, send_b[...], send_a[...]) + choose(odd, recv_b[...], recv_a[...])
    q[:edge_rows, :] = jnp.where((row >= halo) | (strip > 0), low, 0.0)
    q[edge_rows : ext - edge_rows, :] = mid[...]
    q[ext - edge_rows :, :] = jnp.where((row < edge_rows - halo) | (strip < strips - 1), high, 0.0)
    lane = lax.broadcasted_iota(jnp.int32, (ext, LANE), 1)
    edge = q[:, w:]
    to_left = jnp.where(lane < halo, q[:, :LANE], edge)
    to_right = jnp.where(lane >= LANE - halo, q[:, w - LANE : w], edge)
    col_a[...] = choose(odd_col, to_left, to_right)
    col_b[...] = choose(odd_col, to_right, to_left)


def merge_rows(strips, place, send_a, mid, send_b, recv_a, recv_b, halo):
    ext = mid.shape[0] + 2 * send_a.shape[0]
    wide = mid.shape[1]
    return pl.pallas_call(
        functools.partial(rows_kernel, strips, halo, wide - LANE),
        out_shape=[
            jax.ShapeDtypeStruct((ext, wide), f32),
            jax.ShapeDtypeStruct((ext, LANE), f32),
            jax.ShapeDtypeStruct((ext, LANE), f32),
        ],
        in_specs=[SMEM] + [VMEM] * 5,
        out_specs=[VMEM] * 3,
        name="merge_rows",
    )(place, send_a, mid, send_b, recv_a, recv_b)


def cols_kernel(n, rows, halo, place, q, recv_a, recv_b, before, out, block, stat):
    odd = lax.rem(place[0], 2)
    ext, wide = q.shape
    w = wide - LANE
    lane = lax.broadcasted_iota(jnp.int32, (ext, LANE), 1)
    at = jnp.full((ext, LANE), place[0], jnp.int32)
    left = choose(odd, recv_a[...], recv_b[...])
    right = choose(odd, recv_b[...], recv_a[...])
    edge = q[:, w:]
    total = None
    out[:, :LANE] = jnp.where(at > 0, edge + left, 0.0) + damping * before[:, :LANE]
    out[:, LANE + w :] = jnp.where(at < n - 1, edge + right, 0.0) + damping * before[:, LANE + w :]
    for c in range(0, w, LANE):
        x = q[:, c : c + LANE] + damping * before[:, c + LANE : c + 2 * LANE]
        if c == 0:
            x = x + jnp.where(lane < halo, left, 0.0)
        if c == w - LANE:
            x = x + jnp.where(lane >= LANE - halo, right, 0.0)
        out[:, c + LANE : c + 2 * LANE] = x
        own = x[halo : halo + rows]
        block[:, c : c + LANE] = own
        part = jnp.sum((own * own).reshape(rows // 8, 8, LANE), axis=0)
        total = part if total is None else total + part
    stat[...] = total


def merge_cols(n, rows, place, q, recv_a, recv_b, before, halo):
    ext, wide = q.shape
    w = wide - LANE
    return pl.pallas_call(
        functools.partial(cols_kernel, n, rows, halo),
        out_shape=[
            jax.ShapeDtypeStruct((ext, w + 2 * LANE), f32),
            jax.ShapeDtypeStruct((rows, w), f32),
            jax.ShapeDtypeStruct((8, LANE), f32),
        ],
        in_specs=[SMEM] + [VMEM] * 4,
        out_specs=[VMEM] * 3,
        name="merge_cols",
    )(place, q, recv_a, recv_b, before)


def wrap_kernel(rows, halo, w, place, send_a, mid, send_b, recv_a, recv_b, before, out):
    odd = lax.rem(place[1], 2)
    keep = rows - 2 * halo
    pieces = (
        (0, halo, mid[:halo, :] + choose(odd, recv_a[...], recv_b[...])),
        (halo, keep, mid[halo : rows - halo, :]),
        (rows - halo, halo, mid[rows - halo :, :] + choose(odd, recv_b[...], recv_a[...])),
    )
    edges = []
    for start, size, value in pieces:
        span = slice(start, start + size)
        out[span, :] = value[:, :w] + damping * before[span, :]
        edges.append(value[:, w:])
    out[rows:, :] = pack_edge(jnp.concatenate(edges, axis=0), halo, w)


def wrap(place, send_a, mid, send_b, recv_a, recv_b, before, halo):
    rows, w = before.shape
    height = rows + rows * 2 * halo // w
    return pl.pallas_call(
        functools.partial(wrap_kernel, rows, halo, w),
        out_shape=jax.ShapeDtypeStruct((height, w), f32),
        in_specs=[SMEM] + [VMEM] * 6,
        out_specs=VMEM,
        name="wrap",
    )(place, send_a, mid, send_b, recv_a, recv_b, before)


def solution_kernel(n, w, place, est, sums, *refs):
    k0, k1 = refs[:n], refs[n : 2 * n]
    sol, res, coef = refs[2 * n :]
    total = [
        jnp.sum(jnp.sum(sums[i], axis=0, keepdims=True), axis=1, keepdims=True) for i in range(4)
    ]
    k00, k11 = total[0], total[2]
    k01 = total[1] + damping * k00
    k12 = total[3] + damping * k11
    alpha0 = k00 / k01
    norm1 = k00 - 2.0 * alpha0 * k01 + alpha0 * alpha0 * k11
    beta = norm1 / k00
    curve1 = (1.0 + beta) * (1.0 + beta) * k01 - 2.0 * (1.0 + beta) * alpha0 * k11
    curve1 = curve1 + alpha0 * alpha0 * k12
    alpha1 = norm1 / curve1
    c1 = alpha0 + alpha1 * (1.0 + beta)
    c2 = alpha0 * alpha1
    coef[...] = jnp.broadcast_to(c2, coef.shape)
    for i in range(n):
        cols = pl.ds(pl.multiple_of(jnp.bitwise_xor(place[0], i) * w, LANE), w)
        a0, a1 = k0[i][...], k1[i][...]
        sol[:, cols] = est[:, cols] + c1 * a0 - c2 * a1
        res[:, cols] = a0 - c1 * a1


def solution_image(place, est, sums, k0, k1):
    n = len(k0)
    w = k0[0].shape[1]
    return pl.pallas_call(
        functools.partial(solution_kernel, n, w),
        out_shape=[jax.ShapeDtypeStruct(est.shape, f32)] * 2
        + [jax.ShapeDtypeStruct((8, LANE), f32)],
        in_specs=[SMEM] + [VMEM] * (2 + 2 * n),
        out_specs=[VMEM] * 3,
        name="solution_image",
    )(place, est, sums, *k0, *k1)


def residual_kernel(n, rows, halo, w, place, base, coef, *refs):
    k2, (res, full) = refs[:n], refs[n:]
    c2 = coef[0:1, 0:1]
    lane = lax.broadcasted_iota(jnp.int32, (rows, LANE), 1)
    spot = [jnp.bitwise_xor(place[0], i) for i in range(n)]
    full[:, :LANE] = jnp.zeros((rows, LANE), f32)
    full[:, LANE + n * w :] = jnp.zeros((rows, LANE), f32)
    for i in range(n):
        full[:, pl.ds(pl.multiple_of(spot[i] * w + LANE, LANE), w)] = k2[i][:rows, :]
    for i in range(n):
        edge = unpack_edge(k2[i][rows:, :], halo)
        left = pl.ds(pl.multiple_of(spot[i] * w, LANE), LANE)
        right = pl.ds(pl.multiple_of(spot[i] * w + w + LANE, LANE), LANE)
        full[:, left] += jnp.where(lane >= LANE - halo, edge, 0.0)
        full[:, right] += jnp.where(lane < halo, edge, 0.0)
    for c in range(0, n * w, LANE):
        res[:, c : c + LANE] = base[:, c : c + LANE] + c2 * full[:, c + LANE : c + 2 * LANE]


def residual_image(place, base, coef, k2, halo):
    n = len(k2)
    rows, cols = base.shape
    w = cols // n
    return pl.pallas_call(
        functools.partial(residual_kernel, n, rows, halo, w),
        out_shape=jax.ShapeDtypeStruct(base.shape, f32),
        in_specs=[SMEM] + [VMEM] * (2 + n),
        out_specs=VMEM,
        scratch_shapes=[pltpu.VMEM((rows, cols + 2 * LANE), f32)],
        name="residual_image",
    )(place, base, coef, *k2)


def neighbours(send_a, send_b, axis):
    n = lax.axis_size(axis)
    out = []
    for lead, x in ((0, send_a), (1, send_b)):
        pairs = [(i, i + 1) for i in range(lead, n - 1, 2)]
        out.append(lax.ppermute(x, axis, pairs + [(b, a) for a, b in pairs]))
    return out


def swap(x, axis, distance):
    n = lax.axis_size(axis)
    return lax.ppermute(x, axis, [(i, i ^ distance) for i in range(n)])


def steps(estimate, observed, weights, column_kernels, row_kernels):
    n = lax.axis_size("frame")
    me = lax.axis_index("frame")
    strips = lax.axis_size("strip")
    strip = lax.axis_index("strip")
    place = jnp.stack([me, strip]).astype(jnp.int32)
    rows, cols = estimate.shape
    frames = weights.shape[0]
    halo = column_kernels.shape[1] // 2
    w = cols // n
    distances = [1 << k for k in range(n.bit_length() - 1)]

    low, high = estimate[:halo], estimate[rows - halo :]
    odd = strip % 2 == 1
    est_a, est_b = neighbours(
        jnp.where(odd, low, high), jnp.where(odd, high, low), "strip"
    )

    plan = [(d, True) for d in range(1, n - 1)] + [(n - 1, False)]
    packed, tile, own_mats = prepare(plan, place, column_kernels, row_kernels, weights, w, halo)
    far_tile = swap(tile[:, : 2 * LANE], "frame", n - 1)
    moved = []
    for i in range(n - 2):
        moved.append(swap(packed[i], "frame", i + 1))
    middle = range(n // 4, n - n // 4)
    for members in (middle, [i for i in range(n) if i not in middle]):
        moved.append(lax.ppermute(packed[-1], "frame", [(i, n - 1 - i) for i in members]))
    starts = [0] + [frames * rows] * (n - 2) + [0]

    send_a, mid, send_b = first_terms(
        place, estimate, est_a, est_b, own_mats, weights, observed
    )
    mats = setup_matrices([tile] + moved[: n - 2] + [far_tile], starts, frames, rows, halo)
    recv_a, recv_b = neighbours(send_a, send_b, "strip")

    part = list(column_blocks(n, place, send_a, mid, send_b, recv_a, recv_b, w))
    mine = [part[0]]
    for i in range(n - 1, 0, -1):
        d = i & -i
        got = swap(part[i], "frame", d)
        if i == d:
            mine.append(got)
        else:
            part[i ^ d] = part[i ^ d] + got
    k0, wide, send_a, send_b, k00_part = start_image(n, place, estimate, mine, halo)
    recv_a, recv_b = neighbours(send_a, send_b, "strip")

    send_a, mid, send_b, stat1, k0x = apply_terms(
        place, (wide, recv_a, recv_b), mats, weights, moved, 2 * halo, halo
    )
    recv_a, recv_b = neighbours(send_a, send_b, "strip")
    q, col_a, col_b = merge_rows(strips, place, send_a, mid, send_b, recv_a, recv_b, halo)
    recv_a, recv_b = neighbours(col_a, col_b, "frame")
    k1x, k1, k11_part = merge_cols(n, rows, place, q, recv_a, recv_b, k0x, halo)

    send_a, mid, send_b, stat2 = apply_terms(place, (k1x,), mats, weights, moved, halo, halo)
    recv_a, recv_b = neighbours(send_a, send_b, "strip")
    sums = jnp.stack([k00_part, stat1, k11_part, stat2])
    for axis, size in (("frame", n), ("strip", strips)):
        d = 1
        while d < size:
            sums = sums + swap(sums, axis, d)
            d *= 2
    k2 = wrap(place, send_a, mid, send_b, recv_a, recv_b, k1, halo)

    def gathered(x):
        parts = [x]
        for d in range(1, n):
            parts.append(swap(x, "frame", d))
        return parts

    def gathered_tree(x):
        parts = [x] + [None] * (n - 1)
        for i in range(n):
            for d in reversed(distances):
                if i % (2 * d) == 0:
                    parts[i + d] = swap(parts[i], "frame", d)
        return parts

    g0, g1, g2 = gathered(k0), gathered(k1), gathered_tree(k2)
    result, base, coef = solution_image(place, estimate, sums, g0, g1)
    return result, residual_image(place, base, coef, g2, halo)


def solution(mesh):
    return jax.shard_map(
        steps,
        mesh=mesh,
        in_specs=(
            P("strip", None),
            P("frame", "strip", None),
            P("frame", "strip", None),
            P("frame", None),
            P("frame", None),
        ),
        out_specs=(P("strip", None), P("strip", None)),
        check_vma=False,
    )
```

```python
import functools

import jax
import jax.numpy as jnp
from jax import lax
from jax.experimental import pallas as pl
from jax.experimental.pallas import tpu as pltpu
from jax.sharding import PartitionSpec as P


damping = 0.05
f32 = jnp.float32
bf16 = jnp.bfloat16
LANE = 128
VMEM = pl.BlockSpec(memory_space=pltpu.VMEM)
ANY = pl.BlockSpec(memory_space=pl.ANY)
SMEM = pl.BlockSpec(memory_space=pltpu.SMEM)


def room(mib):
    return pltpu.CompilerParams(vmem_limit_bytes=mib * 2**20)


def split(x):
    hi = x.astype(bf16)
    lo = (x - hi.astype(f32)).astype(bf16)
    return hi, lo


def dot(a, b):
    return jnp.dot(a, b, preferred_element_type=f32)


def choose(flag, a, b):
    return jnp.where(jnp.full(a.shape, flag, jnp.int32) == 1, a, b)


def pack_edge(edge, halo, w):
    rows = edge.shape[0]
    per = LANE // (2 * halo)
    short = rows * 2 * halo // w
    edge = pltpu.roll(edge, halo, 1)
    lane = lax.broadcasted_iota(jnp.int32, (short, LANE), 1)
    out = []
    for t in range(w // LANE):
        tile = None
        for p in range(per):
            k = t * per + p
            part = edge[k * short : (k + 1) * short]
            part = pltpu.roll(part, p * 2 * halo, 1) if p else part
            tile = part if tile is None else jnp.where(lane >= p * 2 * halo, part, tile)
        out.append(tile)
    return jnp.concatenate(out, axis=1)


def unpack_edge(packed, halo):
    _, w = packed.shape
    per = LANE // (2 * halo)
    parts = []
    for k in range(w // (2 * halo)):
        t, p = divmod(k, per)
        part = packed[:, t * LANE : (t + 1) * LANE]
        back = (LANE - halo - p * 2 * halo) % LANE
        parts.append(pltpu.roll(part, back, 1) if back else part)
    return jnp.concatenate(parts, axis=0)


def tiles(width, step=256):
    return [(s, min(step, width - s)) for s in range(0, width, step)]


def toeplitz(base, count):
    wide = base.shape[1]
    return pltpu.roll(jnp.broadcast_to(base, (count, wide)), 0, 1, stride=1, stride_axis=0)


def build_group(taps, g, frames, rows, halo, t_ref, b_ref, bp_ref, ta_ref):
    ext = rows + 2 * halo
    unit = taps / jnp.sum(taps, axis=1, keepdims=True)
    for s in range(frames):
        f = g * frames + s
        col = unit[s : s + 1]
        row = unit[frames + s : frames + s + 1]
        by_rows = toeplitz(row, rows)
        hi, lo = split(by_rows)
        t_ref[f, :rows, :] = hi
        t_ref[f, rows:, :] = lo
        hi, lo = split(by_rows.T[:ext])
        ta_ref[g, :ext, s * rows : (s + 1) * rows] = hi
        ta_ref[g, ext:, s * rows : (s + 1) * rows] = lo
        hi, lo = split(toeplitz(col, LANE).T)
        b_ref[f, :, :LANE] = hi
        b_ref[f, :, LANE:] = lo
        hi, lo = split(toeplitz(pltpu.roll(col, LANE, 1), 2 * LANE)[:, :LANE])
        bp_ref[f, :, :LANE] = hi
        bp_ref[f, :, LANE:] = lo


def matrix_shapes(groups, frames, rows, halo):
    ext = rows + 2 * halo
    return [
        jax.ShapeDtypeStruct(s, bf16)
        for s in (
            (groups * frames, 2 * rows, 2 * LANE),
            (groups * frames, 2 * LANE, 2 * LANE),
            (groups * frames, 2 * LANE, 2 * LANE),
            (groups, 2 * ext, frames * rows),
        )
    ]


def tile_height(frames):
    return -(-2 * frames // 8) * 8


def setup_kernel(frames, rows, halo, starts, *refs):
    tiles_in = refs[: len(starts)]
    mats, taps, sem = refs[len(starts) : -2], refs[-2], refs[-1]
    height = tile_height(frames)

    def copy(g):
        source = tiles_in[g].at[pl.ds(starts[g], height), pl.ds(0, 2 * LANE)]
        return pltpu.make_async_copy(source, taps.at[g], sem.at[g])

    for g in range(len(starts)):
        copy(g).start()
    for g in range(len(starts)):
        copy(g).wait()
        build_group(taps[g], g, frames, rows, halo, *mats)


def setup_matrices(tiles_in, starts, frames, rows, halo):
    groups = len(tiles_in)
    return pl.pallas_call(
        functools.partial(setup_kernel, frames, rows, halo, starts),
        out_shape=matrix_shapes(groups, frames, rows, halo),
        in_specs=[ANY] * groups,
        out_specs=[VMEM] * 4,
        scratch_shapes=[
            pltpu.VMEM((groups, tile_height(frames), 2 * LANE), f32),
            pltpu.SemaphoreType.DMA((groups,)),
        ],
        compiler_params=room(24),
        name="setup_all",
    )(*tiles_in)


def load_image(y_hi, y_lo, image, halo):
    ext, full = image.shape
    shift = LANE - halo
    y = pltpu.roll(image, full - shift, 1)[:, : full - LANE]
    hi, lo = split(y)
    y_hi[:ext, :] = hi
    y_lo[:ext, :] = lo


def group_terms(frames, rows, w, y_hi, y_lo, t, b, bp, ta, weight, data, us, qs, vs_hi, vs_lo, acc, stat, ready=None):
    total = None
    for f in range(frames):
        for c, size in tiles(w + LANE):
            r1 = dot(t(f)[...], y_hi[:, c : c + size])
            r2 = dot(t(f)[:rows, :], y_lo[:, c : c + size])
            hi, lo = split(r1[:rows] + r1[rows:] + r2)
            us[:rows, c : c + size] = hi
            us[rows:, c : c + size] = lo
        if ready is not None:
            ready(f)
        for k in range(w // LANE):
            c = k * LANE
            r = dot(us[:, c : c + 2 * LANE], b(f)[...])
            a = r[:rows, :LANE] + r[:rows, LANE:] + r[rows:, :LANE]
            if data is not None:
                a = a - data(f)[:, c : c + LANE]
            q = weight(f)[:, c : c + LANE] * a
            if stat is not None:
                part = jnp.sum((a * q).reshape(rows // 8, 8, LANE), axis=0)
                total = part if total is None else total + part
            hi, lo = split(q)
            qs[:rows, c + LANE : c + 2 * LANE] = hi
            qs[rows:, c + LANE : c + 2 * LANE] = lo
        for k in range(w // LANE + 1):
            c = k * LANE
            r = dot(qs[:, c : c + 2 * LANE], bp(f)[...])
            hi, lo = split(r[:rows, :LANE] + r[:rows, LANE:] + r[rows:, :LANE])
            vs_hi[f * rows : (f + 1) * rows, c : c + LANE] = hi
            vs_lo[f * rows : (f + 1) * rows, c : c + LANE] = lo
    ext = acc.shape[0]
    for c, size in tiles(w + LANE):
        r1 = dot(ta[...], vs_hi[:, c : c + size])
        r2 = dot(ta[:ext, :], vs_lo[:, c : c + size])
        acc[:, c : c + size] += r1[:ext] + r1[ext:] + r2
    if stat is not None:
        stat[...] += total


def work_scratch(frames, rows, halo, w):
    ext = rows + 2 * halo
    return [
        pltpu.VMEM((2 * LANE, w + LANE), bf16),
        pltpu.VMEM((2 * LANE, w + LANE), bf16),
        pltpu.VMEM((2 * rows, w + LANE), bf16),
        pltpu.VMEM((2 * rows, w + 2 * LANE), bf16),
        pltpu.VMEM((frames * rows, w + LANE), bf16),
        pltpu.VMEM((frames * rows, w + LANE), bf16),
        pltpu.VMEM((ext, w + LANE), f32),
    ]


def clear_edges(y_hi, y_lo, qs, ext, rows, w):
    zero = jnp.zeros((y_hi.shape[0] - ext, y_hi.shape[1]), bf16)
    y_hi[ext:, :] = zero
    y_lo[ext:, :] = zero
    qs[:, :LANE] = jnp.zeros((2 * rows, LANE), bf16)
    qs[:, w + LANE :] = jnp.zeros((2 * rows, LANE), bf16)


def unshift(acc, halo):
    return pltpu.roll(acc, acc.shape[1] - halo, 1)


def first_kernel(
    frames, rows, halo,
    place, est, recv_a, recv_b, t_ref, b_ref, bp_ref, ta_ref, w_hbm, d_hbm,
    send_a, mid, send_b,
    y_hi, y_lo, us, qs, vs_hi, vs_lo, acc, wbuf, dbuf, sem,
):
    ext = rows + 2 * halo
    cols = est.shape[1]
    copies = [
        (
            pltpu.make_async_copy(w_hbm.at[f], wbuf.at[f], sem.at[0, f]),
            pltpu.make_async_copy(d_hbm.at[f], dbuf.at[f], sem.at[1, f]),
        )
        for f in range(frames)
    ]
    for pair in copies:
        for c in pair:
            c.start()
    clear_edges(y_hi, y_lo, qs, ext, rows, cols)
    odd = lax.rem(place[1], 2)
    none = jnp.zeros((ext, LANE), f32)
    for start in range(0, cols, 4 * LANE):
        size = 4 * LANE + LANE
        left = max(start - LANE, 0)
        span = slice(left, min(start + 4 * LANE, cols))
        x = jnp.concatenate(
            [
                choose(odd, recv_a[:, span], recv_b[:, span]),
                est[:, span],
                choose(odd, recv_b[:, span], recv_a[:, span]),
            ],
            axis=0,
        )
        if start == 0:
            x = jnp.concatenate([none, x], axis=1)
        if x.shape[1] < size:
            x = jnp.concatenate([x, jnp.zeros((ext, size - x.shape[1]), f32)], axis=1)
        hi, lo = split(pltpu.roll(x, halo, 1)[:, LANE:])
        y_hi[:ext, start : start + 4 * LANE] = hi
        y_lo[:ext, start : start + 4 * LANE] = lo
        if start + 4 * LANE >= cols:
            tail = jnp.concatenate([x[:, 4 * LANE :], none], axis=1)
            hi, lo = split(pltpu.roll(tail, halo, 1)[:, LANE:])
            y_hi[:ext, cols:] = hi
            y_lo[:ext, cols:] = lo
    acc[...] = jnp.zeros_like(acc)

    def ready(f):
        for c in copies[f]:
            c.wait()

    group_terms(
        frames, rows, cols, y_hi, y_lo,
        lambda f: t_ref.at[f], lambda f: b_ref.at[f], lambda f: bp_ref.at[f], ta_ref.at[0],
        lambda f: wbuf.at[f], lambda f: dbuf.at[f],
        us, qs, vs_hi, vs_lo, acc, None, ready,
    )
    for start in range(0, cols, 4 * LANE):
        size = min(4 * LANE, cols - start)
        z = pltpu.roll(acc[:, start : start + size + LANE], size + LANE - halo, 1)[:, :size]
        span = slice(start, start + size)
        low, high = z[:halo], z[halo + rows :]
        send_a[:, span] = choose(odd, low, high)
        send_b[:, span] = choose(odd, high, low)
        mid[:, span] = z[halo : halo + rows]


def first_terms(place, est, recv_a, recv_b, mats, weights, observed):
    frames, rows, cols = weights.shape
    halo = recv_a.shape[0]
    return pl.pallas_call(
        functools.partial(first_kernel, frames, rows, halo),
        out_shape=[
            jax.ShapeDtypeStruct((halo, cols), f32),
            jax.ShapeDtypeStruct((rows, cols), f32),
            jax.ShapeDtypeStruct((halo, cols), f32),
        ],
        in_specs=[SMEM] + [VMEM] * 7 + [ANY, ANY],
        out_specs=[VMEM] * 3,
        scratch_shapes=work_scratch(frames, rows, halo, cols)
        + [
            pltpu.VMEM((frames, rows, cols), f32),
            pltpu.VMEM((frames, rows, cols), f32),
            pltpu.SemaphoreType.DMA((2, frames)),
        ],
        cost_estimate=pl.CostEstimate(flops=8 * 10**9, bytes_accessed=8 * 2**20, transcendentals=0),
        compiler_params=room(36),
        name="first_terms",
    )(place, est, recv_a, recv_b, *mats, weights, observed)


def prepare_kernel(plan, frames, rows, halo, w, place, cols_in, rows_in, weights, *refs):
    outs, tile, mats, sem = refs[: len(plan)], refs[len(plan)], refs[len(plan) + 1 : -1], refs[-1]
    taps = cols_in.shape[1]
    pending = []
    for i, (distance, _) in enumerate(plan):
        start = pl.multiple_of(jnp.bitwise_xor(place[0], distance) * w, LANE)
        for k in range(frames):
            copy = pltpu.make_async_copy(
                weights.at[k, :, pl.ds(start, w)],
                outs[i].at[pl.ds(k * rows, rows), :],
                sem.at[i, k],
            )
            copy.start()
            pending.append(copy)
    tile[...] = jnp.zeros_like(tile)
    tile[:frames, :taps] = cols_in[...]
    tile[frames : 2 * frames, :taps] = rows_in[...]
    for i, (_, with_taps) in enumerate(plan):
        if with_taps:
            outs[i][frames * rows :, :] = tile[...]
    build_group(tile[:, : 2 * LANE], 0, frames, rows, halo, *mats)
    for copy in pending:
        copy.wait()


def prepare(plan, place, column_kernels, row_kernels, weights, w, halo):
    frames, rows, _ = weights.shape
    height = tile_height(frames)
    out = pl.pallas_call(
        functools.partial(prepare_kernel, plan, frames, rows, halo, w),
        out_shape=[
            jax.ShapeDtypeStruct((frames * rows + (height if taps else 0), w), f32)
            for _, taps in plan
        ]
        + [jax.ShapeDtypeStruct((height, w), f32)]
        + matrix_shapes(1, frames, rows, halo),
        in_specs=[SMEM, VMEM, VMEM, ANY],
        out_specs=[VMEM] * (len(plan) + 5),
        scratch_shapes=[pltpu.SemaphoreType.DMA((len(plan), frames))],
        compiler_params=room(24),
        name="prepare",
    )(place, column_kernels, row_kernels, weights)
    return out[: len(plan)], out[len(plan)], out[len(plan) + 1 :]


def blocks_kernel(n, halo, w, place, send_a, mid, send_b, recv_a, recv_b, *refs):
    outs, full = refs[:-1], refs[-1]
    rows, cols = mid.shape
    odd = lax.rem(place[1], 2)
    inner = slice(LANE, LANE + cols)
    for end in (0, LANE + cols):
        full[:, end : end + LANE] = jnp.zeros((rows, LANE), f32)
    full[:halo, inner] = mid[:halo, :] + choose(odd, recv_a[...], recv_b[...])
    full[halo : rows - halo, inner] = mid[halo : rows - halo, :]
    full[rows - halo :, inner] = mid[rows - halo :, :] + choose(odd, recv_b[...], recv_a[...])
    lane = lax.broadcasted_iota(jnp.int32, (rows, LANE), 1)
    for i in range(n):
        start = jnp.bitwise_xor(place[0], i) * w
        outs[i][:rows, :] = full[:, pl.ds(pl.multiple_of(start + LANE, LANE), w)]
        before = full[:, pl.ds(pl.multiple_of(start, LANE), LANE)]
        after = full[:, pl.ds(pl.multiple_of(start + LANE + w, LANE), LANE)]
        outs[i][rows:, :] = pack_edge(jnp.where(lane >= LANE - halo, before, after), halo, w)


def column_blocks(n, place, send_a, mid, send_b, recv_a, recv_b, w):
    rows, cols = mid.shape
    halo = send_a.shape[0]
    height = rows + rows * 2 * halo // w
    return pl.pallas_call(
        functools.partial(blocks_kernel, n, halo, w),
        out_shape=[jax.ShapeDtypeStruct((height, w), f32)] * n,
        in_specs=[SMEM] + [VMEM] * 5,
        out_specs=[VMEM] * n,
        scratch_shapes=[pltpu.VMEM((rows, cols + 2 * LANE), f32)],
        compiler_params=room(16),
        name="column_blocks",
    )(place, send_a, mid, send_b, recv_a, recv_b)


def start_kernel(n, rows, halo, w, place, est, *refs):
    parts = refs[:-5]
    k0, wide, send_a, send_b, stat = refs[-5:]
    total = parts[0][...]
    for p in parts[1:]:
        total = total + p[...]
    me = place[0]
    odd = lax.rem(place[1], 2)
    at = lambda start, size: est[:, pl.ds(pl.multiple_of(start, LANE), size)]
    own = -(total[:rows] + damping * at(me * w, w))
    edge = unpack_edge(total[rows:], halo)
    before = at(jnp.maximum(me * w - LANE, 0), LANE)
    after = at(jnp.minimum(me * w + w, (n * w) - LANE), LANE)
    none = jnp.zeros((rows, LANE), f32)
    left = choose((me > 0).astype(jnp.int32), -(edge + damping * before), none)
    right = choose((me < n - 1).astype(jnp.int32), -(edge + damping * after), none)
    k0[...] = own
    wide[:, :LANE] = left
    wide[:, LANE : LANE + w] = own
    wide[:, LANE + w :] = right
    low, high = wide[:halo, :], wide[rows - halo :, :]
    send_a[...] = choose(odd, low, high)
    send_b[...] = choose(odd, high, low)
    square = own * own
    acc = square[:, :LANE]
    for c in range(LANE, w, LANE):
        acc = acc + square[:, c : c + LANE]
    stat[...] = jnp.sum(acc.reshape(rows // 8, 8, LANE), axis=0)


def start_image(n, place, est, parts, halo):
    rows, cols = est.shape
    w = cols // n
    return pl.pallas_call(
        functools.partial(start_kernel, n, rows, halo, w),
        out_shape=[
            jax.ShapeDtypeStruct((rows, w), f32),
            jax.ShapeDtypeStruct((rows, w + 2 * LANE), f32),
            jax.ShapeDtypeStruct((halo, w + 2 * LANE), f32),
            jax.ShapeDtypeStruct((halo, w + 2 * LANE), f32),
            jax.ShapeDtypeStruct((8, LANE), f32),
        ],
        in_specs=[SMEM] + [VMEM] * (1 + len(parts)),
        out_specs=[VMEM] * 5,
        compiler_params=room(12),
        name="start_image",
    )(place, est, *parts)


def apply_kernel(frames, rows, halo, w, groups, cut, count, pieces, place, *refs):
    image, refs = refs[:pieces], refs[pieces:]
    t_hbm, b_hbm, bp_hbm, ta_hbm, own = refs[:5]
    moved = refs[5 : 5 + count]
    send_a, mid, send_b, stat = refs[5 + count : 9 + count]
    refs = refs[9 + count :]
    if pieces > 1:
        whole, refs = refs[0], refs[1:]
    y_hi, y_lo, us, qs, vs_hi, vs_lo, acc, tb, bb, bpb, tab, wbuf, sem, wsem = refs
    odd = lax.rem(place[1], 2)
    ext = rows + 2 * halo

    def copies(g):
        span = pl.ds(g * frames, frames)
        return [
            pltpu.make_async_copy(t_hbm.at[span], tb.at[g], sem.at[0, g]),
            pltpu.make_async_copy(b_hbm.at[span], bb.at[g], sem.at[1, g]),
            pltpu.make_async_copy(bp_hbm.at[span], bpb.at[g], sem.at[2, g]),
            pltpu.make_async_copy(ta_hbm.at[g], tab.at[g], sem.at[3, g]),
        ]

    mine = pl.ds(pl.multiple_of(place[0] * w, LANE), w)
    for g in range(groups):
        for c in copies(g):
            c.start()
        for f in range(frames):
            span = pl.ds(f * rows, rows)
            if g == 0:
                pltpu.make_async_copy(own.at[f, :, mine], wbuf.at[g, f], wsem.at[g, f]).start()
            elif g < groups - 1:
                pltpu.make_async_copy(moved[g - 1].at[span, :], wbuf.at[g, f], wsem.at[g, f]).start()
            else:
                inside = (place[0] >= groups // 4) & (place[0] < groups - groups // 4)
                for flag, ref in ((inside, moved[-2]), (jnp.logical_not(inside), moved[-1])):

                    @pl.when(flag)
                    def _(ref=ref, span=span, g=g, f=f):
                        pltpu.make_async_copy(ref.at[span, :], wbuf.at[g, f], wsem.at[g, f]).start()
    clear_edges(y_hi, y_lo, qs, ext, rows, w)
    if pieces > 1:
        wide, recv_a, recv_b = image
        whole[:halo, :] = choose(odd, recv_a[...], recv_b[...])
        whole[halo : halo + rows, :] = wide[...]
        whole[halo + rows :, :] = choose(odd, recv_b[...], recv_a[...])
        load_image(y_hi, y_lo, whole[...], halo)
    else:
        load_image(y_hi, y_lo, image[0][...], halo)
    acc[...] = jnp.zeros_like(acc)
    stat[...] = jnp.zeros_like(stat)

    @pl.loop(0, groups)
    def _(g):
        for c in copies(g):
            c.wait()
        for f in range(frames):
            pltpu.make_async_copy(own.at[f, :, mine], wbuf.at[g, f], wsem.at[g, f]).wait()
        group_terms(
            frames, rows, w, y_hi, y_lo,
            lambda f: tb.at[g, f], lambda f: bb.at[g, f], lambda f: bpb.at[g, f], tab.at[g],
            lambda f: wbuf.at[g, f], None,
            us, qs, vs_hi, vs_lo, acc, stat,
        )

    z = unshift(acc[...], halo)
    send_a[...] = choose(odd, z[:cut], z[ext - cut :])
    send_b[...] = choose(odd, z[ext - cut :], z[:cut])
    mid[...] = z[cut : ext - cut]


def apply_terms(place, image, mats, weights, moved, cut, halo):
    frames, rows, _ = weights.shape
    w = image[0].shape[1] - 2 * LANE
    ext = rows + 2 * halo
    t, b, bp, ta = mats
    groups = ta.shape[0]
    wide = w + LANE
    return pl.pallas_call(
        functools.partial(apply_kernel, frames, rows, halo, w, groups, cut, len(moved), len(image)),
        out_shape=[
            jax.ShapeDtypeStruct((cut, wide), f32),
            jax.ShapeDtypeStruct((ext - 2 * cut, wide), f32),
            jax.ShapeDtypeStruct((cut, wide), f32),
            jax.ShapeDtypeStruct((8, LANE), f32),
        ]
        + [jax.ShapeDtypeStruct((ext, w + 2 * LANE), f32)] * (len(image) > 1),
        in_specs=[SMEM] + [VMEM] * len(image) + [ANY] * (5 + len(moved)),
        out_specs=[VMEM] * (4 + (len(image) > 1)),
        scratch_shapes=work_scratch(frames, rows, halo, w)
        + [
            pltpu.VMEM((groups, frames) + t.shape[1:], bf16),
            pltpu.VMEM((groups, frames) + b.shape[1:], bf16),
            pltpu.VMEM((groups, frames) + bp.shape[1:], bf16),
            pltpu.VMEM((groups,) + ta.shape[1:], bf16),
            pltpu.VMEM((groups, frames, rows, w), f32),
            pltpu.SemaphoreType.DMA((4, groups)),
            pltpu.SemaphoreType.DMA((groups, frames)),
        ],
        cost_estimate=pl.CostEstimate(
            flops=groups * 3 * 10**9, bytes_accessed=groups * 2**20, transcendentals=0
        ),
        compiler_params=room(28),
    )(place, *image, t, b, bp, ta, weights, *moved)


def rows_kernel(strips, halo, w, place, send_a, mid, send_b, recv_a, recv_b, q, col_a, col_b):
    odd = lax.rem(place[1], 2)
    odd_col = lax.rem(place[0], 2)
    edge_rows, wide = send_a.shape
    ext = q.shape[0]
    row = lax.broadcasted_iota(jnp.int32, (edge_rows, wide), 0)
    strip = jnp.full((edge_rows, wide), place[1], jnp.int32)
    low = choose(odd, send_a[...], send_b[...]) + choose(odd, recv_a[...], recv_b[...])
    high = choose(odd, send_b[...], send_a[...]) + choose(odd, recv_b[...], recv_a[...])
    q[:edge_rows, :] = jnp.where((row >= halo) | (strip > 0), low, 0.0)
    q[edge_rows : ext - edge_rows, :] = mid[...]
    q[ext - edge_rows :, :] = jnp.where((row < edge_rows - halo) | (strip < strips - 1), high, 0.0)
    lane = lax.broadcasted_iota(jnp.int32, (ext, LANE), 1)
    edge = q[:, w:]
    to_left = jnp.where(lane < halo, q[:, :LANE], edge)
    to_right = jnp.where(lane >= LANE - halo, q[:, w - LANE : w], edge)
    col_a[...] = choose(odd_col, to_left, to_right)
    col_b[...] = choose(odd_col, to_right, to_left)


def merge_rows(strips, place, send_a, mid, send_b, recv_a, recv_b, halo):
    ext = mid.shape[0] + 2 * send_a.shape[0]
    wide = mid.shape[1]
    return pl.pallas_call(
        functools.partial(rows_kernel, strips, halo, wide - LANE),
        out_shape=[
            jax.ShapeDtypeStruct((ext, wide), f32),
            jax.ShapeDtypeStruct((ext, LANE), f32),
            jax.ShapeDtypeStruct((ext, LANE), f32),
        ],
        in_specs=[SMEM] + [VMEM] * 5,
        out_specs=[VMEM] * 3,
        compiler_params=room(8),
        name="merge_rows",
    )(place, send_a, mid, send_b, recv_a, recv_b)


def cols_kernel(n, rows, halo, place, q, recv_a, recv_b, before, out, block, stat):
    odd = lax.rem(place[0], 2)
    ext, wide = q.shape
    w = wide - LANE
    lane = lax.broadcasted_iota(jnp.int32, (ext, LANE), 1)
    at = jnp.full((ext, LANE), place[0], jnp.int32)
    left = choose(odd, recv_a[...], recv_b[...])
    right = choose(odd, recv_b[...], recv_a[...])
    edge = q[:, w:]
    total = None
    out[:, :LANE] = jnp.where(at > 0, edge + left, 0.0) + damping * before[:, :LANE]
    out[:, LANE + w :] = jnp.where(at < n - 1, edge + right, 0.0) + damping * before[:, LANE + w :]
    for c in range(0, w, LANE):
        x = q[:, c : c + LANE] + damping * before[:, c + LANE : c + 2 * LANE]
        if c == 0:
            x = x + jnp.where(lane < halo, left, 0.0)
        if c == w - LANE:
            x = x + jnp.where(lane >= LANE - halo, right, 0.0)
        out[:, c + LANE : c + 2 * LANE] = x
        own = x[halo : halo + rows]
        block[:, c : c + LANE] = own
        part = jnp.sum((own * own).reshape(rows // 8, 8, LANE), axis=0)
        total = part if total is None else total + part
    stat[...] = total


def merge_cols(n, rows, place, q, recv_a, recv_b, before, halo):
    ext, wide = q.shape
    w = wide - LANE
    return pl.pallas_call(
        functools.partial(cols_kernel, n, rows, halo),
        out_shape=[
            jax.ShapeDtypeStruct((ext, w + 2 * LANE), f32),
            jax.ShapeDtypeStruct((rows, w), f32),
            jax.ShapeDtypeStruct((8, LANE), f32),
        ],
        in_specs=[SMEM] + [VMEM] * 4,
        out_specs=[VMEM] * 3,
        compiler_params=room(10),
        name="merge_cols",
    )(place, q, recv_a, recv_b, before)


def wrap_kernel(rows, halo, w, place, send_a, mid, send_b, recv_a, recv_b, before, out):
    odd = lax.rem(place[1], 2)
    keep = rows - 2 * halo
    pieces = (
        (0, halo, mid[:halo, :] + choose(odd, recv_a[...], recv_b[...])),
        (halo, keep, mid[halo : rows - halo, :]),
        (rows - halo, halo, mid[rows - halo :, :] + choose(odd, recv_b[...], recv_a[...])),
    )
    edges = []
    for start, size, value in pieces:
        span = slice(start, start + size)
        out[span, :] = value[:, :w] + damping * before[span, :]
        edges.append(value[:, w:])
    out[rows:, :] = pack_edge(jnp.concatenate(edges, axis=0), halo, w)


def wrap(place, send_a, mid, send_b, recv_a, recv_b, before, halo):
    rows, w = before.shape
    height = rows + rows * 2 * halo // w
    return pl.pallas_call(
        functools.partial(wrap_kernel, rows, halo, w),
        out_shape=jax.ShapeDtypeStruct((height, w), f32),
        in_specs=[SMEM] + [VMEM] * 6,
        out_specs=VMEM,
        compiler_params=room(8),
        name="wrap",
    )(place, send_a, mid, send_b, recv_a, recv_b, before)


def solution_kernel(n, w, place, est, sums, *refs):
    k0, k1 = refs[:n], refs[n : 2 * n]
    sol, res, coef = refs[2 * n :]
    total = [
        jnp.sum(jnp.sum(sums[i], axis=0, keepdims=True), axis=1, keepdims=True) for i in range(4)
    ]
    k00, k11 = total[0], total[2]
    k01 = total[1] + damping * k00
    k12 = total[3] + damping * k11
    alpha0 = k00 / k01
    norm1 = k00 - 2.0 * alpha0 * k01 + alpha0 * alpha0 * k11
    beta = norm1 / k00
    curve1 = (1.0 + beta) * (1.0 + beta) * k01 - 2.0 * (1.0 + beta) * alpha0 * k11
    curve1 = curve1 + alpha0 * alpha0 * k12
    alpha1 = norm1 / curve1
    c1 = alpha0 + alpha1 * (1.0 + beta)
    c2 = alpha0 * alpha1
    coef[...] = jnp.broadcast_to(c2, coef.shape)
    for i in range(n):
        cols = pl.ds(pl.multiple_of(jnp.bitwise_xor(place[0], i) * w, LANE), w)
        a0, a1 = k0[i][...], k1[i][...]
        sol[:, cols] = est[:, cols] + c1 * a0 - c2 * a1
        res[:, cols] = a0 - c1 * a1


def solution_image(place, est, sums, k0, k1):
    n = len(k0)
    w = k0[0].shape[1]
    return pl.pallas_call(
        functools.partial(solution_kernel, n, w),
        out_shape=[jax.ShapeDtypeStruct(est.shape, f32)] * 2
        + [jax.ShapeDtypeStruct((8, LANE), f32)],
        in_specs=[SMEM] + [VMEM] * (2 + 2 * n),
        out_specs=[VMEM] * 3,
        compiler_params=room(20),
        name="solution_image",
    )(place, est, sums, *k0, *k1)


def residual_kernel(n, rows, halo, w, place, base, coef, *refs):
    k2, (res, full) = refs[:n], refs[n:]
    c2 = coef[0:1, 0:1]
    lane = lax.broadcasted_iota(jnp.int32, (rows, LANE), 1)
    spot = [jnp.bitwise_xor(place[0], i) for i in range(n)]
    full[:, :LANE] = jnp.zeros((rows, LANE), f32)
    full[:, LANE + n * w :] = jnp.zeros((rows, LANE), f32)
    for i in range(n):
        full[:, pl.ds(pl.multiple_of(spot[i] * w + LANE, LANE), w)] = k2[i][:rows, :]
    for i in range(n):
        edge = unpack_edge(k2[i][rows:, :], halo)
        left = pl.ds(pl.multiple_of(spot[i] * w, LANE), LANE)
        right = pl.ds(pl.multiple_of(spot[i] * w + w + LANE, LANE), LANE)
        full[:, left] += jnp.where(lane >= LANE - halo, edge, 0.0)
        full[:, right] += jnp.where(lane < halo, edge, 0.0)
    for c in range(0, n * w, LANE):
        res[:, c : c + LANE] = base[:, c : c + LANE] + c2 * full[:, c + LANE : c + 2 * LANE]


def residual_image(place, base, coef, k2, halo):
    n = len(k2)
    rows, cols = base.shape
    w = cols // n
    return pl.pallas_call(
        functools.partial(residual_kernel, n, rows, halo, w),
        out_shape=jax.ShapeDtypeStruct(base.shape, f32),
        in_specs=[SMEM] + [VMEM] * (2 + n),
        out_specs=VMEM,
        scratch_shapes=[pltpu.VMEM((rows, cols + 2 * LANE), f32)],
        compiler_params=room(16),
        name="residual_image",
    )(place, base, coef, *k2)


def neighbours(send_a, send_b, axis):
    n = lax.axis_size(axis)
    out = []
    for lead, x in ((0, send_a), (1, send_b)):
        pairs = [(i, i + 1) for i in range(lead, n - 1, 2)]
        out.append(lax.ppermute(x, axis, pairs + [(b, a) for a, b in pairs]))
    return out


def swap(x, axis, distance):
    n = lax.axis_size(axis)
    return lax.ppermute(x, axis, [(i, i ^ distance) for i in range(n)])


def steps(estimate, observed, weights, column_kernels, row_kernels):
    n = lax.axis_size("frame")
    me = lax.axis_index("frame")
    strips = lax.axis_size("strip")
    strip = lax.axis_index("strip")
    place = jnp.stack([me, strip]).astype(jnp.int32)
    rows, cols = estimate.shape
    frames = weights.shape[0]
    halo = column_kernels.shape[1] // 2
    w = cols // n
    distances = [1 << k for k in range(n.bit_length() - 1)]

    low, high = estimate[:halo], estimate[rows - halo :]
    odd = strip % 2 == 1
    est_a, est_b = neighbours(
        jnp.where(odd, low, high), jnp.where(odd, high, low), "strip"
    )

    plan = [(d, True) for d in range(1, n - 1)] + [(n - 1, False)]
    packed, tile, own_mats = prepare(plan, place, column_kernels, row_kernels, weights, w, halo)
    far_tile = swap(tile[:, : 2 * LANE], "frame", n - 1)
    moved = []
    for i in range(n - 2):
        moved.append(swap(packed[i], "frame", i + 1))
    middle = range(n // 4, n - n // 4)
    for members in (middle, [i for i in range(n) if i not in middle]):
        moved.append(lax.ppermute(packed[-1], "frame", [(i, n - 1 - i) for i in members]))
    starts = [0] + [frames * rows] * (n - 2) + [0]

    send_a, mid, send_b = first_terms(
        place, estimate, est_a, est_b, own_mats, weights, observed
    )
    mats = setup_matrices([tile] + moved[: n - 2] + [far_tile], starts, frames, rows, halo)
    recv_a, recv_b = neighbours(send_a, send_b, "strip")

    part = list(column_blocks(n, place, send_a, mid, send_b, recv_a, recv_b, w))
    mine = [part[0]]
    for i in range(n - 1, 0, -1):
        d = i & -i
        got = swap(part[i], "frame", d)
        if i == d:
            mine.append(got)
        else:
            part[i ^ d] = part[i ^ d] + got
    k0, wide, send_a, send_b, k00_part = start_image(n, place, estimate, mine, halo)
    recv_a, recv_b = neighbours(send_a, send_b, "strip")

    send_a, mid, send_b, stat1, k0x = apply_terms(
        place, (wide, recv_a, recv_b), mats, weights, moved, 2 * halo, halo
    )
    recv_a, recv_b = neighbours(send_a, send_b, "strip")
    q, col_a, col_b = merge_rows(strips, place, send_a, mid, send_b, recv_a, recv_b, halo)
    recv_a, recv_b = neighbours(col_a, col_b, "frame")
    k1x, k1, k11_part = merge_cols(n, rows, place, q, recv_a, recv_b, k0x, halo)

    send_a, mid, send_b, stat2 = apply_terms(place, (k1x,), mats, weights, moved, halo, halo)
    recv_a, recv_b = neighbours(send_a, send_b, "strip")
    sums = jnp.stack([k00_part, stat1, k11_part, stat2])
    for axis, size in (("frame", n), ("strip", strips)):
        d = 1
        while d < size:
            sums = sums + swap(sums, axis, d)
            d *= 2
    k2 = wrap(place, send_a, mid, send_b, recv_a, recv_b, k1, halo)

    def gathered(x):
        parts = [x]
        for d in range(1, n):
            parts.append(swap(x, "frame", d))
        return parts

    def gathered_tree(x):
        parts = [x] + [None] * (n - 1)
        for i in range(n):
            for d in reversed(distances):
                if i % (2 * d) == 0:
                    parts[i + d] = swap(parts[i], "frame", d)
        return parts

    g0, g1, g2 = gathered(k0), gathered(k1), gathered_tree(k2)
    result, base, coef = solution_image(place, estimate, sums, g0, g1)
    return result, residual_image(place, base, coef, g2, halo)


def solution(mesh):
    return jax.shard_map(
        steps,
        mesh=mesh,
        in_specs=(
            P("strip", None),
            P("frame", "strip", None),
            P("frame", "strip", None),
            P("frame", None),
            P("frame", None),
        ),
        out_specs=(P("strip", None), P("strip", None)),
        check_vma=False,
    )
```

```python
import functools

import jax
import jax.numpy as jnp
from jax import lax
from jax.experimental import pallas as pl
from jax.experimental.pallas import tpu as pltpu
from jax.sharding import PartitionSpec as P


damping = 0.05
f32 = jnp.float32
bf16 = jnp.bfloat16
LANE = 128
VMEM = pl.BlockSpec(memory_space=pltpu.VMEM)
ANY = pl.BlockSpec(memory_space=pl.ANY)
SMEM = pl.BlockSpec(memory_space=pltpu.SMEM)
HBM = pl.BlockSpec(memory_space=pltpu.HBM)


def room(mib):
    return pltpu.CompilerParams(vmem_limit_bytes=mib * 2**20)


def split(x):
    hi = x.astype(bf16)
    lo = (x - hi.astype(f32)).astype(bf16)
    return hi, lo


def dot(a, b):
    return jnp.dot(a, b, preferred_element_type=f32)


def choose(flag, a, b):
    return jnp.where(jnp.full(a.shape, flag, jnp.int32) == 1, a, b)


def pack_edge(edge, halo, w):
    rows = edge.shape[0]
    per = LANE // (2 * halo)
    short = rows * 2 * halo // w
    edge = pltpu.roll(edge, halo, 1)
    lane = lax.broadcasted_iota(jnp.int32, (short, LANE), 1)
    out = []
    for t in range(w // LANE):
        tile = None
        for p in range(per):
            k = t * per + p
            part = edge[k * short : (k + 1) * short]
            part = pltpu.roll(part, p * 2 * halo, 1) if p else part
            tile = part if tile is None else jnp.where(lane >= p * 2 * halo, part, tile)
        out.append(tile)
    return jnp.concatenate(out, axis=1)


def unpack_edge(packed, halo):
    _, w = packed.shape
    per = LANE // (2 * halo)
    parts = []
    for k in range(w // (2 * halo)):
        t, p = divmod(k, per)
        part = packed[:, t * LANE : (t + 1) * LANE]
        back = (LANE - halo - p * 2 * halo) % LANE
        parts.append(pltpu.roll(part, back, 1) if back else part)
    return jnp.concatenate(parts, axis=0)


def tiles(width, step=256):
    return [(s, min(step, width - s)) for s in range(0, width, step)]


def toeplitz(base, count):
    wide = base.shape[1]
    return pltpu.roll(jnp.broadcast_to(base, (count, wide)), 0, 1, stride=1, stride_axis=0)


def build_group(taps, g, frames, rows, halo, t_ref, b_ref, bp_ref, ta_ref):
    ext = rows + 2 * halo
    unit = taps / jnp.sum(taps, axis=1, keepdims=True)
    for s in range(frames):
        f = g * frames + s
        col = unit[s : s + 1]
        row = unit[frames + s : frames + s + 1]
        by_rows = toeplitz(row, rows)
        hi, lo = split(by_rows)
        t_ref[f, :rows, :] = hi
        t_ref[f, rows:, :] = lo
        hi, lo = split(by_rows.T[:ext])
        ta_ref[g, :ext, s * rows : (s + 1) * rows] = hi
        ta_ref[g, ext:, s * rows : (s + 1) * rows] = lo
        hi, lo = split(toeplitz(col, LANE).T)
        b_ref[f, :, :LANE] = hi
        b_ref[f, :, LANE:] = lo
        hi, lo = split(toeplitz(pltpu.roll(col, LANE, 1), 2 * LANE)[:, :LANE])
        bp_ref[f, :, :LANE] = hi
        bp_ref[f, :, LANE:] = lo


def matrix_shapes(groups, frames, rows, halo):
    ext = rows + 2 * halo
    return [
        jax.ShapeDtypeStruct(s, bf16)
        for s in (
            (groups * frames, 2 * rows, 2 * LANE),
            (groups * frames, 2 * LANE, 2 * LANE),
            (groups * frames, 2 * LANE, 2 * LANE),
            (groups, 2 * ext, frames * rows),
        )
    ]


def tile_height(frames):
    return -(-2 * frames // 8) * 8


def setup_kernel(frames, rows, halo, starts, *refs):
    tiles_in = refs[: len(starts)]
    mats, taps, sem = refs[len(starts) : -2], refs[-2], refs[-1]
    height = tile_height(frames)

    def copy(g):
        source = tiles_in[g].at[pl.ds(starts[g], height), pl.ds(0, 2 * LANE)]
        return pltpu.make_async_copy(source, taps.at[g], sem.at[g])

    for g in range(len(starts)):
        copy(g).start()
    for g in range(len(starts)):
        copy(g).wait()
        build_group(taps[g], g, frames, rows, halo, *mats)


def setup_matrices(tiles_in, starts, frames, rows, halo):
    groups = len(tiles_in)
    return pl.pallas_call(
        functools.partial(setup_kernel, frames, rows, halo, starts),
        out_shape=matrix_shapes(groups, frames, rows, halo),
        in_specs=[ANY] * groups,
        out_specs=[VMEM] * 4,
        scratch_shapes=[
            pltpu.VMEM((groups, tile_height(frames), 2 * LANE), f32),
            pltpu.SemaphoreType.DMA((groups,)),
        ],
        compiler_params=room(24),
        name="setup_all",
    )(*tiles_in)


def load_image(y_hi, y_lo, image, halo):
    ext, full = image.shape
    shift = LANE - halo
    y = pltpu.roll(image, full - shift, 1)[:, : full - LANE]
    hi, lo = split(y)
    y_hi[:ext, :] = hi
    y_lo[:ext, :] = lo


def group_terms(frames, rows, w, y_hi, y_lo, t, b, bp, ta, weight, data, us, qs, vs_hi, vs_lo, acc, stat, ready=None):
    total = None
    for f in range(frames):
        for c, size in tiles(w + LANE):
            r1 = dot(t(f)[...], y_hi[:, c : c + size])
            r2 = dot(t(f)[:rows, :], y_lo[:, c : c + size])
            hi, lo = split(r1[:rows] + r1[rows:] + r2)
            us[:rows, c : c + size] = hi
            us[rows:, c : c + size] = lo
        if ready is not None:
            ready(f)
        for k in range(w // LANE):
            c = k * LANE
            r = dot(us[:, c : c + 2 * LANE], b(f)[...])
            a = r[:rows, :LANE] + r[:rows, LANE:] + r[rows:, :LANE]
            if data is not None:
                a = a - data(f)[:, c : c + LANE]
            q = weight(f)[:, c : c + LANE] * a
            if stat is not None:
                part = jnp.sum((a * q).reshape(rows // 8, 8, LANE), axis=0)
                total = part if total is None else total + part
            hi, lo = split(q)
            qs[:rows, c + LANE : c + 2 * LANE] = hi
            qs[rows:, c + LANE : c + 2 * LANE] = lo
        for k in range(w // LANE + 1):
            c = k * LANE
            r = dot(qs[:, c : c + 2 * LANE], bp(f)[...])
            hi, lo = split(r[:rows, :LANE] + r[:rows, LANE:] + r[rows:, :LANE])
            vs_hi[f * rows : (f + 1) * rows, c : c + LANE] = hi
            vs_lo[f * rows : (f + 1) * rows, c : c + LANE] = lo
    ext = acc.shape[0]
    for c, size in tiles(w + LANE):
        r1 = dot(ta[...], vs_hi[:, c : c + size])
        r2 = dot(ta[:ext, :], vs_lo[:, c : c + size])
        acc[:, c : c + size] += r1[:ext] + r1[ext:] + r2
    if stat is not None:
        stat[...] += total


def work_scratch(frames, rows, halo, w):
    ext = rows + 2 * halo
    return [
        pltpu.VMEM((2 * LANE, w + LANE), bf16),
        pltpu.VMEM((2 * LANE, w + LANE), bf16),
        pltpu.VMEM((2 * rows, w + LANE), bf16),
        pltpu.VMEM((2 * rows, w + 2 * LANE), bf16),
        pltpu.VMEM((frames * rows, w + LANE), bf16),
        pltpu.VMEM((frames * rows, w + LANE), bf16),
        pltpu.VMEM((ext, w + LANE), f32),
    ]


def clear_edges(y_hi, y_lo, qs, ext, rows, w):
    zero = jnp.zeros((y_hi.shape[0] - ext, y_hi.shape[1]), bf16)
    y_hi[ext:, :] = zero
    y_lo[ext:, :] = zero
    qs[:, :LANE] = jnp.zeros((2 * rows, LANE), bf16)
    qs[:, w + LANE :] = jnp.zeros((2 * rows, LANE), bf16)


def unshift(acc, halo):
    return pltpu.roll(acc, acc.shape[1] - halo, 1)


def first_kernel(
    frames, rows, halo,
    place, est, recv_a, recv_b, t_ref, b_ref, bp_ref, ta_ref, w_hbm, d_hbm,
    send_a, mid, send_b,
    y_hi, y_lo, us, qs, vs_hi, vs_lo, acc, wbuf, dbuf, sem,
):
    ext = rows + 2 * halo
    cols = est.shape[1]
    copies = [
        (
            pltpu.make_async_copy(w_hbm.at[f], wbuf.at[f], sem.at[0, f]),
            pltpu.make_async_copy(d_hbm.at[f], dbuf.at[f], sem.at[1, f]),
        )
        for f in range(frames)
    ]
    for pair in copies:
        for c in pair:
            c.start()
    clear_edges(y_hi, y_lo, qs, ext, rows, cols)
    odd = lax.rem(place[1], 2)
    none = jnp.zeros((ext, LANE), f32)
    for start in range(0, cols, 4 * LANE):
        size = 4 * LANE + LANE
        left = max(start - LANE, 0)
        span = slice(left, min(start + 4 * LANE, cols))
        x = jnp.concatenate(
            [
                choose(odd, recv_a[:, span], recv_b[:, span]),
                est[:, span],
                choose(odd, recv_b[:, span], recv_a[:, span]),
            ],
            axis=0,
        )
        if start == 0:
            x = jnp.concatenate([none, x], axis=1)
        if x.shape[1] < size:
            x = jnp.concatenate([x, jnp.zeros((ext, size - x.shape[1]), f32)], axis=1)
        hi, lo = split(pltpu.roll(x, halo, 1)[:, LANE:])
        y_hi[:ext, start : start + 4 * LANE] = hi
        y_lo[:ext, start : start + 4 * LANE] = lo
        if start + 4 * LANE >= cols:
            tail = jnp.concatenate([x[:, 4 * LANE :], none], axis=1)
            hi, lo = split(pltpu.roll(tail, halo, 1)[:, LANE:])
            y_hi[:ext, cols:] = hi
            y_lo[:ext, cols:] = lo
    acc[...] = jnp.zeros_like(acc)

    def ready(f):
        for c in copies[f]:
            c.wait()

    group_terms(
        frames, rows, cols, y_hi, y_lo,
        lambda f: t_ref.at[f], lambda f: b_ref.at[f], lambda f: bp_ref.at[f], ta_ref.at[0],
        lambda f: wbuf.at[f], lambda f: dbuf.at[f],
        us, qs, vs_hi, vs_lo, acc, None, ready,
    )
    for start in range(0, cols, 4 * LANE):
        size = min(4 * LANE, cols - start)
        z = pltpu.roll(acc[:, start : start + size + LANE], size + LANE - halo, 1)[:, :size]
        span = slice(start, start + size)
        low, high = z[:halo], z[halo + rows :]
        send_a[:, span] = choose(odd, low, high)
        send_b[:, span] = choose(odd, high, low)
        mid[:, span] = z[halo : halo + rows]


def first_terms(place, est, recv_a, recv_b, mats, weights, observed):
    frames, rows, cols = weights.shape
    halo = recv_a.shape[0]
    return pl.pallas_call(
        functools.partial(first_kernel, frames, rows, halo),
        out_shape=[
            jax.ShapeDtypeStruct((halo, cols), f32),
            jax.ShapeDtypeStruct((rows, cols), f32),
            jax.ShapeDtypeStruct((halo, cols), f32),
        ],
        in_specs=[SMEM] + [VMEM] * 7 + [HBM, HBM],
        out_specs=[VMEM] * 3,
        scratch_shapes=work_scratch(frames, rows, halo, cols)
        + [
            pltpu.VMEM((frames, rows, cols), f32),
            pltpu.VMEM((frames, rows, cols), f32),
            pltpu.SemaphoreType.DMA((2, frames)),
        ],
        cost_estimate=pl.CostEstimate(flops=8 * 10**9, bytes_accessed=8 * 2**20, transcendentals=0),
        compiler_params=room(36),
        name="first_terms",
    )(place, est, recv_a, recv_b, *mats, weights, observed)


def prepare_kernel(plan, frames, rows, halo, w, place, cols_in, rows_in, weights, *refs):
    outs, tile, mats = refs[: len(plan)], refs[len(plan)], refs[len(plan) + 1 : -4]
    cols_buf, rows_buf, taps_sem, sem = refs[-4:]
    taps = cols_in.shape[1]
    taps_copies = (
        pltpu.make_async_copy(cols_in, cols_buf, taps_sem.at[0]),
        pltpu.make_async_copy(rows_in, rows_buf, taps_sem.at[1]),
    )
    for copy in taps_copies:
        copy.start()
    pending = []
    for i, (distance, _) in enumerate(plan):
        start = pl.multiple_of(jnp.bitwise_xor(place[0], distance) * w, LANE)
        for k in range(frames):
            copy = pltpu.make_async_copy(
                weights.at[k, :, pl.ds(start, w)],
                outs[i].at[pl.ds(k * rows, rows), :],
                sem.at[i, k],
            )
            copy.start()
            pending.append(copy)
    tile[...] = jnp.zeros_like(tile)
    for copy in taps_copies:
        copy.wait()
    tile[:frames, :taps] = cols_buf[...]
    tile[frames : 2 * frames, :taps] = rows_buf[...]
    for i, (_, with_taps) in enumerate(plan):
        if with_taps:
            outs[i][frames * rows :, :] = tile[...]
    build_group(tile[:, : 2 * LANE], 0, frames, rows, halo, *mats)
    for copy in pending:
        copy.wait()


def prepare(plan, place, column_kernels, row_kernels, weights, w, halo):
    frames, rows, _ = weights.shape
    height = tile_height(frames)
    out = pl.pallas_call(
        functools.partial(prepare_kernel, plan, frames, rows, halo, w),
        out_shape=[
            jax.ShapeDtypeStruct((frames * rows + (height if taps else 0), w), f32)
            for _, taps in plan
        ]
        + [jax.ShapeDtypeStruct((height, w), f32)]
        + matrix_shapes(1, frames, rows, halo),
        in_specs=[SMEM, HBM, HBM, HBM],
        out_specs=[VMEM] * (len(plan) + 5),
        scratch_shapes=[
            pltpu.VMEM(column_kernels.shape, f32),
            pltpu.VMEM(row_kernels.shape, f32),
            pltpu.SemaphoreType.DMA((2,)),
            pltpu.SemaphoreType.DMA((len(plan), frames)),
        ],
        compiler_params=room(24),
        name="prepare",
    )(place, column_kernels, row_kernels, weights)
    return out[: len(plan)], out[len(plan)], out[len(plan) + 1 :]


def blocks_kernel(n, halo, w, place, send_a, mid, send_b, recv_a, recv_b, *refs):
    outs, full = refs[:-1], refs[-1]
    rows, cols = mid.shape
    odd = lax.rem(place[1], 2)
    inner = slice(LANE, LANE + cols)
    for end in (0, LANE + cols):
        full[:, end : end + LANE] = jnp.zeros((rows, LANE), f32)
    full[:halo, inner] = mid[:halo, :] + choose(odd, recv_a[...], recv_b[...])
    full[halo : rows - halo, inner] = mid[halo : rows - halo, :]
    full[rows - halo :, inner] = mid[rows - halo :, :] + choose(odd, recv_b[...], recv_a[...])
    lane = lax.broadcasted_iota(jnp.int32, (rows, LANE), 1)
    for i in range(n):
        start = jnp.bitwise_xor(place[0], i) * w
        outs[i][:rows, :] = full[:, pl.ds(pl.multiple_of(start + LANE, LANE), w)]
        before = full[:, pl.ds(pl.multiple_of(start, LANE), LANE)]
        after = full[:, pl.ds(pl.multiple_of(start + LANE + w, LANE), LANE)]
        outs[i][rows:, :] = pack_edge(jnp.where(lane >= LANE - halo, before, after), halo, w)


def column_blocks(n, place, send_a, mid, send_b, recv_a, recv_b, w):
    rows, cols = mid.shape
    halo = send_a.shape[0]
    height = rows + rows * 2 * halo // w
    return pl.pallas_call(
        functools.partial(blocks_kernel, n, halo, w),
        out_shape=[jax.ShapeDtypeStruct((height, w), f32)] * n,
        in_specs=[SMEM] + [VMEM] * 5,
        out_specs=[VMEM] * n,
        scratch_shapes=[pltpu.VMEM((rows, cols + 2 * LANE), f32)],
        compiler_params=room(16),
        name="column_blocks",
    )(place, send_a, mid, send_b, recv_a, recv_b)


def start_kernel(n, rows, halo, w, place, est, *refs):
    parts = refs[:-5]
    k0, wide, send_a, send_b, stat = refs[-5:]
    total = parts[0][...]
    for p in parts[1:]:
        total = total + p[...]
    me = place[0]
    odd = lax.rem(place[1], 2)
    at = lambda start, size: est[:, pl.ds(pl.multiple_of(start, LANE), size)]
    own = -(total[:rows] + damping * at(me * w, w))
    edge = unpack_edge(total[rows:], halo)
    before = at(jnp.maximum(me * w - LANE, 0), LANE)
    after = at(jnp.minimum(me * w + w, (n * w) - LANE), LANE)
    none = jnp.zeros((rows, LANE), f32)
    left = choose((me > 0).astype(jnp.int32), -(edge + damping * before), none)
    right = choose((me < n - 1).astype(jnp.int32), -(edge + damping * after), none)
    k0[...] = own
    wide[:, :LANE] = left
    wide[:, LANE : LANE + w] = own
    wide[:, LANE + w :] = right
    low, high = wide[:halo, :], wide[rows - halo :, :]
    send_a[...] = choose(odd, low, high)
    send_b[...] = choose(odd, high, low)
    square = own * own
    acc = square[:, :LANE]
    for c in range(LANE, w, LANE):
        acc = acc + square[:, c : c + LANE]
    stat[...] = jnp.sum(acc.reshape(rows // 8, 8, LANE), axis=0)


def start_image(n, place, est, parts, halo):
    rows, cols = est.shape
    w = cols // n
    return pl.pallas_call(
        functools.partial(start_kernel, n, rows, halo, w),
        out_shape=[
            jax.ShapeDtypeStruct((rows, w), f32),
            jax.ShapeDtypeStruct((rows, w + 2 * LANE), f32),
            jax.ShapeDtypeStruct((halo, w + 2 * LANE), f32),
            jax.ShapeDtypeStruct((halo, w + 2 * LANE), f32),
            jax.ShapeDtypeStruct((8, LANE), f32),
        ],
        in_specs=[SMEM] + [VMEM] * (1 + len(parts)),
        out_specs=[VMEM] * 5,
        compiler_params=room(12),
        name="start_image",
    )(place, est, *parts)


def apply_kernel(frames, rows, halo, w, groups, cut, count, pieces, place, *refs):
    image, refs = refs[:pieces], refs[pieces:]
    t_hbm, b_hbm, bp_hbm, ta_hbm, own = refs[:5]
    moved = refs[5 : 5 + count]
    send_a, mid, send_b, stat = refs[5 + count : 9 + count]
    refs = refs[9 + count :]
    if pieces > 1:
        whole, refs = refs[0], refs[1:]
    y_hi, y_lo, us, qs, vs_hi, vs_lo, acc, tb, bb, bpb, tab, wbuf, sem, wsem = refs
    odd = lax.rem(place[1], 2)
    ext = rows + 2 * halo

    def copies(g):
        span = pl.ds(g * frames, frames)
        return [
            pltpu.make_async_copy(t_hbm.at[span], tb.at[g], sem.at[0, g]),
            pltpu.make_async_copy(b_hbm.at[span], bb.at[g], sem.at[1, g]),
            pltpu.make_async_copy(bp_hbm.at[span], bpb.at[g], sem.at[2, g]),
            pltpu.make_async_copy(ta_hbm.at[g], tab.at[g], sem.at[3, g]),
        ]

    mine = pl.ds(pl.multiple_of(place[0] * w, LANE), w)
    for g in range(groups):
        for c in copies(g):
            c.start()
        for f in range(frames):
            span = pl.ds(f * rows, rows)
            if g == 0:
                pltpu.make_async_copy(own.at[f, :, mine], wbuf.at[g, f], wsem.at[g, f]).start()
            elif g < groups - 1:
                pltpu.make_async_copy(moved[g - 1].at[span, :], wbuf.at[g, f], wsem.at[g, f]).start()
            else:
                inside = (place[0] >= groups // 4) & (place[0] < groups - groups // 4)
                for flag, ref in ((inside, moved[-2]), (jnp.logical_not(inside), moved[-1])):

                    @pl.when(flag)
                    def _(ref=ref, span=span, g=g, f=f):
                        pltpu.make_async_copy(ref.at[span, :], wbuf.at[g, f], wsem.at[g, f]).start()
    clear_edges(y_hi, y_lo, qs, ext, rows, w)
    if pieces > 1:
        wide, recv_a, recv_b = image
        whole[:halo, :] = choose(odd, recv_a[...], recv_b[...])
        whole[halo : halo + rows, :] = wide[...]
        whole[halo + rows :, :] = choose(odd, recv_b[...], recv_a[...])
        load_image(y_hi, y_lo, whole[...], halo)
    else:
        load_image(y_hi, y_lo, image[0][...], halo)
    acc[...] = jnp.zeros_like(acc)
    stat[...] = jnp.zeros_like(stat)

    @pl.loop(0, groups)
    def _(g):
        for c in copies(g):
            c.wait()
        for f in range(frames):
            pltpu.make_async_copy(own.at[f, :, mine], wbuf.at[g, f], wsem.at[g, f]).wait()
        group_terms(
            frames, rows, w, y_hi, y_lo,
            lambda f: tb.at[g, f], lambda f: bb.at[g, f], lambda f: bpb.at[g, f], tab.at[g],
            lambda f: wbuf.at[g, f], None,
            us, qs, vs_hi, vs_lo, acc, stat,
        )

    z = unshift(acc[...], halo)
    send_a[...] = choose(odd, z[:cut], z[ext - cut :])
    send_b[...] = choose(odd, z[ext - cut :], z[:cut])
    mid[...] = z[cut : ext - cut]


def apply_terms(place, image, mats, weights, moved, cut, halo):
    frames, rows, _ = weights.shape
    w = image[0].shape[1] - 2 * LANE
    ext = rows + 2 * halo
    t, b, bp, ta = mats
    groups = ta.shape[0]
    wide = w + LANE
    return pl.pallas_call(
        functools.partial(apply_kernel, frames, rows, halo, w, groups, cut, len(moved), len(image)),
        out_shape=[
            jax.ShapeDtypeStruct((cut, wide), f32),
            jax.ShapeDtypeStruct((ext - 2 * cut, wide), f32),
            jax.ShapeDtypeStruct((cut, wide), f32),
            jax.ShapeDtypeStruct((8, LANE), f32),
        ]
        + [jax.ShapeDtypeStruct((ext, w + 2 * LANE), f32)] * (len(image) > 1),
        in_specs=[SMEM] + [VMEM] * len(image) + [ANY] * 4 + [HBM] + [ANY] * len(moved),
        out_specs=[VMEM] * (4 + (len(image) > 1)),
        scratch_shapes=work_scratch(frames, rows, halo, w)
        + [
            pltpu.VMEM((groups, frames) + t.shape[1:], bf16),
            pltpu.VMEM((groups, frames) + b.shape[1:], bf16),
            pltpu.VMEM((groups, frames) + bp.shape[1:], bf16),
            pltpu.VMEM((groups,) + ta.shape[1:], bf16),
            pltpu.VMEM((groups, frames, rows, w), f32),
            pltpu.SemaphoreType.DMA((4, groups)),
            pltpu.SemaphoreType.DMA((groups, frames)),
        ],
        cost_estimate=pl.CostEstimate(
            flops=groups * 3 * 10**9, bytes_accessed=groups * 2**20, transcendentals=0
        ),
        compiler_params=room(28),
    )(place, *image, t, b, bp, ta, weights, *moved)


def rows_kernel(strips, halo, w, place, send_a, mid, send_b, recv_a, recv_b, q, col_a, col_b):
    odd = lax.rem(place[1], 2)
    odd_col = lax.rem(place[0], 2)
    edge_rows, wide = send_a.shape
    ext = q.shape[0]
    row = lax.broadcasted_iota(jnp.int32, (edge_rows, wide), 0)
    strip = jnp.full((edge_rows, wide), place[1], jnp.int32)
    low = choose(odd, send_a[...], send_b[...]) + choose(odd, recv_a[...], recv_b[...])
    high = choose(odd, send_b[...], send_a[...]) + choose(odd, recv_b[...], recv_a[...])
    q[:edge_rows, :] = jnp.where((row >= halo) | (strip > 0), low, 0.0)
    q[edge_rows : ext - edge_rows, :] = mid[...]
    q[ext - edge_rows :, :] = jnp.where((row < edge_rows - halo) | (strip < strips - 1), high, 0.0)
    lane = lax.broadcasted_iota(jnp.int32, (ext, LANE), 1)
    edge = q[:, w:]
    to_left = jnp.where(lane < halo, q[:, :LANE], edge)
    to_right = jnp.where(lane >= LANE - halo, q[:, w - LANE : w], edge)
    col_a[...] = choose(odd_col, to_left, to_right)
    col_b[...] = choose(odd_col, to_right, to_left)


def merge_rows(strips, place, send_a, mid, send_b, recv_a, recv_b, halo):
    ext = mid.shape[0] + 2 * send_a.shape[0]
    wide = mid.shape[1]
    return pl.pallas_call(
        functools.partial(rows_kernel, strips, halo, wide - LANE),
        out_shape=[
            jax.ShapeDtypeStruct((ext, wide), f32),
            jax.ShapeDtypeStruct((ext, LANE), f32),
            jax.ShapeDtypeStruct((ext, LANE), f32),
        ],
        in_specs=[SMEM] + [VMEM] * 5,
        out_specs=[VMEM] * 3,
        compiler_params=room(8),
        name="merge_rows",
    )(place, send_a, mid, send_b, recv_a, recv_b)


def cols_kernel(n, rows, halo, place, q, recv_a, recv_b, before, out, block, stat):
    odd = lax.rem(place[0], 2)
    ext, wide = q.shape
    w = wide - LANE
    lane = lax.broadcasted_iota(jnp.int32, (ext, LANE), 1)
    at = jnp.full((ext, LANE), place[0], jnp.int32)
    left = choose(odd, recv_a[...], recv_b[...])
    right = choose(odd, recv_b[...], recv_a[...])
    edge = q[:, w:]
    total = None
    out[:, :LANE] = jnp.where(at > 0, edge + left, 0.0) + damping * before[:, :LANE]
    out[:, LANE + w :] = jnp.where(at < n - 1, edge + right, 0.0) + damping * before[:, LANE + w :]
    for c in range(0, w, LANE):
        x = q[:, c : c + LANE] + damping * before[:, c + LANE : c + 2 * LANE]
        if c == 0:
            x = x + jnp.where(lane < halo, left, 0.0)
        if c == w - LANE:
            x = x + jnp.where(lane >= LANE - halo, right, 0.0)
        out[:, c + LANE : c + 2 * LANE] = x
        own = x[halo : halo + rows]
        block[:, c : c + LANE] = own
        part = jnp.sum((own * own).reshape(rows // 8, 8, LANE), axis=0)
        total = part if total is None else total + part
    stat[...] = total


def merge_cols(n, rows, place, q, recv_a, recv_b, before, halo):
    ext, wide = q.shape
    w = wide - LANE
    return pl.pallas_call(
        functools.partial(cols_kernel, n, rows, halo),
        out_shape=[
            jax.ShapeDtypeStruct((ext, w + 2 * LANE), f32),
            jax.ShapeDtypeStruct((rows, w), f32),
            jax.ShapeDtypeStruct((8, LANE), f32),
        ],
        in_specs=[SMEM] + [VMEM] * 4,
        out_specs=[VMEM] * 3,
        compiler_params=room(10),
        name="merge_cols",
    )(place, q, recv_a, recv_b, before)


def wrap_kernel(rows, halo, w, place, send_a, mid, send_b, recv_a, recv_b, before, out):
    odd = lax.rem(place[1], 2)
    keep = rows - 2 * halo
    pieces = (
        (0, halo, mid[:halo, :] + choose(odd, recv_a[...], recv_b[...])),
        (halo, keep, mid[halo : rows - halo, :]),
        (rows - halo, halo, mid[rows - halo :, :] + choose(odd, recv_b[...], recv_a[...])),
    )
    edges = []
    for start, size, value in pieces:
        span = slice(start, start + size)
        out[span, :] = value[:, :w] + damping * before[span, :]
        edges.append(value[:, w:])
    out[rows:, :] = pack_edge(jnp.concatenate(edges, axis=0), halo, w)


def wrap(place, send_a, mid, send_b, recv_a, recv_b, before, halo):
    rows, w = before.shape
    height = rows + rows * 2 * halo // w
    return pl.pallas_call(
        functools.partial(wrap_kernel, rows, halo, w),
        out_shape=jax.ShapeDtypeStruct((height, w), f32),
        in_specs=[SMEM] + [VMEM] * 6,
        out_specs=VMEM,
        compiler_params=room(8),
        name="wrap",
    )(place, send_a, mid, send_b, recv_a, recv_b, before)


def solution_kernel(n, w, place, est, sums, *refs):
    k0, k1 = refs[:n], refs[n : 2 * n]
    sol, res, coef = refs[2 * n :]
    total = [
        jnp.sum(jnp.sum(sums[i], axis=0, keepdims=True), axis=1, keepdims=True) for i in range(4)
    ]
    k00, k11 = total[0], total[2]
    k01 = total[1] + damping * k00
    k12 = total[3] + damping * k11
    alpha0 = k00 / k01
    norm1 = k00 - 2.0 * alpha0 * k01 + alpha0 * alpha0 * k11
    beta = norm1 / k00
    curve1 = (1.0 + beta) * (1.0 + beta) * k01 - 2.0 * (1.0 + beta) * alpha0 * k11
    curve1 = curve1 + alpha0 * alpha0 * k12
    alpha1 = norm1 / curve1
    c1 = alpha0 + alpha1 * (1.0 + beta)
    c2 = alpha0 * alpha1
    coef[...] = jnp.broadcast_to(c2, coef.shape)
    for i in range(n):
        cols = pl.ds(pl.multiple_of(jnp.bitwise_xor(place[0], i) * w, LANE), w)
        a0, a1 = k0[i][...], k1[i][...]
        sol[:, cols] = est[:, cols] + c1 * a0 - c2 * a1
        res[:, cols] = a0 - c1 * a1


def solution_image(place, est, sums, k0, k1):
    n = len(k0)
    w = k0[0].shape[1]
    return pl.pallas_call(
        functools.partial(solution_kernel, n, w),
        out_shape=[jax.ShapeDtypeStruct(est.shape, f32)] * 2
        + [jax.ShapeDtypeStruct((8, LANE), f32)],
        in_specs=[SMEM] + [VMEM] * (2 + 2 * n),
        out_specs=[VMEM] * 3,
        compiler_params=room(20),
        name="solution_image",
    )(place, est, sums, *k0, *k1)


def residual_kernel(n, rows, halo, w, place, base, coef, *refs):
    k2, (res, full) = refs[:n], refs[n:]
    c2 = coef[0:1, 0:1]
    lane = lax.broadcasted_iota(jnp.int32, (rows, LANE), 1)
    spot = [jnp.bitwise_xor(place[0], i) for i in range(n)]
    full[:, :LANE] = jnp.zeros((rows, LANE), f32)
    full[:, LANE + n * w :] = jnp.zeros((rows, LANE), f32)
    for i in range(n):
        full[:, pl.ds(pl.multiple_of(spot[i] * w + LANE, LANE), w)] = k2[i][:rows, :]
    for i in range(n):
        edge = unpack_edge(k2[i][rows:, :], halo)
        left = pl.ds(pl.multiple_of(spot[i] * w, LANE), LANE)
        right = pl.ds(pl.multiple_of(spot[i] * w + w + LANE, LANE), LANE)
        full[:, left] += jnp.where(lane >= LANE - halo, edge, 0.0)
        full[:, right] += jnp.where(lane < halo, edge, 0.0)
    for c in range(0, n * w, LANE):
        res[:, c : c + LANE] = base[:, c : c + LANE] + c2 * full[:, c + LANE : c + 2 * LANE]


def residual_image(place, base, coef, k2, halo):
    n = len(k2)
    rows, cols = base.shape
    w = cols // n
    return pl.pallas_call(
        functools.partial(residual_kernel, n, rows, halo, w),
        out_shape=jax.ShapeDtypeStruct(base.shape, f32),
        in_specs=[SMEM] + [VMEM] * (2 + n),
        out_specs=VMEM,
        scratch_shapes=[pltpu.VMEM((rows, cols + 2 * LANE), f32)],
        compiler_params=room(16),
        name="residual_image",
    )(place, base, coef, *k2)


def neighbours(send_a, send_b, axis):
    n = lax.axis_size(axis)
    out = []
    for lead, x in ((0, send_a), (1, send_b)):
        pairs = [(i, i + 1) for i in range(lead, n - 1, 2)]
        out.append(lax.ppermute(x, axis, pairs + [(b, a) for a, b in pairs]))
    return out


def swap(x, axis, distance):
    n = lax.axis_size(axis)
    return lax.ppermute(x, axis, [(i, i ^ distance) for i in range(n)])


def steps(estimate, observed, weights, column_kernels, row_kernels):
    n = lax.axis_size("frame")
    me = lax.axis_index("frame")
    strips = lax.axis_size("strip")
    strip = lax.axis_index("strip")
    place = jnp.stack([me, strip]).astype(jnp.int32)
    rows, cols = estimate.shape
    frames = weights.shape[0]
    halo = column_kernels.shape[1] // 2
    stay = lambda x: pltpu.with_memory_space_constraint(x, pltpu.HBM)
    weights, observed = stay(weights), stay(observed)
    column_kernels, row_kernels = stay(column_kernels), stay(row_kernels)
    w = cols // n
    distances = [1 << k for k in range(n.bit_length() - 1)]

    low, high = estimate[:halo], estimate[rows - halo :]
    odd = strip % 2 == 1
    est_a, est_b = neighbours(
        jnp.where(odd, low, high), jnp.where(odd, high, low), "strip"
    )

    plan = [(d, True) for d in range(1, n - 1)] + [(n - 1, False)]
    packed, tile, own_mats = prepare(plan, place, column_kernels, row_kernels, weights, w, halo)
    far_tile = swap(tile[:, : 2 * LANE], "frame", n - 1)
    moved = []
    for i in range(n - 2):
        moved.append(swap(packed[i], "frame", i + 1))
    middle = range(n // 4, n - n // 4)
    for members in (middle, [i for i in range(n) if i not in middle]):
        moved.append(lax.ppermute(packed[-1], "frame", [(i, n - 1 - i) for i in members]))
    starts = [0] + [frames * rows] * (n - 2) + [0]

    send_a, mid, send_b = first_terms(
        place, estimate, est_a, est_b, own_mats, weights, observed
    )
    mats = setup_matrices([tile] + moved[: n - 2] + [far_tile], starts, frames, rows, halo)
    recv_a, recv_b = neighbours(send_a, send_b, "strip")

    part = list(column_blocks(n, place, send_a, mid, send_b, recv_a, recv_b, w))
    mine = [part[0]]
    for i in range(n - 1, 0, -1):
        d = i & -i
        got = swap(part[i], "frame", d)
        if i == d:
            mine.append(got)
        else:
            part[i ^ d] = part[i ^ d] + got
    k0, wide, send_a, send_b, k00_part = start_image(n, place, estimate, mine, halo)
    recv_a, recv_b = neighbours(send_a, send_b, "strip")

    send_a, mid, send_b, stat1, k0x = apply_terms(
        place, (wide, recv_a, recv_b), mats, weights, moved, 2 * halo, halo
    )
    recv_a, recv_b = neighbours(send_a, send_b, "strip")
    q, col_a, col_b = merge_rows(strips, place, send_a, mid, send_b, recv_a, recv_b, halo)
    recv_a, recv_b = neighbours(col_a, col_b, "frame")
    k1x, k1, k11_part = merge_cols(n, rows, place, q, recv_a, recv_b, k0x, halo)

    send_a, mid, send_b, stat2 = apply_terms(place, (k1x,), mats, weights, moved, halo, halo)
    recv_a, recv_b = neighbours(send_a, send_b, "strip")
    sums = jnp.stack([k00_part, stat1, k11_part, stat2])
    for axis, size in (("frame", n), ("strip", strips)):
        d = 1
        while d < size:
            sums = sums + swap(sums, axis, d)
            d *= 2
    k2 = wrap(place, send_a, mid, send_b, recv_a, recv_b, k1, halo)

    def gathered(x):
        parts = [x]
        for d in range(1, n):
            parts.append(swap(x, "frame", d))
        return parts

    def gathered_tree(x):
        parts = [x] + [None] * (n - 1)
        for i in range(n):
            for d in reversed(distances):
                if i % (2 * d) == 0:
                    parts[i + d] = swap(parts[i], "frame", d)
        return parts

    g0, g1, g2 = gathered(k0), gathered(k1), gathered_tree(k2)
    result, base, coef = solution_image(place, estimate, sums, g0, g1)
    return result, residual_image(place, base, coef, g2, halo)


def solution(mesh):
    return jax.shard_map(
        steps,
        mesh=mesh,
        in_specs=(
            P("strip", None),
            P("frame", "strip", None),
            P("frame", "strip", None),
            P("frame", None),
            P("frame", None),
        ),
        out_specs=(P("strip", None), P("strip", None)),
        check_vma=False,
    )
```

```python
import functools

import jax
import jax.numpy as jnp
from jax import lax
from jax.experimental import pallas as pl
from jax.experimental.pallas import tpu as pltpu
from jax.sharding import PartitionSpec as P


damping = 0.05
f32 = jnp.float32
bf16 = jnp.bfloat16
LANE = 128
VMEM = pl.BlockSpec(memory_space=pltpu.VMEM)
ANY = pl.BlockSpec(memory_space=pl.ANY)
SMEM = pl.BlockSpec(memory_space=pltpu.SMEM)
HBM = pl.BlockSpec(memory_space=pltpu.HBM)


def room(mib):
    return pltpu.CompilerParams(vmem_limit_bytes=mib * 2**20)


def split(x):
    hi = x.astype(bf16)
    lo = (x - hi.astype(f32)).astype(bf16)
    return hi, lo


def dot(a, b):
    return jnp.dot(a, b, preferred_element_type=f32)


def choose(flag, a, b):
    return jnp.where(jnp.full(a.shape, flag, jnp.int32) == 1, a, b)


def pack_edge(edge, halo, w):
    rows = edge.shape[0]
    per = LANE // (2 * halo)
    short = rows * 2 * halo // w
    edge = pltpu.roll(edge, halo, 1)
    lane = lax.broadcasted_iota(jnp.int32, (short, LANE), 1)
    out = []
    for t in range(w // LANE):
        tile = None
        for p in range(per):
            k = t * per + p
            part = edge[k * short : (k + 1) * short]
            part = pltpu.roll(part, p * 2 * halo, 1) if p else part
            tile = part if tile is None else jnp.where(lane >= p * 2 * halo, part, tile)
        out.append(tile)
    return jnp.concatenate(out, axis=1)


def unpack_edge(packed, halo):
    _, w = packed.shape
    per = LANE // (2 * halo)
    parts = []
    for k in range(w // (2 * halo)):
        t, p = divmod(k, per)
        part = packed[:, t * LANE : (t + 1) * LANE]
        back = (LANE - halo - p * 2 * halo) % LANE
        parts.append(pltpu.roll(part, back, 1) if back else part)
    return jnp.concatenate(parts, axis=0)


def tiles(width, step=256):
    return [(s, min(step, width - s)) for s in range(0, width, step)]


def toeplitz(base, count):
    wide = base.shape[1]
    return pltpu.roll(jnp.broadcast_to(base, (count, wide)), 0, 1, stride=1, stride_axis=0)


def build_group(taps, g, frames, rows, halo, t_ref, b_ref, bp_ref, ta_ref):
    ext = rows + 2 * halo
    unit = taps / jnp.sum(taps, axis=1, keepdims=True)
    for s in range(frames):
        f = g * frames + s
        col = unit[s : s + 1]
        row = unit[frames + s : frames + s + 1]
        by_rows = toeplitz(row, rows)
        hi, lo = split(by_rows)
        t_ref[f, :rows, :] = hi
        t_ref[f, rows:, :] = lo
        hi, lo = split(by_rows.T[:ext])
        ta_ref[g, :ext, s * rows : (s + 1) * rows] = hi
        ta_ref[g, ext:, s * rows : (s + 1) * rows] = lo
        hi, lo = split(toeplitz(col, LANE).T)
        b_ref[f, :, :LANE] = hi
        b_ref[f, :, LANE:] = lo
        hi, lo = split(toeplitz(pltpu.roll(col, LANE, 1), 2 * LANE)[:, :LANE])
        bp_ref[f, :, :LANE] = hi
        bp_ref[f, :, LANE:] = lo


def matrix_shapes(groups, frames, rows, halo):
    ext = rows + 2 * halo
    return [
        jax.ShapeDtypeStruct(s, bf16)
        for s in (
            (groups * frames, 2 * rows, 2 * LANE),
            (groups * frames, 2 * LANE, 2 * LANE),
            (groups * frames, 2 * LANE, 2 * LANE),
            (groups, 2 * ext, frames * rows),
        )
    ]


def tile_height(frames):
    return -(-2 * frames // 8) * 8


def setup_kernel(frames, rows, halo, starts, *refs):
    tiles_in = refs[: len(starts)]
    mats, taps, sem = refs[len(starts) : -2], refs[-2], refs[-1]
    height = tile_height(frames)

    def copy(g):
        source = tiles_in[g].at[pl.ds(starts[g], height), pl.ds(0, 2 * LANE)]
        return pltpu.make_async_copy(source, taps.at[g], sem.at[g])

    for g in range(len(starts)):
        copy(g).start()
    for g in range(len(starts)):
        copy(g).wait()
        build_group(taps[g], g, frames, rows, halo, *mats)


def setup_matrices(tiles_in, starts, frames, rows, halo):
    groups = len(tiles_in)
    return pl.pallas_call(
        functools.partial(setup_kernel, frames, rows, halo, starts),
        out_shape=matrix_shapes(groups, frames, rows, halo),
        in_specs=[ANY] * groups,
        out_specs=[VMEM] * 4,
        scratch_shapes=[
            pltpu.VMEM((groups, tile_height(frames), 2 * LANE), f32),
            pltpu.SemaphoreType.DMA((groups,)),
        ],
        compiler_params=room(24),
        name="setup_all",
    )(*tiles_in)


def load_image(y_hi, y_lo, image, halo):
    ext, full = image.shape
    shift = LANE - halo
    y = pltpu.roll(image, full - shift, 1)[:, : full - LANE]
    hi, lo = split(y)
    y_hi[:ext, :] = hi
    y_lo[:ext, :] = lo


def group_terms(frames, rows, w, y_hi, y_lo, t, b, bp, ta, weight, data, us, qs, vs_hi, vs_lo, acc, stat, ready=None):
    total = None
    for f in range(frames):
        for c, size in tiles(w + LANE):
            r1 = dot(t(f)[...], y_hi[:, c : c + size])
            r2 = dot(t(f)[:rows, :], y_lo[:, c : c + size])
            hi, lo = split(r1[:rows] + r1[rows:] + r2)
            us[:rows, c : c + size] = hi
            us[rows:, c : c + size] = lo
        if ready is not None:
            ready(f)
        for k in range(w // LANE):
            c = k * LANE
            r = dot(us[:, c : c + 2 * LANE], b(f)[...])
            a = r[:rows, :LANE] + r[:rows, LANE:] + r[rows:, :LANE]
            if data is not None:
                a = a - data(f)[:, c : c + LANE]
            q = weight(f)[:, c : c + LANE] * a
            if stat is not None:
                part = jnp.sum((a * q).reshape(rows // 8, 8, LANE), axis=0)
                total = part if total is None else total + part
            hi, lo = split(q)
            qs[:rows, c + LANE : c + 2 * LANE] = hi
            qs[rows:, c + LANE : c + 2 * LANE] = lo
        for k in range(w // LANE + 1):
            c = k * LANE
            r = dot(qs[:, c : c + 2 * LANE], bp(f)[...])
            hi, lo = split(r[:rows, :LANE] + r[:rows, LANE:] + r[rows:, :LANE])
            vs_hi[f * rows : (f + 1) * rows, c : c + LANE] = hi
            vs_lo[f * rows : (f + 1) * rows, c : c + LANE] = lo
    ext = acc.shape[0]
    for c, size in tiles(w + LANE):
        r1 = dot(ta[...], vs_hi[:, c : c + size])
        r2 = dot(ta[:ext, :], vs_lo[:, c : c + size])
        acc[:, c : c + size] += r1[:ext] + r1[ext:] + r2
    if stat is not None:
        stat[...] += total


def work_scratch(frames, rows, halo, w):
    ext = rows + 2 * halo
    return [
        pltpu.VMEM((2 * LANE, w + LANE), bf16),
        pltpu.VMEM((2 * LANE, w + LANE), bf16),
        pltpu.VMEM((2 * rows, w + LANE), bf16),
        pltpu.VMEM((2 * rows, w + 2 * LANE), bf16),
        pltpu.VMEM((frames * rows, w + LANE), bf16),
        pltpu.VMEM((frames * rows, w + LANE), bf16),
        pltpu.VMEM((ext, w + LANE), f32),
    ]


def clear_edges(y_hi, y_lo, qs, ext, rows, w):
    zero = jnp.zeros((y_hi.shape[0] - ext, y_hi.shape[1]), bf16)
    y_hi[ext:, :] = zero
    y_lo[ext:, :] = zero
    qs[:, :LANE] = jnp.zeros((2 * rows, LANE), bf16)
    qs[:, w + LANE :] = jnp.zeros((2 * rows, LANE), bf16)


def unshift(acc, halo):
    return pltpu.roll(acc, acc.shape[1] - halo, 1)


def first_kernel(
    frames, rows, halo,
    place, est, recv_a, recv_b, t_ref, b_ref, bp_ref, ta_ref, w_hbm, d_hbm,
    send_a, mid, send_b,
    y_hi, y_lo, us, qs, vs_hi, vs_lo, acc, wbuf, dbuf, sem,
):
    ext = rows + 2 * halo
    cols = est.shape[1]
    copies = [
        (
            pltpu.make_async_copy(w_hbm.at[f], wbuf.at[f], sem.at[0, f]),
            pltpu.make_async_copy(d_hbm.at[f], dbuf.at[f], sem.at[1, f]),
        )
        for f in range(frames)
    ]
    for pair in copies:
        for c in pair:
            c.start()
    clear_edges(y_hi, y_lo, qs, ext, rows, cols)
    odd = lax.rem(place[1], 2)
    none = jnp.zeros((ext, LANE), f32)
    for start in range(0, cols, 4 * LANE):
        size = 4 * LANE + LANE
        left = max(start - LANE, 0)
        span = slice(left, min(start + 4 * LANE, cols))
        x = jnp.concatenate(
            [
                choose(odd, recv_a[:, span], recv_b[:, span]),
                est[:, span],
                choose(odd, recv_b[:, span], recv_a[:, span]),
            ],
            axis=0,
        )
        if start == 0:
            x = jnp.concatenate([none, x], axis=1)
        if x.shape[1] < size:
            x = jnp.concatenate([x, jnp.zeros((ext, size - x.shape[1]), f32)], axis=1)
        hi, lo = split(pltpu.roll(x, halo, 1)[:, LANE:])
        y_hi[:ext, start : start + 4 * LANE] = hi
        y_lo[:ext, start : start + 4 * LANE] = lo
        if start + 4 * LANE >= cols:
            tail = jnp.concatenate([x[:, 4 * LANE :], none], axis=1)
            hi, lo = split(pltpu.roll(tail, halo, 1)[:, LANE:])
            y_hi[:ext, cols:] = hi
            y_lo[:ext, cols:] = lo
    acc[...] = jnp.zeros_like(acc)

    def ready(f):
        for c in copies[f]:
            c.wait()

    group_terms(
        frames, rows, cols, y_hi, y_lo,
        lambda f: t_ref.at[f], lambda f: b_ref.at[f], lambda f: bp_ref.at[f], ta_ref.at[0],
        lambda f: wbuf.at[f], lambda f: dbuf.at[f],
        us, qs, vs_hi, vs_lo, acc, None, ready,
    )
    for start in range(0, cols, 4 * LANE):
        size = min(4 * LANE, cols - start)
        z = pltpu.roll(acc[:, start : start + size + LANE], size + LANE - halo, 1)[:, :size]
        span = slice(start, start + size)
        low, high = z[:halo], z[halo + rows :]
        send_a[:, span] = choose(odd, low, high)
        send_b[:, span] = choose(odd, high, low)
        mid[:, span] = z[halo : halo + rows]


def first_terms(place, est, recv_a, recv_b, mats, weights, observed):
    frames, rows, cols = weights.shape
    halo = recv_a.shape[0]
    return pl.pallas_call(
        functools.partial(first_kernel, frames, rows, halo),
        out_shape=[
            jax.ShapeDtypeStruct((halo, cols), f32),
            jax.ShapeDtypeStruct((rows, cols), f32),
            jax.ShapeDtypeStruct((halo, cols), f32),
        ],
        in_specs=[SMEM] + [VMEM] * 7 + [HBM, HBM],
        out_specs=[VMEM] * 3,
        scratch_shapes=work_scratch(frames, rows, halo, cols)
        + [
            pltpu.VMEM((frames, rows, cols), f32),
            pltpu.VMEM((frames, rows, cols), f32),
            pltpu.SemaphoreType.DMA((2, frames)),
        ],
        cost_estimate=pl.CostEstimate(flops=8 * 10**9, bytes_accessed=8 * 2**20, transcendentals=0),
        compiler_params=room(36),
        name="first_terms",
    )(place, est, recv_a, recv_b, *mats, weights, observed)


def prepare_kernel(plan, frames, rows, halo, w, place, cols_in, rows_in, weights, *refs):
    outs, tile, mats = refs[: len(plan)], refs[len(plan)], refs[len(plan) + 1 : -4]
    cols_buf, rows_buf, taps_sem, sem = refs[-4:]
    taps = cols_in.shape[1]
    taps_copies = (
        pltpu.make_async_copy(cols_in, cols_buf, taps_sem.at[0]),
        pltpu.make_async_copy(rows_in, rows_buf, taps_sem.at[1]),
    )
    for copy in taps_copies:
        copy.start()
    pending = []
    for i, (distance, _) in enumerate(plan):
        start = pl.multiple_of(jnp.bitwise_xor(place[0], distance) * w, LANE)
        for k in range(frames):
            copy = pltpu.make_async_copy(
                weights.at[k, :, pl.ds(start, w)],
                outs[i].at[pl.ds(k * rows, rows), :],
                sem.at[i, k],
            )
            copy.start()
            pending.append(copy)
    tile[...] = jnp.zeros_like(tile)
    for copy in taps_copies:
        copy.wait()
    tile[:frames, :taps] = cols_buf[...]
    tile[frames : 2 * frames, :taps] = rows_buf[...]
    for i, (_, with_taps) in enumerate(plan):
        if with_taps:
            outs[i][frames * rows :, :] = tile[...]
    build_group(tile[:, : 2 * LANE], 0, frames, rows, halo, *mats)
    for copy in pending:
        copy.wait()


def prepare(plan, place, column_kernels, row_kernels, weights, w, halo):
    frames, rows, _ = weights.shape
    height = tile_height(frames)
    out = pl.pallas_call(
        functools.partial(prepare_kernel, plan, frames, rows, halo, w),
        out_shape=[
            jax.ShapeDtypeStruct((frames * rows + (height if taps else 0), w), f32)
            for _, taps in plan
        ]
        + [jax.ShapeDtypeStruct((height, w), f32)]
        + matrix_shapes(1, frames, rows, halo),
        in_specs=[SMEM, HBM, HBM, HBM],
        out_specs=[VMEM] * (len(plan) + 5),
        scratch_shapes=[
            pltpu.VMEM(column_kernels.shape, f32),
            pltpu.VMEM(row_kernels.shape, f32),
            pltpu.SemaphoreType.DMA((2,)),
            pltpu.SemaphoreType.DMA((len(plan), frames)),
        ],
        compiler_params=room(24),
        name="prepare",
    )(place, column_kernels, row_kernels, weights)
    return out[: len(plan)], out[len(plan)], out[len(plan) + 1 :]


def blocks_kernel(n, halo, w, place, send_a, mid, send_b, recv_a, recv_b, *refs):
    outs, full = refs[:-1], refs[-1]
    rows, cols = mid.shape
    odd = lax.rem(place[1], 2)
    inner = slice(LANE, LANE + cols)
    for end in (0, LANE + cols):
        full[:, end : end + LANE] = jnp.zeros((rows, LANE), f32)
    full[:halo, inner] = mid[:halo, :] + choose(odd, recv_a[...], recv_b[...])
    full[halo : rows - halo, inner] = mid[halo : rows - halo, :]
    full[rows - halo :, inner] = mid[rows - halo :, :] + choose(odd, recv_b[...], recv_a[...])
    lane = lax.broadcasted_iota(jnp.int32, (rows, LANE), 1)
    for i in range(n):
        start = jnp.bitwise_xor(place[0], i) * w
        outs[i][:rows, :] = full[:, pl.ds(pl.multiple_of(start + LANE, LANE), w)]
        before = full[:, pl.ds(pl.multiple_of(start, LANE), LANE)]
        after = full[:, pl.ds(pl.multiple_of(start + LANE + w, LANE), LANE)]
        outs[i][rows:, :] = pack_edge(jnp.where(lane >= LANE - halo, before, after), halo, w)


def column_blocks(n, place, send_a, mid, send_b, recv_a, recv_b, w):
    rows, cols = mid.shape
    halo = send_a.shape[0]
    height = rows + rows * 2 * halo // w
    return pl.pallas_call(
        functools.partial(blocks_kernel, n, halo, w),
        out_shape=[jax.ShapeDtypeStruct((height, w), f32)] * n,
        in_specs=[SMEM] + [VMEM] * 5,
        out_specs=[VMEM] * n,
        scratch_shapes=[pltpu.VMEM((rows, cols + 2 * LANE), f32)],
        compiler_params=room(16),
        name="column_blocks",
    )(place, send_a, mid, send_b, recv_a, recv_b)


def start_kernel(n, rows, halo, w, place, est, *refs):
    parts = refs[:-5]
    k0, wide, send_a, send_b, stat = refs[-5:]
    total = parts[0][...]
    for p in parts[1:]:
        total = total + p[...]
    me = place[0]
    odd = lax.rem(place[1], 2)
    at = lambda start, size: est[:, pl.ds(pl.multiple_of(start, LANE), size)]
    own = -(total[:rows] + damping * at(me * w, w))
    edge = unpack_edge(total[rows:], halo)
    before = at(jnp.maximum(me * w - LANE, 0), LANE)
    after = at(jnp.minimum(me * w + w, (n * w) - LANE), LANE)
    none = jnp.zeros((rows, LANE), f32)
    left = choose((me > 0).astype(jnp.int32), -(edge + damping * before), none)
    right = choose((me < n - 1).astype(jnp.int32), -(edge + damping * after), none)
    k0[...] = own
    wide[:, :LANE] = left
    wide[:, LANE : LANE + w] = own
    wide[:, LANE + w :] = right
    low, high = wide[:halo, :], wide[rows - halo :, :]
    send_a[...] = choose(odd, low, high)
    send_b[...] = choose(odd, high, low)
    square = own * own
    acc = square[:, :LANE]
    for c in range(LANE, w, LANE):
        acc = acc + square[:, c : c + LANE]
    stat[...] = jnp.sum(acc.reshape(rows // 8, 8, LANE), axis=0)


def start_image(n, place, est, parts, halo):
    rows, cols = est.shape
    w = cols // n
    return pl.pallas_call(
        functools.partial(start_kernel, n, rows, halo, w),
        out_shape=[
            jax.ShapeDtypeStruct((rows, w), f32),
            jax.ShapeDtypeStruct((rows, w + 2 * LANE), f32),
            jax.ShapeDtypeStruct((halo, w + 2 * LANE), f32),
            jax.ShapeDtypeStruct((halo, w + 2 * LANE), f32),
            jax.ShapeDtypeStruct((8, LANE), f32),
        ],
        in_specs=[SMEM] + [VMEM] * (1 + len(parts)),
        out_specs=[VMEM] * 5,
        compiler_params=room(12),
        name="start_image",
    )(place, est, *parts)


def apply_kernel(n, frames, rows, halo, w, slots, cut, count, pieces, carried, place, *refs):
    image, refs = refs[:pieces], refs[pieces:]
    t_hbm, b_hbm, bp_hbm, ta_hbm, own = refs[:5]
    moved, refs = refs[5 : 5 + count], refs[5 + count :]
    if carried:
        (acc_in, stat_in), refs = refs[:2], refs[2:]
    if cut is None:
        (acc_out, stat), refs = refs[:2], refs[2:]
    else:
        (send_a, mid, send_b, stat), refs = refs[:4], refs[4:]
    if pieces > 1:
        whole, refs = refs[0], refs[1:]
    y_hi, y_lo, us, qs, vs_hi, vs_lo, acc, tb, bb, bpb, tab, wbuf, sem, wsem = refs
    odd = lax.rem(place[1], 2)
    ext = rows + 2 * halo
    quarter = n // 4
    inner = ((place[0] >= quarter) & (place[0] < n - quarter)).astype(jnp.int32)

    def copies(i, g):
        span = pl.ds(g * frames, frames)
        return [
            pltpu.make_async_copy(t_hbm.at[span], tb.at[i], sem.at[0, i]),
            pltpu.make_async_copy(b_hbm.at[span], bb.at[i], sem.at[1, i]),
            pltpu.make_async_copy(bp_hbm.at[span], bpb.at[i], sem.at[2, i]),
            pltpu.make_async_copy(ta_hbm.at[g], tab.at[i], sem.at[3, i]),
        ]

    mine = pl.ds(pl.multiple_of(place[0] * w, LANE), w)
    for i, (distance, late, sources) in enumerate(slots):
        if len(sources) == 2:
            group = distance + (1 - inner if late else inner) * quarter
        else:
            group = distance
        for c in copies(i, group):
            c.start()
        for f in range(frames):
            span = pl.ds(f * rows, rows)
            if not sources:
                pltpu.make_async_copy(own.at[f, :, mine], wbuf.at[i, f], wsem.at[i, f]).start()
            elif len(sources) == 1:
                source = moved[sources[0]].at[span, :]
                pltpu.make_async_copy(source, wbuf.at[i, f], wsem.at[i, f]).start()
            else:
                for k in range(2):

                    @pl.when((group - distance) == k * quarter)
                    def _(source=moved[sources[k]].at[span, :], i=i, f=f):
                        pltpu.make_async_copy(source, wbuf.at[i, f], wsem.at[i, f]).start()

    clear_edges(y_hi, y_lo, qs, ext, rows, w)
    if pieces > 1:
        wide, recv_a, recv_b = image
        whole[:halo, :] = choose(odd, recv_a[...], recv_b[...])
        whole[halo : halo + rows, :] = wide[...]
        whole[halo + rows :, :] = choose(odd, recv_b[...], recv_a[...])
        load_image(y_hi, y_lo, whole[...], halo)
    else:
        load_image(y_hi, y_lo, image[0][...], halo)
    acc[...] = acc_in[...] if carried else jnp.zeros_like(acc)
    stat[...] = stat_in[...] if carried else jnp.zeros_like(stat)

    @pl.loop(0, len(slots))
    def _(i):
        for c in copies(i, 0):
            c.wait()
        for f in range(frames):
            pltpu.make_async_copy(own.at[f, :, mine], wbuf.at[i, f], wsem.at[i, f]).wait()
        group_terms(
            frames, rows, w, y_hi, y_lo,
            lambda f: tb.at[i, f], lambda f: bb.at[i, f], lambda f: bpb.at[i, f], tab.at[i],
            lambda f: wbuf.at[i, f], None,
            us, qs, vs_hi, vs_lo, acc, stat,
        )

    if cut is None:
        acc_out[...] = acc[...]
    else:
        z = unshift(acc[...], halo)
        send_a[...] = choose(odd, z[:cut], z[ext - cut :])
        send_b[...] = choose(odd, z[ext - cut :], z[:cut])
        mid[...] = z[cut : ext - cut]


def apply_terms(n, place, image, mats, weights, moved, slots, cut, halo, carry=()):
    frames, rows, _ = weights.shape
    w = image[0].shape[1] - 2 * LANE
    ext = rows + 2 * halo
    t, b, bp, ta = mats
    count = len(slots)
    wide = w + LANE
    shapes = [(ext, wide)] if cut is None else [(cut, wide), (ext - 2 * cut, wide), (cut, wide)]
    shapes += [(8, LANE)] + [(ext, w + 2 * LANE)] * (len(image) > 1)
    return pl.pallas_call(
        functools.partial(
            apply_kernel, n, frames, rows, halo, w, slots, cut, len(moved), len(image), bool(carry)
        ),
        out_shape=[jax.ShapeDtypeStruct(s, f32) for s in shapes],
        in_specs=[SMEM]
        + [VMEM] * len(image)
        + [ANY] * 4
        + [HBM]
        + [ANY] * len(moved)
        + [VMEM] * len(carry),
        out_specs=[VMEM] * len(shapes),
        scratch_shapes=work_scratch(frames, rows, halo, w)
        + [
            pltpu.VMEM((count, frames) + t.shape[1:], bf16),
            pltpu.VMEM((count, frames) + b.shape[1:], bf16),
            pltpu.VMEM((count, frames) + bp.shape[1:], bf16),
            pltpu.VMEM((count,) + ta.shape[1:], bf16),
            pltpu.VMEM((count, frames, rows, w), f32),
            pltpu.SemaphoreType.DMA((4, count)),
            pltpu.SemaphoreType.DMA((count, frames)),
        ],
        cost_estimate=pl.CostEstimate(
            flops=count * 3 * 10**9, bytes_accessed=count * 2**20, transcendentals=0
        ),
        compiler_params=room(28),
    )(place, *image, t, b, bp, ta, weights, *moved, *carry)


def rows_kernel(strips, halo, w, place, send_a, mid, send_b, recv_a, recv_b, q, col_a, col_b):
    odd = lax.rem(place[1], 2)
    odd_col = lax.rem(place[0], 2)
    edge_rows, wide = send_a.shape
    ext = q.shape[0]
    row = lax.broadcasted_iota(jnp.int32, (edge_rows, wide), 0)
    strip = jnp.full((edge_rows, wide), place[1], jnp.int32)
    low = choose(odd, send_a[...], send_b[...]) + choose(odd, recv_a[...], recv_b[...])
    high = choose(odd, send_b[...], send_a[...]) + choose(odd, recv_b[...], recv_a[...])
    q[:edge_rows, :] = jnp.where((row >= halo) | (strip > 0), low, 0.0)
    q[edge_rows : ext - edge_rows, :] = mid[...]
    q[ext - edge_rows :, :] = jnp.where((row < edge_rows - halo) | (strip < strips - 1), high, 0.0)
    lane = lax.broadcasted_iota(jnp.int32, (ext, LANE), 1)
    edge = q[:, w:]
    to_left = jnp.where(lane < halo, q[:, :LANE], edge)
    to_right = jnp.where(lane >= LANE - halo, q[:, w - LANE : w], edge)
    col_a[...] = choose(odd_col, to_left, to_right)
    col_b[...] = choose(odd_col, to_right, to_left)


def merge_rows(strips, place, send_a, mid, send_b, recv_a, recv_b, halo):
    ext = mid.shape[0] + 2 * send_a.shape[0]
    wide = mid.shape[1]
    return pl.pallas_call(
        functools.partial(rows_kernel, strips, halo, wide - LANE),
        out_shape=[
            jax.ShapeDtypeStruct((ext, wide), f32),
            jax.ShapeDtypeStruct((ext, LANE), f32),
            jax.ShapeDtypeStruct((ext, LANE), f32),
        ],
        in_specs=[SMEM] + [VMEM] * 5,
        out_specs=[VMEM] * 3,
        compiler_params=room(8),
        name="merge_rows",
    )(place, send_a, mid, send_b, recv_a, recv_b)


def cols_kernel(n, rows, halo, place, q, recv_a, recv_b, before, out, block, stat):
    odd = lax.rem(place[0], 2)
    ext, wide = q.shape
    w = wide - LANE
    lane = lax.broadcasted_iota(jnp.int32, (ext, LANE), 1)
    at = jnp.full((ext, LANE), place[0], jnp.int32)
    left = choose(odd, recv_a[...], recv_b[...])
    right = choose(odd, recv_b[...], recv_a[...])
    edge = q[:, w:]
    total = None
    out[:, :LANE] = jnp.where(at > 0, edge + left, 0.0) + damping * before[:, :LANE]
    out[:, LANE + w :] = jnp.where(at < n - 1, edge + right, 0.0) + damping * before[:, LANE + w :]
    for c in range(0, w, LANE):
        x = q[:, c : c + LANE] + damping * before[:, c + LANE : c + 2 * LANE]
        if c == 0:
            x = x + jnp.where(lane < halo, left, 0.0)
        if c == w - LANE:
            x = x + jnp.where(lane >= LANE - halo, right, 0.0)
        out[:, c + LANE : c + 2 * LANE] = x
        own = x[halo : halo + rows]
        block[:, c : c + LANE] = own
        part = jnp.sum((own * own).reshape(rows // 8, 8, LANE), axis=0)
        total = part if total is None else total + part
    stat[...] = total


def merge_cols(n, rows, place, q, recv_a, recv_b, before, halo):
    ext, wide = q.shape
    w = wide - LANE
    return pl.pallas_call(
        functools.partial(cols_kernel, n, rows, halo),
        out_shape=[
            jax.ShapeDtypeStruct((ext, w + 2 * LANE), f32),
            jax.ShapeDtypeStruct((rows, w), f32),
            jax.ShapeDtypeStruct((8, LANE), f32),
        ],
        in_specs=[SMEM] + [VMEM] * 4,
        out_specs=[VMEM] * 3,
        compiler_params=room(10),
        name="merge_cols",
    )(place, q, recv_a, recv_b, before)


def wrap_kernel(rows, halo, w, place, send_a, mid, send_b, recv_a, recv_b, before, out):
    odd = lax.rem(place[1], 2)
    keep = rows - 2 * halo
    pieces = (
        (0, halo, mid[:halo, :] + choose(odd, recv_a[...], recv_b[...])),
        (halo, keep, mid[halo : rows - halo, :]),
        (rows - halo, halo, mid[rows - halo :, :] + choose(odd, recv_b[...], recv_a[...])),
    )
    edges = []
    for start, size, value in pieces:
        span = slice(start, start + size)
        out[span, :] = value[:, :w] + damping * before[span, :]
        edges.append(value[:, w:])
    out[rows:, :] = pack_edge(jnp.concatenate(edges, axis=0), halo, w)


def wrap(place, send_a, mid, send_b, recv_a, recv_b, before, halo):
    rows, w = before.shape
    height = rows + rows * 2 * halo // w
    return pl.pallas_call(
        functools.partial(wrap_kernel, rows, halo, w),
        out_shape=jax.ShapeDtypeStruct((height, w), f32),
        in_specs=[SMEM] + [VMEM] * 6,
        out_specs=VMEM,
        compiler_params=room(8),
        name="wrap",
    )(place, send_a, mid, send_b, recv_a, recv_b, before)


def solution_kernel(n, w, place, est, sums, *refs):
    k0, k1 = refs[:n], refs[n : 2 * n]
    sol, res, coef = refs[2 * n :]
    total = [
        jnp.sum(jnp.sum(sums[i], axis=0, keepdims=True), axis=1, keepdims=True) for i in range(4)
    ]
    k00, k11 = total[0], total[2]
    k01 = total[1] + damping * k00
    k12 = total[3] + damping * k11
    alpha0 = k00 / k01
    norm1 = k00 - 2.0 * alpha0 * k01 + alpha0 * alpha0 * k11
    beta = norm1 / k00
    curve1 = (1.0 + beta) * (1.0 + beta) * k01 - 2.0 * (1.0 + beta) * alpha0 * k11
    curve1 = curve1 + alpha0 * alpha0 * k12
    alpha1 = norm1 / curve1
    c1 = alpha0 + alpha1 * (1.0 + beta)
    c2 = alpha0 * alpha1
    coef[...] = jnp.broadcast_to(c2, coef.shape)
    for i in range(n):
        cols = pl.ds(pl.multiple_of(jnp.bitwise_xor(place[0], i) * w, LANE), w)
        a0, a1 = k0[i][...], k1[i][...]
        sol[:, cols] = est[:, cols] + c1 * a0 - c2 * a1
        res[:, cols] = a0 - c1 * a1


def solution_image(place, est, sums, k0, k1):
    n = len(k0)
    w = k0[0].shape[1]
    return pl.pallas_call(
        functools.partial(solution_kernel, n, w),
        out_shape=[jax.ShapeDtypeStruct(est.shape, f32)] * 2
        + [jax.ShapeDtypeStruct((8, LANE), f32)],
        in_specs=[SMEM] + [VMEM] * (2 + 2 * n),
        out_specs=[VMEM] * 3,
        compiler_params=room(20),
        name="solution_image",
    )(place, est, sums, *k0, *k1)


def residual_kernel(n, rows, halo, w, place, base, coef, *refs):
    k2, (res, full) = refs[:n], refs[n:]
    c2 = coef[0:1, 0:1]
    lane = lax.broadcasted_iota(jnp.int32, (rows, LANE), 1)
    spot = [jnp.bitwise_xor(place[0], i) for i in range(n)]
    full[:, :LANE] = jnp.zeros((rows, LANE), f32)
    full[:, LANE + n * w :] = jnp.zeros((rows, LANE), f32)
    for i in range(n):
        full[:, pl.ds(pl.multiple_of(spot[i] * w + LANE, LANE), w)] = k2[i][:rows, :]
    for i in range(n):
        edge = unpack_edge(k2[i][rows:, :], halo)
        left = pl.ds(pl.multiple_of(spot[i] * w, LANE), LANE)
        right = pl.ds(pl.multiple_of(spot[i] * w + w + LANE, LANE), LANE)
        full[:, left] += jnp.where(lane >= LANE - halo, edge, 0.0)
        full[:, right] += jnp.where(lane < halo, edge, 0.0)
    for c in range(0, n * w, LANE):
        res[:, c : c + LANE] = base[:, c : c + LANE] + c2 * full[:, c + LANE : c + 2 * LANE]


def residual_image(place, base, coef, k2, halo):
    n = len(k2)
    rows, cols = base.shape
    w = cols // n
    return pl.pallas_call(
        functools.partial(residual_kernel, n, rows, halo, w),
        out_shape=jax.ShapeDtypeStruct(base.shape, f32),
        in_specs=[SMEM] + [VMEM] * (2 + n),
        out_specs=VMEM,
        scratch_shapes=[pltpu.VMEM((rows, cols + 2 * LANE), f32)],
        compiler_params=room(16),
        name="residual_image",
    )(place, base, coef, *k2)


def neighbours(send_a, send_b, axis):
    n = lax.axis_size(axis)
    out = []
    for lead, x in ((0, send_a), (1, send_b)):
        pairs = [(i, i + 1) for i in range(lead, n - 1, 2)]
        out.append(lax.ppermute(x, axis, pairs + [(b, a) for a, b in pairs]))
    return out


def swap(x, axis, distance):
    n = lax.axis_size(axis)
    return lax.ppermute(x, axis, [(i, i ^ distance) for i in range(n)])


def steps(estimate, observed, weights, column_kernels, row_kernels):
    n = lax.axis_size("frame")
    me = lax.axis_index("frame")
    strips = lax.axis_size("strip")
    strip = lax.axis_index("strip")
    place = jnp.stack([me, strip]).astype(jnp.int32)
    rows, cols = estimate.shape
    frames = weights.shape[0]
    halo = column_kernels.shape[1] // 2
    stay = lambda x: pltpu.with_memory_space_constraint(x, pltpu.HBM)
    weights, observed = stay(weights), stay(observed)
    column_kernels, row_kernels = stay(column_kernels), stay(row_kernels)
    w = cols // n
    distances = [1 << k for k in range(n.bit_length() - 1)]

    low, high = estimate[:halo], estimate[rows - halo :]
    odd = strip % 2 == 1
    est_a, est_b = neighbours(
        jnp.where(odd, low, high), jnp.where(odd, high, low), "strip"
    )

    half, quarter = n // 2, n // 4
    plan = [(d, d < half) for d in range(1, n)]
    packed, tile, own_mats = prepare(plan, place, column_kernels, row_kernels, weights, w, halo)
    far_tiles = []
    for d in range(half, n):
        far_tiles.append(swap(tile[:, : 2 * LANE], "frame", d))
    moved = []
    slots = [(0, False, ())]
    for d in range(1, half):
        moved.append(swap(packed[d - 1], "frame", d))
        slots.append((d, False, (d - 1,)))
    middle = range(quarter, n - quarter)
    where = {}
    for late in (False, True):
        for d in range(half, n):
            pairs = [(i, i ^ d) for i in range(n) if (i in middle) != late]
            where[d, late] = len(moved)
            moved.append(lax.ppermute(packed[d - 1], "frame", pairs))
    late_slots = []
    for late, out in ((False, slots), (True, late_slots)):
        for u in range(half, half + quarter):
            out.append((u, late, (where[u, late], where[u + quarter, late])))
    starts = [0] + [frames * rows] * (half - 1) + [0] * half

    send_a, mid, send_b = first_terms(
        place, estimate, est_a, est_b, own_mats, weights, observed
    )
    mats = setup_matrices(
        [tile] + moved[: half - 1] + far_tiles, starts, frames, rows, halo
    )
    recv_a, recv_b = neighbours(send_a, send_b, "strip")

    part = list(column_blocks(n, place, send_a, mid, send_b, recv_a, recv_b, w))
    mine = [part[0]]
    for i in range(n - 1, 0, -1):
        d = i & -i
        got = swap(part[i], "frame", d)
        if i == d:
            mine.append(got)
        else:
            part[i ^ d] = part[i ^ d] + got
    k0, wide, send_a, send_b, k00_part = start_image(n, place, estimate, mine, halo)
    recv_a, recv_b = neighbours(send_a, send_b, "strip")

    acc, stat1, k0x = apply_terms(
        n, place, (wide, recv_a, recv_b), mats, weights, moved[: where[half, True]],
        slots, None, halo,
    )
    send_a, mid, send_b, stat1 = apply_terms(
        n, place, (k0x,), mats, weights, moved, late_slots, 2 * halo, halo,
        carry=(acc, stat1),
    )
    recv_a, recv_b = neighbours(send_a, send_b, "strip")
    q, col_a, col_b = merge_rows(strips, place, send_a, mid, send_b, recv_a, recv_b, halo)
    recv_a, recv_b = neighbours(col_a, col_b, "frame")
    k1x, k1, k11_part = merge_cols(n, rows, place, q, recv_a, recv_b, k0x, halo)

    send_a, mid, send_b, stat2 = apply_terms(
        n, place, (k1x,), mats, weights, moved, slots + late_slots, halo, halo
    )
    recv_a, recv_b = neighbours(send_a, send_b, "strip")
    sums = jnp.stack([k00_part, stat1, k11_part, stat2])
    for axis, size in (("frame", n), ("strip", strips)):
        d = 1
        while d < size:
            sums = sums + swap(sums, axis, d)
            d *= 2
    k2 = wrap(place, send_a, mid, send_b, recv_a, recv_b, k1, halo)

    def gathered(x):
        parts = [x]
        for d in range(1, n):
            parts.append(swap(x, "frame", d))
        return parts

    def gathered_tree(x):
        parts = [x] + [None] * (n - 1)
        for i in range(n):
            for d in reversed(distances):
                if i % (2 * d) == 0:
                    parts[i + d] = swap(parts[i], "frame", d)
        return parts

    g0, g1, g2 = gathered(k0), gathered(k1), gathered_tree(k2)
    result, base, coef = solution_image(place, estimate, sums, g0, g1)
    return result, residual_image(place, base, coef, g2, halo)


def solution(mesh):
    return jax.shard_map(
        steps,
        mesh=mesh,
        in_specs=(
            P("strip", None),
            P("frame", "strip", None),
            P("frame", "strip", None),
            P("frame", None),
            P("frame", None),
        ),
        out_specs=(P("strip", None), P("strip", None)),
        check_vma=False,
    )
```

```python
import functools

import jax
import jax.numpy as jnp
from jax import lax
from jax.experimental import pallas as pl
from jax.experimental.pallas import tpu as pltpu
from jax.sharding import PartitionSpec as P


damping = 0.05
f32 = jnp.float32
bf16 = jnp.bfloat16
LANE = 128
VMEM = pl.BlockSpec(memory_space=pltpu.VMEM)
ANY = pl.BlockSpec(memory_space=pl.ANY)
SMEM = pl.BlockSpec(memory_space=pltpu.SMEM)
HBM = pl.BlockSpec(memory_space=pltpu.HBM)


def room(mib):
    return pltpu.CompilerParams(vmem_limit_bytes=mib * 2**20)


def split(x):
    hi = x.astype(bf16)
    lo = (x - hi.astype(f32)).astype(bf16)
    return hi, lo


def dot(a, b):
    return jnp.dot(a, b, preferred_element_type=f32)


def choose(flag, a, b):
    return jnp.where(jnp.full(a.shape, flag, jnp.int32) == 1, a, b)


def pack_edge(edge, halo, w):
    rows = edge.shape[0]
    per = LANE // (2 * halo)
    short = rows * 2 * halo // w
    edge = pltpu.roll(edge, halo, 1)
    lane = lax.broadcasted_iota(jnp.int32, (short, LANE), 1)
    out = []
    for t in range(w // LANE):
        tile = None
        for p in range(per):
            k = t * per + p
            part = edge[k * short : (k + 1) * short]
            part = pltpu.roll(part, p * 2 * halo, 1) if p else part
            tile = part if tile is None else jnp.where(lane >= p * 2 * halo, part, tile)
        out.append(tile)
    return jnp.concatenate(out, axis=1)


def unpack_edge(packed, halo):
    _, w = packed.shape
    per = LANE // (2 * halo)
    parts = []
    for k in range(w // (2 * halo)):
        t, p = divmod(k, per)
        part = packed[:, t * LANE : (t + 1) * LANE]
        back = (LANE - halo - p * 2 * halo) % LANE
        parts.append(pltpu.roll(part, back, 1) if back else part)
    return jnp.concatenate(parts, axis=0)


def tiles(width, step=256):
    return [(s, min(step, width - s)) for s in range(0, width, step)]


def toeplitz(base, count):
    wide = base.shape[1]
    return pltpu.roll(jnp.broadcast_to(base, (count, wide)), 0, 1, stride=1, stride_axis=0)


def build_group(taps, g, frames, rows, halo, t_ref, b_ref, bp_ref, ta_ref):
    ext = rows + 2 * halo
    unit = taps / jnp.sum(taps, axis=1, keepdims=True)
    for s in range(frames):
        f = g * frames + s
        col = unit[s : s + 1]
        row = unit[frames + s : frames + s + 1]
        by_rows = toeplitz(row, rows)
        hi, lo = split(by_rows)
        t_ref[f, :rows, :] = hi
        t_ref[f, rows:, :] = lo
        hi, lo = split(by_rows.T[:ext])
        ta_ref[g, :ext, s * rows : (s + 1) * rows] = hi
        ta_ref[g, ext:, s * rows : (s + 1) * rows] = lo
        hi, lo = split(toeplitz(col, LANE).T)
        b_ref[f, :, :LANE] = hi
        b_ref[f, :, LANE:] = lo
        hi, lo = split(toeplitz(pltpu.roll(col, LANE, 1), 2 * LANE)[:, :LANE])
        bp_ref[f, :, :LANE] = hi
        bp_ref[f, :, LANE:] = lo


def matrix_shapes(groups, frames, rows, halo):
    ext = rows + 2 * halo
    return [
        jax.ShapeDtypeStruct(s, bf16)
        for s in (
            (groups * frames, 2 * rows, 2 * LANE),
            (groups * frames, 2 * LANE, 2 * LANE),
            (groups * frames, 2 * LANE, 2 * LANE),
            (groups, 2 * ext, frames * rows),
        )
    ]


def tile_height(frames):
    return -(-2 * frames // 8) * 8


def setup_kernel(frames, rows, halo, starts, *refs):
    tiles_in = refs[: len(starts)]
    mats, taps, sem = refs[len(starts) : -2], refs[-2], refs[-1]
    height = tile_height(frames)

    def copy(g):
        source = tiles_in[g].at[pl.ds(starts[g], height), pl.ds(0, 2 * LANE)]
        return pltpu.make_async_copy(source, taps.at[g], sem.at[g])

    for g in range(len(starts)):
        copy(g).start()
    for g in range(len(starts)):
        copy(g).wait()
        build_group(taps[g], g, frames, rows, halo, *mats)


def setup_matrices(tiles_in, starts, frames, rows, halo):
    groups = len(tiles_in)
    return pl.pallas_call(
        functools.partial(setup_kernel, frames, rows, halo, starts),
        out_shape=matrix_shapes(groups, frames, rows, halo),
        in_specs=[ANY] * groups,
        out_specs=[VMEM] * 4,
        scratch_shapes=[
            pltpu.VMEM((groups, tile_height(frames), 2 * LANE), f32),
            pltpu.SemaphoreType.DMA((groups,)),
        ],
        compiler_params=room(24),
        name="setup_all",
    )(*tiles_in)


def load_image(y_hi, y_lo, image, halo):
    ext, full = image.shape
    shift = LANE - halo
    y = pltpu.roll(image, full - shift, 1)[:, : full - LANE]
    hi, lo = split(y)
    y_hi[:ext, :] = hi
    y_lo[:ext, :] = lo


def group_terms(frames, rows, w, y_hi, y_lo, t, b, bp, ta, weight, data, us, qs, vs_hi, vs_lo, acc, stat, ready=None):
    total = None
    for f in range(frames):
        for c, size in tiles(w + LANE):
            r1 = dot(t(f)[...], y_hi[:, c : c + size])
            r2 = dot(t(f)[:rows, :], y_lo[:, c : c + size])
            hi, lo = split(r1[:rows] + r1[rows:] + r2)
            us[:rows, c : c + size] = hi
            us[rows:, c : c + size] = lo
        if ready is not None:
            ready(f)
        for k in range(w // LANE):
            c = k * LANE
            r = dot(us[:, c : c + 2 * LANE], b(f)[...])
            a = r[:rows, :LANE] + r[:rows, LANE:] + r[rows:, :LANE]
            if data is not None:
                a = a - data(f)[:, c : c + LANE]
            q = weight(f)[:, c : c + LANE] * a
            if stat is not None:
                part = jnp.sum((a * q).reshape(rows // 8, 8, LANE), axis=0)
                total = part if total is None else total + part
            hi, lo = split(q)
            qs[:rows, c + LANE : c + 2 * LANE] = hi
            qs[rows:, c + LANE : c + 2 * LANE] = lo
        for k in range(w // LANE + 1):
            c = k * LANE
            r = dot(qs[:, c : c + 2 * LANE], bp(f)[...])
            hi, lo = split(r[:rows, :LANE] + r[:rows, LANE:] + r[rows:, :LANE])
            vs_hi[f * rows : (f + 1) * rows, c : c + LANE] = hi
            vs_lo[f * rows : (f + 1) * rows, c : c + LANE] = lo
    ext = acc.shape[0]
    for c, size in tiles(w + LANE):
        r1 = dot(ta[...], vs_hi[:, c : c + size])
        r2 = dot(ta[:ext, :], vs_lo[:, c : c + size])
        acc[:, c : c + size] += r1[:ext] + r1[ext:] + r2
    if stat is not None:
        stat[...] += total


def work_scratch(frames, rows, halo, w):
    ext = rows + 2 * halo
    return [
        pltpu.VMEM((2 * LANE, w + LANE), bf16),
        pltpu.VMEM((2 * LANE, w + LANE), bf16),
        pltpu.VMEM((2 * rows, w + LANE), bf16),
        pltpu.VMEM((2 * rows, w + 2 * LANE), bf16),
        pltpu.VMEM((frames * rows, w + LANE), bf16),
        pltpu.VMEM((frames * rows, w + LANE), bf16),
        pltpu.VMEM((ext, w + LANE), f32),
    ]


def clear_edges(y_hi, y_lo, qs, ext, rows, w):
    zero = jnp.zeros((y_hi.shape[0] - ext, y_hi.shape[1]), bf16)
    y_hi[ext:, :] = zero
    y_lo[ext:, :] = zero
    qs[:, :LANE] = jnp.zeros((2 * rows, LANE), bf16)
    qs[:, w + LANE :] = jnp.zeros((2 * rows, LANE), bf16)


def unshift(acc, halo):
    return pltpu.roll(acc, acc.shape[1] - halo, 1)


def first_kernel(
    frames, rows, halo,
    place, est, recv_a, recv_b, t_ref, b_ref, bp_ref, ta_ref, w_hbm, d_hbm,
    send_a, mid, send_b,
    y_hi, y_lo, us, qs, vs_hi, vs_lo, acc, wbuf, dbuf, sem,
):
    ext = rows + 2 * halo
    cols = est.shape[1]
    copies = [
        (
            pltpu.make_async_copy(w_hbm.at[f], wbuf.at[f], sem.at[0, f]),
            pltpu.make_async_copy(d_hbm.at[f], dbuf.at[f], sem.at[1, f]),
        )
        for f in range(frames)
    ]
    for pair in copies:
        for c in pair:
            c.start()
    clear_edges(y_hi, y_lo, qs, ext, rows, cols)
    odd = lax.rem(place[1], 2)
    none = jnp.zeros((ext, LANE), f32)
    for start in range(0, cols, 4 * LANE):
        size = 4 * LANE + LANE
        left = max(start - LANE, 0)
        span = slice(left, min(start + 4 * LANE, cols))
        x = jnp.concatenate(
            [
                choose(odd, recv_a[:, span], recv_b[:, span]),
                est[:, span],
                choose(odd, recv_b[:, span], recv_a[:, span]),
            ],
            axis=0,
        )
        if start == 0:
            x = jnp.concatenate([none, x], axis=1)
        if x.shape[1] < size:
            x = jnp.concatenate([x, jnp.zeros((ext, size - x.shape[1]), f32)], axis=1)
        hi, lo = split(pltpu.roll(x, halo, 1)[:, LANE:])
        y_hi[:ext, start : start + 4 * LANE] = hi
        y_lo[:ext, start : start + 4 * LANE] = lo
        if start + 4 * LANE >= cols:
            tail = jnp.concatenate([x[:, 4 * LANE :], none], axis=1)
            hi, lo = split(pltpu.roll(tail, halo, 1)[:, LANE:])
            y_hi[:ext, cols:] = hi
            y_lo[:ext, cols:] = lo
    acc[...] = jnp.zeros_like(acc)

    def ready(f):
        for c in copies[f]:
            c.wait()

    group_terms(
        frames, rows, cols, y_hi, y_lo,
        lambda f: t_ref.at[f], lambda f: b_ref.at[f], lambda f: bp_ref.at[f], ta_ref.at[0],
        lambda f: wbuf.at[f], lambda f: dbuf.at[f],
        us, qs, vs_hi, vs_lo, acc, None, ready,
    )
    for start in range(0, cols, 4 * LANE):
        size = min(4 * LANE, cols - start)
        z = pltpu.roll(acc[:, start : start + size + LANE], size + LANE - halo, 1)[:, :size]
        span = slice(start, start + size)
        low, high = z[:halo], z[halo + rows :]
        send_a[:, span] = choose(odd, low, high)
        send_b[:, span] = choose(odd, high, low)
        mid[:, span] = z[halo : halo + rows]


def first_terms(place, est, recv_a, recv_b, mats, weights, observed):
    frames, rows, cols = weights.shape
    halo = recv_a.shape[0]
    return pl.pallas_call(
        functools.partial(first_kernel, frames, rows, halo),
        out_shape=[
            jax.ShapeDtypeStruct((halo, cols), f32),
            jax.ShapeDtypeStruct((rows, cols), f32),
            jax.ShapeDtypeStruct((halo, cols), f32),
        ],
        in_specs=[SMEM] + [VMEM] * 7 + [HBM, HBM],
        out_specs=[VMEM] * 3,
        scratch_shapes=work_scratch(frames, rows, halo, cols)
        + [
            pltpu.VMEM((frames, rows, cols), f32),
            pltpu.VMEM((frames, rows, cols), f32),
            pltpu.SemaphoreType.DMA((2, frames)),
        ],
        cost_estimate=pl.CostEstimate(flops=8 * 10**9, bytes_accessed=8 * 2**20, transcendentals=0),
        compiler_params=room(36),
        name="first_terms",
    )(place, est, recv_a, recv_b, *mats, weights, observed)


def prepare_kernel(plan, frames, rows, halo, w, place, cols_in, rows_in, weights, *refs):
    outs, tile, mats = refs[: len(plan)], refs[len(plan)], refs[len(plan) + 1 : -4]
    cols_buf, rows_buf, taps_sem, sem = refs[-4:]
    taps = cols_in.shape[1]
    taps_copies = (
        pltpu.make_async_copy(cols_in, cols_buf, taps_sem.at[0]),
        pltpu.make_async_copy(rows_in, rows_buf, taps_sem.at[1]),
    )
    for copy in taps_copies:
        copy.start()
    pending = []
    for i, (distance, _) in enumerate(plan):
        start = pl.multiple_of(jnp.bitwise_xor(place[0], distance) * w, LANE)
        for k in range(frames):
            copy = pltpu.make_async_copy(
                weights.at[k, :, pl.ds(start, w)],
                outs[i].at[pl.ds(k * rows, rows), :],
                sem.at[i, k],
            )
            copy.start()
            pending.append(copy)
    tile[...] = jnp.zeros_like(tile)
    for copy in taps_copies:
        copy.wait()
    tile[:frames, :taps] = cols_buf[...]
    tile[frames : 2 * frames, :taps] = rows_buf[...]
    for i, (_, with_taps) in enumerate(plan):
        if with_taps:
            outs[i][frames * rows :, :] = tile[...]
    build_group(tile[:, : 2 * LANE], 0, frames, rows, halo, *mats)
    for copy in pending:
        copy.wait()


def prepare(plan, place, column_kernels, row_kernels, weights, w, halo):
    frames, rows, _ = weights.shape
    height = tile_height(frames)
    out = pl.pallas_call(
        functools.partial(prepare_kernel, plan, frames, rows, halo, w),
        out_shape=[
            jax.ShapeDtypeStruct((frames * rows + (height if taps else 0), w), f32)
            for _, taps in plan
        ]
        + [jax.ShapeDtypeStruct((height, w), f32)]
        + matrix_shapes(1, frames, rows, halo),
        in_specs=[SMEM, HBM, HBM, HBM],
        out_specs=[VMEM] * (len(plan) + 5),
        scratch_shapes=[
            pltpu.VMEM(column_kernels.shape, f32),
            pltpu.VMEM(row_kernels.shape, f32),
            pltpu.SemaphoreType.DMA((2,)),
            pltpu.SemaphoreType.DMA((len(plan), frames)),
        ],
        compiler_params=room(24),
        name="prepare",
    )(place, column_kernels, row_kernels, weights)
    return out[: len(plan)], out[len(plan)], out[len(plan) + 1 :]


def blocks_kernel(n, halo, w, place, send_a, mid, send_b, recv_a, recv_b, *refs):
    outs, full = refs[:-1], refs[-1]
    rows, cols = mid.shape
    odd = lax.rem(place[1], 2)
    inner = slice(LANE, LANE + cols)
    for end in (0, LANE + cols):
        full[:, end : end + LANE] = jnp.zeros((rows, LANE), f32)
    full[:halo, inner] = mid[:halo, :] + choose(odd, recv_a[...], recv_b[...])
    full[halo : rows - halo, inner] = mid[halo : rows - halo, :]
    full[rows - halo :, inner] = mid[rows - halo :, :] + choose(odd, recv_b[...], recv_a[...])
    lane = lax.broadcasted_iota(jnp.int32, (rows, LANE), 1)
    for i in range(n):
        start = jnp.bitwise_xor(place[0], i) * w
        outs[i][:rows, :] = full[:, pl.ds(pl.multiple_of(start + LANE, LANE), w)]
        before = full[:, pl.ds(pl.multiple_of(start, LANE), LANE)]
        after = full[:, pl.ds(pl.multiple_of(start + LANE + w, LANE), LANE)]
        outs[i][rows:, :] = pack_edge(jnp.where(lane >= LANE - halo, before, after), halo, w)


def column_blocks(n, place, send_a, mid, send_b, recv_a, recv_b, w):
    rows, cols = mid.shape
    halo = send_a.shape[0]
    height = rows + rows * 2 * halo // w
    return pl.pallas_call(
        functools.partial(blocks_kernel, n, halo, w),
        out_shape=[jax.ShapeDtypeStruct((height, w), f32)] * n,
        in_specs=[SMEM] + [VMEM] * 5,
        out_specs=[VMEM] * n,
        scratch_shapes=[pltpu.VMEM((rows, cols + 2 * LANE), f32)],
        compiler_params=room(16),
        name="column_blocks",
    )(place, send_a, mid, send_b, recv_a, recv_b)


def start_kernel(n, rows, halo, w, place, est, *refs):
    parts = refs[:-5]
    k0, wide, send_a, send_b, stat = refs[-5:]
    total = parts[0][...]
    for p in parts[1:]:
        total = total + p[...]
    me = place[0]
    odd = lax.rem(place[1], 2)
    at = lambda start, size: est[:, pl.ds(pl.multiple_of(start, LANE), size)]
    own = -(total[:rows] + damping * at(me * w, w))
    edge = unpack_edge(total[rows:], halo)
    before = at(jnp.maximum(me * w - LANE, 0), LANE)
    after = at(jnp.minimum(me * w + w, (n * w) - LANE), LANE)
    none = jnp.zeros((rows, LANE), f32)
    left = choose((me > 0).astype(jnp.int32), -(edge + damping * before), none)
    right = choose((me < n - 1).astype(jnp.int32), -(edge + damping * after), none)
    k0[...] = own
    wide[:, :LANE] = left
    wide[:, LANE : LANE + w] = own
    wide[:, LANE + w :] = right
    low, high = wide[:halo, :], wide[rows - halo :, :]
    send_a[...] = choose(odd, low, high)
    send_b[...] = choose(odd, high, low)
    square = own * own
    acc = square[:, :LANE]
    for c in range(LANE, w, LANE):
        acc = acc + square[:, c : c + LANE]
    stat[...] = jnp.sum(acc.reshape(rows // 8, 8, LANE), axis=0)


def start_image(n, place, est, parts, halo):
    rows, cols = est.shape
    w = cols // n
    return pl.pallas_call(
        functools.partial(start_kernel, n, rows, halo, w),
        out_shape=[
            jax.ShapeDtypeStruct((rows, w), f32),
            jax.ShapeDtypeStruct((rows, w + 2 * LANE), f32),
            jax.ShapeDtypeStruct((halo, w + 2 * LANE), f32),
            jax.ShapeDtypeStruct((halo, w + 2 * LANE), f32),
            jax.ShapeDtypeStruct((8, LANE), f32),
        ],
        in_specs=[SMEM] + [VMEM] * (1 + len(parts)),
        out_specs=[VMEM] * 5,
        compiler_params=room(12),
        name="start_image",
    )(place, est, *parts)


def apply_kernel(n, frames, rows, halo, w, slots, cut, count, pieces, carried, place, *refs):
    image, refs = refs[:pieces], refs[pieces:]
    t_hbm, b_hbm, bp_hbm, ta_hbm, own = refs[:5]
    moved, refs = refs[5 : 5 + count], refs[5 + count :]
    if carried:
        (acc_in, stat_in), refs = refs[:2], refs[2:]
    if cut is None:
        (acc_out, stat), refs = refs[:2], refs[2:]
    else:
        (send_a, mid, send_b, stat), refs = refs[:4], refs[4:]
    if pieces > 1:
        whole, refs = refs[0], refs[1:]
    y_hi, y_lo, us, qs, vs_hi, vs_lo, acc, tb, bb, bpb, tab, wbuf, sem, wsem = refs
    odd = lax.rem(place[1], 2)
    ext = rows + 2 * halo
    quarter = n // 4
    inner = ((place[0] >= quarter) & (place[0] < n - quarter)).astype(jnp.int32)

    def copies(i, g):
        span = pl.ds(g * frames, frames)
        return [
            pltpu.make_async_copy(t_hbm.at[span], tb.at[i], sem.at[0, i]),
            pltpu.make_async_copy(b_hbm.at[span], bb.at[i], sem.at[1, i]),
            pltpu.make_async_copy(bp_hbm.at[span], bpb.at[i], sem.at[2, i]),
            pltpu.make_async_copy(ta_hbm.at[g], tab.at[i], sem.at[3, i]),
        ]

    mine = pl.ds(pl.multiple_of(place[0] * w, LANE), w)
    for i, (distance, late, sources) in enumerate(slots):
        if len(sources) == 2:
            group = distance + (1 - inner if late else inner) * quarter
        else:
            group = distance
        for c in copies(i, group):
            c.start()
        for f in range(frames):
            span = pl.ds(f * rows, rows)
            if not sources:
                pltpu.make_async_copy(own.at[f, :, mine], wbuf.at[i, f], wsem.at[i, f]).start()
            elif len(sources) == 1:
                source = moved[sources[0]].at[span, :]
                pltpu.make_async_copy(source, wbuf.at[i, f], wsem.at[i, f]).start()
            else:
                for k in range(2):

                    @pl.when((group - distance) == k * quarter)
                    def _(source=moved[sources[k]].at[span, :], i=i, f=f):
                        pltpu.make_async_copy(source, wbuf.at[i, f], wsem.at[i, f]).start()

    clear_edges(y_hi, y_lo, qs, ext, rows, w)
    if pieces > 1:
        wide, recv_a, recv_b = image
        whole[:halo, :] = choose(odd, recv_a[...], recv_b[...])
        whole[halo : halo + rows, :] = wide[...]
        whole[halo + rows :, :] = choose(odd, recv_b[...], recv_a[...])
        load_image(y_hi, y_lo, whole[...], halo)
    else:
        load_image(y_hi, y_lo, image[0][...], halo)
    acc[...] = acc_in[...] if carried else jnp.zeros_like(acc)
    stat[...] = stat_in[...] if carried else jnp.zeros_like(stat)

    @pl.loop(0, len(slots))
    def _(i):
        for c in copies(i, 0):
            c.wait()
        for f in range(frames):
            pltpu.make_async_copy(own.at[f, :, mine], wbuf.at[i, f], wsem.at[i, f]).wait()
        group_terms(
            frames, rows, w, y_hi, y_lo,
            lambda f: tb.at[i, f], lambda f: bb.at[i, f], lambda f: bpb.at[i, f], tab.at[i],
            lambda f: wbuf.at[i, f], None,
            us, qs, vs_hi, vs_lo, acc, stat,
        )

    if cut is None:
        acc_out[...] = acc[...]
    else:
        z = unshift(acc[...], halo)
        send_a[...] = choose(odd, z[:cut], z[ext - cut :])
        send_b[...] = choose(odd, z[ext - cut :], z[:cut])
        mid[...] = z[cut : ext - cut]


def apply_terms(n, place, image, mats, weights, moved, slots, cut, halo, carry=()):
    frames, rows, _ = weights.shape
    w = image[0].shape[1] - 2 * LANE
    ext = rows + 2 * halo
    t, b, bp, ta = mats
    count = len(slots)
    wide = w + LANE
    shapes = [(ext, wide)] if cut is None else [(cut, wide), (ext - 2 * cut, wide), (cut, wide)]
    shapes += [(8, LANE)] + [(ext, w + 2 * LANE)] * (len(image) > 1)
    return pl.pallas_call(
        functools.partial(
            apply_kernel, n, frames, rows, halo, w, slots, cut, len(moved), len(image), bool(carry)
        ),
        out_shape=[jax.ShapeDtypeStruct(s, f32) for s in shapes],
        in_specs=[SMEM]
        + [VMEM] * len(image)
        + [ANY] * 4
        + [HBM]
        + [ANY] * len(moved)
        + [VMEM] * len(carry),
        out_specs=[VMEM] * len(shapes),
        scratch_shapes=work_scratch(frames, rows, halo, w)
        + [
            pltpu.VMEM((count, frames) + t.shape[1:], bf16),
            pltpu.VMEM((count, frames) + b.shape[1:], bf16),
            pltpu.VMEM((count, frames) + bp.shape[1:], bf16),
            pltpu.VMEM((count,) + ta.shape[1:], bf16),
            pltpu.VMEM((count, frames, rows, w), f32),
            pltpu.SemaphoreType.DMA((4, count)),
            pltpu.SemaphoreType.DMA((count, frames)),
        ],
        cost_estimate=pl.CostEstimate(
            flops=count * 3 * 10**9, bytes_accessed=count * 2**20, transcendentals=0
        ),
        compiler_params=room(28),
    )(place, *image, t, b, bp, ta, weights, *moved, *carry)


def rows_kernel(strips, halo, w, place, send_a, mid, send_b, recv_a, recv_b, q, col_a, col_b):
    odd = lax.rem(place[1], 2)
    odd_col = lax.rem(place[0], 2)
    edge_rows, wide = send_a.shape
    ext = q.shape[0]
    row = lax.broadcasted_iota(jnp.int32, (edge_rows, wide), 0)
    strip = jnp.full((edge_rows, wide), place[1], jnp.int32)
    low = choose(odd, send_a[...], send_b[...]) + choose(odd, recv_a[...], recv_b[...])
    high = choose(odd, send_b[...], send_a[...]) + choose(odd, recv_b[...], recv_a[...])
    q[:edge_rows, :] = jnp.where((row >= halo) | (strip > 0), low, 0.0)
    q[edge_rows : ext - edge_rows, :] = mid[...]
    q[ext - edge_rows :, :] = jnp.where((row < edge_rows - halo) | (strip < strips - 1), high, 0.0)
    lane = lax.broadcasted_iota(jnp.int32, (ext, LANE), 1)
    edge = q[:, w:]
    to_left = jnp.where(lane < halo, q[:, :LANE], edge)
    to_right = jnp.where(lane >= LANE - halo, q[:, w - LANE : w], edge)
    col_a[...] = choose(odd_col, to_left, to_right)
    col_b[...] = choose(odd_col, to_right, to_left)


def merge_rows(strips, place, send_a, mid, send_b, recv_a, recv_b, halo):
    ext = mid.shape[0] + 2 * send_a.shape[0]
    wide = mid.shape[1]
    return pl.pallas_call(
        functools.partial(rows_kernel, strips, halo, wide - LANE),
        out_shape=[
            jax.ShapeDtypeStruct((ext, wide), f32),
            jax.ShapeDtypeStruct((ext, LANE), f32),
            jax.ShapeDtypeStruct((ext, LANE), f32),
        ],
        in_specs=[SMEM] + [VMEM] * 5,
        out_specs=[VMEM] * 3,
        compiler_params=room(8),
        name="merge_rows",
    )(place, send_a, mid, send_b, recv_a, recv_b)


def cols_kernel(n, rows, halo, place, q, recv_a, recv_b, before, out, block, stat):
    odd = lax.rem(place[0], 2)
    ext, wide = q.shape
    w = wide - LANE
    lane = lax.broadcasted_iota(jnp.int32, (ext, LANE), 1)
    at = jnp.full((ext, LANE), place[0], jnp.int32)
    left = choose(odd, recv_a[...], recv_b[...])
    right = choose(odd, recv_b[...], recv_a[...])
    edge = q[:, w:]
    total = None
    out[:, :LANE] = jnp.where(at > 0, edge + left, 0.0) + damping * before[:, :LANE]
    out[:, LANE + w :] = jnp.where(at < n - 1, edge + right, 0.0) + damping * before[:, LANE + w :]
    for c in range(0, w, LANE):
        x = q[:, c : c + LANE] + damping * before[:, c + LANE : c + 2 * LANE]
        if c == 0:
            x = x + jnp.where(lane < halo, left, 0.0)
        if c == w - LANE:
            x = x + jnp.where(lane >= LANE - halo, right, 0.0)
        out[:, c + LANE : c + 2 * LANE] = x
        own = x[halo : halo + rows]
        block[:, c : c + LANE] = own
        part = jnp.sum((own * own).reshape(rows // 8, 8, LANE), axis=0)
        total = part if total is None else total + part
    stat[...] = total


def merge_cols(n, rows, place, q, recv_a, recv_b, before, halo):
    ext, wide = q.shape
    w = wide - LANE
    return pl.pallas_call(
        functools.partial(cols_kernel, n, rows, halo),
        out_shape=[
            jax.ShapeDtypeStruct((ext, w + 2 * LANE), f32),
            jax.ShapeDtypeStruct((rows, w), f32),
            jax.ShapeDtypeStruct((8, LANE), f32),
        ],
        in_specs=[SMEM] + [VMEM] * 4,
        out_specs=[VMEM] * 3,
        compiler_params=room(10),
        name="merge_cols",
    )(place, q, recv_a, recv_b, before)


def wrap_kernel(rows, halo, w, place, send_a, mid, send_b, recv_a, recv_b, before, out):
    odd = lax.rem(place[1], 2)
    keep = rows - 2 * halo
    pieces = (
        (0, halo, mid[:halo, :] + choose(odd, recv_a[...], recv_b[...])),
        (halo, keep, mid[halo : rows - halo, :]),
        (rows - halo, halo, mid[rows - halo :, :] + choose(odd, recv_b[...], recv_a[...])),
    )
    edges = []
    for start, size, value in pieces:
        span = slice(start, start + size)
        out[span, :] = value[:, :w] + damping * before[span, :]
        edges.append(value[:, w:])
    out[rows:, :] = pack_edge(jnp.concatenate(edges, axis=0), halo, w)


def wrap(place, send_a, mid, send_b, recv_a, recv_b, before, halo):
    rows, w = before.shape
    height = rows + rows * 2 * halo // w
    return pl.pallas_call(
        functools.partial(wrap_kernel, rows, halo, w),
        out_shape=jax.ShapeDtypeStruct((height, w), f32),
        in_specs=[SMEM] + [VMEM] * 6,
        out_specs=VMEM,
        compiler_params=room(8),
        name="wrap",
    )(place, send_a, mid, send_b, recv_a, recv_b, before)


def solution_kernel(n, w, place, est, sums, *refs):
    k0, k1 = refs[:n], refs[n : 2 * n]
    sol, res, coef = refs[2 * n :]
    total = [
        jnp.sum(jnp.sum(sums[i], axis=0, keepdims=True), axis=1, keepdims=True) for i in range(4)
    ]
    k00, k11 = total[0], total[2]
    k01 = total[1] + damping * k00
    k12 = total[3] + damping * k11
    alpha0 = k00 / k01
    norm1 = k00 - 2.0 * alpha0 * k01 + alpha0 * alpha0 * k11
    beta = norm1 / k00
    curve1 = (1.0 + beta) * (1.0 + beta) * k01 - 2.0 * (1.0 + beta) * alpha0 * k11
    curve1 = curve1 + alpha0 * alpha0 * k12
    alpha1 = norm1 / curve1
    c1 = alpha0 + alpha1 * (1.0 + beta)
    c2 = alpha0 * alpha1
    coef[...] = jnp.broadcast_to(c2, coef.shape)
    for i in range(n):
        cols = pl.ds(pl.multiple_of(jnp.bitwise_xor(place[0], i) * w, LANE), w)
        a0, a1 = k0[i][...], k1[i][...]
        sol[:, cols] = est[:, cols] + c1 * a0 - c2 * a1
        res[:, cols] = a0 - c1 * a1


def solution_image(place, est, sums, k0, k1):
    n = len(k0)
    w = k0[0].shape[1]
    return pl.pallas_call(
        functools.partial(solution_kernel, n, w),
        out_shape=[jax.ShapeDtypeStruct(est.shape, f32)] * 2
        + [jax.ShapeDtypeStruct((8, LANE), f32)],
        in_specs=[SMEM] + [VMEM] * (2 + 2 * n),
        out_specs=[VMEM] * 3,
        compiler_params=room(20),
        name="solution_image",
    )(place, est, sums, *k0, *k1)


def residual_kernel(n, rows, halo, w, place, base, coef, *refs):
    k2, (res, full) = refs[:n], refs[n:]
    c2 = coef[0:1, 0:1]
    lane = lax.broadcasted_iota(jnp.int32, (rows, LANE), 1)
    spot = [jnp.bitwise_xor(place[0], i) for i in range(n)]
    full[:, :LANE] = jnp.zeros((rows, LANE), f32)
    full[:, LANE + n * w :] = jnp.zeros((rows, LANE), f32)
    for i in range(n):
        full[:, pl.ds(pl.multiple_of(spot[i] * w + LANE, LANE), w)] = k2[i][:rows, :]
    for i in range(n):
        edge = unpack_edge(k2[i][rows:, :], halo)
        left = pl.ds(pl.multiple_of(spot[i] * w, LANE), LANE)
        right = pl.ds(pl.multiple_of(spot[i] * w + w + LANE, LANE), LANE)
        full[:, left] += jnp.where(lane >= LANE - halo, edge, 0.0)
        full[:, right] += jnp.where(lane < halo, edge, 0.0)
    for c in range(0, n * w, LANE):
        res[:, c : c + LANE] = base[:, c : c + LANE] + c2 * full[:, c + LANE : c + 2 * LANE]


def residual_image(place, base, coef, k2, halo):
    n = len(k2)
    rows, cols = base.shape
    w = cols // n
    return pl.pallas_call(
        functools.partial(residual_kernel, n, rows, halo, w),
        out_shape=jax.ShapeDtypeStruct(base.shape, f32),
        in_specs=[SMEM] + [VMEM] * (2 + n),
        out_specs=VMEM,
        scratch_shapes=[pltpu.VMEM((rows, cols + 2 * LANE), f32)],
        compiler_params=room(16),
        name="residual_image",
    )(place, base, coef, *k2)


def neighbours(send_a, send_b, axis):
    n = lax.axis_size(axis)
    out = []
    for lead, x in ((0, send_a), (1, send_b)):
        pairs = [(i, i + 1) for i in range(lead, n - 1, 2)]
        out.append(lax.ppermute(x, axis, pairs + [(b, a) for a, b in pairs]))
    return out


def swap(x, axis, distance):
    n = lax.axis_size(axis)
    return lax.ppermute(x, axis, [(i, i ^ distance) for i in range(n)])


def steps(estimate, observed, weights, column_kernels, row_kernels):
    n = lax.axis_size("frame")
    me = lax.axis_index("frame")
    strips = lax.axis_size("strip")
    strip = lax.axis_index("strip")
    place = jnp.stack([me, strip]).astype(jnp.int32)
    rows, cols = estimate.shape
    frames = weights.shape[0]
    halo = column_kernels.shape[1] // 2
    stay = lambda x: pltpu.with_memory_space_constraint(x, pltpu.HBM)
    weights, observed = stay(weights), stay(observed)
    column_kernels, row_kernels = stay(column_kernels), stay(row_kernels)
    w = cols // n
    distances = [1 << k for k in range(n.bit_length() - 1)]

    low, high = estimate[:halo], estimate[rows - halo :]
    odd = strip % 2 == 1
    est_a, est_b = neighbours(
        jnp.where(odd, low, high), jnp.where(odd, high, low), "strip"
    )

    half, quarter = n // 2, n // 4
    plan = [(d, d < half) for d in range(1, n)]
    packed, tile, own_mats = prepare(plan, place, column_kernels, row_kernels, weights, w, halo)
    far_tiles = []
    for d in range(half, n):
        far_tiles.append(swap(tile[:, : 2 * LANE], "frame", d))
    moved = []
    slots = [(0, False, ())]
    for d in range(1, half):
        moved.append(swap(packed[d - 1], "frame", d))
        slots.append((d, False, (d - 1,)))
    middle = range(quarter, n - quarter)
    where = {}
    for late in (False, True):
        for d in range(half, n):
            pairs = [(i, i ^ d) for i in range(n) if (i in middle) != late]
            where[d, late] = len(moved)
            moved.append(lax.ppermute(packed[d - 1], "frame", pairs))
    late_slots = []
    for late, out in ((False, slots), (True, late_slots)):
        for u in range(half, half + quarter):
            out.append((u, late, (where[u, late], where[u + quarter, late])))
    starts = [0] + [frames * rows] * (half - 1) + [0] * half

    send_a, mid, send_b = first_terms(
        place, estimate, est_a, est_b, own_mats, weights, observed
    )
    mats = setup_matrices(
        [tile] + moved[: half - 1] + far_tiles, starts, frames, rows, halo
    )
    recv_a, recv_b = neighbours(send_a, send_b, "strip")

    part = list(column_blocks(n, place, send_a, mid, send_b, recv_a, recv_b, w))
    mine = [part[0]]
    for i in range(n - 1, 0, -1):
        d = i & -i
        got = swap(part[i], "frame", d)
        if i == d:
            mine.append(got)
        else:
            part[i ^ d] = part[i ^ d] + got
    k0, wide, send_a, send_b, k00_part = start_image(n, place, estimate, mine, halo)
    recv_a, recv_b = neighbours(send_a, send_b, "strip")

    acc, stat1, k0x = apply_terms(
        n, place, (wide, recv_a, recv_b), mats, weights, moved[: where[half, True]],
        slots, None, halo,
    )
    send_a, mid, send_b, stat1 = apply_terms(
        n, place, (k0x,), mats, weights, moved, late_slots, 2 * halo, halo,
        carry=(acc, stat1),
    )
    recv_a, recv_b = neighbours(send_a, send_b, "strip")
    q, col_a, col_b = merge_rows(strips, place, send_a, mid, send_b, recv_a, recv_b, halo)
    recv_a, recv_b = neighbours(col_a, col_b, "frame")
    k1x, k1, k11_part = merge_cols(n, rows, place, q, recv_a, recv_b, k0x, halo)

    send_a, mid, send_b, stat2 = apply_terms(
        n, place, (k1x,), mats, weights, moved, slots + late_slots, halo, halo
    )
    recv_a, recv_b = neighbours(send_a, send_b, "strip")
    sums = jnp.stack([k00_part, stat1, k11_part, stat2])
    for axis, size in (("frame", n), ("strip", strips)):
        d = 1
        while d < size:
            sums = sums + swap(sums, axis, d)
            d *= 2
    k2 = wrap(place, send_a, mid, send_b, recv_a, recv_b, k1, halo)

    def gathered(x):
        parts = [x] + [None] * (n - 1)
        for i in range(n):
            for d in reversed(distances):
                if i % (2 * d) == 0:
                    parts[i + d] = swap(parts[i], "frame", d)
        return parts

    g0, g1, g2 = gathered(k0), gathered(k1), gathered(k2)
    result, base, coef = solution_image(place, estimate, sums, g0, g1)
    return result, residual_image(place, base, coef, g2, halo)


def solution(mesh):
    return jax.shard_map(
        steps,
        mesh=mesh,
        in_specs=(
            P("strip", None),
            P("frame", "strip", None),
            P("frame", "strip", None),
            P("frame", None),
            P("frame", None),
        ),
        out_specs=(P("strip", None), P("strip", None)),
        check_vma=False,
    )
```

```python
import functools

import jax
import jax.numpy as jnp
from jax import lax
from jax.experimental import pallas as pl
from jax.experimental.pallas import tpu as pltpu
from jax.sharding import PartitionSpec as P


damping = 0.05
f32 = jnp.float32
bf16 = jnp.bfloat16
LANE = 128
VMEM = pl.BlockSpec(memory_space=pltpu.VMEM)
ANY = pl.BlockSpec(memory_space=pl.ANY)
SMEM = pl.BlockSpec(memory_space=pltpu.SMEM)
HBM = pl.BlockSpec(memory_space=pltpu.HBM)


def room(mib):
    return pltpu.CompilerParams(vmem_limit_bytes=mib * 2**20)


def split(x):
    hi = x.astype(bf16)
    lo = (x - hi.astype(f32)).astype(bf16)
    return hi, lo


def dot(a, b):
    return jnp.dot(a, b, preferred_element_type=f32)


def choose(flag, a, b):
    return jnp.where(jnp.full(a.shape, flag, jnp.int32) == 1, a, b)


def pack_edge(edge, halo, w):
    rows = edge.shape[0]
    per = LANE // (2 * halo)
    short = rows * 2 * halo // w
    edge = pltpu.roll(edge, halo, 1)
    lane = lax.broadcasted_iota(jnp.int32, (short, LANE), 1)
    out = []
    for t in range(w // LANE):
        tile = None
        for p in range(per):
            k = t * per + p
            part = edge[k * short : (k + 1) * short]
            part = pltpu.roll(part, p * 2 * halo, 1) if p else part
            tile = part if tile is None else jnp.where(lane >= p * 2 * halo, part, tile)
        out.append(tile)
    return jnp.concatenate(out, axis=1)


def unpack_edge(packed, halo):
    _, w = packed.shape
    per = LANE // (2 * halo)
    parts = []
    for k in range(w // (2 * halo)):
        t, p = divmod(k, per)
        part = packed[:, t * LANE : (t + 1) * LANE]
        back = (LANE - halo - p * 2 * halo) % LANE
        parts.append(pltpu.roll(part, back, 1) if back else part)
    return jnp.concatenate(parts, axis=0)


def tiles(width, step=256):
    return [(s, min(step, width - s)) for s in range(0, width, step)]


def toeplitz(base, count):
    wide = base.shape[1]
    return pltpu.roll(jnp.broadcast_to(base, (count, wide)), 0, 1, stride=1, stride_axis=0)


def build_group(taps, g, frames, rows, halo, t_ref, b_ref, bp_ref, ta_ref):
    ext = rows + 2 * halo
    unit = taps / jnp.sum(taps, axis=1, keepdims=True)
    for s in range(frames):
        f = g * frames + s
        col = unit[s : s + 1]
        row = unit[frames + s : frames + s + 1]
        by_rows = toeplitz(row, rows)
        hi, lo = split(by_rows)
        t_ref[f, :rows, :] = hi
        t_ref[f, rows:, :] = lo
        hi, lo = split(by_rows.T[:ext])
        ta_ref[g, :ext, s * rows : (s + 1) * rows] = hi
        ta_ref[g, ext:, s * rows : (s + 1) * rows] = lo
        hi, lo = split(toeplitz(col, LANE).T)
        b_ref[f, :, :LANE] = hi
        b_ref[f, :, LANE:] = lo
        hi, lo = split(toeplitz(pltpu.roll(col, LANE, 1), 2 * LANE)[:, :LANE])
        bp_ref[f, :, :LANE] = hi
        bp_ref[f, :, LANE:] = lo


def matrix_shapes(groups, frames, rows, halo):
    ext = rows + 2 * halo
    return [
        jax.ShapeDtypeStruct(s, bf16)
        for s in (
            (groups * frames, 2 * rows, 2 * LANE),
            (groups * frames, 2 * LANE, 2 * LANE),
            (groups * frames, 2 * LANE, 2 * LANE),
            (groups, 2 * ext, frames * rows),
        )
    ]


def tile_height(frames):
    return -(-2 * frames // 8) * 8


def setup_kernel(frames, rows, halo, starts, *refs):
    tiles_in = refs[: len(starts)]
    mats, taps, sem = refs[len(starts) : -2], refs[-2], refs[-1]
    height = tile_height(frames)

    def copy(g):
        source = tiles_in[g].at[pl.ds(starts[g], height), pl.ds(0, 2 * LANE)]
        return pltpu.make_async_copy(source, taps.at[g], sem.at[g])

    for g in range(len(starts)):
        copy(g).start()
    for g in range(len(starts)):
        copy(g).wait()
        build_group(taps[g], g, frames, rows, halo, *mats)


def setup_matrices(tiles_in, starts, frames, rows, halo):
    groups = len(tiles_in)
    return pl.pallas_call(
        functools.partial(setup_kernel, frames, rows, halo, starts),
        out_shape=matrix_shapes(groups, frames, rows, halo),
        in_specs=[ANY] * groups,
        out_specs=[VMEM] * 4,
        scratch_shapes=[
            pltpu.VMEM((groups, tile_height(frames), 2 * LANE), f32),
            pltpu.SemaphoreType.DMA((groups,)),
        ],
        compiler_params=room(24),
        name="setup_all",
    )(*tiles_in)


def load_image(y_hi, y_lo, image, halo):
    ext, full = image.shape
    shift = LANE - halo
    y = pltpu.roll(image, full - shift, 1)[:, : full - LANE]
    hi, lo = split(y)
    y_hi[:ext, :] = hi
    y_lo[:ext, :] = lo


def group_terms(frames, rows, w, y_hi, y_lo, t, b, bp, ta, weight, data, us, qs, vs_hi, vs_lo, acc, stat, ready=None):
    total = None
    for f in range(frames):
        for c, size in tiles(w + LANE):
            r1 = dot(t(f)[...], y_hi[:, c : c + size])
            r2 = dot(t(f)[:rows, :], y_lo[:, c : c + size])
            hi, lo = split(r1[:rows] + r1[rows:] + r2)
            us[:rows, c : c + size] = hi
            us[rows:, c : c + size] = lo
        if ready is not None:
            ready(f)
        for k in range(w // LANE):
            c = k * LANE
            r = dot(us[:, c : c + 2 * LANE], b(f)[...])
            a = r[:rows, :LANE] + r[:rows, LANE:] + r[rows:, :LANE]
            if data is not None:
                a = a - data(f)[:, c : c + LANE]
            q = weight(f)[:, c : c + LANE] * a
            if stat is not None:
                part = jnp.sum((a * q).reshape(rows // 8, 8, LANE), axis=0)
                total = part if total is None else total + part
            hi, lo = split(q)
            qs[:rows, c + LANE : c + 2 * LANE] = hi
            qs[rows:, c + LANE : c + 2 * LANE] = lo
        for k in range(w // LANE + 1):
            c = k * LANE
            r = dot(qs[:, c : c + 2 * LANE], bp(f)[...])
            hi, lo = split(r[:rows, :LANE] + r[:rows, LANE:] + r[rows:, :LANE])
            vs_hi[f * rows : (f + 1) * rows, c : c + LANE] = hi
            vs_lo[f * rows : (f + 1) * rows, c : c + LANE] = lo
    ext = acc.shape[0]
    for c, size in tiles(w + LANE):
        r1 = dot(ta[...], vs_hi[:, c : c + size])
        r2 = dot(ta[:ext, :], vs_lo[:, c : c + size])
        acc[:, c : c + size] += r1[:ext] + r1[ext:] + r2
    if stat is not None:
        stat[...] += total


def work_scratch(frames, rows, halo, w):
    ext = rows + 2 * halo
    return [
        pltpu.VMEM((2 * LANE, w + LANE), bf16),
        pltpu.VMEM((2 * LANE, w + LANE), bf16),
        pltpu.VMEM((2 * rows, w + LANE), bf16),
        pltpu.VMEM((2 * rows, w + 2 * LANE), bf16),
        pltpu.VMEM((frames * rows, w + LANE), bf16),
        pltpu.VMEM((frames * rows, w + LANE), bf16),
        pltpu.VMEM((ext, w + LANE), f32),
    ]


def clear_edges(y_hi, y_lo, qs, ext, rows, w):
    zero = jnp.zeros((y_hi.shape[0] - ext, y_hi.shape[1]), bf16)
    y_hi[ext:, :] = zero
    y_lo[ext:, :] = zero
    qs[:, :LANE] = jnp.zeros((2 * rows, LANE), bf16)
    qs[:, w + LANE :] = jnp.zeros((2 * rows, LANE), bf16)


def unshift(acc, halo):
    return pltpu.roll(acc, acc.shape[1] - halo, 1)


def first_kernel(
    frames, rows, halo,
    place, est, recv_a, recv_b, t_ref, b_ref, bp_ref, ta_ref, w_hbm, d_hbm,
    send_a, mid, send_b,
    y_hi, y_lo, us, qs, vs_hi, vs_lo, acc, wbuf, dbuf, sem,
):
    ext = rows + 2 * halo
    cols = est.shape[1]
    copies = [
        (
            pltpu.make_async_copy(w_hbm.at[f], wbuf.at[f], sem.at[0, f]),
            pltpu.make_async_copy(d_hbm.at[f], dbuf.at[f], sem.at[1, f]),
        )
        for f in range(frames)
    ]
    for pair in copies:
        for c in pair:
            c.start()
    clear_edges(y_hi, y_lo, qs, ext, rows, cols)
    odd = lax.rem(place[1], 2)
    none = jnp.zeros((ext, LANE), f32)
    for start in range(0, cols, 4 * LANE):
        size = 4 * LANE + LANE
        left = max(start - LANE, 0)
        span = slice(left, min(start + 4 * LANE, cols))
        x = jnp.concatenate(
            [
                choose(odd, recv_a[:, span], recv_b[:, span]),
                est[:, span],
                choose(odd, recv_b[:, span], recv_a[:, span]),
            ],
            axis=0,
        )
        if start == 0:
            x = jnp.concatenate([none, x], axis=1)
        if x.shape[1] < size:
            x = jnp.concatenate([x, jnp.zeros((ext, size - x.shape[1]), f32)], axis=1)
        hi, lo = split(pltpu.roll(x, halo, 1)[:, LANE:])
        y_hi[:ext, start : start + 4 * LANE] = hi
        y_lo[:ext, start : start + 4 * LANE] = lo
        if start + 4 * LANE >= cols:
            tail = jnp.concatenate([x[:, 4 * LANE :], none], axis=1)
            hi, lo = split(pltpu.roll(tail, halo, 1)[:, LANE:])
            y_hi[:ext, cols:] = hi
            y_lo[:ext, cols:] = lo
    acc[...] = jnp.zeros_like(acc)

    def ready(f):
        for c in copies[f]:
            c.wait()

    group_terms(
        frames, rows, cols, y_hi, y_lo,
        lambda f: t_ref.at[f], lambda f: b_ref.at[f], lambda f: bp_ref.at[f], ta_ref.at[0],
        lambda f: wbuf.at[f], lambda f: dbuf.at[f],
        us, qs, vs_hi, vs_lo, acc, None, ready,
    )
    for start in range(0, cols, 4 * LANE):
        size = min(4 * LANE, cols - start)
        z = pltpu.roll(acc[:, start : start + size + LANE], size + LANE - halo, 1)[:, :size]
        span = slice(start, start + size)
        low, high = z[:halo], z[halo + rows :]
        send_a[:, span] = choose(odd, low, high)
        send_b[:, span] = choose(odd, high, low)
        mid[:, span] = z[halo : halo + rows]


def first_terms(place, est, recv_a, recv_b, mats, weights, observed):
    frames, rows, cols = weights.shape
    halo = recv_a.shape[0]
    return pl.pallas_call(
        functools.partial(first_kernel, frames, rows, halo),
        out_shape=[
            jax.ShapeDtypeStruct((halo, cols), f32),
            jax.ShapeDtypeStruct((rows, cols), f32),
            jax.ShapeDtypeStruct((halo, cols), f32),
        ],
        in_specs=[SMEM] + [VMEM] * 7 + [HBM, HBM],
        out_specs=[VMEM] * 3,
        scratch_shapes=work_scratch(frames, rows, halo, cols)
        + [
            pltpu.VMEM((frames, rows, cols), f32),
            pltpu.VMEM((frames, rows, cols), f32),
            pltpu.SemaphoreType.DMA((2, frames)),
        ],
        cost_estimate=pl.CostEstimate(flops=8 * 10**9, bytes_accessed=8 * 2**20, transcendentals=0),
        compiler_params=room(36),
        name="first_terms",
    )(place, est, recv_a, recv_b, *mats, weights, observed)


def prepare_kernel(plan, frames, rows, halo, w, place, cols_in, rows_in, weights, *refs):
    outs, tile, mats = refs[: len(plan)], refs[len(plan)], refs[len(plan) + 1 : -4]
    cols_buf, rows_buf, taps_sem, sem = refs[-4:]
    taps = cols_in.shape[1]
    taps_copies = (
        pltpu.make_async_copy(cols_in, cols_buf, taps_sem.at[0]),
        pltpu.make_async_copy(rows_in, rows_buf, taps_sem.at[1]),
    )
    for copy in taps_copies:
        copy.start()
    pending = []
    for i, (distance, _) in enumerate(plan):
        start = pl.multiple_of(jnp.bitwise_xor(place[0], distance) * w, LANE)
        for k in range(frames):
            copy = pltpu.make_async_copy(
                weights.at[k, :, pl.ds(start, w)],
                outs[i].at[pl.ds(k * rows, rows), :],
                sem.at[i, k],
            )
            copy.start()
            pending.append(copy)
    tile[...] = jnp.zeros_like(tile)
    for copy in taps_copies:
        copy.wait()
    tile[:frames, :taps] = cols_buf[...]
    tile[frames : 2 * frames, :taps] = rows_buf[...]
    for i, (_, with_taps) in enumerate(plan):
        if with_taps:
            outs[i][frames * rows :, :] = tile[...]
    build_group(tile[:, : 2 * LANE], 0, frames, rows, halo, *mats)
    for copy in pending:
        copy.wait()


def prepare(plan, place, column_kernels, row_kernels, weights, w, halo):
    frames, rows, _ = weights.shape
    height = tile_height(frames)
    out = pl.pallas_call(
        functools.partial(prepare_kernel, plan, frames, rows, halo, w),
        out_shape=[
            jax.ShapeDtypeStruct((frames * rows + (height if taps else 0), w), f32)
            for _, taps in plan
        ]
        + [jax.ShapeDtypeStruct((height, w), f32)]
        + matrix_shapes(1, frames, rows, halo),
        in_specs=[SMEM, HBM, HBM, HBM],
        out_specs=[VMEM] * (len(plan) + 5),
        scratch_shapes=[
            pltpu.VMEM(column_kernels.shape, f32),
            pltpu.VMEM(row_kernels.shape, f32),
            pltpu.SemaphoreType.DMA((2,)),
            pltpu.SemaphoreType.DMA((len(plan), frames)),
        ],
        compiler_params=room(24),
        name="prepare",
    )(place, column_kernels, row_kernels, weights)
    return out[: len(plan)], out[len(plan)], out[len(plan) + 1 :]


def blocks_kernel(n, halo, w, place, send_a, mid, send_b, recv_a, recv_b, *refs):
    outs, full = refs[:-1], refs[-1]
    rows, cols = mid.shape
    odd = lax.rem(place[1], 2)
    inner = slice(LANE, LANE + cols)
    for end in (0, LANE + cols):
        full[:, end : end + LANE] = jnp.zeros((rows, LANE), f32)
    full[:halo, inner] = mid[:halo, :] + choose(odd, recv_a[...], recv_b[...])
    full[halo : rows - halo, inner] = mid[halo : rows - halo, :]
    full[rows - halo :, inner] = mid[rows - halo :, :] + choose(odd, recv_b[...], recv_a[...])
    lane = lax.broadcasted_iota(jnp.int32, (rows, LANE), 1)
    for i in range(n):
        start = jnp.bitwise_xor(place[0], i) * w
        outs[i][:rows, :] = full[:, pl.ds(pl.multiple_of(start + LANE, LANE), w)]
        before = full[:, pl.ds(pl.multiple_of(start, LANE), LANE)]
        after = full[:, pl.ds(pl.multiple_of(start + LANE + w, LANE), LANE)]
        outs[i][rows:, :] = pack_edge(jnp.where(lane >= LANE - halo, before, after), halo, w)


def column_blocks(n, place, send_a, mid, send_b, recv_a, recv_b, w):
    rows, cols = mid.shape
    halo = send_a.shape[0]
    height = rows + rows * 2 * halo // w
    return pl.pallas_call(
        functools.partial(blocks_kernel, n, halo, w),
        out_shape=[jax.ShapeDtypeStruct((height, w), f32)] * n,
        in_specs=[SMEM] + [VMEM] * 5,
        out_specs=[VMEM] * n,
        scratch_shapes=[pltpu.VMEM((rows, cols + 2 * LANE), f32)],
        compiler_params=room(16),
        name="column_blocks",
    )(place, send_a, mid, send_b, recv_a, recv_b)


def start_kernel(n, rows, halo, w, place, est, *refs):
    parts = refs[:-5]
    k0, wide, send_a, send_b, stat = refs[-5:]
    total = parts[0][...]
    for p in parts[1:]:
        total = total + p[...]
    me = place[0]
    odd = lax.rem(place[1], 2)
    at = lambda start, size: est[:, pl.ds(pl.multiple_of(start, LANE), size)]
    own = -(total[:rows] + damping * at(me * w, w))
    edge = unpack_edge(total[rows:], halo)
    before = at(jnp.maximum(me * w - LANE, 0), LANE)
    after = at(jnp.minimum(me * w + w, (n * w) - LANE), LANE)
    none = jnp.zeros((rows, LANE), f32)
    left = choose((me > 0).astype(jnp.int32), -(edge + damping * before), none)
    right = choose((me < n - 1).astype(jnp.int32), -(edge + damping * after), none)
    k0[...] = own
    wide[:, :LANE] = left
    wide[:, LANE : LANE + w] = own
    wide[:, LANE + w :] = right
    low, high = wide[:halo, :], wide[rows - halo :, :]
    send_a[...] = choose(odd, low, high)
    send_b[...] = choose(odd, high, low)
    square = own * own
    acc = square[:, :LANE]
    for c in range(LANE, w, LANE):
        acc = acc + square[:, c : c + LANE]
    stat[...] = jnp.sum(acc.reshape(rows // 8, 8, LANE), axis=0)


def start_image(n, place, est, parts, halo):
    rows, cols = est.shape
    w = cols // n
    return pl.pallas_call(
        functools.partial(start_kernel, n, rows, halo, w),
        out_shape=[
            jax.ShapeDtypeStruct((rows, w), f32),
            jax.ShapeDtypeStruct((rows, w + 2 * LANE), f32),
            jax.ShapeDtypeStruct((halo, w + 2 * LANE), f32),
            jax.ShapeDtypeStruct((halo, w + 2 * LANE), f32),
            jax.ShapeDtypeStruct((8, LANE), f32),
        ],
        in_specs=[SMEM] + [VMEM] * (1 + len(parts)),
        out_specs=[VMEM] * 5,
        compiler_params=room(12),
        name="start_image",
    )(place, est, *parts)


def apply_kernel(n, frames, rows, halo, w, slots, cut, count, pieces, carried, place, *refs):
    image, refs = refs[:pieces], refs[pieces:]
    t_hbm, b_hbm, bp_hbm, ta_hbm, own = refs[:5]
    moved, refs = refs[5 : 5 + count], refs[5 + count :]
    if carried:
        (acc_in, stat_in), refs = refs[:2], refs[2:]
    if cut is None:
        (acc_out, stat), refs = refs[:2], refs[2:]
    else:
        (send_a, mid, send_b, stat), refs = refs[:4], refs[4:]
    if pieces > 1:
        whole, refs = refs[0], refs[1:]
    y_hi, y_lo, us, qs, vs_hi, vs_lo, acc, tb, bb, bpb, tab, wbuf, sem, wsem = refs
    odd = lax.rem(place[1], 2)
    ext = rows + 2 * halo
    quarter = n // 4
    inner = ((place[0] >= quarter) & (place[0] < n - quarter)).astype(jnp.int32)

    def copies(i, g):
        span = pl.ds(g * frames, frames)
        return [
            pltpu.make_async_copy(t_hbm.at[span], tb.at[i], sem.at[0, i]),
            pltpu.make_async_copy(b_hbm.at[span], bb.at[i], sem.at[1, i]),
            pltpu.make_async_copy(bp_hbm.at[span], bpb.at[i], sem.at[2, i]),
            pltpu.make_async_copy(ta_hbm.at[g], tab.at[i], sem.at[3, i]),
        ]

    mine = pl.ds(pl.multiple_of(place[0] * w, LANE), w)
    for i, (distance, late, sources) in enumerate(slots):
        if len(sources) == 2:
            group = distance + (1 - inner if late else inner) * quarter
        else:
            group = distance
        for c in copies(i, group):
            c.start()
        for f in range(frames):
            if not sources:
                pltpu.make_async_copy(own.at[f, :, mine], wbuf.at[i, f], wsem.at[i, f]).start()
                continue
            picked = []
            for source in sources:
                ref, row = source[f]
                picked.append(moved[ref].at[pl.ds(row, rows), :])
            if len(picked) == 1:
                pltpu.make_async_copy(picked[0], wbuf.at[i, f], wsem.at[i, f]).start()
                continue
            for k in range(2):

                @pl.when((group - distance) == k * quarter)
                def _(source=picked[k], i=i, f=f):
                    pltpu.make_async_copy(source, wbuf.at[i, f], wsem.at[i, f]).start()

    clear_edges(y_hi, y_lo, qs, ext, rows, w)
    if pieces > 1:
        wide, recv_a, recv_b = image
        whole[:halo, :] = choose(odd, recv_a[...], recv_b[...])
        whole[halo : halo + rows, :] = wide[...]
        whole[halo + rows :, :] = choose(odd, recv_b[...], recv_a[...])
        load_image(y_hi, y_lo, whole[...], halo)
    else:
        load_image(y_hi, y_lo, image[0][...], halo)
    acc[...] = acc_in[...] if carried else jnp.zeros_like(acc)
    stat[...] = stat_in[...] if carried else jnp.zeros_like(stat)

    @pl.loop(0, len(slots))
    def _(i):
        for c in copies(i, 0):
            c.wait()
        for f in range(frames):
            pltpu.make_async_copy(own.at[f, :, mine], wbuf.at[i, f], wsem.at[i, f]).wait()
        group_terms(
            frames, rows, w, y_hi, y_lo,
            lambda f: tb.at[i, f], lambda f: bb.at[i, f], lambda f: bpb.at[i, f], tab.at[i],
            lambda f: wbuf.at[i, f], None,
            us, qs, vs_hi, vs_lo, acc, stat,
        )

    if cut is None:
        acc_out[...] = acc[...]
    else:
        z = unshift(acc[...], halo)
        send_a[...] = choose(odd, z[:cut], z[ext - cut :])
        send_b[...] = choose(odd, z[ext - cut :], z[:cut])
        mid[...] = z[cut : ext - cut]


def apply_terms(n, place, image, mats, weights, moved, slots, cut, halo, carry=()):
    frames, rows, _ = weights.shape
    w = image[0].shape[1] - 2 * LANE
    ext = rows + 2 * halo
    t, b, bp, ta = mats
    count = len(slots)
    wide = w + LANE
    shapes = [(ext, wide)] if cut is None else [(cut, wide), (ext - 2 * cut, wide), (cut, wide)]
    shapes += [(8, LANE)] + [(ext, w + 2 * LANE)] * (len(image) > 1)
    return pl.pallas_call(
        functools.partial(
            apply_kernel, n, frames, rows, halo, w, slots, cut, len(moved), len(image), bool(carry)
        ),
        out_shape=[jax.ShapeDtypeStruct(s, f32) for s in shapes],
        in_specs=[SMEM]
        + [VMEM] * len(image)
        + [ANY] * 4
        + [HBM]
        + [ANY] * len(moved)
        + [VMEM] * len(carry),
        out_specs=[VMEM] * len(shapes),
        scratch_shapes=work_scratch(frames, rows, halo, w)
        + [
            pltpu.VMEM((count, frames) + t.shape[1:], bf16),
            pltpu.VMEM((count, frames) + b.shape[1:], bf16),
            pltpu.VMEM((count, frames) + bp.shape[1:], bf16),
            pltpu.VMEM((count,) + ta.shape[1:], bf16),
            pltpu.VMEM((count, frames, rows, w), f32),
            pltpu.SemaphoreType.DMA((4, count)),
            pltpu.SemaphoreType.DMA((count, frames)),
        ],
        cost_estimate=pl.CostEstimate(
            flops=count * 3 * 10**9, bytes_accessed=count * 2**20, transcendentals=0
        ),
        compiler_params=room(28),
    )(place, *image, t, b, bp, ta, weights, *moved, *carry)


def rows_kernel(strips, halo, w, place, send_a, mid, send_b, recv_a, recv_b, q, col_a, col_b):
    odd = lax.rem(place[1], 2)
    odd_col = lax.rem(place[0], 2)
    edge_rows, wide = send_a.shape
    ext = q.shape[0]
    row = lax.broadcasted_iota(jnp.int32, (edge_rows, wide), 0)
    strip = jnp.full((edge_rows, wide), place[1], jnp.int32)
    low = choose(odd, send_a[...], send_b[...]) + choose(odd, recv_a[...], recv_b[...])
    high = choose(odd, send_b[...], send_a[...]) + choose(odd, recv_b[...], recv_a[...])
    q[:edge_rows, :] = jnp.where((row >= halo) | (strip > 0), low, 0.0)
    q[edge_rows : ext - edge_rows, :] = mid[...]
    q[ext - edge_rows :, :] = jnp.where((row < edge_rows - halo) | (strip < strips - 1), high, 0.0)
    lane = lax.broadcasted_iota(jnp.int32, (ext, LANE), 1)
    edge = q[:, w:]
    to_left = jnp.where(lane < halo, q[:, :LANE], edge)
    to_right = jnp.where(lane >= LANE - halo, q[:, w - LANE : w], edge)
    col_a[...] = choose(odd_col, to_left, to_right)
    col_b[...] = choose(odd_col, to_right, to_left)


def merge_rows(strips, place, send_a, mid, send_b, recv_a, recv_b, halo):
    ext = mid.shape[0] + 2 * send_a.shape[0]
    wide = mid.shape[1]
    return pl.pallas_call(
        functools.partial(rows_kernel, strips, halo, wide - LANE),
        out_shape=[
            jax.ShapeDtypeStruct((ext, wide), f32),
            jax.ShapeDtypeStruct((ext, LANE), f32),
            jax.ShapeDtypeStruct((ext, LANE), f32),
        ],
        in_specs=[SMEM] + [VMEM] * 5,
        out_specs=[VMEM] * 3,
        compiler_params=room(8),
        name="merge_rows",
    )(place, send_a, mid, send_b, recv_a, recv_b)


def cols_kernel(n, rows, halo, place, q, recv_a, recv_b, before, out, block, stat):
    odd = lax.rem(place[0], 2)
    ext, wide = q.shape
    w = wide - LANE
    lane = lax.broadcasted_iota(jnp.int32, (ext, LANE), 1)
    at = jnp.full((ext, LANE), place[0], jnp.int32)
    left = choose(odd, recv_a[...], recv_b[...])
    right = choose(odd, recv_b[...], recv_a[...])
    edge = q[:, w:]
    total = None
    out[:, :LANE] = jnp.where(at > 0, edge + left, 0.0) + damping * before[:, :LANE]
    out[:, LANE + w :] = jnp.where(at < n - 1, edge + right, 0.0) + damping * before[:, LANE + w :]
    for c in range(0, w, LANE):
        x = q[:, c : c + LANE] + damping * before[:, c + LANE : c + 2 * LANE]
        if c == 0:
            x = x + jnp.where(lane < halo, left, 0.0)
        if c == w - LANE:
            x = x + jnp.where(lane >= LANE - halo, right, 0.0)
        out[:, c + LANE : c + 2 * LANE] = x
        own = x[halo : halo + rows]
        block[:, c : c + LANE] = own
        part = jnp.sum((own * own).reshape(rows // 8, 8, LANE), axis=0)
        total = part if total is None else total + part
    stat[...] = total


def merge_cols(n, rows, place, q, recv_a, recv_b, before, halo):
    ext, wide = q.shape
    w = wide - LANE
    return pl.pallas_call(
        functools.partial(cols_kernel, n, rows, halo),
        out_shape=[
            jax.ShapeDtypeStruct((ext, w + 2 * LANE), f32),
            jax.ShapeDtypeStruct((rows, w), f32),
            jax.ShapeDtypeStruct((8, LANE), f32),
        ],
        in_specs=[SMEM] + [VMEM] * 4,
        out_specs=[VMEM] * 3,
        compiler_params=room(10),
        name="merge_cols",
    )(place, q, recv_a, recv_b, before)


def wrap_kernel(rows, halo, w, place, send_a, mid, send_b, recv_a, recv_b, before, out):
    odd = lax.rem(place[1], 2)
    keep = rows - 2 * halo
    pieces = (
        (0, halo, mid[:halo, :] + choose(odd, recv_a[...], recv_b[...])),
        (halo, keep, mid[halo : rows - halo, :]),
        (rows - halo, halo, mid[rows - halo :, :] + choose(odd, recv_b[...], recv_a[...])),
    )
    edges = []
    for start, size, value in pieces:
        span = slice(start, start + size)
        out[span, :] = value[:, :w] + damping * before[span, :]
        edges.append(value[:, w:])
    out[rows:, :] = pack_edge(jnp.concatenate(edges, axis=0), halo, w)


def wrap(place, send_a, mid, send_b, recv_a, recv_b, before, halo):
    rows, w = before.shape
    height = rows + rows * 2 * halo // w
    return pl.pallas_call(
        functools.partial(wrap_kernel, rows, halo, w),
        out_shape=jax.ShapeDtypeStruct((height, w), f32),
        in_specs=[SMEM] + [VMEM] * 6,
        out_specs=VMEM,
        compiler_params=room(8),
        name="wrap",
    )(place, send_a, mid, send_b, recv_a, recv_b, before)


def solution_kernel(n, w, place, est, sums, *refs):
    k0, k1 = refs[:n], refs[n : 2 * n]
    sol, res, coef = refs[2 * n :]
    total = [
        jnp.sum(jnp.sum(sums[i], axis=0, keepdims=True), axis=1, keepdims=True) for i in range(4)
    ]
    k00, k11 = total[0], total[2]
    k01 = total[1] + damping * k00
    k12 = total[3] + damping * k11
    alpha0 = k00 / k01
    norm1 = k00 - 2.0 * alpha0 * k01 + alpha0 * alpha0 * k11
    beta = norm1 / k00
    curve1 = (1.0 + beta) * (1.0 + beta) * k01 - 2.0 * (1.0 + beta) * alpha0 * k11
    curve1 = curve1 + alpha0 * alpha0 * k12
    alpha1 = norm1 / curve1
    c1 = alpha0 + alpha1 * (1.0 + beta)
    c2 = alpha0 * alpha1
    coef[...] = jnp.broadcast_to(c2, coef.shape)
    for i in range(n):
        cols = pl.ds(pl.multiple_of(jnp.bitwise_xor(place[0], i) * w, LANE), w)
        a0, a1 = k0[i][...], k1[i][...]
        sol[:, cols] = est[:, cols] + c1 * a0 - c2 * a1
        res[:, cols] = a0 - c1 * a1


def solution_image(place, est, sums, k0, k1):
    n = len(k0)
    w = k0[0].shape[1]
    return pl.pallas_call(
        functools.partial(solution_kernel, n, w),
        out_shape=[jax.ShapeDtypeStruct(est.shape, f32)] * 2
        + [jax.ShapeDtypeStruct((8, LANE), f32)],
        in_specs=[SMEM] + [VMEM] * (2 + 2 * n),
        out_specs=[VMEM] * 3,
        compiler_params=room(20),
        name="solution_image",
    )(place, est, sums, *k0, *k1)


def residual_kernel(n, rows, halo, w, place, base, coef, *refs):
    k2, (res, full) = refs[:n], refs[n:]
    c2 = coef[0:1, 0:1]
    lane = lax.broadcasted_iota(jnp.int32, (rows, LANE), 1)
    spot = [jnp.bitwise_xor(place[0], i) for i in range(n)]
    full[:, :LANE] = jnp.zeros((rows, LANE), f32)
    full[:, LANE + n * w :] = jnp.zeros((rows, LANE), f32)
    for i in range(n):
        full[:, pl.ds(pl.multiple_of(spot[i] * w + LANE, LANE), w)] = k2[i][:rows, :]
    for i in range(n):
        edge = unpack_edge(k2[i][rows:, :], halo)
        left = pl.ds(pl.multiple_of(spot[i] * w, LANE), LANE)
        right = pl.ds(pl.multiple_of(spot[i] * w + w + LANE, LANE), LANE)
        full[:, left] += jnp.where(lane >= LANE - halo, edge, 0.0)
        full[:, right] += jnp.where(lane < halo, edge, 0.0)
    for c in range(0, n * w, LANE):
        res[:, c : c + LANE] = base[:, c : c + LANE] + c2 * full[:, c + LANE : c + 2 * LANE]


def residual_image(place, base, coef, k2, halo):
    n = len(k2)
    rows, cols = base.shape
    w = cols // n
    return pl.pallas_call(
        functools.partial(residual_kernel, n, rows, halo, w),
        out_shape=jax.ShapeDtypeStruct(base.shape, f32),
        in_specs=[SMEM] + [VMEM] * (2 + n),
        out_specs=VMEM,
        scratch_shapes=[pltpu.VMEM((rows, cols + 2 * LANE), f32)],
        compiler_params=room(16),
        name="residual_image",
    )(place, base, coef, *k2)


def neighbours(send_a, send_b, axis):
    n = lax.axis_size(axis)
    out = []
    for lead, x in ((0, send_a), (1, send_b)):
        pairs = [(i, i + 1) for i in range(lead, n - 1, 2)]
        out.append(lax.ppermute(x, axis, pairs + [(b, a) for a, b in pairs]))
    return out


def swap(x, axis, distance):
    n = lax.axis_size(axis)
    return lax.ppermute(x, axis, [(i, i ^ distance) for i in range(n)])


def steps(estimate, observed, weights, column_kernels, row_kernels):
    n = lax.axis_size("frame")
    me = lax.axis_index("frame")
    strips = lax.axis_size("strip")
    strip = lax.axis_index("strip")
    place = jnp.stack([me, strip]).astype(jnp.int32)
    rows, cols = estimate.shape
    frames = weights.shape[0]
    halo = column_kernels.shape[1] // 2
    stay = lambda x: pltpu.with_memory_space_constraint(x, pltpu.HBM)
    weights, observed = stay(weights), stay(observed)
    column_kernels, row_kernels = stay(column_kernels), stay(row_kernels)
    w = cols // n
    distances = [1 << k for k in range(n.bit_length() - 1)]

    low, high = estimate[:halo], estimate[rows - halo :]
    odd = strip % 2 == 1
    est_a, est_b = neighbours(
        jnp.where(odd, low, high), jnp.where(odd, high, low), "strip"
    )

    half, quarter = n // 2, n // 4
    plan = [(d, d < half) for d in range(1, n)]
    packed, tile, own_mats = prepare(plan, place, column_kernels, row_kernels, weights, w, halo)
    far_tiles = []
    for d in range(half, n):
        far_tiles.append(swap(tile[:, : 2 * LANE], "frame", d))
    moved = []

    def move(x, pairs, lead=0):
        moved.append(lax.ppermute(x, "frame", pairs))
        return tuple((len(moved) - 1, k * rows) for k in range(frames - lead))

    slots = [(0, False, ())]
    for d in range(1, half):
        slots.append((d, False, (move(packed[d - 1], [(i, i ^ d) for i in range(n)]),)))
    middle = range(quarter, n - quarter)
    where = {}
    for d in range(half, n):
        pairs = [(i, i ^ d) for i in middle]
        where[d, False] = move(packed[d - 1], pairs)
    early_count = len(moved)
    lead = frames // 2
    for d in range(half, n):
        pairs = [(i, i ^ d) for i in range(n) if i not in middle]
        x = packed[d - 1]
        if d == half and lead:
            ahead = move(x[: lead * rows], pairs, frames - lead)
            where[d, True] = ahead + move(x[lead * rows :], pairs, lead)
        else:
            where[d, True] = move(x, pairs)
    late_slots = []
    for late, out in ((False, slots), (True, late_slots)):
        for u in range(half, half + quarter):
            out.append((u, late, (where[u, late], where[u + quarter, late])))
    starts = [0] + [frames * rows] * (half - 1) + [0] * half

    send_a, mid, send_b = first_terms(
        place, estimate, est_a, est_b, own_mats, weights, observed
    )
    mats = setup_matrices(
        [tile] + moved[: half - 1] + far_tiles, starts, frames, rows, halo
    )
    recv_a, recv_b = neighbours(send_a, send_b, "strip")

    part = list(column_blocks(n, place, send_a, mid, send_b, recv_a, recv_b, w))
    mine = [part[0]]
    for i in range(n - 1, 0, -1):
        d = i & -i
        got = swap(part[i], "frame", d)
        if i == d:
            mine.append(got)
        else:
            part[i ^ d] = part[i ^ d] + got
    k0, wide, send_a, send_b, k00_part = start_image(n, place, estimate, mine, halo)
    recv_a, recv_b = neighbours(send_a, send_b, "strip")

    acc, stat1, k0x = apply_terms(
        n, place, (wide, recv_a, recv_b), mats, weights, moved[:early_count],
        slots, None, halo,
    )
    send_a, mid, send_b, stat1 = apply_terms(
        n, place, (k0x,), mats, weights, moved, late_slots, 2 * halo, halo,
        carry=(acc, stat1),
    )
    recv_a, recv_b = neighbours(send_a, send_b, "strip")
    q, col_a, col_b = merge_rows(strips, place, send_a, mid, send_b, recv_a, recv_b, halo)
    recv_a, recv_b = neighbours(col_a, col_b, "frame")
    k1x, k1, k11_part = merge_cols(n, rows, place, q, recv_a, recv_b, k0x, halo)

    send_a, mid, send_b, stat2 = apply_terms(
        n, place, (k1x,), mats, weights, moved, slots + late_slots, halo, halo
    )
    recv_a, recv_b = neighbours(send_a, send_b, "strip")
    sums = jnp.stack([k00_part, stat1, k11_part, stat2])
    for axis, size in (("frame", n), ("strip", strips)):
        d = 1
        while d < size:
            sums = sums + swap(sums, axis, d)
            d *= 2
    k2 = wrap(place, send_a, mid, send_b, recv_a, recv_b, k1, halo)

    def gathered(x):
        parts = [x] + [None] * (n - 1)
        for i in range(n):
            for d in reversed(distances):
                if i % (2 * d) == 0:
                    parts[i + d] = swap(parts[i], "frame", d)
        return parts

    g0, g1, g2 = gathered(k0), gathered(k1), gathered(k2)
    result, base, coef = solution_image(place, estimate, sums, g0, g1)
    return result, residual_image(place, base, coef, g2, halo)


def solution(mesh):
    return jax.shard_map(
        steps,
        mesh=mesh,
        in_specs=(
            P("strip", None),
            P("frame", "strip", None),
            P("frame", "strip", None),
            P("frame", None),
            P("frame", None),
        ),
        out_specs=(P("strip", None), P("strip", None)),
        check_vma=False,
    )
```

```python
import functools

import jax
import jax.numpy as jnp
from jax import lax
from jax.experimental import pallas as pl
from jax.experimental.pallas import tpu as pltpu
from jax.sharding import PartitionSpec as P


damping = 0.05
f32 = jnp.float32
bf16 = jnp.bfloat16
LANE = 128
VMEM = pl.BlockSpec(memory_space=pltpu.VMEM)
ANY = pl.BlockSpec(memory_space=pl.ANY)
SMEM = pl.BlockSpec(memory_space=pltpu.SMEM)
HBM = pl.BlockSpec(memory_space=pltpu.HBM)


def room(mib):
    return pltpu.CompilerParams(vmem_limit_bytes=mib * 2**20)


def split(x):
    hi = x.astype(bf16)
    lo = (x - hi.astype(f32)).astype(bf16)
    return hi, lo


def dot(a, b):
    return jnp.dot(a, b, preferred_element_type=f32)


def choose(flag, a, b):
    return jnp.where(jnp.full(a.shape, flag, jnp.int32) == 1, a, b)


def pack_edge(edge, halo, w):
    rows = edge.shape[0]
    per = LANE // (2 * halo)
    short = rows * 2 * halo // w
    edge = pltpu.roll(edge, halo, 1)
    lane = lax.broadcasted_iota(jnp.int32, (short, LANE), 1)
    out = []
    for t in range(w // LANE):
        tile = None
        for p in range(per):
            k = t * per + p
            part = edge[k * short : (k + 1) * short]
            part = pltpu.roll(part, p * 2 * halo, 1) if p else part
            tile = part if tile is None else jnp.where(lane >= p * 2 * halo, part, tile)
        out.append(tile)
    return jnp.concatenate(out, axis=1)


def unpack_edge(packed, halo):
    _, w = packed.shape
    per = LANE // (2 * halo)
    parts = []
    for k in range(w // (2 * halo)):
        t, p = divmod(k, per)
        part = packed[:, t * LANE : (t + 1) * LANE]
        back = (LANE - halo - p * 2 * halo) % LANE
        parts.append(pltpu.roll(part, back, 1) if back else part)
    return jnp.concatenate(parts, axis=0)


def tiles(width, step=256):
    return [(s, min(step, width - s)) for s in range(0, width, step)]


def toeplitz(base, count):
    wide = base.shape[1]
    return pltpu.roll(jnp.broadcast_to(base, (count, wide)), 0, 1, stride=1, stride_axis=0)


def build_group(taps, g, frames, rows, halo, t_ref, b_ref, bp_ref, ta_ref):
    ext = rows + 2 * halo
    unit = taps / jnp.sum(taps, axis=1, keepdims=True)
    for s in range(frames):
        f = g * frames + s
        col = unit[s : s + 1]
        row = unit[frames + s : frames + s + 1]
        by_rows = toeplitz(row, rows)
        hi, lo = split(by_rows)
        t_ref[f, :rows, :] = hi
        t_ref[f, rows:, :] = lo
        hi, lo = split(by_rows.T[:ext])
        ta_ref[g, :ext, s * rows : (s + 1) * rows] = hi
        ta_ref[g, ext:, s * rows : (s + 1) * rows] = lo
        hi, lo = split(toeplitz(col, LANE).T)
        b_ref[f, :, :LANE] = hi
        b_ref[f, :, LANE:] = lo
        hi, lo = split(toeplitz(pltpu.roll(col, LANE, 1), 2 * LANE)[:, :LANE])
        bp_ref[f, :, :LANE] = hi
        bp_ref[f, :, LANE:] = lo


def matrix_shapes(groups, frames, rows, halo):
    ext = rows + 2 * halo
    return [
        jax.ShapeDtypeStruct(s, bf16)
        for s in (
            (groups * frames, 2 * rows, 2 * LANE),
            (groups * frames, 2 * LANE, 2 * LANE),
            (groups * frames, 2 * LANE, 2 * LANE),
            (groups, 2 * ext, frames * rows),
        )
    ]


def tile_height(frames):
    return -(-2 * frames // 8) * 8


def setup_kernel(frames, rows, halo, starts, *refs):
    tiles_in = refs[: len(starts)]
    mats, taps, sem = refs[len(starts) : -2], refs[-2], refs[-1]
    height = tile_height(frames)

    def copy(g):
        source = tiles_in[g].at[pl.ds(starts[g], height), pl.ds(0, 2 * LANE)]
        return pltpu.make_async_copy(source, taps.at[g], sem.at[g])

    for g in range(len(starts)):
        copy(g).start()
    for g in range(len(starts)):
        copy(g).wait()
        build_group(taps[g], g, frames, rows, halo, *mats)


def setup_matrices(tiles_in, starts, frames, rows, halo):
    groups = len(tiles_in)
    return pl.pallas_call(
        functools.partial(setup_kernel, frames, rows, halo, starts),
        out_shape=matrix_shapes(groups, frames, rows, halo),
        in_specs=[ANY] * groups,
        out_specs=[VMEM] * 4,
        scratch_shapes=[
            pltpu.VMEM((groups, tile_height(frames), 2 * LANE), f32),
            pltpu.SemaphoreType.DMA((groups,)),
        ],
        compiler_params=room(24),
        name="setup_all",
    )(*tiles_in)


def load_image(y_hi, y_lo, image, halo):
    ext, full = image.shape
    shift = LANE - halo
    y = pltpu.roll(image, full - shift, 1)[:, : full - LANE]
    hi, lo = split(y)
    y_hi[:ext, :] = hi
    y_lo[:ext, :] = lo


def three_products(left, hi, lo, rows, c, size):
    span = slice(c, c + size)
    if size == LANE:
        r = dot(left[...], jnp.concatenate([hi[:, span], lo[:, span]], axis=1))
        return r[:rows, :LANE] + r[rows:, :LANE] + r[:rows, LANE:]
    r = dot(left[...], hi[:, span])
    return r[:rows] + r[rows:] + dot(left[:rows, :], lo[:, span])


def group_terms(frames, rows, w, y_hi, y_lo, t, b, bp, ta, weight, data, us, qs, vs_hi, vs_lo, acc, stat, ready=None):
    total = None
    for f in range(frames):
        for c, size in tiles(w + LANE):
            r = three_products(t(f), y_hi, y_lo, rows, c, size)
            hi, lo = split(r)
            us[:rows, c : c + size] = hi
            us[rows:, c : c + size] = lo
        if ready is not None:
            ready(f)
        for k in range(w // LANE):
            c = k * LANE
            r = dot(us[:, c : c + 2 * LANE], b(f)[...])
            a = r[:rows, :LANE] + r[:rows, LANE:] + r[rows:, :LANE]
            if data is not None:
                a = a - data(f)[:, c : c + LANE]
            q = weight(f)[:, c : c + LANE] * a
            if stat is not None:
                part = jnp.sum((a * q).reshape(rows // 8, 8, LANE), axis=0)
                total = part if total is None else total + part
            hi, lo = split(q)
            qs[:rows, c + LANE : c + 2 * LANE] = hi
            qs[rows:, c + LANE : c + 2 * LANE] = lo
        for k in range(w // LANE + 1):
            c = k * LANE
            r = dot(qs[:, c : c + 2 * LANE], bp(f)[...])
            hi, lo = split(r[:rows, :LANE] + r[:rows, LANE:] + r[rows:, :LANE])
            vs_hi[f * rows : (f + 1) * rows, c : c + LANE] = hi
            vs_lo[f * rows : (f + 1) * rows, c : c + LANE] = lo
    ext = acc.shape[0]
    for c, size in tiles(w + LANE):
        acc[:, c : c + size] += three_products(ta, vs_hi, vs_lo, ext, c, size)
    if stat is not None:
        stat[...] += total


def work_scratch(frames, rows, halo, w):
    ext = rows + 2 * halo
    return [
        pltpu.VMEM((2 * LANE, w + LANE), bf16),
        pltpu.VMEM((2 * LANE, w + LANE), bf16),
        pltpu.VMEM((2 * rows, w + LANE), bf16),
        pltpu.VMEM((2 * rows, w + 2 * LANE), bf16),
        pltpu.VMEM((frames * rows, w + LANE), bf16),
        pltpu.VMEM((frames * rows, w + LANE), bf16),
        pltpu.VMEM((ext, w + LANE), f32),
    ]


def clear_edges(y_hi, y_lo, qs, ext, rows, w):
    zero = jnp.zeros((y_hi.shape[0] - ext, y_hi.shape[1]), bf16)
    y_hi[ext:, :] = zero
    y_lo[ext:, :] = zero
    qs[:, :LANE] = jnp.zeros((2 * rows, LANE), bf16)
    qs[:, w + LANE :] = jnp.zeros((2 * rows, LANE), bf16)


def unshift(acc, halo):
    return pltpu.roll(acc, acc.shape[1] - halo, 1)


def first_kernel(
    frames, rows, halo,
    place, est, recv_a, recv_b, t_ref, b_ref, bp_ref, ta_ref, w_hbm, d_hbm,
    send_a, mid, send_b,
    y_hi, y_lo, us, qs, vs_hi, vs_lo, acc, wbuf, dbuf, sem,
):
    ext = rows + 2 * halo
    cols = est.shape[1]
    copies = [
        (
            pltpu.make_async_copy(w_hbm.at[f], wbuf.at[f], sem.at[0, f]),
            pltpu.make_async_copy(d_hbm.at[f], dbuf.at[f], sem.at[1, f]),
        )
        for f in range(frames)
    ]
    for pair in copies:
        for c in pair:
            c.start()
    clear_edges(y_hi, y_lo, qs, ext, rows, cols)
    odd = lax.rem(place[1], 2)
    none = jnp.zeros((ext, LANE), f32)
    for start in range(0, cols, 4 * LANE):
        size = 4 * LANE + LANE
        left = max(start - LANE, 0)
        span = slice(left, min(start + 4 * LANE, cols))
        x = jnp.concatenate(
            [
                choose(odd, recv_a[:, span], recv_b[:, span]),
                est[:, span],
                choose(odd, recv_b[:, span], recv_a[:, span]),
            ],
            axis=0,
        )
        if start == 0:
            x = jnp.concatenate([none, x], axis=1)
        if x.shape[1] < size:
            x = jnp.concatenate([x, jnp.zeros((ext, size - x.shape[1]), f32)], axis=1)
        hi, lo = split(pltpu.roll(x, halo, 1)[:, LANE:])
        y_hi[:ext, start : start + 4 * LANE] = hi
        y_lo[:ext, start : start + 4 * LANE] = lo
        if start + 4 * LANE >= cols:
            tail = jnp.concatenate([x[:, 4 * LANE :], none], axis=1)
            hi, lo = split(pltpu.roll(tail, halo, 1)[:, LANE:])
            y_hi[:ext, cols:] = hi
            y_lo[:ext, cols:] = lo
    acc[...] = jnp.zeros_like(acc)

    def ready(f):
        for c in copies[f]:
            c.wait()

    group_terms(
        frames, rows, cols, y_hi, y_lo,
        lambda f: t_ref.at[f], lambda f: b_ref.at[f], lambda f: bp_ref.at[f], ta_ref.at[0],
        lambda f: wbuf.at[f], lambda f: dbuf.at[f],
        us, qs, vs_hi, vs_lo, acc, None, ready,
    )
    for start in range(0, cols, 4 * LANE):
        size = min(4 * LANE, cols - start)
        z = pltpu.roll(acc[:, start : start + size + LANE], size + LANE - halo, 1)[:, :size]
        span = slice(start, start + size)
        low, high = z[:halo], z[halo + rows :]
        send_a[:, span] = choose(odd, low, high)
        send_b[:, span] = choose(odd, high, low)
        mid[:, span] = z[halo : halo + rows]


def first_terms(place, est, recv_a, recv_b, mats, weights, observed):
    frames, rows, cols = weights.shape
    halo = recv_a.shape[0]
    return pl.pallas_call(
        functools.partial(first_kernel, frames, rows, halo),
        out_shape=[
            jax.ShapeDtypeStruct((halo, cols), f32),
            jax.ShapeDtypeStruct((rows, cols), f32),
            jax.ShapeDtypeStruct((halo, cols), f32),
        ],
        in_specs=[SMEM] + [VMEM] * 7 + [HBM, HBM],
        out_specs=[VMEM] * 3,
        scratch_shapes=work_scratch(frames, rows, halo, cols)
        + [
            pltpu.VMEM((frames, rows, cols), f32),
            pltpu.VMEM((frames, rows, cols), f32),
            pltpu.SemaphoreType.DMA((2, frames)),
        ],
        cost_estimate=pl.CostEstimate(flops=8 * 10**9, bytes_accessed=8 * 2**20, transcendentals=0),
        compiler_params=room(36),
        name="first_terms",
    )(place, est, recv_a, recv_b, *mats, weights, observed)


def prepare_kernel(plan, frames, rows, halo, w, place, cols_in, rows_in, weights, *refs):
    outs, tile, mats = refs[: len(plan)], refs[len(plan)], refs[len(plan) + 1 : -4]
    cols_buf, rows_buf, taps_sem, sem = refs[-4:]
    taps = cols_in.shape[1]
    taps_copies = (
        pltpu.make_async_copy(cols_in, cols_buf, taps_sem.at[0]),
        pltpu.make_async_copy(rows_in, rows_buf, taps_sem.at[1]),
    )
    for copy in taps_copies:
        copy.start()
    pending = []
    for i, (distance, _) in enumerate(plan):
        start = pl.multiple_of(jnp.bitwise_xor(place[0], distance) * w, LANE)
        for k in range(frames):
            copy = pltpu.make_async_copy(
                weights.at[k, :, pl.ds(start, w)],
                outs[i].at[pl.ds(k * rows, rows), :],
                sem.at[i, k],
            )
            copy.start()
            pending.append(copy)
    tile[...] = jnp.zeros_like(tile)
    for copy in taps_copies:
        copy.wait()
    tile[:frames, :taps] = cols_buf[...]
    tile[frames : 2 * frames, :taps] = rows_buf[...]
    for i, (_, with_taps) in enumerate(plan):
        if with_taps:
            outs[i][frames * rows :, :] = tile[...]
    build_group(tile[:, : 2 * LANE], 0, frames, rows, halo, *mats)
    for copy in pending:
        copy.wait()


def prepare(plan, place, column_kernels, row_kernels, weights, w, halo):
    frames, rows, _ = weights.shape
    height = tile_height(frames)
    out = pl.pallas_call(
        functools.partial(prepare_kernel, plan, frames, rows, halo, w),
        out_shape=[
            jax.ShapeDtypeStruct((frames * rows + (height if taps else 0), w), f32)
            for _, taps in plan
        ]
        + [jax.ShapeDtypeStruct((height, w), f32)]
        + matrix_shapes(1, frames, rows, halo),
        in_specs=[SMEM, HBM, HBM, HBM],
        out_specs=[VMEM] * (len(plan) + 5),
        scratch_shapes=[
            pltpu.VMEM(column_kernels.shape, f32),
            pltpu.VMEM(row_kernels.shape, f32),
            pltpu.SemaphoreType.DMA((2,)),
            pltpu.SemaphoreType.DMA((len(plan), frames)),
        ],
        compiler_params=room(24),
        name="prepare",
    )(place, column_kernels, row_kernels, weights)
    return out[: len(plan)], out[len(plan)], out[len(plan) + 1 :]


def blocks_kernel(n, halo, w, place, send_a, mid, send_b, recv_a, recv_b, *refs):
    outs, full = refs[:-1], refs[-1]
    rows, cols = mid.shape
    odd = lax.rem(place[1], 2)
    inner = slice(LANE, LANE + cols)
    for end in (0, LANE + cols):
        full[:, end : end + LANE] = jnp.zeros((rows, LANE), f32)
    full[:halo, inner] = mid[:halo, :] + choose(odd, recv_a[...], recv_b[...])
    full[halo : rows - halo, inner] = mid[halo : rows - halo, :]
    full[rows - halo :, inner] = mid[rows - halo :, :] + choose(odd, recv_b[...], recv_a[...])
    lane = lax.broadcasted_iota(jnp.int32, (rows, LANE), 1)
    for i in range(n):
        start = jnp.bitwise_xor(place[0], i) * w
        outs[i][:rows, :] = full[:, pl.ds(pl.multiple_of(start + LANE, LANE), w)]
        before = full[:, pl.ds(pl.multiple_of(start, LANE), LANE)]
        after = full[:, pl.ds(pl.multiple_of(start + LANE + w, LANE), LANE)]
        outs[i][rows:, :] = pack_edge(jnp.where(lane >= LANE - halo, before, after), halo, w)


def column_blocks(n, place, send_a, mid, send_b, recv_a, recv_b, w):
    rows, cols = mid.shape
    halo = send_a.shape[0]
    height = rows + rows * 2 * halo // w
    return pl.pallas_call(
        functools.partial(blocks_kernel, n, halo, w),
        out_shape=[jax.ShapeDtypeStruct((height, w), f32)] * n,
        in_specs=[SMEM] + [VMEM] * 5,
        out_specs=[VMEM] * n,
        scratch_shapes=[pltpu.VMEM((rows, cols + 2 * LANE), f32)],
        compiler_params=room(16),
        name="column_blocks",
    )(place, send_a, mid, send_b, recv_a, recv_b)


def start_kernel(n, rows, halo, w, place, est, *refs):
    parts = refs[:-5]
    k0, wide, send_a, send_b, stat = refs[-5:]
    total = parts[0][...]
    for p in parts[1:]:
        total = total + p[...]
    me = place[0]
    odd = lax.rem(place[1], 2)
    at = lambda start, size: est[:, pl.ds(pl.multiple_of(start, LANE), size)]
    own = -(total[:rows] + damping * at(me * w, w))
    edge = unpack_edge(total[rows:], halo)
    before = at(jnp.maximum(me * w - LANE, 0), LANE)
    after = at(jnp.minimum(me * w + w, (n * w) - LANE), LANE)
    none = jnp.zeros((rows, LANE), f32)
    left = choose((me > 0).astype(jnp.int32), -(edge + damping * before), none)
    right = choose((me < n - 1).astype(jnp.int32), -(edge + damping * after), none)
    k0[...] = own
    wide[:, :LANE] = left
    wide[:, LANE : LANE + w] = own
    wide[:, LANE + w :] = right
    low, high = wide[:halo, :], wide[rows - halo :, :]
    send_a[...] = choose(odd, low, high)
    send_b[...] = choose(odd, high, low)
    square = own * own
    acc = square[:, :LANE]
    for c in range(LANE, w, LANE):
        acc = acc + square[:, c : c + LANE]
    stat[...] = jnp.sum(acc.reshape(rows // 8, 8, LANE), axis=0)


def start_image(n, place, est, parts, halo):
    rows, cols = est.shape
    w = cols // n
    return pl.pallas_call(
        functools.partial(start_kernel, n, rows, halo, w),
        out_shape=[
            jax.ShapeDtypeStruct((rows, w), f32),
            jax.ShapeDtypeStruct((rows, w + 2 * LANE), f32),
            jax.ShapeDtypeStruct((halo, w + 2 * LANE), f32),
            jax.ShapeDtypeStruct((halo, w + 2 * LANE), f32),
            jax.ShapeDtypeStruct((8, LANE), f32),
        ],
        in_specs=[SMEM] + [VMEM] * (1 + len(parts)),
        out_specs=[VMEM] * 5,
        compiler_params=room(12),
        name="start_image",
    )(place, est, *parts)


def apply_kernel(n, frames, rows, halo, w, slots, cut, count, pieces, carried, place, *refs):
    image, refs = refs[:pieces], refs[pieces:]
    t_hbm, b_hbm, bp_hbm, ta_hbm, own = refs[:5]
    moved, refs = refs[5 : 5 + count], refs[5 + count :]
    if carried:
        (acc_in, stat_in), refs = refs[:2], refs[2:]
    if cut is None:
        (acc_out, stat), refs = refs[:2], refs[2:]
    else:
        (send_a, mid, send_b, stat), refs = refs[:4], refs[4:]
    if pieces > 1:
        whole, refs = refs[0], refs[1:]
    y_hi, y_lo, us, qs, vs_hi, vs_lo, acc, tb, bb, bpb, tab, wbuf, sem, wsem = refs
    odd = lax.rem(place[1], 2)
    ext = rows + 2 * halo
    quarter = n // 4
    inner = ((place[0] >= quarter) & (place[0] < n - quarter)).astype(jnp.int32)

    def copies(i, g):
        span = pl.ds(g * frames, frames)
        return [
            pltpu.make_async_copy(t_hbm.at[span], tb.at[i], sem.at[0, i]),
            pltpu.make_async_copy(b_hbm.at[span], bb.at[i], sem.at[1, i]),
            pltpu.make_async_copy(bp_hbm.at[span], bpb.at[i], sem.at[2, i]),
            pltpu.make_async_copy(ta_hbm.at[g], tab.at[i], sem.at[3, i]),
        ]

    mine = pl.ds(pl.multiple_of(place[0] * w, LANE), w)
    for i, (distance, late, sources) in enumerate(slots):
        if len(sources) == 2:
            group = distance + (1 - inner if late else inner) * quarter
        else:
            group = distance
        for c in copies(i, group):
            c.start()
        for f in range(frames):
            span = pl.ds(f * rows, rows)
            if not sources:
                pltpu.make_async_copy(own.at[f, :, mine], wbuf.at[i, f], wsem.at[i, f]).start()
            elif len(sources) == 1:
                source = moved[sources[0]].at[span, :]
                pltpu.make_async_copy(source, wbuf.at[i, f], wsem.at[i, f]).start()
            else:
                for k in range(2):

                    @pl.when((group - distance) == k * quarter)
                    def _(source=moved[sources[k]].at[span, :], i=i, f=f):
                        pltpu.make_async_copy(source, wbuf.at[i, f], wsem.at[i, f]).start()

    clear_edges(y_hi, y_lo, qs, ext, rows, w)
    if pieces > 1:
        wide, recv_a, recv_b = image
        whole[:halo, :] = choose(odd, recv_a[...], recv_b[...])
        whole[halo : halo + rows, :] = wide[...]
        whole[halo + rows :, :] = choose(odd, recv_b[...], recv_a[...])
        load_image(y_hi, y_lo, whole[...], halo)
    else:
        load_image(y_hi, y_lo, image[0][...], halo)
    acc[...] = acc_in[...] if carried else jnp.zeros_like(acc)
    stat[...] = stat_in[...] if carried else jnp.zeros_like(stat)

    @pl.loop(0, len(slots))
    def _(i):
        for c in copies(i, 0):
            c.wait()
        for f in range(frames):
            pltpu.make_async_copy(own.at[f, :, mine], wbuf.at[i, f], wsem.at[i, f]).wait()
        group_terms(
            frames, rows, w, y_hi, y_lo,
            lambda f: tb.at[i, f], lambda f: bb.at[i, f], lambda f: bpb.at[i, f], tab.at[i],
            lambda f: wbuf.at[i, f], None,
            us, qs, vs_hi, vs_lo, acc, stat,
        )

    if cut is None:
        acc_out[...] = acc[...]
    else:
        z = unshift(acc[...], halo)
        send_a[...] = choose(odd, z[:cut], z[ext - cut :])
        send_b[...] = choose(odd, z[ext - cut :], z[:cut])
        mid[...] = z[cut : ext - cut]


def apply_terms(n, place, image, mats, weights, moved, slots, cut, halo, carry=()):
    frames, rows, _ = weights.shape
    w = image[0].shape[1] - 2 * LANE
    ext = rows + 2 * halo
    t, b, bp, ta = mats
    count = len(slots)
    wide = w + LANE
    shapes = [(ext, wide)] if cut is None else [(cut, wide), (ext - 2 * cut, wide), (cut, wide)]
    shapes += [(8, LANE)] + [(ext, w + 2 * LANE)] * (len(image) > 1)
    return pl.pallas_call(
        functools.partial(
            apply_kernel, n, frames, rows, halo, w, slots, cut, len(moved), len(image), bool(carry)
        ),
        out_shape=[jax.ShapeDtypeStruct(s, f32) for s in shapes],
        in_specs=[SMEM]
        + [VMEM] * len(image)
        + [ANY] * 4
        + [HBM]
        + [ANY] * len(moved)
        + [VMEM] * len(carry),
        out_specs=[VMEM] * len(shapes),
        scratch_shapes=work_scratch(frames, rows, halo, w)
        + [
            pltpu.VMEM((count, frames) + t.shape[1:], bf16),
            pltpu.VMEM((count, frames) + b.shape[1:], bf16),
            pltpu.VMEM((count, frames) + bp.shape[1:], bf16),
            pltpu.VMEM((count,) + ta.shape[1:], bf16),
            pltpu.VMEM((count, frames, rows, w), f32),
            pltpu.SemaphoreType.DMA((4, count)),
            pltpu.SemaphoreType.DMA((count, frames)),
        ],
        cost_estimate=pl.CostEstimate(
            flops=count * 3 * 10**9, bytes_accessed=count * 2**20, transcendentals=0
        ),
        compiler_params=room(28),
    )(place, *image, t, b, bp, ta, weights, *moved, *carry)


def rows_kernel(strips, halo, w, place, send_a, mid, send_b, recv_a, recv_b, q, col_a, col_b):
    odd = lax.rem(place[1], 2)
    odd_col = lax.rem(place[0], 2)
    edge_rows, wide = send_a.shape
    ext = q.shape[0]
    row = lax.broadcasted_iota(jnp.int32, (edge_rows, wide), 0)
    strip = jnp.full((edge_rows, wide), place[1], jnp.int32)
    low = choose(odd, send_a[...], send_b[...]) + choose(odd, recv_a[...], recv_b[...])
    high = choose(odd, send_b[...], send_a[...]) + choose(odd, recv_b[...], recv_a[...])
    q[:edge_rows, :] = jnp.where((row >= halo) | (strip > 0), low, 0.0)
    q[edge_rows : ext - edge_rows, :] = mid[...]
    q[ext - edge_rows :, :] = jnp.where((row < edge_rows - halo) | (strip < strips - 1), high, 0.0)
    lane = lax.broadcasted_iota(jnp.int32, (ext, LANE), 1)
    edge = q[:, w:]
    to_left = jnp.where(lane < halo, q[:, :LANE], edge)
    to_right = jnp.where(lane >= LANE - halo, q[:, w - LANE : w], edge)
    col_a[...] = choose(odd_col, to_left, to_right)
    col_b[...] = choose(odd_col, to_right, to_left)


def merge_rows(strips, place, send_a, mid, send_b, recv_a, recv_b, halo):
    ext = mid.shape[0] + 2 * send_a.shape[0]
    wide = mid.shape[1]
    return pl.pallas_call(
        functools.partial(rows_kernel, strips, halo, wide - LANE),
        out_shape=[
            jax.ShapeDtypeStruct((ext, wide), f32),
            jax.ShapeDtypeStruct((ext, LANE), f32),
            jax.ShapeDtypeStruct((ext, LANE), f32),
        ],
        in_specs=[SMEM] + [VMEM] * 5,
        out_specs=[VMEM] * 3,
        compiler_params=room(8),
        name="merge_rows",
    )(place, send_a, mid, send_b, recv_a, recv_b)


def cols_kernel(n, rows, halo, place, q, recv_a, recv_b, before, out, block, stat):
    odd = lax.rem(place[0], 2)
    ext, wide = q.shape
    w = wide - LANE
    lane = lax.broadcasted_iota(jnp.int32, (ext, LANE), 1)
    at = jnp.full((ext, LANE), place[0], jnp.int32)
    left = choose(odd, recv_a[...], recv_b[...])
    right = choose(odd, recv_b[...], recv_a[...])
    edge = q[:, w:]
    total = None
    out[:, :LANE] = jnp.where(at > 0, edge + left, 0.0) + damping * before[:, :LANE]
    out[:, LANE + w :] = jnp.where(at < n - 1, edge + right, 0.0) + damping * before[:, LANE + w :]
    for c in range(0, w, LANE):
        x = q[:, c : c + LANE] + damping * before[:, c + LANE : c + 2 * LANE]
        if c == 0:
            x = x + jnp.where(lane < halo, left, 0.0)
        if c == w - LANE:
            x = x + jnp.where(lane >= LANE - halo, right, 0.0)
        out[:, c + LANE : c + 2 * LANE] = x
        own = x[halo : halo + rows]
        block[:, c : c + LANE] = own
        part = jnp.sum((own * own).reshape(rows // 8, 8, LANE), axis=0)
        total = part if total is None else total + part
    stat[...] = total


def merge_cols(n, rows, place, q, recv_a, recv_b, before, halo):
    ext, wide = q.shape
    w = wide - LANE
    return pl.pallas_call(
        functools.partial(cols_kernel, n, rows, halo),
        out_shape=[
            jax.ShapeDtypeStruct((ext, w + 2 * LANE), f32),
            jax.ShapeDtypeStruct((rows, w), f32),
            jax.ShapeDtypeStruct((8, LANE), f32),
        ],
        in_specs=[SMEM] + [VMEM] * 4,
        out_specs=[VMEM] * 3,
        compiler_params=room(10),
        name="merge_cols",
    )(place, q, recv_a, recv_b, before)


def wrap_kernel(rows, halo, w, place, send_a, mid, send_b, recv_a, recv_b, before, out):
    odd = lax.rem(place[1], 2)
    keep = rows - 2 * halo
    pieces = (
        (0, halo, mid[:halo, :] + choose(odd, recv_a[...], recv_b[...])),
        (halo, keep, mid[halo : rows - halo, :]),
        (rows - halo, halo, mid[rows - halo :, :] + choose(odd, recv_b[...], recv_a[...])),
    )
    edges = []
    for start, size, value in pieces:
        span = slice(start, start + size)
        out[span, :] = value[:, :w] + damping * before[span, :]
        edges.append(value[:, w:])
    out[rows:, :] = pack_edge(jnp.concatenate(edges, axis=0), halo, w)


def wrap(place, send_a, mid, send_b, recv_a, recv_b, before, halo):
    rows, w = before.shape
    height = rows + rows * 2 * halo // w
    return pl.pallas_call(
        functools.partial(wrap_kernel, rows, halo, w),
        out_shape=jax.ShapeDtypeStruct((height, w), f32),
        in_specs=[SMEM] + [VMEM] * 6,
        out_specs=VMEM,
        compiler_params=room(8),
        name="wrap",
    )(place, send_a, mid, send_b, recv_a, recv_b, before)


def solution_kernel(n, w, place, est, sums, *refs):
    k0, k1 = refs[:n], refs[n : 2 * n]
    sol, res, coef = refs[2 * n :]
    total = [
        jnp.sum(jnp.sum(sums[i], axis=0, keepdims=True), axis=1, keepdims=True) for i in range(4)
    ]
    k00, k11 = total[0], total[2]
    k01 = total[1] + damping * k00
    k12 = total[3] + damping * k11
    alpha0 = k00 / k01
    norm1 = k00 - 2.0 * alpha0 * k01 + alpha0 * alpha0 * k11
    beta = norm1 / k00
    curve1 = (1.0 + beta) * (1.0 + beta) * k01 - 2.0 * (1.0 + beta) * alpha0 * k11
    curve1 = curve1 + alpha0 * alpha0 * k12
    alpha1 = norm1 / curve1
    c1 = alpha0 + alpha1 * (1.0 + beta)
    c2 = alpha0 * alpha1
    coef[...] = jnp.broadcast_to(c2, coef.shape)
    for i in range(n):
        cols = pl.ds(pl.multiple_of(jnp.bitwise_xor(place[0], i) * w, LANE), w)
        a0, a1 = k0[i][...], k1[i][...]
        sol[:, cols] = est[:, cols] + c1 * a0 - c2 * a1
        res[:, cols] = a0 - c1 * a1


def solution_image(place, est, sums, k0, k1):
    n = len(k0)
    w = k0[0].shape[1]
    return pl.pallas_call(
        functools.partial(solution_kernel, n, w),
        out_shape=[jax.ShapeDtypeStruct(est.shape, f32)] * 2
        + [jax.ShapeDtypeStruct((8, LANE), f32)],
        in_specs=[SMEM] + [VMEM] * (2 + 2 * n),
        out_specs=[VMEM] * 3,
        compiler_params=room(20),
        name="solution_image",
    )(place, est, sums, *k0, *k1)


def residual_kernel(n, rows, halo, w, place, base, coef, *refs):
    k2, (res, full) = refs[:n], refs[n:]
    c2 = coef[0:1, 0:1]
    lane = lax.broadcasted_iota(jnp.int32, (rows, LANE), 1)
    spot = [jnp.bitwise_xor(place[0], i) for i in range(n)]
    full[:, :LANE] = jnp.zeros((rows, LANE), f32)
    full[:, LANE + n * w :] = jnp.zeros((rows, LANE), f32)
    for i in range(n):
        full[:, pl.ds(pl.multiple_of(spot[i] * w + LANE, LANE), w)] = k2[i][:rows, :]
    for i in range(n):
        edge = unpack_edge(k2[i][rows:, :], halo)
        left = pl.ds(pl.multiple_of(spot[i] * w, LANE), LANE)
        right = pl.ds(pl.multiple_of(spot[i] * w + w + LANE, LANE), LANE)
        full[:, left] += jnp.where(lane >= LANE - halo, edge, 0.0)
        full[:, right] += jnp.where(lane < halo, edge, 0.0)
    for c in range(0, n * w, LANE):
        res[:, c : c + LANE] = base[:, c : c + LANE] + c2 * full[:, c + LANE : c + 2 * LANE]


def residual_image(place, base, coef, k2, halo):
    n = len(k2)
    rows, cols = base.shape
    w = cols // n
    return pl.pallas_call(
        functools.partial(residual_kernel, n, rows, halo, w),
        out_shape=jax.ShapeDtypeStruct(base.shape, f32),
        in_specs=[SMEM] + [VMEM] * (2 + n),
        out_specs=VMEM,
        scratch_shapes=[pltpu.VMEM((rows, cols + 2 * LANE), f32)],
        compiler_params=room(16),
        name="residual_image",
    )(place, base, coef, *k2)


def neighbours(send_a, send_b, axis):
    n = lax.axis_size(axis)
    out = []
    for lead, x in ((0, send_a), (1, send_b)):
        pairs = [(i, i + 1) for i in range(lead, n - 1, 2)]
        out.append(lax.ppermute(x, axis, pairs + [(b, a) for a, b in pairs]))
    return out


def swap(x, axis, distance):
    n = lax.axis_size(axis)
    return lax.ppermute(x, axis, [(i, i ^ distance) for i in range(n)])


def steps(estimate, observed, weights, column_kernels, row_kernels):
    n = lax.axis_size("frame")
    me = lax.axis_index("frame")
    strips = lax.axis_size("strip")
    strip = lax.axis_index("strip")
    place = jnp.stack([me, strip]).astype(jnp.int32)
    rows, cols = estimate.shape
    frames = weights.shape[0]
    halo = column_kernels.shape[1] // 2
    stay = lambda x: pltpu.with_memory_space_constraint(x, pltpu.HBM)
    weights, observed = stay(weights), stay(observed)
    column_kernels, row_kernels = stay(column_kernels), stay(row_kernels)
    w = cols // n
    distances = [1 << k for k in range(n.bit_length() - 1)]

    low, high = estimate[:halo], estimate[rows - halo :]
    odd = strip % 2 == 1
    est_a, est_b = neighbours(
        jnp.where(odd, low, high), jnp.where(odd, high, low), "strip"
    )

    half, quarter = n // 2, n // 4
    plan = [(d, d < half) for d in range(1, n)]
    packed, tile, own_mats = prepare(plan, place, column_kernels, row_kernels, weights, w, halo)
    far_tiles = []
    for d in range(half, n):
        far_tiles.append(swap(tile[:, : 2 * LANE], "frame", d))
    moved = []
    slots = [(0, False, ())]
    for d in range(1, half):
        moved.append(swap(packed[d - 1], "frame", d))
        slots.append((d, False, (d - 1,)))
    middle = range(quarter, n - quarter)
    where = {}
    for late in (False, True):
        for d in range(half, n):
            pairs = [(i, i ^ d) for i in range(n) if (i in middle) != late]
            where[d, late] = len(moved)
            moved.append(lax.ppermute(packed[d - 1], "frame", pairs))
    late_slots = []
    for late, out in ((False, slots), (True, late_slots)):
        for u in range(half, half + quarter):
            out.append((u, late, (where[u, late], where[u + quarter, late])))
    starts = [0] + [frames * rows] * (half - 1) + [0] * half

    send_a, mid, send_b = first_terms(
        place, estimate, est_a, est_b, own_mats, weights, observed
    )
    mats = setup_matrices(
        [tile] + moved[: half - 1] + far_tiles, starts, frames, rows, halo
    )
    recv_a, recv_b = neighbours(send_a, send_b, "strip")

    part = list(column_blocks(n, place, send_a, mid, send_b, recv_a, recv_b, w))
    mine = [part[0]]
    for i in range(n - 1, 0, -1):
        d = i & -i
        got = swap(part[i], "frame", d)
        if i == d:
            mine.append(got)
        else:
            part[i ^ d] = part[i ^ d] + got
    k0, wide, send_a, send_b, k00_part = start_image(n, place, estimate, mine, halo)
    recv_a, recv_b = neighbours(send_a, send_b, "strip")

    acc, stat1, k0x = apply_terms(
        n, place, (wide, recv_a, recv_b), mats, weights, moved[: where[half, True]],
        slots, None, halo,
    )
    send_a, mid, send_b, stat1 = apply_terms(
        n, place, (k0x,), mats, weights, moved, late_slots, 2 * halo, halo,
        carry=(acc, stat1),
    )
    recv_a, recv_b = neighbours(send_a, send_b, "strip")
    q, col_a, col_b = merge_rows(strips, place, send_a, mid, send_b, recv_a, recv_b, halo)
    recv_a, recv_b = neighbours(col_a, col_b, "frame")
    k1x, k1, k11_part = merge_cols(n, rows, place, q, recv_a, recv_b, k0x, halo)

    send_a, mid, send_b, stat2 = apply_terms(
        n, place, (k1x,), mats, weights, moved, slots + late_slots, halo, halo
    )
    recv_a, recv_b = neighbours(send_a, send_b, "strip")
    sums = jnp.stack([k00_part, stat1, k11_part, stat2])
    for axis, size in (("frame", n), ("strip", strips)):
        d = 1
        while d < size:
            sums = sums + swap(sums, axis, d)
            d *= 2
    k2 = wrap(place, send_a, mid, send_b, recv_a, recv_b, k1, halo)

    def gathered(x):
        parts = [x] + [None] * (n - 1)
        for i in range(n):
            for d in reversed(distances):
                if i % (2 * d) == 0:
                    parts[i + d] = swap(parts[i], "frame", d)
        return parts

    g0, g1, g2 = gathered(k0), gathered(k1), gathered(k2)
    result, base, coef = solution_image(place, estimate, sums, g0, g1)
    return result, residual_image(place, base, coef, g2, halo)


def solution(mesh):
    return jax.shard_map(
        steps,
        mesh=mesh,
        in_specs=(
            P("strip", None),
            P("frame", "strip", None),
            P("frame", "strip", None),
            P("frame", None),
            P("frame", None),
        ),
        out_specs=(P("strip", None), P("strip", None)),
        check_vma=False,
    )
```
